32 devices in a mesh: dp: 8 (over y, x, core), mp: 4 (over z).
Axes of the slice: x: 2, y: 2, z: 4, core: 2. Of those that a mesh axis runs over, the one named last changes fastest.
Arguments:
- inputs: bfloat16 [8192, 2048], P(('dp', 'mp')), may hold values from -6 to 6
- keys_values: bfloat16 [8192, 2, 2048], P('dp', None, 'mp'), may hold values from -6 to 6
- segment_ids: int32 [8, 1024], P('dp'), may hold values from 0 to 15, never falling along the last dimension, each value on 1 to 512 neighbouring positions
- gain_first: float32 [2048], replicated, may hold values from 0.25 to 1.75
- gain_second: float32 [2048], replicated, may hold values from 0.25 to 1.75
- w_query: bfloat16 [2048, 2048], P('dp', 'mp'), may hold values from -0.125 to 0.125
- w_out: bfloat16 [2048, 2048], P('mp', 'dp'), may hold values from -0.5 to 0.5
- w_gate: bfloat16 [2048, 5504], P('dp', 'mp'), may hold values from -0.125 to 0.125
- w_up: bfloat16 [2048, 5504], P('dp', 'mp'), may hold values from -0.125 to 0.125
- w_down: bfloat16 [5504, 2048], P('mp', 'dp'), may hold values from -0.15625 to 0.15625
- cotangent: bfloat16 [8192, 2048], P(('dp', 'mp')), may hold values from -6 to 6
Outputs:
- output: bfloat16 [8192, 2048], P(('dp', 'mp'))
- grad_input: float32 [8192, 2048], P(('dp', 'mp'))
- grad_kv: float32 [8192, 2, 2048], P('dp', None, 'mp')
- grad_gain_first: float32 [2048], replicated
- grad_gain_second: float32 [2048], replicated
- grad_query: float32 [2048, 2048], P('dp', 'mp')
- grad_out: float32 [2048, 2048], P('mp', 'dp')
- grad_gate: float32 [2048, 5504], P('dp', 'mp')
- grad_up: float32 [2048, 5504], P('dp', 'mp')
- grad_down: float32 [5504, 2048], P('mp', 'dp')
The draws below stay inside these ranges and needn't reach their ends.
Inputs may be any that keep to these rules, and one draw needn't show every extreme that they name: `segment_ids`: along each sequence the id never falls; each of the 16 documents holds 1 to 512 tokens, and one holds exactly 512.
All inputs are finite; a program needn't handle non-finite values.
Results may differ from the reference program's by a relative error of at most 0.017.
Values may be sent and summed in bfloat16 or wider, within the bound.
A program may use at most 192 MiB of HBM per device.

```python
import math
import jax
import jax.numpy as jnp
import numpy as np
from jax import lax

D = 2048
HEAD_DIM = 128
FF = 5504
SEQ_LEN = 1024
TOKENS = 8192
DOCS = 16
DOC_MOST = 512
N_DP = 8


def strengthened(values, rng, source, target, shards_of, factor):
    owner, partner = [(jnp.arange(values.shape[position]) // (values.shape[position] // shards_of)).reshape([-1 if axis == position else 1 for axis in range(values.ndim)]) for position in (source, target)]
    chosen = jax.random.permutation(rng, shards_of)[partner]
    strong = (owner == chosen) | (owner == (partner + shards_of // 2) % shards_of)
    return jnp.where(strong, factor * values, values)


def levels(key, extent, shards, least, largest):
    def one(axis_at, shards_of):
        heights = jax.random.uniform(jax.random.fold_in(jax.random.fold_in(key, 6), axis_at), (shards_of,), jnp.float32, least / len(shards), largest / len(shards))
        return jnp.repeat(jnp.exp(heights), extent[axis_at] // shards_of).reshape((-1,) + (1,) * (len(extent) - axis_at - 1))

    factor_of = one(*shards[0])
    for cut in shards[1:]:
        factor_of = factor_of * one(*cut)
    return factor_of


def length_profile(number_of, total, most, skew):
    weights = [(1 << 20) // math.isqrt(rank ** skew) + 1 for rank in range(2, number_of + 1)]
    rest, holding = total - most - (number_of - 1), [1] * (number_of - 1)
    while rest > 0:
        candidates = [i for i in range(number_of - 1) if holding[i] < most]
        pool, left = sum([weights[i] for i in candidates]), rest
        for i in candidates:
            extra = min(most - holding[i], max(1, left * weights[i] // pool), rest)
            holding[i] = holding[i] + extra
            rest = rest - extra
    return np.array([most] + holding)


def uneven(own_key, number_of, total, most, skew):
    if number_of == 2:
        one = jax.random.randint(own_key, (), max(1, total - most), min(most, total - 1) + 1)
        return jnp.stack([one, total - one])
    sizes = jnp.asarray(length_profile(number_of, total, most, skew), jnp.int32)
    couples = (number_of - 1) // 2
    source_of, receiver = sizes[1:1 + 2 * couples:2], sizes[2:2 + 2 * couples:2]
    slack = jnp.minimum(source_of - 1, most - receiver)
    moved = jax.random.randint(jax.random.fold_in(own_key, 1), (couples,), 0, 1 << 20) % (slack + 1)
    sizes = sizes.at[1:1 + 2 * couples:2].set(source_of - moved).at[2:2 + 2 * couples:2].set(receiver + moved)
    return sizes[jax.random.permutation(jax.random.fold_in(own_key, 2), number_of)]


def noise(stream_key, dims, scale, bound, cuts=(), kind=jnp.bfloat16):
    drawn = jax.random.normal(stream_key, dims, jnp.float32) * scale
    if len(cuts) > 0:
        drawn = levels(stream_key, dims, cuts, -0.22, 0.18) * drawn
    return jnp.clip(drawn, min=-bound, max=bound).astype(kind)


def gaussian_with(key, extent, deviation, bound, split, heavy, kind=jnp.bfloat16):
    values = deviation * jax.random.normal(key, extent, jnp.float32)
    if split:
        values = values * levels(key, extent, split, -0.22, 0.18)
    return jnp.clip(strengthened(values, jax.random.fold_in(key, 3), *heavy), -bound, bound).astype(kind)


def setup_inputs(seed: int = 0) -> dict:
    streams_of = jax.random.split(jax.random.key(seed), 12)
    inputs = gaussian_with(streams_of[0], (TOKENS, D), 1.0, 6.0, ((0, 32),), (0, 1, 32, 2.75))
    keys_values = noise(streams_of[1], (TOKENS, 2, D), 1.0, 6.0, ((0, 8), (2, 4)))
    segment_ids = jax.vmap(lambda own: jnp.searchsorted(jnp.cumsum(uneven(own, DOCS, SEQ_LEN, DOC_MOST, 2)), jnp.arange(SEQ_LEN), side="right"))(jax.random.split(streams_of[2], N_DP)).reshape((N_DP, SEQ_LEN)).astype(jnp.int32)
    gain_first = jnp.clip(1.0 + 0.15 * jax.random.normal(streams_of[3], (D,), jnp.float32), 0.25, 1.75)
    gain_second = jnp.clip(1.0 + 0.15 * jax.random.normal(streams_of[4], (D,), jnp.float32), 0.25, 1.75)
    w_query = noise(streams_of[5], (D, D), D ** -0.5, 0.125, ((0, 8), (1, 4)))
    w_out = noise(streams_of[6], (D, D), (D // 16) ** -0.5, 0.5, ((0, 4), (1, 8)))
    w_gate = noise(streams_of[7], (D, FF), D ** -0.5, 0.125, ((0, 8), (1, 4)))
    w_up = noise(streams_of[8], (D, FF), D ** -0.5, 0.125, ((0, 8), (1, 4)))
    w_down = noise(streams_of[9], (FF, D), (FF // 4) ** -0.5, 0.15625, ((0, 4), (1, 8)))
    cotangent = noise(streams_of[10], (TOKENS, D), 1.0, 6.0, ((0, 32),))
    return {"inputs": inputs, "keys_values": keys_values, "segment_ids": segment_ids, "gain_first": gain_first, "gain_second": gain_second, "w_query": w_query, "w_out": w_out, "w_gate": w_gate, "w_up": w_up, "w_down": w_down, "cotangent": cotangent}


@jax.custom_vjp
def low(v):
    return lax.optimization_barrier(v.astype(jnp.bfloat16)).astype(jnp.float32)

@jax.custom_vjp
def low_back(v):
    return v

def low_keep(v):
    return (low(v), None)

def low_pass(kept, grad):
    return (grad,)

def back_keep(v):
    return (v, None)

def back_low(kept, grad):
    return (low(grad),)
low.defvjp(low_keep, low_pass)
low_back.defvjp(back_keep, back_low)
epsilon = 1e-06

def normalize(values, gain):
    return values * lax.rsqrt(lax.optimization_barrier(jnp.mean(values * values, axis=-1, keepdims=True)) + epsilon) * gain

def matmul(left, right):
    return jnp.dot(left, right, precision=lax.Precision.HIGHEST)

def attend(queries, keys_values, segments):
    length = queries.shape[0]
    block_rows = min(512, length)
    head_count = queries.shape[1] // HEAD_DIM
    score_scale = HEAD_DIM ** (-0.5)
    query_heads = queries.reshape(length, head_count, HEAD_DIM)
    key_heads = keys_values[:, 0, :].reshape(length, head_count, HEAD_DIM)
    value_heads = keys_values[:, 1, :].reshape(length, head_count, HEAD_DIM)
    key_pos = jnp.arange(length, dtype=jnp.int32)

    def one_block(block_index):
        first_row = block_index * block_rows
        query_block = lax.dynamic_slice_in_dim(query_heads, first_row, block_rows, 0)
        query_pos = first_row + jnp.arange(block_rows, dtype=jnp.int32)
        query_seg = lax.dynamic_slice_in_dim(segments, first_row, block_rows, 0)
        scores = jnp.einsum('qhd,khd->hqk', query_block, key_heads, precision=lax.Precision.HIGHEST) * score_scale
        scores = low_back(scores)
        allowed = (query_pos[:, None] >= key_pos[None, :]) & (query_seg[:, None] == segments[None, :])
        scores = jnp.where(allowed[None], scores, -1e+30)
        row_max = lax.optimization_barrier(jnp.max(scores, axis=-1, keepdims=True))
        raised = jnp.exp(scores - row_max)
        weights_low = low(raised / lax.optimization_barrier(jnp.sum(raised, axis=-1, keepdims=True)))
        blended = jnp.einsum('hqk,khd->qhd', weights_low, value_heads, precision=lax.Precision.HIGHEST)
        return blended.reshape(block_rows, head_count * HEAD_DIM)
    blocks = lax.map(jax.checkpoint(one_block), jnp.arange(length // block_rows, dtype=jnp.int32))
    return blocks.reshape(length, head_count * HEAD_DIM)

def layer(tokens, keys_values, segments, gain_first, gain_second, w_query, w_out, w_gate, w_up, w_down):
    normed = low(normalize(tokens, gain_first))
    queries = low(low_back(matmul(normed, w_query)))
    context = low(low_back(attend(queries, keys_values, segments)))
    residual = tokens + low_back(matmul(context, w_out))
    normed_ffn = low(normalize(residual, gain_second))
    gate_proj = low_back(matmul(normed_ffn, w_gate))
    up_proj = low_back(matmul(normed_ffn, w_up))
    hidden = low(jax.nn.silu(gate_proj) * up_proj)
    return residual + low_back(matmul(hidden, w_down))

def reference(inputs, keys_values, segment_ids, gain_first, gain_second, w_query, w_out, w_gate, w_up, w_down, cotangent):
    seq_count = segment_ids.shape[0]
    seq_len = segment_ids.shape[1]
    width = inputs.shape[1]
    tokens = inputs.astype(jnp.float32).reshape(seq_count, seq_len, width)
    pairs = keys_values.astype(jnp.float32).reshape(seq_count, seq_len, 2, width)

    def forward(tokens_in, pairs_in, gain_one, gain_two, query_w, out_w, gate_w, up_w, down_w):

        def per_sequence(packed):
            return layer(packed[0], packed[1], packed[2], gain_one, gain_two, query_w, out_w, gate_w, up_w, down_w)
        return lax.map(jax.checkpoint(per_sequence), (tokens_in, pairs_in, segment_ids))
    result, pullback = jax.vjp(forward, tokens, pairs, gain_first, gain_second, w_query.astype(jnp.float32), w_out.astype(jnp.float32), w_gate.astype(jnp.float32), w_up.astype(jnp.float32), w_down.astype(jnp.float32))
    grads = pullback(cotangent.astype(jnp.float32).reshape(seq_count, seq_len, width))
    return (result.reshape(seq_count * seq_len, width).astype(jnp.bfloat16), grads[0].reshape(seq_count * seq_len, width), grads[1].reshape(seq_count * seq_len, 2, width), grads[2], grads[3], grads[4], grads[5], grads[6], grads[7], grads[8])
```

```python
import jax
import jax.numpy as jnp
from jax import lax
from jax.experimental import pallas as pl
from jax.experimental.pallas import tpu as pltpu
from jax.sharding import PartitionSpec as P

f32 = jnp.float32
bf16 = jnp.bfloat16
HEAD_DIM = 128
epsilon = 1e-06
MESH = pl.DeviceIdType.MESH
Z_LOW, Z_HIGH, CORE, SIDE, DEEP = 1, 2, 4, 8, 16
ANY = pl.BlockSpec(memory_space=pl.ANY)
VM = pl.BlockSpec(memory_space=pltpu.VMEM)


class Place:
    def __init__(self):
        self.dp = lax.axis_index("dp")
        self.mp = lax.axis_index("mp")

    def bit(self, mask):
        return ((self.dp * 4 + self.mp) // mask) % 2

    def partner(self, mask):
        flip_dp, flip_mp = mask // 4, mask % 4
        return (self.flip(self.dp, flip_dp), self.flip(self.mp, flip_mp))

    def flip(self, value, flips):
        for mask in (1, 2, 4):
            if flips & mask:
                value = value + mask - 2 * mask * ((value // mask) % 2)
        return value


class Copies:
    def __init__(self, place, send_sems, recv_sems, local_sems=None):
        self.place, self.send_sems, self.recv_sems = place, send_sems, recv_sems
        self.local_sems = local_sems
        self.count = 0
        self.local_count = 0
        self.pending = []

    def describe(self, source, target, device, slot):
        return pltpu.make_async_remote_copy(
            src_ref=source, dst_ref=target, send_sem=self.send_sems.at[slot],
            recv_sem=self.recv_sems.at[slot], device_id=device, device_id_type=MESH)

    def swap(self, source, target, mask):
        slot = self.count
        self.count += 1
        copy = self.describe(source, target, self.place.partner(mask), slot)
        copy.start()
        item = {"copy": copy, "got": False}
        self.pending.append(item)
        return item

    def got(self, item):
        if not item["got"]:
            item["got"] = True
            if "get_if" in item:
                @pl.when(item["get_if"])
                def _():
                    item["get"].wait_recv()
            else:
                item["copy"].wait_recv()

    def step(self, block, mp_send, mp_get, direction, send_if, get_if):
        slot = self.count
        self.count += 1
        place = self.place
        other = jnp.clip(place.mp + direction, 0, 3)
        sent, target = block(mp_send)
        copy = self.describe(sent, target, (place.dp, other), slot)

        @pl.when(send_if)
        def _():
            copy.start()
        sent2, target2 = block(mp_get)
        get = self.describe(sent2, target2, (place.dp, other), slot)
        item = {"copy": copy, "got": False, "send_if": send_if, "get_if": get_if, "get": get}
        self.pending.append(item)
        return item

    def local(self, source, target):
        copy = pltpu.make_async_copy(source, target, self.local_sems.at[self.local_count])
        self.local_count += 1
        copy.start()
        return copy

    def finish(self):
        for item in self.pending:
            self.got(item)
        for item in self.pending:
            if "send_if" in item:
                @pl.when(item["send_if"])
                def _():
                    item["copy"].wait_send()
            elif "sent" not in item:
                item["copy"].wait_send()


def greet(place, masks):
    barrier = pltpu.get_barrier_semaphore()
    for mask in masks:
        pl.semaphore_signal(barrier, inc=1, device_id=place.partner(mask), device_id_type=MESH)
    pl.semaphore_wait(barrier, len(masks))


def gather_kernel(first, cot, wq, wo, wg, wu, wd, rows, cots, query, wide, out, gate, up, down,
                  send_sems, recv_sems, local_sems):
    place = Place()
    dp, mp = place.dp, place.mp
    side, high = place.bit(SIDE), place.bit(Z_HIGH)
    locals_ = []
    copies = Copies(place, send_sems, recv_sems, local_sems)

    half = wd.shape[0] // 2
    blk = wd.shape[1]
    share = first.shape[0]
    zrow = wo.shape[0]
    flip = place.flip
    greet(place, (1, 2, 3, CORE, SIDE, DEEP))

    locals_.append(copies.local(first, rows.at[pl.ds(mp * share, share), :]))
    locals_.append(copies.local(cot, cots.at[0:share, :]))
    locals_.append(copies.local(wq, query.at[pl.ds(dp * blk, blk), :]))
    locals_.append(copies.local(wo, out.at[pl.ds(mp * zrow, zrow), pl.ds(dp * blk, blk)]))
    mats = ((wg, gate), (wu, up), (wd, down))
    for weight, whole in mats:
        locals_.append(copies.local(weight.at[pl.ds(side * half, half), :],
                                    whole.at[pl.ds(high * half, half), pl.ds(dp * blk, blk)]))

    zcol = wq.shape[1]
    locals_.append(copies.local(wq, wide.at[:, pl.ds(mp * zcol, zcol)]))
    def tile(whole, z, d):
        return whole.at[pl.ds(z * half, half), pl.ds(d * blk, blk)]

    nchunk = 2
    chunk = share // nchunk

    def row_block(c, source_is_input):
        def get(m):
            target = rows.at[pl.ds(m * share + c * chunk, chunk), :]
            source = first.at[pl.ds(c * chunk, chunk), :] if source_is_input else target
            return source, target
        return get

    def out_block(source_is_input):
        def get(m):
            target = out.at[pl.ds(m * zrow, zrow), pl.ds(dp * blk, blk)]
            return (wo if source_is_input else target), target
        return get

    def wide_block(source_is_input):
        def get(m):
            target = wide.at[:, pl.ds(m * zcol, zcol)]
            return (wq if source_is_input else target), target
        return get

    def line(store, step, block_of, key):
        lead = (key, step)
        store[("r",) + lead] = copies.step(block_of, mp - (step - 1), mp - step, 1,
                                           (mp >= step - 1) & (mp < 3), mp >= step)
        store[("l",) + lead] = copies.step(block_of, mp + (step - 1), mp + step, -1,
                                           (mp <= 3 - (step - 1)) & (mp > 0), mp <= 3 - step)

    store = {}
    core = []

    def spread_core(piece):
        core.append(copies.swap(piece, piece, CORE))

    def arrive(key, step):
        copies.got(store[("r", key, step)])
        copies.got(store[("l", key, step)])

    dy = flip(dp, DEEP // 4)
    dx = flip(dp, SIDE // 4)
    dxy = flip(dy, SIDE // 4)
    own_piece = [weight.at[pl.ds(side * half, half), :] for weight, _ in mats]
    zhop = [[], [], []]
    yhop = [[], [], []]

    def send_z(i, source, d):
        zhop[i].append(copies.swap(source, tile(mats[i][1], high, d), Z_HIGH))

    def send_y(i, source, z, d):
        yhop[i].append((copies.swap(source, tile(mats[i][1], z, d), DEEP), z, flip(d, DEEP // 4)))

    line(store, 1, out_block(True), "o")
    send_z(0, own_piece[0], dp)
    xhop = [copies.swap(weight.at[pl.ds((1 - side) * half, half), :], tile(whole, high, dp), SIDE)
            for weight, whole in mats]
    wq_y = copies.swap(wq, query.at[pl.ds(dp * blk, blk), :], DEEP)
    for i in range(3):
        send_y(i, own_piece[i], high, dp)
    wq_x = [copies.swap(wq, query.at[pl.ds(dp * blk, blk), :], SIDE)]
    for i in range(3):
        core.append(copies.swap(own_piece[i], tile(mats[i][1], high, dp), CORE))
    spread_wq = [copies.swap(wq, query.at[pl.ds(dp * blk, blk), :], CORE)]
    copies.got(wq_y)
    piece = query.at[pl.ds(dy * blk, blk), :]
    wq_x.append(copies.swap(piece, piece, SIDE))
    spread_core(piece)
    cot_x = copies.swap(cot, cots.at[share:2 * share, :], SIDE)
    arrive("o", 1)
    line(store, 2, out_block(False), "o")
    send_z(1, own_piece[1], dp)
    arrive("o", 2)
    line(store, 3, out_block(False), "o")
    send_z(2, own_piece[2], dp)
    for c in range(nchunk):
        line(store, 1, row_block(c, True), c)
    for i in range(3):
        copies.got(xhop[i])
        piece = tile(mats[i][1], high, dx)
        send_y(i, piece, high, dx)
        send_z(i, piece, dx)
        spread_core(piece)
    for item, d in zip(wq_x, (dx, dxy)):
        copies.got(item)
        spread_core(query.at[pl.ds(d * blk, blk), :])
    arrive("o", 3)
    for copy in locals_:
        copy.wait()

    def columns(d):
        return out.at[:, pl.ds(d * blk, blk)]

    out_y = copies.swap(columns(dp), columns(dp), DEEP)
    out_x = [copies.swap(columns(dp), columns(dp), SIDE)]
    spread_core(columns(dp))
    for i in range(3):
        copies.got(zhop[i][0])
        piece = tile(mats[i][1], 1 - high, dp)
        send_y(i, piece, 1 - high, dp)
        spread_core(piece)
    line(store, 1, wide_block(True), "w")
    for c in range(nchunk):
        arrive(c, 1)
        line(store, 2, row_block(c, False), c)
    copies.got(out_y)
    out_x.append(copies.swap(columns(dy), columns(dy), SIDE))
    spread_core(columns(dy))
    cot_z = copies.swap(cot, cots.at[2 * share:3 * share, :], Z_LOW)
    for i in range(3):
        copies.got(zhop[i][1])
        piece = tile(mats[i][1], 1 - high, dx)
        send_y(i, piece, 1 - high, dx)
        spread_core(piece)
    arrive("w", 1)
    line(store, 2, wide_block(False), "w")
    for c in range(nchunk):
        arrive(c, 2)
        line(store, 3, row_block(c, False), c)
    arrive("w", 2)
    line(store, 3, wide_block(False), "w")
    copies.got(out_x[0])
    spread_core(columns(dx))
    copies.got(cot_z)
    cot_xz = copies.swap(cots.at[2 * share:3 * share, :], cots.at[3 * share:4 * share, :], SIDE)
    for j in range(4):
        for i in range(3):
            item, z, d = yhop[i][j]
            copies.got(item)
            spread_core(tile(mats[i][1], z, d))
    copies.got(out_x[1])
    spread_core(columns(dxy))
    copies.finish()


def gather_call(first, cot, wq, wo, wg, wu, wd):
    share, width = first.shape
    hidden = wd.shape[0]
    shapes = (
        (share * 4, width), (share * 4, width), (width, wq.shape[1]), (wq.shape[0], width), (width, width),
        (hidden, width), (hidden, width), (hidden, width),
    )
    return pl.pallas_call(
        gather_kernel,
        out_shape=tuple(jax.ShapeDtypeStruct(s, bf16) for s in shapes),
        in_specs=[VM] * 7,
        out_specs=(ANY,) * 8,
        scratch_shapes=[pltpu.SemaphoreType.DMA((110,)), pltpu.SemaphoreType.DMA((110,)),
                        pltpu.SemaphoreType.DMA((9,))],
        compiler_params=pltpu.CompilerParams(collective_id=1, has_side_effects=True, vmem_limit_bytes=16 << 20),
        name="gather_all",
    )(first, cot, wq, wo, wg, wu, wd)

DMA = pltpu.SemaphoreType.DMA


def params(ident, vmem=32 << 20):
    return pltpu.CompilerParams(collective_id=ident, has_side_effects=True, vmem_limit_bytes=vmem)


def tokens_kernel(heads, query_y, query_0, query_x, own, whole, send_sems, recv_sems, local_sems):
    place = Place()
    mp, dp = place.mp, place.dp
    share, local = own.shape[0], heads.shape[1]
    blk = query_0.shape[0]
    copies = Copies(place, send_sems, recv_sems, local_sems)
    dy = place.flip(dp, 4)
    dx = place.flip(dp, 2)
    dxy = place.flip(dy, 2)

    def rows(d):
        return whole.at[pl.ds(d * blk, blk), :]

    greet(place, (1, 2, 3, SIDE, CORE))
    across = copies.swap(query_y, rows(dy), SIDE)
    for mask in (2, 3, 1):
        other = place.partner(mask)[1]
        copies.swap(heads.at[pl.ds(other * share, share), :], own.at[:, pl.ds(mp * local, local)], mask)
    held = [copies.local(query_0, rows(dp)), copies.local(query_y, rows(dy)), copies.local(query_x, rows(dx))]
    copies.swap(query_0, rows(dp), CORE)
    copies.swap(query_y, rows(dy), CORE)
    copies.swap(query_x, rows(dx), CORE)
    own[:, pl.ds(mp * local, local)] = heads[pl.ds(mp * share, share), :]
    for copy in held:
        copy.wait()
    copies.got(across)
    copies.swap(rows(dxy), rows(dxy), CORE)
    copies.finish()


def tokens_hop_kernel(heads, block, own, hopped, send_sems, recv_sems):
    place = Place()
    mp = place.mp
    share, local = own.shape[0], heads.shape[1]
    greet(place, (1, 2, 3, DEEP))
    copies = Copies(place, send_sems, recv_sems)
    for mask in (2, 3, 1):
        other = place.partner(mask)[1]
        copies.swap(heads.at[pl.ds(other * share, share), :], own.at[:, pl.ds(mp * local, local)], mask)
    copies.swap(block, hopped, DEEP)
    own[:, pl.ds(mp * local, local)] = heads[pl.ds(mp * share, share), :]
    copies.finish()


def heads_hop_kernel(own, block, heads, hopped, send_sems, recv_sems):
    place = Place()
    mp = place.mp
    share, local = own.shape[0], heads.shape[1]
    greet(place, (1, 2, 3, SIDE))
    copies = Copies(place, send_sems, recv_sems)
    for mask in (2, 3, 1):
        other = place.partner(mask)[1]
        copies.swap(own.at[:, pl.ds(other * local, local)], heads.at[pl.ds(mp * share, share), :], mask)
    copies.swap(block, hopped, SIDE)
    heads[pl.ds(mp * share, share), :] = own[:, pl.ds(mp * local, local)]
    copies.finish()


def to_tokens(heads, block, ident):
    shape = (heads.shape[0] // 4, heads.shape[1] * 4)
    return pl.pallas_call(
        tokens_hop_kernel,
        out_shape=(jax.ShapeDtypeStruct(shape, bf16), jax.ShapeDtypeStruct(block.shape, bf16)),
        in_specs=[VM, VM], out_specs=(VM, VM),
        scratch_shapes=[DMA((4,)), DMA((4,))], compiler_params=params(ident), name="to_tokens")(heads, block)


def to_tokens_last(heads, query_y, query_0, query_x, ident):
    shape = (heads.shape[0] // 4, heads.shape[1] * 4)
    width = query_0.shape[1]
    return pl.pallas_call(
        tokens_kernel,
        out_shape=(jax.ShapeDtypeStruct(shape, bf16), jax.ShapeDtypeStruct((width, width), bf16)),
        in_specs=[VM] * 4, out_specs=(VM, ANY),
        scratch_shapes=[DMA((8,)), DMA((8,)), DMA((3,))], compiler_params=params(ident),
        name="to_tokens_last")(heads, query_y, query_0, query_x)


def to_heads(own, block, ident):
    shape = (own.shape[0] * 4, own.shape[1] // 4)
    return pl.pallas_call(
        heads_hop_kernel,
        out_shape=(jax.ShapeDtypeStruct(shape, bf16), jax.ShapeDtypeStruct(block.shape, bf16)),
        in_specs=[VM, VM], out_specs=(VM, VM),
        scratch_shapes=[DMA((4,)), DMA((4,))], compiler_params=params(ident), name="to_heads")(own, block)


def quad_gather_kernel(own, rows, send_sems, recv_sems):
    place = Place()
    share = own.shape[0]
    half = share // 2
    greet(place, (Z_LOW, SIDE))
    copies = Copies(place, send_sems, recv_sems)
    a, b = pl.ds(0, half), pl.ds(half, half)

    def at(quarter, part):
        return rows.at[pl.ds(quarter * share + part * half, half), :]

    low_a = copies.swap(own.at[a, :], at(2, 0), Z_LOW)
    side_b = copies.swap(own.at[b, :], at(1, 1), SIDE)
    low_b = copies.swap(own.at[b, :], at(2, 1), Z_LOW)
    side_a = copies.swap(own.at[a, :], at(1, 0), SIDE)
    rows[0:share, :] = own[...]
    copies.got(low_a)
    copies.swap(at(2, 0), at(3, 0), SIDE)
    copies.got(side_b)
    copies.swap(at(1, 1), at(3, 1), Z_LOW)
    copies.finish()


def quad_gather(own, ident):
    return pl.pallas_call(
        quad_gather_kernel, out_shape=jax.ShapeDtypeStruct((own.shape[0] * 4, own.shape[1]), bf16),
        in_specs=[VM], out_specs=VM, scratch_shapes=[DMA((6,)), DMA((6,))],
        compiler_params=params(ident), name="quad_gather")(own)


def add_into(target, rows, *others, step=32):
    start, count = rows
    pieces = count // step

    def one(i, carry):
        total = target[pl.ds(start + i * step, step), :].astype(f32)
        for other in others:
            total = total + other[pl.ds(i * step, step), :].astype(f32)
        target[pl.ds(start + i * step, step), :] = total.astype(target.dtype)
        return carry

    lax.fori_loop(0, pieces, one, 0)


class QuadReduce:
    def __init__(self, copies, parts, relay, landed):
        self.copies, self.parts, self.relay, self.landed = copies, parts, relay, landed
        self.share = parts.shape[0] // 4
        self.half = self.share // 2

    def start(self):
        share, half = self.share, self.half
        self.first = self.copies.swap(self.parts.at[pl.ds(3 * share, half), :], self.relay.at[0], SIDE)
        self.second = self.copies.swap(self.parts.at[pl.ds(3 * share + half, half), :], self.relay.at[1], Z_LOW)
        self.side = [self.copies.swap(self.parts.at[pl.ds(share, half), :], self.landed.at[0, pl.ds(0, half), :], SIDE)]
        self.low = [self.copies.swap(self.parts.at[pl.ds(2 * share + half, half), :], self.landed.at[1, pl.ds(half, half), :], Z_LOW)]

    def relayed(self):
        share, half = self.share, self.half
        self.copies.got(self.first)
        add_into(self.parts, (2 * share, half), self.relay.at[0])
        self.low.append(self.copies.swap(self.parts.at[pl.ds(2 * share, half), :], self.landed.at[1, pl.ds(0, half), :], Z_LOW))
        self.copies.got(self.second)
        add_into(self.parts, (share + half, half), self.relay.at[1])
        self.side.append(self.copies.swap(self.parts.at[pl.ds(share + half, half), :], self.landed.at[0, pl.ds(half, half), :], SIDE))

    def arrived(self):
        for item in self.side + self.low:
            self.copies.got(item)


def quad_reduce_kernel(parts_in, total, parts, relay, landed, send_sems, recv_sems, local_sem):
    place = Place()
    load = pltpu.make_async_copy(parts_in, parts, local_sem)
    load.start()
    greet(place, (Z_LOW, SIDE))
    copies = Copies(place, send_sems, recv_sems)
    load.wait()
    reduce = QuadReduce(copies, parts, relay, landed)
    reduce.start()
    reduce.relayed()
    reduce.arrived()
    share = total.shape[0]

    def one(i, carry):
        here = pl.ds(i * 32, 32)
        total[here, :] = (parts[here, :].astype(f32) + landed[0, here, :].astype(f32)
                          + landed[1, here, :].astype(f32))
        return carry

    lax.fori_loop(0, share // 32, one, 0)
    copies.finish()


def quad_reduce(parts, ident):
    share, width = parts.shape[0] // 4, parts.shape[1]
    return pl.pallas_call(
        quad_reduce_kernel, out_shape=jax.ShapeDtypeStruct((share, width), f32),
        in_specs=[ANY], out_specs=VM,
        scratch_shapes=[pltpu.VMEM((share * 4, width), bf16), pltpu.VMEM((2, share // 2, width), bf16),
                        pltpu.VMEM((2, share, width), bf16), DMA((6,)), DMA((6,)), DMA],
        compiler_params=params(ident), name="quad_reduce")(parts)


def reduce_kernel(gd, gg, gu, go, gq, parts_in, gains_in, down, gate, up, out, query, total, gains,
                  own_f, core_f, deep_f, high_f, side_f, own_o, core_o, side_o, deep_o, z_o,
                  own_q, core_q, side_q, deep_q, parts, relay, landed, gains_got,
                  send_sems, recv_sems, local_sems):
    place = Place()
    dp, mp = place.dp, place.mp
    flip = place.flip
    high = place.bit(Z_HIGH)
    side = place.bit(SIDE)
    blk = down.shape[1]
    hidden = down.shape[0]
    half = hidden // 2
    share = total.shape[0]
    zrow = out.shape[0]
    spots = ((0, 0), (0, 1), (1, 0), (1, 1))
    copies = Copies(place, send_sems, recv_sems, local_sems)
    mats = (gd, gg, gu)

    def place_of(spot, core):
        return flip(flip(flip(dp, 4 * spot[0]), 2 * spot[1]), core)

    def cols(array, d):
        return array.at[:, pl.ds(d * blk, blk)]

    def brows(array, d):
        return array.at[pl.ds(d * blk, blk), :]

    loads_f = [[copies.local(cols(m, place_of(s, 0)), own_f.at[i, j]) for j, s in enumerate(spots)]
               for i, m in enumerate(mats)]
    loads_o = [copies.local(cols(go, place_of(s, 0)), own_o.at[j]) for j, s in enumerate(spots)]
    loads_q = [copies.local(brows(gq, place_of(s, 0)), own_q.at[j]) for j, s in enumerate(spots)]
    load_p = copies.local(parts_in, parts)
    greet(place, (1, 2, 3, CORE, SIDE, DEEP))
    gains[...] = gains_in[...]
    gain_masks = [1, 2, CORE, SIDE, DEEP]
    gain_state = {"item": None, "at": 0}

    def gain_hop():
        if gain_state["item"] is not None:
            copies.got(gain_state["item"])
            copies_wait_send(gain_state["item"])
            gains[...] = gains[...] + gains_got[gain_state["at"] - 1]
            gain_state["item"] = None
        if gain_state["at"] < len(gain_masks):
            gain_state["item"] = copies.swap(gains, gains_got.at[gain_state["at"]], gain_masks[gain_state["at"]])
            gain_state["at"] += 1

    def copies_wait_send(item):
        item["copy"].wait_send()
        item["sent"] = True

    order = ((1, 0), (1, 1), (0, 0), (0, 1))
    index = {s: j for j, s in enumerate(spots)}
    core_in = []
    for i, m in enumerate(mats):
        core_in.append({s: copies.swap(cols(m, place_of(s, 1)), core_f.at[i, index[s]], CORE) for s in order})
    order_o = ((0, 1), (1, 1), (0, 0), (1, 0))
    core_in_o = {s: copies.swap(cols(go, place_of(s, 1)), core_o.at[index[s]], CORE) for s in order_o}
    core_in_q = {s: copies.swap(brows(gq, place_of(s, 1)), core_q.at[index[s]], CORE) for s in order_o}
    gain_hop()
    load_p.wait()
    reduce = QuadReduce(copies, parts, relay, landed)
    deep_in = []
    for i in range(3):
        sent = {}
        for s in order:
            j = index[s]
            copies.got(core_in[i][s])
            loads_f[i][j].wait()
            add_into(own_f.at[i, j], (0, hidden), core_f.at[i, j])
            if s[0]:
                sent[s[1]] = copies.swap(own_f.at[i, j], deep_f.at[i, s[1]], DEEP)
        deep_in.append(sent)
        if i == 0:
            reduce.start()
        gain_hop()
    side_in_o, side_in_q = {}, {}
    for s in order_o:
        j = index[s]
        copies.got(core_in_q[s])
        loads_q[j].wait()
        add_into(own_q.at[j], (0, blk), core_q.at[j])
        if s[1]:
            side_in_q[s[0]] = copies.swap(own_q.at[j], side_q.at[s[0]], SIDE)
    for s in order_o:
        j = index[s]
        copies.got(core_in_o[s])
        loads_o[j].wait()
        add_into(own_o.at[j], (0, own_o.shape[1]), core_o.at[j])
        if s[1]:
            side_in_o[s[0]] = copies.swap(own_o.at[j], side_o.at[s[0]], SIDE)
    gain_hop()
    reduce.relayed()
    gain_hop()
    high_in = []
    for i in range(3):
        sent = {}
        for x in (1, 0):
            j = index[(0, x)]
            copies.got(deep_in[i][x])
            add_into(own_f.at[i, j], ((1 - high) * half, half), deep_f.at[i, x, pl.ds((1 - high) * half, half), :], step=16)
            sent[x] = copies.swap(own_f.at[i, j, pl.ds((1 - high) * half, half), :], high_f.at[i, x], Z_HIGH)
            add_into(own_f.at[i, j], (high * half, half), deep_f.at[i, x, pl.ds(high * half, half), :], step=16)
        high_in.append(sent)
    gain_hop()
    deep_in_q = None
    deep_in_o = None
    for y in (1, 0):
        j = index[(y, 0)]
        copies.got(side_in_q[y])
        add_into(own_q.at[j], (0, blk), side_q.at[y])
        if y:
            deep_in_q = copies.swap(own_q.at[j], deep_q, DEEP)
    for y in (1, 0):
        j = index[(y, 0)]
        copies.got(side_in_o[y])
        add_into(own_o.at[j], (0, own_o.shape[1]), side_o.at[y])
        if y:
            deep_in_o = copies.swap(own_o.at[j], deep_o, DEEP)
    copies.got(deep_in_o)
    add_into(own_o.at[0], (0, own_o.shape[1]), deep_o)
    z_in = []
    for n, mask in enumerate((2, 3, 1)):
        other = place.partner(mask)[1]
        z_in.append(copies.swap(own_o.at[0, pl.ds(other * zrow, zrow), :], z_o.at[n], mask))
    side_in = []
    outs = (down, gate, up)
    for i in range(3):
        for x in (1, 0):
            j = index[(0, x)]
            copies.got(high_in[i][x])
            add_into(own_f.at[i, j], (high * half, half), high_f.at[i, x], step=16)
            if x:
                side_in.append(copies.swap(own_f.at[i, j, pl.ds(high * half, half), :], side_f.at[i], SIDE))
    copies.got(deep_in_q)
    query[...] = own_q[0].astype(f32) + deep_q[...].astype(f32)
    reduce.arrived()

    def one(i, carry):
        here = pl.ds(i * 32, 32)
        total[here, :] = (parts[here, :].astype(f32) + landed[0, here, :].astype(f32)
                          + landed[1, here, :].astype(f32))
        return carry

    lax.fori_loop(0, share // 32, one, 0)
    for item in z_in:
        copies.got(item)

    def add_z(i, carry):
        here = pl.ds(i * 32, 32)
        sum_ = own_o[0, pl.ds(mp * zrow + i * 32, 32), :].astype(f32)
        for n in range(3):
            sum_ = sum_ + z_o[n, here, :].astype(f32)
        out[here, :] = sum_
        return carry

    lax.fori_loop(0, zrow // 32, add_z, 0)
    for i in range(3):
        copies.got(side_in[i])

        def write(n, carry, i=i):
            here = pl.ds(side * half + n * 16, 16)
            there = pl.ds((1 - side) * half + n * 16, 16)
            outs[i][here, :] = own_f[i, 0, pl.ds(high * half + n * 16, 16), :].astype(f32)
            outs[i][there, :] = side_f[i, pl.ds(n * 16, 16), :].astype(f32)
            return carry

        lax.fori_loop(0, half // 16, write, 0)
    copies.finish()


def reduce_call(gd, gg, gu, go, gq, parts, gains, ident):
    hidden, width = gd.shape
    blk = width // 8
    half = hidden // 2
    local = gq.shape[1]
    share = parts.shape[0] // 4
    V = pltpu.VMEM
    return pl.pallas_call(
        reduce_kernel,
        out_shape=(jax.ShapeDtypeStruct((hidden, blk), f32),) * 3
        + (jax.ShapeDtypeStruct((width // 4, blk), f32), jax.ShapeDtypeStruct((blk, local), f32),
           jax.ShapeDtypeStruct((share, width), f32), jax.ShapeDtypeStruct(gains.shape, f32)),
        in_specs=[ANY] * 6 + [VM],
        out_specs=(VM,) * 7,
        scratch_shapes=[
            V((3, 4, hidden, blk), bf16), V((3, 4, hidden, blk), bf16), V((3, 2, hidden, blk), bf16),
            V((3, 2, half, blk), bf16), V((3, half, blk), bf16),
            V((4, width, blk), bf16), V((4, width, blk), bf16), V((2, width, blk), bf16), V((width, blk), bf16),
            V((3, width // 4, blk), bf16),
            V((4, blk, local), bf16), V((4, blk, local), bf16), V((2, blk, local), bf16), V((blk, local), bf16),
            V((share * 4, width), bf16), V((2, share // 2, width), bf16), V((2, share, width), bf16),
            V((5,) + gains.shape, f32),
            DMA((60,)), DMA((60,)), DMA((24,))],
        compiler_params=params(ident, 63 << 20), name="reduce_all",
    )(gd, gg, gu, go, gq, parts, gains)
ROWS=256
DOC_MOST=512


def dot(left, right, left_dim, right_dim):
    return lax.dot_general(left, right, (((left_dim,), (right_dim,)), ((), ())), preferred_element_type=f32)


def key_range(block, seq_len):
    low = max(0, block * ROWS - DOC_MOST + 1) // ROWS * ROWS
    return low, min(seq_len, (block + 1) * ROWS)


def scores_turned(q, k, starts, low, first, scale):
    s = dot(k, q, 1, 1) * scale
    key_pos = low + lax.broadcasted_iota(jnp.int32, s.shape, 0)
    query_pos = first + lax.broadcasted_iota(jnp.int32, s.shape, 1)
    return jnp.where((key_pos >= starts) & (key_pos <= query_pos), s, -1e30)


def forward_kernel(starts_ref, q_ref, k_ref, v_ref, ctx_ref, lse_ref):
    seq_len = q_ref.shape[0]
    scale = HEAD_DIM ** -0.5
    for block in range(seq_len // ROWS):
        low, high = key_range(block, seq_len)
        here = pl.ds(block * ROWS, ROWS)
        k = k_ref[low:high, :]
        v = v_ref[low:high, :]
        s = scores_turned(q_ref[here, :], k, starts_ref[:, here], low, block * ROWS, scale)
        top = jnp.max(s, axis=0, keepdims=True)
        raised = jnp.exp(s - top)
        total = jnp.sum(raised, axis=0, keepdims=True)
        low_probs = (raised * (1.0 / total)).astype(bf16)
        ctx_ref[here, :] = dot(low_probs, v, 0, 0).astype(bf16)
        lse_ref[0, :, here] = top + jnp.log(total)


def backward_kernel(starts_ref, q_ref, k_ref, v_ref, grad_ref, lse_ref, dq_ref, dk_ref, dv_ref):
    seq_len = q_ref.shape[0]
    scale = HEAD_DIM ** -0.5
    for block in range(seq_len // ROWS):
        low, high = key_range(block, seq_len)
        here = pl.ds(block * ROWS, ROWS)
        k = k_ref[low:high, :]
        v = v_ref[low:high, :]
        q = q_ref[here, :]
        grad = grad_ref[here, :]
        s = scores_turned(q, k, starts_ref[:, here], low, block * ROWS, scale)
        probs = jnp.exp(s - lse_ref[0, :, here])
        grad_probs = dot(v, grad, 1, 1)
        spread = jnp.sum(probs * grad_probs, axis=0, keepdims=True)
        grad_s = (probs * (grad_probs - spread)).astype(bf16)
        dq_ref[here, :] = (dot(grad_s, k, 0, 0) * scale).astype(bf16)
        dk = dot(grad_s, q, 1, 0) * scale
        dv = dot(probs.astype(bf16), grad, 1, 0)
        old = max(low, min(high, block * ROWS))
        if low == 0 and block == 0:
            dk_ref[low:high, :] = dk
            dv_ref[low:high, :] = dv
        else:
            n = old - low
            dk_ref[low:old, :] += dk[:n]
            dv_ref[low:old, :] += dv[:n]
            dk_ref[old:high, :] = dk[n:]
            dv_ref[old:high, :] = dv[n:]


def specs(seq_len):
    row = pl.BlockSpec((1, seq_len), lambda h: (0, 0))
    head = pl.BlockSpec((seq_len, HEAD_DIM), lambda h: (0, h))
    lse = pl.BlockSpec((1, 1, seq_len), lambda h: (h, 0, 0))
    return row, head, lse


def attend(starts, q, k, v):
    seq_len, width = q.shape
    heads = width // HEAD_DIM
    row, head, lse = specs(seq_len)
    flops = heads * seq_len * seq_len * HEAD_DIM * 3
    return pl.pallas_call(
        forward_kernel, grid=(heads,),
        in_specs=[row, head, head, head], out_specs=(head, lse),
        out_shape=(jax.ShapeDtypeStruct(q.shape, bf16), jax.ShapeDtypeStruct((heads, 1, seq_len), f32)),
        cost_estimate=pl.CostEstimate(flops=flops, bytes_accessed=4 * q.size * 2, transcendentals=heads * seq_len * seq_len // 2),
        name="attend",
    )(starts, q, k, v)


def attend_back(starts, q, k, v, grad, lse_array):
    seq_len, width = q.shape
    heads = width // HEAD_DIM
    row, head, lse = specs(seq_len)
    flops = heads * seq_len * seq_len * HEAD_DIM * 7
    wide = jax.ShapeDtypeStruct(q.shape, f32)
    return pl.pallas_call(
        backward_kernel, grid=(heads,),
        in_specs=[row, head, head, head, head, lse], out_specs=(head, head, head),
        out_shape=(jax.ShapeDtypeStruct(q.shape, bf16), wide, wide),
        cost_estimate=pl.CostEstimate(flops=flops, bytes_accessed=9 * q.size * 2, transcendentals=heads * seq_len * seq_len // 2),
        name="attend_back",
    )(starts, q, k, v, grad, lse_array)


def starts_of(segments):
    return jnp.sum((segments[0][None, :] < segments[0][:, None]).astype(jnp.int32), axis=1)[None, :]


def contract(left, right, left_dim, right_dim):
    return lax.dot_general(
        left, right, (((left_dim,), (right_dim,)), ((), ())), preferred_element_type=jnp.float32
    )


def root_inverse(values):
    return lax.rsqrt(jnp.mean(values * values, axis=-1, keepdims=True) + epsilon)


def norm_back(grad_normed, scaled, inverse, gain):
    grad_scaled = grad_normed * gain
    grad_values = inverse * (
        grad_scaled - scaled * jnp.mean(grad_scaled * scaled, axis=-1, keepdims=True)
    )
    return (grad_values, jnp.sum(grad_normed * scaled, axis=0))


def plain_body(
    inputs,
    keys_values,
    segment_ids,
    gain_first,
    gain_second,
    w_query,
    w_out,
    w_gate,
    w_up,
    w_down,
    cotangent,
):
    query_full, out_full = (
        lax.all_gather(w_query, "dp", axis=0, tiled=True),
        lax.all_gather(w_out, "dp", axis=1, tiled=True),
    )
    gate_full, up_full, down_full = (
        lax.all_gather(w_gate, "dp", axis=0, tiled=True),
        lax.all_gather(w_up, "dp", axis=0, tiled=True),
        lax.all_gather(w_down, "dp", axis=1, tiled=True),
    )
    tokens = inputs.astype(jnp.float32)
    inverse_first = root_inverse(tokens)
    scaled_first = tokens * inverse_first
    normed_first = (scaled_first * gain_first).astype(jnp.bfloat16)
    rows_first = lax.all_gather(normed_first, "mp", axis=0, tiled=True)
    queries = contract(rows_first, query_full, 1, 0).astype(jnp.bfloat16)
    seq_len = rows_first.shape[0]
    local_width = queries.shape[1]
    head_count = local_width // HEAD_DIM
    block_rows = min(512, seq_len)
    block_count = seq_len // block_rows
    score_scale = HEAD_DIM ** (-0.5)
    key_heads = keys_values[:, 0, :].reshape(seq_len, head_count, HEAD_DIM)
    value_heads = keys_values[:, 1, :].reshape(seq_len, head_count, HEAD_DIM)
    segments = segment_ids[0]
    key_pos = jnp.arange(seq_len, dtype=jnp.int32)

    def block_scores(first_row):
        query_block = lax.dynamic_slice_in_dim(queries, first_row, block_rows, 0).reshape(
            block_rows, head_count, HEAD_DIM
        )
        scores = (
            jnp.einsum("qhd,khd->hqk", query_block, key_heads, preferred_element_type=jnp.float32)
            * score_scale
        )
        query_pos = first_row + jnp.arange(block_rows, dtype=jnp.int32)
        query_seg = lax.dynamic_slice_in_dim(segments, first_row, block_rows, 0)
        allowed = (query_pos[:, None] >= key_pos[None, :]) & (
            query_seg[:, None] == segments[None, :]
        )
        return (query_block, jnp.where(allowed[None], scores, -1e30))

    def forward_block(block_index):
        query_block, scores = block_scores(block_index * block_rows)
        row_max = jnp.max(scores, axis=-1, keepdims=True)
        raised = jnp.exp(scores - row_max)
        row_total = jnp.sum(raised, axis=-1, keepdims=True)
        weights_low = (raised / row_total).astype(jnp.bfloat16)
        blended = jnp.einsum(
            "hqk,khd->qhd", weights_low, value_heads, preferred_element_type=jnp.float32
        )
        return (
            blended.reshape(block_rows, local_width).astype(jnp.bfloat16),
            (row_max + jnp.log(row_total))[..., 0],
        )

    context_blocks, log_totals = lax.map(forward_block, jnp.arange(block_count, dtype=jnp.int32))
    context = context_blocks.reshape(seq_len, local_width)
    attn_part = lax.psum_scatter(
        contract(context, out_full, 1, 0), "mp", scatter_dimension=0, tiled=True
    )
    residual = tokens + attn_part
    inverse_second = root_inverse(residual)
    scaled_second = residual * inverse_second
    normed_second = (scaled_second * gain_second).astype(jnp.bfloat16)
    rows_second = lax.all_gather(normed_second, "mp", axis=0, tiled=True)
    gate_proj = contract(rows_second, gate_full, 1, 0)
    up_proj = contract(rows_second, up_full, 1, 0)
    sigmoid_gate = jax.nn.sigmoid(gate_proj)
    silu_gate = gate_proj * sigmoid_gate
    hidden = (silu_gate * up_proj).astype(jnp.bfloat16)
    ffn_part = lax.psum_scatter(
        contract(hidden, down_full, 1, 0).astype(jnp.bfloat16),
        "mp",
        scatter_dimension=0,
        tiled=True,
    ).astype(jnp.float32)
    output = (residual + ffn_part).astype(jnp.bfloat16)
    cot_rows = lax.all_gather(cotangent, "mp", axis=0, tiled=True)
    grad_down_w = contract(hidden, cot_rows, 0, 0)
    grad_hidden = contract(cot_rows, down_full, 1, 1)
    grad_gate_act = (
        grad_hidden * up_proj * sigmoid_gate * (1.0 + gate_proj * (1.0 - sigmoid_gate))
    ).astype(jnp.bfloat16)
    grad_up_act = (grad_hidden * silu_gate).astype(jnp.bfloat16)
    grad_gate_w = contract(rows_second, grad_gate_act, 0, 0)
    grad_up_w = contract(rows_second, grad_up_act, 0, 0)
    grad_normed_second = lax.psum_scatter(
        contract(grad_gate_act, gate_full, 1, 1) + contract(grad_up_act, up_full, 1, 1),
        "mp",
        scatter_dimension=0,
        tiled=True,
    )
    grad_from_norm, gain_second_part = norm_back(
        grad_normed_second, scaled_second, inverse_second, gain_second
    )
    grad_residual = cotangent.astype(jnp.float32) + grad_from_norm
    attn_cot = lax.all_gather(grad_residual.astype(jnp.bfloat16), "mp", axis=0, tiled=True)
    grad_out_w = contract(context, attn_cot, 0, 0)
    grad_context = contract(attn_cot, out_full, 1, 1).astype(jnp.bfloat16)

    def backward_block(state_pair, block_index):
        grad_keys, grad_values = state_pair
        first_row = block_index * block_rows
        query_block, scores = block_scores(first_row)
        log_total = lax.dynamic_index_in_dim(log_totals, block_index, 0, keepdims=False)
        weights = jnp.exp(scores - log_total[..., None])
        grad_block = lax.dynamic_slice_in_dim(grad_context, first_row, block_rows, 0).reshape(
            block_rows, head_count, HEAD_DIM
        )
        grad_weights = jnp.einsum(
            "qhd,khd->hqk", grad_block, value_heads, preferred_element_type=jnp.float32
        )
        spread = jnp.sum(weights * grad_weights, axis=-1, keepdims=True)
        grad_scores = (weights * (grad_weights - spread)).astype(jnp.bfloat16)
        grad_query_block = (
            jnp.einsum("hqk,khd->qhd", grad_scores, key_heads, preferred_element_type=jnp.float32)
            * score_scale
        ).astype(jnp.bfloat16)
        grad_keys = (
            grad_keys
            + jnp.einsum(
                "hqk,qhd->khd", grad_scores, query_block, preferred_element_type=jnp.float32
            )
            * score_scale
        )
        grad_values = grad_values + jnp.einsum(
            "hqk,qhd->khd",
            weights.astype(jnp.bfloat16),
            grad_block,
            preferred_element_type=jnp.float32,
        )
        return ((grad_keys, grad_values), grad_query_block.reshape(block_rows, local_width))

    zero_state = jnp.zeros((seq_len, head_count, HEAD_DIM), jnp.float32)
    (grad_keys, grad_values), grad_query_blocks = lax.scan(
        backward_block, (zero_state, zero_state), jnp.arange(block_count, dtype=jnp.int32)
    )
    grad_queries = grad_query_blocks.reshape(seq_len, local_width)
    grad_kv = jnp.stack(
        [grad_keys.reshape(seq_len, local_width), grad_values.reshape(seq_len, local_width)], axis=1
    )
    grad_query_w = contract(rows_first, grad_queries, 0, 0)
    grad_normed_first = lax.psum_scatter(
        contract(grad_queries, query_full, 1, 1).astype(jnp.bfloat16),
        "mp",
        scatter_dimension=0,
        tiled=True,
    ).astype(jnp.float32)
    grad_from_first, gain_first_part = norm_back(
        grad_normed_first, scaled_first, inverse_first, gain_first
    )
    grad_input = grad_residual + grad_from_first
    gain_first_sum, gain_second_sum = lax.psum((gain_first_part, gain_second_part), ("dp", "mp"))
    query_shard, out_shard, gate_shard, up_shard, down_shard = (
        lax.psum_scatter(
            grad_query_w.astype(jnp.bfloat16), "dp", scatter_dimension=0, tiled=True
        ).astype(jnp.float32),
        lax.psum_scatter(
            grad_out_w.astype(jnp.bfloat16), "dp", scatter_dimension=1, tiled=True
        ).astype(jnp.float32),
        lax.psum_scatter(
            grad_gate_w.astype(jnp.bfloat16), "dp", scatter_dimension=0, tiled=True
        ).astype(jnp.float32),
        lax.psum_scatter(
            grad_up_w.astype(jnp.bfloat16), "dp", scatter_dimension=0, tiled=True
        ).astype(jnp.float32),
        lax.psum_scatter(
            grad_down_w.astype(jnp.bfloat16), "dp", scatter_dimension=1, tiled=True
        ).astype(jnp.float32),
    )
    return (
        output,
        grad_input,
        grad_kv,
        gain_first_sum,
        gain_second_sum,
        query_shard,
        out_shard,
        gate_shard,
        up_shard,
        down_shard,
    )


def fast_body(inputs, keys_values, segment_ids, gain_first, gain_second, w_query, w_out, w_gate,
              w_up, w_down, cotangent):
    tokens = inputs.astype(f32)
    inverse_first = root_inverse(tokens)
    scaled_first = tokens * inverse_first
    normed_first = (scaled_first * gain_first).astype(bf16)
    share = inputs.shape[0]

    rows_first, cots, query_part, query_0, out_whole, gate_here, up_here, down_here = gather_call(
        normed_first, cotangent, w_query, w_out, w_gate.T, w_up.T, w_down)

    queries = contract(rows_first, query_part, 1, 0).astype(bf16)
    starts = starts_of(segment_ids)
    keys = keys_values[:, 0, :]
    values = keys_values[:, 1, :]
    context, log_totals = attend(starts, queries, keys, values)
    context_own, query_y = to_tokens(context, query_0, 2)
    residual = tokens + contract(context_own, out_whole, 1, 0)
    inverse_second = root_inverse(residual)
    scaled_second = residual * inverse_second
    normed_second = (scaled_second * gain_second).astype(bf16)
    rows = quad_gather(normed_second, 3)

    gate_proj = contract(rows, gate_here, 1, 1)
    up_proj = contract(rows, up_here, 1, 1)
    sigmoid_gate = jax.nn.sigmoid(gate_proj)
    silu_gate = gate_proj * sigmoid_gate
    hidden = (silu_gate * up_proj).astype(bf16)
    ffn_parts = contract(hidden, down_here, 1, 0).astype(bf16)
    grad_hidden = contract(cots, down_here, 1, 1)
    grad_gate_act = (
        grad_hidden * up_proj * sigmoid_gate * (1.0 + gate_proj * (1.0 - sigmoid_gate))
    ).astype(bf16)
    grad_up_act = (grad_hidden * silu_gate).astype(bf16)
    grad_parts = (contract(grad_gate_act, gate_here, 1, 0) + contract(grad_up_act, up_here, 1, 0)).astype(bf16)
    grad_normed_second = quad_reduce(grad_parts, 4)
    grad_down = contract(hidden, cots, 0, 0).astype(bf16)
    grad_gate = contract(grad_gate_act, rows, 0, 0).astype(bf16)
    grad_up = contract(grad_up_act, rows, 0, 0).astype(bf16)

    grad_from_norm, gain_second_part = norm_back(
        grad_normed_second, scaled_second, inverse_second, gain_second
    )
    grad_residual = cotangent.astype(f32) + grad_from_norm
    grad_low = grad_residual.astype(bf16)
    grad_context, query_x = to_heads(contract(grad_low, out_whole, 1, 1).astype(bf16), query_0, 5)
    grad_out = contract(context_own, grad_low, 0, 0).astype(bf16)
    grad_queries, grad_keys, grad_values = attend_back(
        starts, queries, keys, values, grad_context, log_totals)
    grad_kv = jnp.stack([grad_keys, grad_values], axis=1)
    grad_query = contract(rows_first, grad_queries, 0, 0).astype(bf16)
    grad_queries_own, query_whole = to_tokens_last(grad_queries, query_y, query_0, query_x, 6)
    grad_normed_first = contract(grad_queries_own, query_whole, 1, 1)
    grad_from_first, gain_first_part = norm_back(
        grad_normed_first, scaled_first, inverse_first, gain_first
    )
    grad_input = grad_residual + grad_from_first
    gains = jnp.stack([gain_first_part, gain_second_part]).reshape(-1, 256)
    down_shard, gate_shard, up_shard, out_shard, query_shard, ffn_sum, gain_sums = reduce_call(
        grad_down, grad_gate, grad_up, grad_out, grad_query, ffn_parts, gains, 7)
    output = (residual + ffn_sum).astype(bf16)
    gain_sums = gain_sums.reshape(2, -1)
    return (output, grad_input, grad_kv, gain_sums[0], gain_sums[1], query_shard, out_shard,
            gate_shard.T, up_shard.T, down_shard)


def solution(mesh):
    in_specs = (
        P(("dp", "mp"), None),
        P("dp", None, "mp"),
        P("dp", None),
        P(),
        P(),
        P("dp", "mp"),
        P("mp", "dp"),
        P("dp", "mp"),
        P("dp", "mp"),
        P("mp", "dp"),
        P(("dp", "mp"), None),
    )
    out_specs = (
        P(("dp", "mp"), None),
        P(("dp", "mp"), None),
        P("dp", None, "mp"),
        P(),
        P(),
        P("dp", "mp"),
        P("mp", "dp"),
        P("dp", "mp"),
        P("dp", "mp"),
        P("mp", "dp"),
    )
    fast = mesh.shape["dp"] == 8 and mesh.shape["mp"] == 4
    body = fast_body if fast else plain_body
    return jax.shard_map(body, mesh=mesh, in_specs=in_specs, out_specs=out_specs, check_vma=False)
```

```python
import jax
import jax.numpy as jnp
from jax import lax
from jax.experimental import pallas as pl
from jax.experimental.pallas import tpu as pltpu
from jax.sharding import PartitionSpec as P

f32 = jnp.float32
bf16 = jnp.bfloat16
HEAD_DIM = 128
MP = 4
epsilon = 1e-06


MESH = pl.DeviceIdType.MESH
Z_LOW, Z_HIGH, CORE, SIDE, DEEP = 1, 2, 4, 8, 16
ANY = pl.BlockSpec(memory_space=pl.ANY)
VM = pl.BlockSpec(memory_space=pltpu.VMEM)


class Place:
    def __init__(self):
        self.dp = lax.axis_index("dp")
        self.mp = lax.axis_index("mp")

    def bit(self, mask):
        return ((self.dp * 4 + self.mp) // mask) % 2

    def partner(self, mask):
        flip_dp, flip_mp = mask // 4, mask % 4
        return (self.flip(self.dp, flip_dp), self.flip(self.mp, flip_mp))

    def flip(self, value, flips):
        for mask in (1, 2, 4):
            if flips & mask:
                value = value + mask - 2 * mask * ((value // mask) % 2)
        return value


class Copies:
    def __init__(self, place, send_sems, recv_sems, local_sems=None):
        self.place, self.send_sems, self.recv_sems = place, send_sems, recv_sems
        self.local_sems = local_sems
        self.count = 0
        self.local_count = 0
        self.pending = []

    def describe(self, source, target, device, slot):
        return pltpu.make_async_remote_copy(
            src_ref=source, dst_ref=target, send_sem=self.send_sems.at[slot],
            recv_sem=self.recv_sems.at[slot], device_id=device, device_id_type=MESH)

    def swap(self, source, target, mask):
        slot = self.count
        self.count += 1
        copy = self.describe(source, target, self.place.partner(mask), slot)
        copy.start()
        item = {"copy": copy, "got": False}
        self.pending.append(item)
        return item

    def got(self, item):
        if not item["got"]:
            item["got"] = True
            if "get_if" in item:
                @pl.when(item["get_if"])
                def _():
                    item["get"].wait_recv()
            else:
                item["copy"].wait_recv()

    def step(self, block, mp_send, mp_get, direction, send_if, get_if):
        slot = self.count
        self.count += 1
        place = self.place
        other = jnp.clip(place.mp + direction, 0, 3)
        sent, target = block(mp_send)
        copy = self.describe(sent, target, (place.dp, other), slot)

        @pl.when(send_if)
        def _():
            copy.start()
        sent2, target2 = block(mp_get)
        get = self.describe(sent2, target2, (place.dp, other), slot)
        item = {"copy": copy, "got": False, "send_if": send_if, "get_if": get_if, "get": get}
        self.pending.append(item)
        return item

    def local(self, source, target):
        copy = pltpu.make_async_copy(source, target, self.local_sems.at[self.local_count])
        self.local_count += 1
        copy.start()
        return copy

    def finish(self):
        for item in self.pending:
            self.got(item)
        for item in self.pending:
            if "send_if" in item:
                @pl.when(item["send_if"])
                def _():
                    item["copy"].wait_send()
            elif "sent" not in item:
                item["copy"].wait_send()


def greet(place, masks):
    barrier = pltpu.get_barrier_semaphore()
    for mask in masks:
        pl.semaphore_signal(barrier, inc=1, device_id=place.partner(mask), device_id_type=MESH)
    pl.semaphore_wait(barrier, len(masks))


def gather_kernel(first, cot, wq, wo, wg, wu, wd, rows, cots, query, wide, out, gate, up, down,
                  send_sems, recv_sems, local_sems):
    place = Place()
    dp, mp = place.dp, place.mp
    side = place.bit(SIDE)
    locals_ = []
    copies = Copies(place, send_sems, recv_sems, local_sems)
    half = wd.shape[0] // 2
    blk = wd.shape[1]
    share = first.shape[0]
    zrow = wo.shape[0]
    zcol = wq.shape[1]
    nchunk = 2
    chunk = share // nchunk
    mats = ((wg, gate), (wu, up), (wd, down))
    own, across = side, 1 - side
    DEEPER, OTHER = 2, 4
    greet(place, (1, 2, 3, CORE, SIDE, DEEP))

    def tile(whole, z, spot):
        return whole.at[pl.ds(z * half, half), pl.ds(spot * blk, blk)]

    def qrows(spot):
        return query.at[pl.ds(spot * blk, blk), :]

    def columns(spot):
        return out.at[:, pl.ds(spot * blk, blk)]

    def row_block(c, source_is_input):
        def get(m):
            target = rows.at[pl.ds(m * share + c * chunk, chunk), :]
            source = first.at[pl.ds(c * chunk, chunk), :] if source_is_input else target
            return source, target
        return get

    def out_block(source_is_input):
        def get(m):
            target = out.at[pl.ds(m * zrow, zrow), pl.ds(own * blk, blk)]
            return (wo if source_is_input else target), target
        return get

    def wide_block(source_is_input):
        def get(m):
            target = wide.at[:, pl.ds(m * zcol, zcol)]
            return (wq if source_is_input else target), target
        return get

    store = {}

    def line(step, block_of, key):
        store[("r", key, step)] = copies.step(block_of, mp - (step - 1), mp - step, 1,
                                              (mp >= step - 1) & (mp < 3), mp >= step)
        store[("l", key, step)] = copies.step(block_of, mp + (step - 1), mp + step, -1,
                                              (mp <= 3 - (step - 1)) & (mp > 0), mp <= 3 - step)

    def arrive(key, step):
        copies.got(store[("r", key, step)])
        copies.got(store[("l", key, step)])

    own_piece = [weight.at[pl.ds(side * half, half), :] for weight, _ in mats]
    zhop = [[], [], []]
    yhop = [[], [], []]
    core = []

    def send_z(i, source, spot):
        zhop[i].append(copies.swap(source, tile(mats[i][1], 1, spot), Z_HIGH))

    def send_y(i, source, z, spot):
        yhop[i].append((copies.swap(source, tile(mats[i][1], z, spot + DEEPER), DEEP), z, spot + DEEPER))

    def core_tile(i, z, spot, source=None):
        piece = tile(mats[i][1], z, spot)
        core.append(copies.swap(piece if source is None else source, tile(mats[i][1], z, spot + OTHER), CORE))

    def core_query(spot, source=None):
        core.append(copies.swap(qrows(spot) if source is None else source, qrows(spot + OTHER), CORE))

    def core_out(spot):
        core.append(copies.swap(columns(spot), columns(spot + OTHER), CORE))

    line(1, out_block(True), "o")
    send_z(0, own_piece[0], own)
    xhop = [copies.swap(weight.at[pl.ds((1 - side) * half, half), :], tile(whole, 0, own), SIDE)
            for weight, whole in mats]
    wq_y = copies.swap(wq, qrows(own + DEEPER), DEEP)
    for i in range(3):
        send_y(i, own_piece[i], 0, own)
    wq_x = [copies.swap(wq, qrows(own), SIDE)]
    locals_.append(copies.local(first, rows.at[pl.ds(mp * share, share), :]))
    locals_.append(copies.local(cot, cots.at[0:share, :]))
    locals_.append(copies.local(wq, qrows(own)))
    locals_.append(copies.local(wo, out.at[pl.ds(mp * zrow, zrow), pl.ds(own * blk, blk)]))
    for i in range(3):
        locals_.append(copies.local(own_piece[i], tile(mats[i][1], 0, own)))
    locals_.append(copies.local(wq, wide.at[:, pl.ds(mp * zcol, zcol)]))
    for i in range(3):
        core_tile(i, 0, own, own_piece[i])
    core_query(own, wq)
    copies.got(wq_y)
    wq_x.append(copies.swap(qrows(own + DEEPER), qrows(own + DEEPER), SIDE))
    core_query(own + DEEPER)
    cot_x = copies.swap(cot, cots.at[share:2 * share, :], SIDE)
    arrive("o", 1)
    line(2, out_block(False), "o")
    send_z(1, own_piece[1], own)
    arrive("o", 2)
    line(3, out_block(False), "o")
    send_z(2, own_piece[2], own)
    for c in range(nchunk):
        line(1, row_block(c, True), c)
    for i in range(3):
        copies.got(xhop[i])
        piece = tile(mats[i][1], 0, across)
        send_y(i, piece, 0, across)
        send_z(i, piece, across)
        core_tile(i, 0, across)
    for item, spot in zip(wq_x, (across, across + DEEPER)):
        copies.got(item)
        core_query(spot)
    arrive("o", 3)
    for copy in locals_:
        copy.wait()
    out_y = copies.swap(columns(own), columns(own + DEEPER), DEEP)
    out_x = [copies.swap(columns(own), columns(own), SIDE)]
    core_out(own)
    for i in range(3):
        copies.got(zhop[i][0])
        send_y(i, tile(mats[i][1], 1, own), 1, own)
        core_tile(i, 1, own)
    line(1, wide_block(True), "w")
    for c in range(nchunk):
        arrive(c, 1)
        line(2, row_block(c, False), c)
    copies.got(out_y)
    out_x.append(copies.swap(columns(own + DEEPER), columns(own + DEEPER), SIDE))
    core_out(own + DEEPER)
    cot_z = copies.swap(cot, cots.at[2 * share:3 * share, :], Z_LOW)
    for i in range(3):
        copies.got(zhop[i][1])
        send_y(i, tile(mats[i][1], 1, across), 1, across)
        core_tile(i, 1, across)
    arrive("w", 1)
    line(2, wide_block(False), "w")
    for c in range(nchunk):
        arrive(c, 2)
        line(3, row_block(c, False), c)
    arrive("w", 2)
    line(3, wide_block(False), "w")
    copies.got(out_x[0])
    core_out(across)
    copies.got(cot_z)
    cot_xz = copies.swap(cots.at[2 * share:3 * share, :], cots.at[3 * share:4 * share, :], SIDE)
    for j in range(4):
        for i in range(3):
            item, z, spot = yhop[i][j]
            copies.got(item)
            core_tile(i, z, spot)
    copies.got(out_x[1])
    core_out(across + DEEPER)
    copies.finish()


def gather_call(first, cot, wq, wo, wg, wu, wd):
    share, width = first.shape
    hidden = wd.shape[0]
    shapes = (
        (share * 4, width), (share * 4, width), (width, wq.shape[1]), (wq.shape[0], width), (width, width),
        (hidden, width), (hidden, width), (hidden, width),
    )
    return pl.pallas_call(
        gather_kernel,
        out_shape=tuple(jax.ShapeDtypeStruct(s, bf16) for s in shapes),
        in_specs=[VM] * 7,
        out_specs=(ANY,) * 8,
        scratch_shapes=[pltpu.SemaphoreType.DMA((110,)), pltpu.SemaphoreType.DMA((110,)),
                        pltpu.SemaphoreType.DMA((9,))],
        compiler_params=pltpu.CompilerParams(collective_id=1, has_side_effects=True, vmem_limit_bytes=16 << 20),
        name="gather_all",
    )(first, cot, wq, wo, wg, wu, wd)


DMA = pltpu.SemaphoreType.DMA


def dot(left, right, left_dim, right_dim):
    return lax.dot_general(
        left, right, (((left_dim,), (right_dim,)), ((), ())), preferred_element_type=f32)


def params(ident, vmem=32 << 20):
    return pltpu.CompilerParams(collective_id=ident, has_side_effects=True, vmem_limit_bytes=vmem)


def tokens_kernel(heads, query_y, query_0, query_x, own, whole, send_sems, recv_sems, local_sems):
    place = Place()
    mp = place.mp
    side = place.bit(SIDE)
    share, local = own.shape[0], heads.shape[1]
    blk = query_0.shape[0]
    copies = Copies(place, send_sems, recv_sems, local_sems)

    def rows(spot):
        return whole.at[pl.ds(spot * blk, blk), :]

    greet(place, (1, 2, 3, SIDE, CORE))
    across = copies.swap(query_y, rows(side + 2), SIDE)
    for mask in (2, 3, 1):
        other = place.partner(mask)[1]
        copies.swap(heads.at[pl.ds(other * share, share), :], own.at[:, pl.ds(mp * local, local)], mask)
    held = [copies.local(query_0, rows(side)), copies.local(query_y, rows(side + 2)),
            copies.local(query_x, rows(1 - side))]
    copies.swap(query_0, rows(side + 4), CORE)
    copies.swap(query_y, rows(side + 6), CORE)
    copies.swap(query_x, rows(1 - side + 4), CORE)
    own[:, pl.ds(mp * local, local)] = heads[pl.ds(mp * share, share), :]
    for copy in held:
        copy.wait()
    copies.got(across)
    copies.swap(rows(1 - side + 2), rows(1 - side + 6), CORE)
    copies.finish()


def tokens_hop_kernel(heads, block, own, hopped, send_sems, recv_sems):
    place = Place()
    mp = place.mp
    share, local = own.shape[0], heads.shape[1]
    greet(place, (1, 2, 3, DEEP))
    copies = Copies(place, send_sems, recv_sems)
    for mask in (2, 3, 1):
        other = place.partner(mask)[1]
        copies.swap(heads.at[pl.ds(other * share, share), :], own.at[:, pl.ds(mp * local, local)], mask)
    copies.swap(block, hopped, DEEP)
    own[:, pl.ds(mp * local, local)] = heads[pl.ds(mp * share, share), :]
    copies.finish()


def heads_hop_kernel(own, block, heads, hopped, send_sems, recv_sems):
    place = Place()
    mp = place.mp
    share, local = own.shape[0], heads.shape[1]
    greet(place, (1, 2, 3, SIDE))
    copies = Copies(place, send_sems, recv_sems)
    for mask in (2, 3, 1):
        other = place.partner(mask)[1]
        copies.swap(own.at[:, pl.ds(other * local, local)], heads.at[pl.ds(mp * share, share), :], mask)
    copies.swap(block, hopped, SIDE)
    heads[pl.ds(mp * share, share), :] = own[:, pl.ds(mp * local, local)]
    copies.finish()


def to_tokens(heads, block, ident):
    shape = (heads.shape[0] // 4, heads.shape[1] * 4)
    return pl.pallas_call(
        tokens_hop_kernel,
        out_shape=(jax.ShapeDtypeStruct(shape, bf16), jax.ShapeDtypeStruct(block.shape, bf16)),
        in_specs=[VM, VM], out_specs=(VM, VM),
        scratch_shapes=[DMA((4,)), DMA((4,))], compiler_params=params(ident), name="to_tokens")(heads, block)


def to_tokens_last(heads, query_y, query_0, query_x, ident):
    shape = (heads.shape[0] // 4, heads.shape[1] * 4)
    width = query_0.shape[1]
    return pl.pallas_call(
        tokens_kernel,
        out_shape=(jax.ShapeDtypeStruct(shape, bf16), jax.ShapeDtypeStruct((width, width), bf16)),
        in_specs=[VM] * 4, out_specs=(VM, ANY),
        scratch_shapes=[DMA((8,)), DMA((8,)), DMA((3,))], compiler_params=params(ident),
        name="to_tokens_last")(heads, query_y, query_0, query_x)


def to_heads(own, block, ident):
    shape = (own.shape[0] * 4, own.shape[1] // 4)
    return pl.pallas_call(
        heads_hop_kernel,
        out_shape=(jax.ShapeDtypeStruct(shape, bf16), jax.ShapeDtypeStruct(block.shape, bf16)),
        in_specs=[VM, VM], out_specs=(VM, VM),
        scratch_shapes=[DMA((4,)), DMA((4,))], compiler_params=params(ident), name="to_heads")(own, block)


def quad_gather_kernel(own, rows, send_sems, recv_sems):
    place = Place()
    share = own.shape[0]
    half = share // 2
    greet(place, (Z_LOW, SIDE))
    copies = Copies(place, send_sems, recv_sems)
    a, b = pl.ds(0, half), pl.ds(half, half)

    def at(quarter, part):
        return rows.at[pl.ds(quarter * share + part * half, half), :]

    low_a = copies.swap(own.at[a, :], at(2, 0), Z_LOW)
    side_b = copies.swap(own.at[b, :], at(1, 1), SIDE)
    low_b = copies.swap(own.at[b, :], at(2, 1), Z_LOW)
    side_a = copies.swap(own.at[a, :], at(1, 0), SIDE)
    rows[0:share, :] = own[...]
    copies.got(low_a)
    copies.swap(at(2, 0), at(3, 0), SIDE)
    copies.got(side_b)
    copies.swap(at(1, 1), at(3, 1), Z_LOW)
    copies.finish()


def quad_gather(own, ident):
    return pl.pallas_call(
        quad_gather_kernel, out_shape=jax.ShapeDtypeStruct((own.shape[0] * 4, own.shape[1]), bf16),
        in_specs=[VM], out_specs=VM, scratch_shapes=[DMA((6,)), DMA((6,))],
        compiler_params=params(ident), name="quad_gather")(own)


def add_into(target, rows, *others, step=32):
    start, count = rows
    pieces = count // step

    def one(i, carry):
        total = target[pl.ds(start + i * step, step), :].astype(f32)
        for other in others:
            total = total + other[pl.ds(i * step, step), :].astype(f32)
        target[pl.ds(start + i * step, step), :] = total.astype(target.dtype)
        return carry

    lax.fori_loop(0, pieces, one, 0)


class QuadReduce:
    def __init__(self, copies, parts, relay, landed):
        self.copies, self.parts, self.relay, self.landed = copies, parts, relay, landed
        self.share = parts.shape[0] // 4
        self.half = self.share // 2

    def start(self):
        share, half = self.share, self.half
        self.first = self.copies.swap(self.parts.at[pl.ds(3 * share, half), :], self.relay.at[0], SIDE)
        self.second = self.copies.swap(self.parts.at[pl.ds(3 * share + half, half), :], self.relay.at[1], Z_LOW)
        self.side = [self.copies.swap(self.parts.at[pl.ds(share, half), :], self.landed.at[0, pl.ds(0, half), :], SIDE)]
        self.low = [self.copies.swap(self.parts.at[pl.ds(2 * share + half, half), :], self.landed.at[1, pl.ds(half, half), :], Z_LOW)]

    def relayed(self):
        share, half = self.share, self.half
        self.copies.got(self.first)
        add_into(self.parts, (2 * share, half), self.relay.at[0])
        self.low.append(self.copies.swap(self.parts.at[pl.ds(2 * share, half), :], self.landed.at[1, pl.ds(0, half), :], Z_LOW))
        self.copies.got(self.second)
        add_into(self.parts, (share + half, half), self.relay.at[1])
        self.side.append(self.copies.swap(self.parts.at[pl.ds(share + half, half), :], self.landed.at[0, pl.ds(half, half), :], SIDE))

    def arrived(self):
        for item in self.side + self.low:
            self.copies.got(item)


def quad_reduce_kernel(parts_in, total, parts, relay, landed, send_sems, recv_sems, local_sem):
    place = Place()
    load = pltpu.make_async_copy(parts_in, parts, local_sem)
    load.start()
    greet(place, (Z_LOW, SIDE))
    copies = Copies(place, send_sems, recv_sems)
    load.wait()
    reduce = QuadReduce(copies, parts, relay, landed)
    reduce.start()
    reduce.relayed()
    reduce.arrived()
    share = total.shape[0]

    def one(i, carry):
        here = pl.ds(i * 32, 32)
        total[here, :] = (parts[here, :].astype(f32) + landed[0, here, :].astype(f32)
                          + landed[1, here, :].astype(f32))
        return carry

    lax.fori_loop(0, share // 32, one, 0)
    copies.finish()


def quad_reduce(parts, ident):
    share, width = parts.shape[0] // 4, parts.shape[1]
    return pl.pallas_call(
        quad_reduce_kernel, out_shape=jax.ShapeDtypeStruct((share, width), f32),
        in_specs=[ANY], out_specs=VM,
        scratch_shapes=[pltpu.VMEM((share * 4, width), bf16), pltpu.VMEM((2, share // 2, width), bf16),
                        pltpu.VMEM((2, share, width), bf16), DMA((6,)), DMA((6,)), DMA],
        compiler_params=params(ident), name="quad_reduce")(parts)


def all_sum_kernel(value, total, got, send_sems, recv_sems):
    place = Place()
    masks = (1, 2, CORE, SIDE, DEEP)
    greet(place, masks)
    copies = Copies(place, send_sems, recv_sems)
    total[...] = value[...]
    for i, mask in enumerate(masks):
        item = copies.swap(total, got.at[i], mask)
        copies.got(item)
        item["copy"].wait_send()
        item["sent"] = True
        total[...] = total[...] + got[i]
    copies.finish()


def all_sum(value, ident):
    return pl.pallas_call(
        all_sum_kernel, out_shape=jax.ShapeDtypeStruct(value.shape, f32), in_specs=[VM], out_specs=VM,
        scratch_shapes=[pltpu.VMEM((5,) + value.shape, f32), DMA((5,)), DMA((5,))],
        compiler_params=params(ident), name="all_sum")(value)


ROWS=256
DOC_MOST=512


def key_range(block, seq_len):
    low = max(0, block * ROWS - DOC_MOST + 1) // ROWS * ROWS
    return low, min(seq_len, (block + 1) * ROWS)


def scores_turned(q, k, starts, low, first, scale):
    s = dot(k, q, 1, 1) * scale
    key_pos = low + lax.broadcasted_iota(jnp.int32, s.shape, 0)
    query_pos = first + lax.broadcasted_iota(jnp.int32, s.shape, 1)
    return jnp.where((key_pos >= starts) & (key_pos <= query_pos), s, -1e30)


def forward_kernel(starts_ref, q_ref, k_ref, v_ref, ctx_ref, lse_ref):
    seq_len = q_ref.shape[0]
    scale = HEAD_DIM ** -0.5
    for block in range(seq_len // ROWS):
        low, high = key_range(block, seq_len)
        here = pl.ds(block * ROWS, ROWS)
        k = k_ref[low:high, :]
        v = v_ref[low:high, :]
        s = scores_turned(q_ref[here, :], k, starts_ref[:, here], low, block * ROWS, scale)
        top = jnp.max(s, axis=0, keepdims=True)
        raised = jnp.exp(s - top)
        total = jnp.sum(raised, axis=0, keepdims=True)
        low_probs = (raised * (1.0 / total)).astype(bf16)
        ctx_ref[here, :] = dot(low_probs, v, 0, 0).astype(bf16)
        lse_ref[0, :, here] = top + jnp.log(total)


def backward_kernel(starts_ref, q_ref, k_ref, v_ref, grad_ref, lse_ref, dq_ref, dk_ref, dv_ref):
    seq_len = q_ref.shape[0]
    scale = HEAD_DIM ** -0.5
    for block in range(seq_len // ROWS):
        low, high = key_range(block, seq_len)
        here = pl.ds(block * ROWS, ROWS)
        k = k_ref[low:high, :]
        v = v_ref[low:high, :]
        q = q_ref[here, :]
        grad = grad_ref[here, :]
        s = scores_turned(q, k, starts_ref[:, here], low, block * ROWS, scale)
        probs = jnp.exp(s - lse_ref[0, :, here])
        grad_probs = dot(v, grad, 1, 1)
        spread = jnp.sum(probs * grad_probs, axis=0, keepdims=True)
        grad_s = (probs * (grad_probs - spread)).astype(bf16)
        dq_ref[here, :] = (dot(grad_s, k, 0, 0) * scale).astype(bf16)
        dk = dot(grad_s, q, 1, 0) * scale
        dv = dot(probs.astype(bf16), grad, 1, 0)
        old = max(low, min(high, block * ROWS))
        if low == 0 and block == 0:
            dk_ref[low:high, :] = dk
            dv_ref[low:high, :] = dv
        else:
            n = old - low
            dk_ref[low:old, :] += dk[:n]
            dv_ref[low:old, :] += dv[:n]
            dk_ref[old:high, :] = dk[n:]
            dv_ref[old:high, :] = dv[n:]


def specs(seq_len):
    row = pl.BlockSpec((1, seq_len), lambda h: (0, 0))
    head = pl.BlockSpec((seq_len, HEAD_DIM), lambda h: (0, h))
    lse = pl.BlockSpec((1, 1, seq_len), lambda h: (h, 0, 0))
    return row, head, lse


def attend(starts, q, k, v):
    seq_len, width = q.shape
    heads = width // HEAD_DIM
    row, head, lse = specs(seq_len)
    flops = heads * seq_len * seq_len * HEAD_DIM * 3
    return pl.pallas_call(
        forward_kernel, grid=(heads,),
        in_specs=[row, head, head, head], out_specs=(head, lse),
        out_shape=(jax.ShapeDtypeStruct(q.shape, bf16), jax.ShapeDtypeStruct((heads, 1, seq_len), f32)),
        cost_estimate=pl.CostEstimate(flops=flops, bytes_accessed=4 * q.size * 2, transcendentals=heads * seq_len * seq_len // 2),
        name="attend",
    )(starts, q, k, v)


def attend_back(starts, q, k, v, grad, lse_array):
    seq_len, width = q.shape
    heads = width // HEAD_DIM
    row, head, lse = specs(seq_len)
    flops = heads * seq_len * seq_len * HEAD_DIM * 7
    wide = jax.ShapeDtypeStruct(q.shape, f32)
    return pl.pallas_call(
        backward_kernel, grid=(heads,),
        in_specs=[row, head, head, head, head, lse], out_specs=(head, head, head),
        out_shape=(jax.ShapeDtypeStruct(q.shape, bf16), wide, wide),
        cost_estimate=pl.CostEstimate(flops=flops, bytes_accessed=9 * q.size * 2, transcendentals=heads * seq_len * seq_len // 2),
        name="attend_back",
    )(starts, q, k, v, grad, lse_array)


def starts_of(segments):
    return jnp.sum((segments[0][None, :] < segments[0][:, None]).astype(jnp.int32), axis=1)[None, :]


def hidden_cuts(hidden):
    cuts = []
    start = 0
    while start < hidden:
        size = min(512, hidden - start)
        cuts.append((start, size))
        start += size
    return cuts


def ffn_kernel(normed, cots_in, down_in, gate_in, up_in, total, fparts_out, sums_out,
               weights, tokens, acts, dparts, relay, landed, fparts,
               send_sems, recv_sems, local_sems, free_sem):
    place = Place()
    share, width = normed.shape
    hidden = down_in.shape[0]
    half = share // 2
    wide = width // 2
    cuts = hidden_cuts(hidden)
    copies = Copies(place, send_sems, recv_sems, local_sems)
    load_cots = copies.local(cots_in, tokens.at[0])
    load_w = [copies.local(w, weights.at[i]) for i, w in enumerate((down_in, gate_in, up_in))]
    greet(place, (Z_LOW, SIDE, CORE))

    def at(quarter, part):
        return tokens.at[1, pl.ds(quarter * share + part * half, half), :]

    a, b = pl.ds(0, half), pl.ds(half, half)
    low_a = copies.swap(normed.at[a, :], at(2, 0), Z_LOW)
    side_b = copies.swap(normed.at[b, :], at(1, 1), SIDE)
    low_b = copies.swap(normed.at[b, :], at(2, 1), Z_LOW)
    side_a = copies.swap(normed.at[a, :], at(1, 0), SIDE)
    tokens[1, 0:share, :] = normed[...]

    def block(r):
        here = pl.ds(r * share, share)
        for start, size in cuts:
            rows = tokens[1, here, :]
            gate = dot(rows, weights[1, start:start + size, :], 1, 1)
            up = dot(rows, weights[2, start:start + size, :], 1, 1)
            grad = dot(tokens[0, here, :], weights[0, start:start + size, :], 1, 1)
            sigmoid = jax.nn.sigmoid(gate)
            silu = gate * sigmoid
            acts[0, here, start:start + size] = (silu * up).astype(bf16)
            acts[1, here, start:start + size] = (
                grad * up * sigmoid * (1.0 + gate * (1.0 - sigmoid))).astype(bf16)
            acts[2, here, start:start + size] = (grad * silu).astype(bf16)

        def columns(n, carry):
            there = pl.ds(pl.multiple_of(n * 512, 512), 512)
            dparts[here, there] = (dot(acts[1, here, :], weights[1, :, there], 1, 0)
                                   + dot(acts[2, here, :], weights[2, :, there], 1, 0)).astype(bf16)
            fparts[here, there] = dot(acts[0, here, :], weights[0, :, there], 1, 0).astype(bf16)
            return carry

        lax.fori_loop(0, width // 512, columns, 0)

    for copy in load_w:
        copy.wait()
    load_cots.wait()
    got = {"across": None}

    def step(r, carry):
        @pl.when(r == 1)
        def _():
            low_a["copy"].wait_recv()
            side_b["copy"].wait_recv()
            forward[0].start()
            forward[1].start()
            side_a["copy"].wait_recv()
            low_b["copy"].wait_recv()

        @pl.when(r == 3)
        def _():
            forward[0].wait_recv()
            forward[1].wait_recv()
        block(r)
        return carry

    forward = [copies.describe(at(2, 0), at(3, 0), place.partner(SIDE), copies.count),
               copies.describe(at(1, 1), at(3, 1), place.partner(Z_LOW), copies.count + 1)]
    copies.count += 2
    lax.fori_loop(0, 4, step, 0)
    for item in (low_a, side_b, low_b, side_a):
        item["got"] = True
    pl.semaphore_signal(free_sem, inc=1, device_id=place.partner(CORE), device_id_type=MESH)
    reduce = QuadReduce(copies, dparts, relay, landed)
    reduce.start()
    save = copies.local(fparts, fparts_out)

    base = copies.count
    copies.count += 3

    def give_copy(i):
        return copies.describe(weights.at[i, :, pl.ds(0, wide)], weights.at[i, :, pl.ds(wide, wide)],
                               place.partner(CORE), base + i)

    def give(i, carry):
        right = tokens[jnp.minimum(i, 1), :, wide:]
        for start, size in cuts:
            weights[i, start:start + size, 0:wide] = dot(
                acts[i, :, start:start + size], right, 0, 0).astype(bf16)

        @pl.when(i == 0)
        def _():
            pl.semaphore_wait(free_sem, 1)
        give_copy(i).start()
        return carry

    lax.fori_loop(0, 3, give, 0)
    reduce.relayed()

    def keep(i, carry):
        give_copy(i).wait_recv()
        right = tokens[jnp.minimum(i, 1), :, 0:wide]
        for start, size in cuts:
            rows = slice(start, start + size)
            weights[i, rows, wide:] = (dot(acts[i, :, rows], right, 0, 0)
                                       + weights[i, rows, wide:].astype(f32)).astype(bf16)
        pltpu.make_async_copy(weights.at[i, :, pl.ds(wide, wide)], sums_out.at[i], local_sems.at[5 + i]).start()
        return carry

    lax.fori_loop(0, 3, keep, 0)
    reduce.arrived()

    def one(i, carry):
        here = pl.ds(i * 32, 32)
        total[here, :] = (dparts[here, :].astype(f32) + landed[0, here, :].astype(f32)
                          + landed[1, here, :].astype(f32))
        return carry

    lax.fori_loop(0, share // 32, one, 0)
    for i in range(3):
        give_copy(i).wait_send()
        pltpu.make_async_copy(weights.at[i, :, pl.ds(wide, wide)], sums_out.at[i], local_sems.at[5 + i]).wait()
    for copy in forward:
        copy.wait_send()
    save.wait()
    copies.finish()


def ffn_call(normed, cots, down, gate, up, ident):
    share, width = normed.shape
    hidden = down.shape[0]
    V = pltpu.VMEM
    flops = 2 * share * 4 * width * hidden * 9
    return pl.pallas_call(
        ffn_kernel,
        out_shape=(jax.ShapeDtypeStruct((share, width), f32), jax.ShapeDtypeStruct((share * 4, width), bf16),
                   jax.ShapeDtypeStruct((3, hidden, width // 2), bf16)),
        in_specs=[VM] + [ANY] * 4,
        out_specs=(VM, ANY, ANY),
        scratch_shapes=[
            V((3, hidden, width), bf16), V((2, share * 4, width), bf16), V((3, share * 4, hidden), bf16),
            V((share * 4, width), bf16), V((2, share // 2, width), bf16), V((2, share, width), bf16),
            V((share * 4, width), bf16),
            DMA((16,)), DMA((16,)), DMA((8,)), pltpu.SemaphoreType.REGULAR],
        compiler_params=params(ident, 63 << 20),
        cost_estimate=pl.CostEstimate(flops=flops, bytes_accessed=40 << 20, transcendentals=share * 4 * hidden),
        name="feed_forward",
    )(normed, cots, down, gate, up)


class Grid:
    def __init__(self, dp):
        self.dp = dp
        self.size = dp * MP
        self.rest = []
        mask = 16
        while mask < self.size:
            self.rest.append(mask)
            mask *= 2
        self.relative = [CORE] + self.rest
        self.me = lax.axis_index("dp") * MP + lax.axis_index("mp")
        self.me_mp = lax.axis_index("mp")
        self.me_dp = lax.axis_index("dp")

    def swap(self, value, mask):
        return lax.ppermute(value, ("dp", "mp"), [(i, i ^ mask) for i in range(self.size)])

    def bit(self, mask):
        return (self.me // mask) % 2

    def spread(self, value):
        block = value.shape[-1] // self.dp
        pieces = []
        for spot in range(self.dp):
            flips = 0
            digits = spot >> 1
            for place, mask in enumerate(reversed(self.relative)):
                if (digits >> place) & 1:
                    flips |= mask // MP
            source = ((self.me_dp ^ flips) & ~(SIDE // MP)) | ((spot & 1) * (SIDE // MP))
            pieces.append(lax.dynamic_slice_in_dim(value, source * block, block, value.ndim - 1))
        return jnp.concatenate(pieces, axis=-1)

    def restore(self, value):
        block = value.shape[-1] // self.dp
        pieces = []
        for target in range(self.dp):
            flips = (self.me_dp ^ target) * MP
            spot = 0
            for mask in self.relative:
                spot = spot * 2 + (flips // mask) % 2
            spot = spot * 2 + (target * MP // SIDE) % 2
            pieces.append(lax.dynamic_slice_in_dim(value, spot * block, block, value.ndim - 1))
        return jnp.concatenate(pieces, axis=-1)

    def ordered(self, mine, theirs, mask, axis):
        high = self.bit(mask) == 1
        return jnp.concatenate(
            [jnp.where(high, theirs, mine), jnp.where(high, mine, theirs)], axis=axis
        )

    def line_gather(self, value):
        right, left = {0: value}, {0: value}
        for step in range(1, MP):
            right[step] = lax.ppermute(
                right[step - 1], "mp", [(j, j + 1) for j in range(step - 1, MP - 1)]
            )
            left[step] = lax.ppermute(
                left[step - 1], "mp", [(j, j - 1) for j in range(1, MP - step + 1)]
            )
        return [value] + [left[d] + right[MP - d] for d in range(1, MP)]

    def exchange_mp(self, value, split, join):
        return lax.all_to_all(value, "mp", split, join, tiled=True)

    def quad_gather(self, value):
        half = value.shape[0] // 2
        from_side = self.swap(value, SIDE)
        from_low = self.swap(value, Z_LOW)
        across = jnp.concatenate(
            [self.swap(from_low[:half], SIDE), self.swap(from_side[half:], Z_LOW)], axis=0
        )
        return [value, from_side, from_low, across]

    def quad_start(self, across):
        half = across.shape[0] // 2
        return self.swap(across[:half], SIDE), self.swap(across[half:], Z_LOW)

    def quad_finish(self, relayed, for_side, for_low, own):
        by_side, by_low = relayed
        half = own.shape[0] // 2
        low_sum = jnp.concatenate(
            [(for_low[:half] + by_side.astype(f32)), for_low[half:]], axis=0
        ).astype(bf16)
        side_sum = jnp.concatenate(
            [for_side[:half], for_side[half:] + by_low.astype(f32)], axis=0
        ).astype(bf16)
        return own + self.swap(side_sum, SIDE).astype(f32) + self.swap(low_sum, Z_LOW).astype(f32)

    def all_sum(self, value):
        mask = 1
        while mask < self.size:
            value = value + self.swap(value, mask)
            mask *= 2
        return value


def contract(left, right, left_dim, right_dim):
    return lax.dot_general(
        left, right, (((left_dim,), (right_dim,)), ((), ())), preferred_element_type=jnp.float32
    )


def root_inverse(values):
    return lax.rsqrt(jnp.mean(values * values, axis=-1, keepdims=True) + epsilon)


def norm_back(grad_normed, scaled, inverse, gain):
    grad_scaled = grad_normed * gain
    grad_values = inverse * (
        grad_scaled - scaled * jnp.mean(grad_scaled * scaled, axis=-1, keepdims=True)
    )
    return (grad_values, jnp.sum(grad_normed * scaled, axis=0))


def plain_body(
    inputs,
    keys_values,
    segment_ids,
    gain_first,
    gain_second,
    w_query,
    w_out,
    w_gate,
    w_up,
    w_down,
    cotangent,
):
    query_full, out_full = (
        lax.all_gather(w_query, "dp", axis=0, tiled=True),
        lax.all_gather(w_out, "dp", axis=1, tiled=True),
    )
    gate_full, up_full, down_full = (
        lax.all_gather(w_gate, "dp", axis=0, tiled=True),
        lax.all_gather(w_up, "dp", axis=0, tiled=True),
        lax.all_gather(w_down, "dp", axis=1, tiled=True),
    )
    tokens = inputs.astype(jnp.float32)
    inverse_first = root_inverse(tokens)
    scaled_first = tokens * inverse_first
    normed_first = (scaled_first * gain_first).astype(jnp.bfloat16)
    rows_first = lax.all_gather(normed_first, "mp", axis=0, tiled=True)
    queries = contract(rows_first, query_full, 1, 0).astype(jnp.bfloat16)
    seq_len = rows_first.shape[0]
    local_width = queries.shape[1]
    head_count = local_width // HEAD_DIM
    block_rows = min(512, seq_len)
    block_count = seq_len // block_rows
    score_scale = HEAD_DIM ** (-0.5)
    key_heads = keys_values[:, 0, :].reshape(seq_len, head_count, HEAD_DIM)
    value_heads = keys_values[:, 1, :].reshape(seq_len, head_count, HEAD_DIM)
    segments = segment_ids[0]
    key_pos = jnp.arange(seq_len, dtype=jnp.int32)

    def block_scores(first_row):
        query_block = lax.dynamic_slice_in_dim(queries, first_row, block_rows, 0).reshape(
            block_rows, head_count, HEAD_DIM
        )
        scores = (
            jnp.einsum("qhd,khd->hqk", query_block, key_heads, preferred_element_type=jnp.float32)
            * score_scale
        )
        query_pos = first_row + jnp.arange(block_rows, dtype=jnp.int32)
        query_seg = lax.dynamic_slice_in_dim(segments, first_row, block_rows, 0)
        allowed = (query_pos[:, None] >= key_pos[None, :]) & (
            query_seg[:, None] == segments[None, :]
        )
        return (query_block, jnp.where(allowed[None], scores, -1e30))

    def forward_block(block_index):
        query_block, scores = block_scores(block_index * block_rows)
        row_max = jnp.max(scores, axis=-1, keepdims=True)
        raised = jnp.exp(scores - row_max)
        row_total = jnp.sum(raised, axis=-1, keepdims=True)
        weights_low = (raised / row_total).astype(jnp.bfloat16)
        blended = jnp.einsum(
            "hqk,khd->qhd", weights_low, value_heads, preferred_element_type=jnp.float32
        )
        return (
            blended.reshape(block_rows, local_width).astype(jnp.bfloat16),
            (row_max + jnp.log(row_total))[..., 0],
        )

    context_blocks, log_totals = lax.map(forward_block, jnp.arange(block_count, dtype=jnp.int32))
    context = context_blocks.reshape(seq_len, local_width)
    attn_part = lax.psum_scatter(
        contract(context, out_full, 1, 0), "mp", scatter_dimension=0, tiled=True
    )
    residual = tokens + attn_part
    inverse_second = root_inverse(residual)
    scaled_second = residual * inverse_second
    normed_second = (scaled_second * gain_second).astype(jnp.bfloat16)
    rows_second = lax.all_gather(normed_second, "mp", axis=0, tiled=True)
    gate_proj = contract(rows_second, gate_full, 1, 0)
    up_proj = contract(rows_second, up_full, 1, 0)
    sigmoid_gate = jax.nn.sigmoid(gate_proj)
    silu_gate = gate_proj * sigmoid_gate
    hidden = (silu_gate * up_proj).astype(jnp.bfloat16)
    ffn_part = lax.psum_scatter(
        contract(hidden, down_full, 1, 0).astype(jnp.bfloat16),
        "mp",
        scatter_dimension=0,
        tiled=True,
    ).astype(jnp.float32)
    output = (residual + ffn_part).astype(jnp.bfloat16)
    cot_rows = lax.all_gather(cotangent, "mp", axis=0, tiled=True)
    grad_down_w = contract(hidden, cot_rows, 0, 0)
    grad_hidden = contract(cot_rows, down_full, 1, 1)
    grad_gate_act = (
        grad_hidden * up_proj * sigmoid_gate * (1.0 + gate_proj * (1.0 - sigmoid_gate))
    ).astype(jnp.bfloat16)
    grad_up_act = (grad_hidden * silu_gate).astype(jnp.bfloat16)
    grad_gate_w = contract(rows_second, grad_gate_act, 0, 0)
    grad_up_w = contract(rows_second, grad_up_act, 0, 0)
    grad_normed_second = lax.psum_scatter(
        contract(grad_gate_act, gate_full, 1, 1) + contract(grad_up_act, up_full, 1, 1),
        "mp",
        scatter_dimension=0,
        tiled=True,
    )
    grad_from_norm, gain_second_part = norm_back(
        grad_normed_second, scaled_second, inverse_second, gain_second
    )
    grad_residual = cotangent.astype(jnp.float32) + grad_from_norm
    attn_cot = lax.all_gather(grad_residual.astype(jnp.bfloat16), "mp", axis=0, tiled=True)
    grad_out_w = contract(context, attn_cot, 0, 0)
    grad_context = contract(attn_cot, out_full, 1, 1).astype(jnp.bfloat16)

    def backward_block(state_pair, block_index):
        grad_keys, grad_values = state_pair
        first_row = block_index * block_rows
        query_block, scores = block_scores(first_row)
        log_total = lax.dynamic_index_in_dim(log_totals, block_index, 0, keepdims=False)
        weights = jnp.exp(scores - log_total[..., None])
        grad_block = lax.dynamic_slice_in_dim(grad_context, first_row, block_rows, 0).reshape(
            block_rows, head_count, HEAD_DIM
        )
        grad_weights = jnp.einsum(
            "qhd,khd->hqk", grad_block, value_heads, preferred_element_type=jnp.float32
        )
        spread = jnp.sum(weights * grad_weights, axis=-1, keepdims=True)
        grad_scores = (weights * (grad_weights - spread)).astype(jnp.bfloat16)
        grad_query_block = (
            jnp.einsum("hqk,khd->qhd", grad_scores, key_heads, preferred_element_type=jnp.float32)
            * score_scale
        ).astype(jnp.bfloat16)
        grad_keys = (
            grad_keys
            + jnp.einsum(
                "hqk,qhd->khd", grad_scores, query_block, preferred_element_type=jnp.float32
            )
            * score_scale
        )
        grad_values = grad_values + jnp.einsum(
            "hqk,qhd->khd",
            weights.astype(jnp.bfloat16),
            grad_block,
            preferred_element_type=jnp.float32,
        )
        return ((grad_keys, grad_values), grad_query_block.reshape(block_rows, local_width))

    zero_state = jnp.zeros((seq_len, head_count, HEAD_DIM), jnp.float32)
    (grad_keys, grad_values), grad_query_blocks = lax.scan(
        backward_block, (zero_state, zero_state), jnp.arange(block_count, dtype=jnp.int32)
    )
    grad_queries = grad_query_blocks.reshape(seq_len, local_width)
    grad_kv = jnp.stack(
        [grad_keys.reshape(seq_len, local_width), grad_values.reshape(seq_len, local_width)], axis=1
    )
    grad_query_w = contract(rows_first, grad_queries, 0, 0)
    grad_normed_first = lax.psum_scatter(
        contract(grad_queries, query_full, 1, 1).astype(jnp.bfloat16),
        "mp",
        scatter_dimension=0,
        tiled=True,
    ).astype(jnp.float32)
    grad_from_first, gain_first_part = norm_back(
        grad_normed_first, scaled_first, inverse_first, gain_first
    )
    grad_input = grad_residual + grad_from_first
    gain_first_sum, gain_second_sum = lax.psum((gain_first_part, gain_second_part), ("dp", "mp"))
    query_shard, out_shard, gate_shard, up_shard, down_shard = (
        lax.psum_scatter(
            grad_query_w.astype(jnp.bfloat16), "dp", scatter_dimension=0, tiled=True
        ).astype(jnp.float32),
        lax.psum_scatter(
            grad_out_w.astype(jnp.bfloat16), "dp", scatter_dimension=1, tiled=True
        ).astype(jnp.float32),
        lax.psum_scatter(
            grad_gate_w.astype(jnp.bfloat16), "dp", scatter_dimension=0, tiled=True
        ).astype(jnp.float32),
        lax.psum_scatter(
            grad_up_w.astype(jnp.bfloat16), "dp", scatter_dimension=0, tiled=True
        ).astype(jnp.float32),
        lax.psum_scatter(
            grad_down_w.astype(jnp.bfloat16), "dp", scatter_dimension=1, tiled=True
        ).astype(jnp.float32),
    )
    return (
        output,
        grad_input,
        grad_kv,
        gain_first_sum,
        gain_second_sum,
        query_shard,
        out_shard,
        gate_shard,
        up_shard,
        down_shard,
    )


def fast_body(inputs, keys_values, segment_ids, gain_first, gain_second, w_query, w_out, w_gate,
              w_up, w_down, cotangent):
    grid = Grid(8)
    share = inputs.shape[0]
    hidden_half = w_down.shape[0] // 2
    tokens = grid.spread(inputs).astype(f32)
    gain_one = grid.spread(gain_first)
    gain_two = grid.spread(gain_second)
    cot_here = grid.spread(cotangent)
    inverse_first = root_inverse(tokens)
    scaled_first = tokens * inverse_first
    normed_first = (scaled_first * gain_one).astype(bf16)

    rows_first, cots, query_part, query_0, out_whole, gate_here, up_here, down_here = gather_call(
        normed_first, cot_here, w_query, w_out, w_gate.T, w_up.T, w_down)

    queries = contract(rows_first, query_part, 1, 0).astype(bf16)
    starts = starts_of(segment_ids)
    keys = keys_values[:, 0, :]
    values = keys_values[:, 1, :]
    context, log_totals = attend(starts, queries, keys, values)
    context_own, query_y = to_tokens(context, query_0, 2)
    residual = tokens + contract(context_own, out_whole, 1, 0)
    inverse_second = root_inverse(residual)
    scaled_second = residual * inverse_second
    normed_second = (scaled_second * gain_two).astype(bf16)
    grad_normed_second, ffn_parts, ffn_sums = ffn_call(normed_second, cots, down_here, gate_here, up_here, 3)

    def quad_sum(parts):
        own, side_part, low_part, across = (parts[i * share:(i + 1) * share] for i in range(4))
        relayed = grid.quad_start(across)
        return grid.quad_finish(relayed, side_part.astype(f32), low_part.astype(f32), own.astype(f32))

    ffn_sum = quad_sum(ffn_parts)
    output = grid.restore((residual + ffn_sum).astype(bf16))

    def halves_sum(keep, give, mask):
        return keep.astype(f32) + grid.swap(give.astype(bf16), mask).astype(f32)

    def ffn_grad(total):
        for mask in grid.rest:
            half = total.shape[1] // 2
            total = halves_sum(total[:, :half], total[:, half:], mask)
        total = halves_sum(total[:hidden_half], total[hidden_half:], Z_HIGH)
        width = total.shape[1] // 2
        side = grid.bit(SIDE)
        keep = lax.dynamic_slice_in_dim(total, side * width, width, 1)
        give = lax.dynamic_slice_in_dim(total, (1 - side) * width, width, 1)
        theirs = grid.swap(give.astype(bf16), SIDE).astype(f32)
        return grid.ordered(keep, theirs, SIDE, 0)

    down_shard = ffn_grad(ffn_sums[0])
    gate_shard = ffn_grad(ffn_sums[1]).T
    up_shard = ffn_grad(ffn_sums[2]).T

    grad_from_norm, gain_second_part = norm_back(
        grad_normed_second, scaled_second, inverse_second, gain_two
    )
    grad_residual = cot_here.astype(f32) + grad_from_norm
    grad_low = grad_residual.astype(bf16)
    grad_context, query_x = to_heads(contract(grad_low, out_whole, 1, 1).astype(bf16), query_0, 5)

    def rows_reduce(total):
        for mask in [CORE] + grid.rest:
            half = total.shape[0] // 2
            total = halves_sum(total[:half], total[half:], mask)
        width = total.shape[0] // 2
        side = grid.bit(SIDE)
        keep = lax.dynamic_slice_in_dim(total, side * width, width, 0)
        give = lax.dynamic_slice_in_dim(total, (1 - side) * width, width, 0)
        return halves_sum(keep, give, SIDE)

    grad_out_t = rows_reduce(contract(grad_low, context_own, 0, 0))
    pieces = grid.exchange_mp(grad_out_t.astype(bf16), 1, 0).astype(f32)
    out_shard = jnp.sum(pieces.reshape(4, -1, pieces.shape[1]), axis=0).T

    grad_queries, grad_keys, grad_values = attend_back(
        starts, queries, keys, values, grad_context, log_totals)
    grad_kv = jnp.stack([grad_keys, grad_values], axis=1)
    query_shard = rows_reduce(contract(rows_first, grad_queries, 0, 0))
    grad_queries_own, query_whole = to_tokens_last(grad_queries, query_y, query_0, query_x, 6)
    grad_normed_first = contract(grad_queries_own, query_whole, 1, 1)
    grad_from_first, gain_first_part = norm_back(
        grad_normed_first, scaled_first, inverse_first, gain_one
    )
    grad_input = grid.restore(grad_residual + grad_from_first)
    gains = jnp.stack([grid.restore(gain_first_part), grid.restore(gain_second_part)]).reshape(-1, 256)
    gain_sums = all_sum(gains, 7).reshape(2, -1)
    return (output, grad_input, grad_kv, gain_sums[0], gain_sums[1], query_shard, out_shard,
            gate_shard, up_shard, down_shard)


def solution(mesh):
    in_specs = (
        P(("dp", "mp"), None),
        P("dp", None, "mp"),
        P("dp", None),
        P(),
        P(),
        P("dp", "mp"),
        P("mp", "dp"),
        P("dp", "mp"),
        P("dp", "mp"),
        P("mp", "dp"),
        P(("dp", "mp"), None),
    )
    out_specs = (
        P(("dp", "mp"), None),
        P(("dp", "mp"), None),
        P("dp", None, "mp"),
        P(),
        P(),
        P("dp", "mp"),
        P("mp", "dp"),
        P("dp", "mp"),
        P("dp", "mp"),
        P("mp", "dp"),
    )
    fast = mesh.shape["dp"] == 8 and mesh.shape["mp"] == 4
    body = fast_body if fast else plain_body
    return jax.shard_map(body, mesh=mesh, in_specs=in_specs, out_specs=out_specs, check_vma=False)
```

```python
import jax
import jax.numpy as jnp
from jax import lax
from jax.experimental import pallas as pl
from jax.experimental.pallas import tpu as pltpu
from jax.sharding import PartitionSpec as P

f32 = jnp.float32
bf16 = jnp.bfloat16
HEAD_DIM = 128
MP = 4
epsilon = 1e-06


MESH = pl.DeviceIdType.MESH
Z_LOW, Z_HIGH, CORE, SIDE, DEEP = 1, 2, 4, 8, 16
ANY = pl.BlockSpec(memory_space=pl.ANY)
VM = pl.BlockSpec(memory_space=pltpu.VMEM)


class Place:
    def __init__(self):
        self.dp = lax.axis_index("dp")
        self.mp = lax.axis_index("mp")

    def bit(self, mask):
        return ((self.dp * 4 + self.mp) // mask) % 2

    def partner(self, mask):
        flip_dp, flip_mp = mask // 4, mask % 4
        return (self.flip(self.dp, flip_dp), self.flip(self.mp, flip_mp))

    def flip(self, value, flips):
        for mask in (1, 2, 4):
            if flips & mask:
                value = value + mask - 2 * mask * ((value // mask) % 2)
        return value


class Copies:
    def __init__(self, place, send_sems, recv_sems, local_sems=None):
        self.place, self.send_sems, self.recv_sems = place, send_sems, recv_sems
        self.local_sems = local_sems
        self.count = 0
        self.local_count = 0
        self.pending = []

    def describe(self, source, target, device, slot):
        return pltpu.make_async_remote_copy(
            src_ref=source, dst_ref=target, send_sem=self.send_sems.at[slot],
            recv_sem=self.recv_sems.at[slot], device_id=device, device_id_type=MESH)

    def swap(self, source, target, mask):
        slot = self.count
        self.count += 1
        copy = self.describe(source, target, self.place.partner(mask), slot)
        copy.start()
        item = {"copy": copy, "got": False}
        self.pending.append(item)
        return item

    def got(self, item):
        if not item["got"]:
            item["got"] = True
            if "get_if" in item:
                @pl.when(item["get_if"])
                def _():
                    item["get"].wait_recv()
            else:
                item["copy"].wait_recv()

    def step(self, block, mp_send, mp_get, direction, send_if, get_if):
        slot = self.count
        self.count += 1
        place = self.place
        other = jnp.clip(place.mp + direction, 0, 3)
        sent, target = block(mp_send)
        copy = self.describe(sent, target, (place.dp, other), slot)

        @pl.when(send_if)
        def _():
            copy.start()
        sent2, target2 = block(mp_get)
        get = self.describe(sent2, target2, (place.dp, other), slot)
        item = {"copy": copy, "got": False, "send_if": send_if, "get_if": get_if, "get": get}
        self.pending.append(item)
        return item

    def local(self, source, target):
        copy = pltpu.make_async_copy(source, target, self.local_sems.at[self.local_count])
        self.local_count += 1
        copy.start()
        return copy

    def finish(self):
        for item in self.pending:
            self.got(item)
        for item in self.pending:
            if "send_if" in item:
                @pl.when(item["send_if"])
                def _():
                    item["copy"].wait_send()
            elif "sent" not in item:
                item["copy"].wait_send()


def greet(place, masks):
    barrier = pltpu.get_barrier_semaphore()
    for mask in masks:
        pl.semaphore_signal(barrier, inc=1, device_id=place.partner(mask), device_id_type=MESH)
    pl.semaphore_wait(barrier, len(masks))


def gather_kernel(first, cot, wq, wo, wg, wu, wd, rows, cots, query, wide, out, gate, up, down,
                  send_sems, recv_sems, local_sems):
    place = Place()
    dp, mp = place.dp, place.mp
    side = place.bit(SIDE)
    locals_ = []
    copies = Copies(place, send_sems, recv_sems, local_sems)
    half = wd.shape[0] // 2
    blk = wd.shape[1]
    share = first.shape[0]
    zrow = wo.shape[0]
    zcol = wq.shape[1]
    nchunk = 2
    chunk = share // nchunk
    mats = ((wg, gate), (wu, up), (wd, down))
    own, across = side, 1 - side
    DEEPER, OTHER = 2, 4
    greet(place, (1, 2, 3, CORE, SIDE, DEEP))

    def tile(whole, z, spot):
        return whole.at[pl.ds(z * half, half), pl.ds(spot * blk, blk)]

    def qrows(spot):
        return query.at[pl.ds(spot * blk, blk), :]

    def columns(spot):
        return out.at[:, pl.ds(spot * blk, blk)]

    def row_block(c, source_is_input):
        def get(m):
            target = rows.at[pl.ds(m * share + c * chunk, chunk), :]
            source = first.at[pl.ds(c * chunk, chunk), :] if source_is_input else target
            return source, target
        return get

    def out_block(source_is_input):
        def get(m):
            target = out.at[pl.ds(m * zrow, zrow), pl.ds(own * blk, blk)]
            return (wo if source_is_input else target), target
        return get

    def wide_block(source_is_input):
        def get(m):
            target = wide.at[:, pl.ds(m * zcol, zcol)]
            return (wq if source_is_input else target), target
        return get

    store = {}

    def line(step, block_of, key):
        store[("r", key, step)] = copies.step(block_of, mp - (step - 1), mp - step, 1,
                                              (mp >= step - 1) & (mp < 3), mp >= step)
        store[("l", key, step)] = copies.step(block_of, mp + (step - 1), mp + step, -1,
                                              (mp <= 3 - (step - 1)) & (mp > 0), mp <= 3 - step)

    def arrive(key, step):
        copies.got(store[("r", key, step)])
        copies.got(store[("l", key, step)])

    own_piece = [weight.at[pl.ds(side * half, half), :] for weight, _ in mats]
    zhop = [[], [], []]
    yhop = [[], [], []]
    core = []

    def send_z(i, source, spot):
        zhop[i].append(copies.swap(source, tile(mats[i][1], 1, spot), Z_HIGH))

    def send_y(i, source, z, spot):
        yhop[i].append((copies.swap(source, tile(mats[i][1], z, spot + DEEPER), DEEP), z, spot + DEEPER))

    def core_tile(i, z, spot, source=None):
        piece = tile(mats[i][1], z, spot)
        core.append(copies.swap(piece if source is None else source, tile(mats[i][1], z, spot + OTHER), CORE))

    def core_query(spot, source=None):
        core.append(copies.swap(qrows(spot) if source is None else source, qrows(spot + OTHER), CORE))

    def core_out(spot):
        core.append(copies.swap(columns(spot), columns(spot + OTHER), CORE))

    line(1, out_block(True), "o")
    send_z(0, own_piece[0], own)
    xhop = [copies.swap(weight.at[pl.ds((1 - side) * half, half), :], tile(whole, 0, own), SIDE)
            for weight, whole in mats]
    wq_y = copies.swap(wq, qrows(own + DEEPER), DEEP)
    for i in range(3):
        send_y(i, own_piece[i], 0, own)
    wq_x = [copies.swap(wq, qrows(own), SIDE)]
    locals_.append(copies.local(first, rows.at[pl.ds(mp * share, share), :]))
    locals_.append(copies.local(cot, cots.at[0:share, :]))
    locals_.append(copies.local(wq, qrows(own)))
    locals_.append(copies.local(wo, out.at[pl.ds(mp * zrow, zrow), pl.ds(own * blk, blk)]))
    for i in range(3):
        locals_.append(copies.local(own_piece[i], tile(mats[i][1], 0, own)))
    locals_.append(copies.local(wq, wide.at[:, pl.ds(mp * zcol, zcol)]))
    for i in range(3):
        core_tile(i, 0, own, own_piece[i])
    core_query(own, wq)
    copies.got(wq_y)
    wq_x.append(copies.swap(qrows(own + DEEPER), qrows(own + DEEPER), SIDE))
    core_query(own + DEEPER)
    cot_x = copies.swap(cot, cots.at[share:2 * share, :], SIDE)
    arrive("o", 1)
    line(2, out_block(False), "o")
    send_z(1, own_piece[1], own)
    arrive("o", 2)
    line(3, out_block(False), "o")
    send_z(2, own_piece[2], own)
    for c in range(nchunk):
        line(1, row_block(c, True), c)
    for i in range(3):
        copies.got(xhop[i])
        piece = tile(mats[i][1], 0, across)
        send_y(i, piece, 0, across)
        send_z(i, piece, across)
        core_tile(i, 0, across)
    for item, spot in zip(wq_x, (across, across + DEEPER)):
        copies.got(item)
        core_query(spot)
    arrive("o", 3)
    for copy in locals_:
        copy.wait()
    out_y = copies.swap(columns(own), columns(own + DEEPER), DEEP)
    out_x = [copies.swap(columns(own), columns(own), SIDE)]
    core_out(own)
    for i in range(3):
        copies.got(zhop[i][0])
        send_y(i, tile(mats[i][1], 1, own), 1, own)
        core_tile(i, 1, own)
    line(1, wide_block(True), "w")
    for c in range(nchunk):
        arrive(c, 1)
        line(2, row_block(c, False), c)
    copies.got(out_y)
    out_x.append(copies.swap(columns(own + DEEPER), columns(own + DEEPER), SIDE))
    core_out(own + DEEPER)
    cot_z = copies.swap(cot, cots.at[2 * share:3 * share, :], Z_LOW)
    for i in range(3):
        copies.got(zhop[i][1])
        send_y(i, tile(mats[i][1], 1, across), 1, across)
        core_tile(i, 1, across)
    arrive("w", 1)
    line(2, wide_block(False), "w")
    for c in range(nchunk):
        arrive(c, 2)
        line(3, row_block(c, False), c)
    arrive("w", 2)
    line(3, wide_block(False), "w")
    copies.got(out_x[0])
    core_out(across)
    copies.got(cot_z)
    cot_xz = copies.swap(cots.at[2 * share:3 * share, :], cots.at[3 * share:4 * share, :], SIDE)
    for j in range(4):
        for i in range(3):
            item, z, spot = yhop[i][j]
            copies.got(item)
            core_tile(i, z, spot)
    copies.got(out_x[1])
    core_out(across + DEEPER)
    copies.finish()


def gather_call(first, cot, wq, wo, wg, wu, wd):
    share, width = first.shape
    hidden = wd.shape[0]
    shapes = (
        (share * 4, width), (share * 4, width), (width, wq.shape[1]), (wq.shape[0], width), (width, width),
        (hidden, width), (hidden, width), (hidden, width),
    )
    return pl.pallas_call(
        gather_kernel,
        out_shape=tuple(jax.ShapeDtypeStruct(s, bf16) for s in shapes),
        in_specs=[VM] * 7,
        out_specs=(ANY,) * 8,
        scratch_shapes=[pltpu.SemaphoreType.DMA((110,)), pltpu.SemaphoreType.DMA((110,)),
                        pltpu.SemaphoreType.DMA((9,))],
        compiler_params=pltpu.CompilerParams(collective_id=1, has_side_effects=True, vmem_limit_bytes=16 << 20),
        name="gather_all",
    )(first, cot, wq, wo, wg, wu, wd)


DMA = pltpu.SemaphoreType.DMA


def dot(left, right, left_dim, right_dim):
    return lax.dot_general(
        left, right, (((left_dim,), (right_dim,)), ((), ())), preferred_element_type=f32)


def params(ident, vmem=32 << 20):
    return pltpu.CompilerParams(collective_id=ident, has_side_effects=True, vmem_limit_bytes=vmem)


def tokens_kernel(heads, query_y, query_0, query_x, own, whole, send_sems, recv_sems, local_sems):
    place = Place()
    mp = place.mp
    side = place.bit(SIDE)
    share, local = own.shape[0], heads.shape[1]
    blk = query_0.shape[0]
    copies = Copies(place, send_sems, recv_sems, local_sems)

    def rows(spot):
        return whole.at[pl.ds(spot * blk, blk), :]

    greet(place, (1, 2, 3, SIDE, CORE))
    across = copies.swap(query_y, rows(side + 2), SIDE)
    for mask in (2, 3, 1):
        other = place.partner(mask)[1]
        copies.swap(heads.at[pl.ds(other * share, share), :], own.at[:, pl.ds(mp * local, local)], mask)
    held = [copies.local(query_0, rows(side)), copies.local(query_y, rows(side + 2)),
            copies.local(query_x, rows(1 - side))]
    copies.swap(query_0, rows(side + 4), CORE)
    copies.swap(query_y, rows(side + 6), CORE)
    copies.swap(query_x, rows(1 - side + 4), CORE)
    own[:, pl.ds(mp * local, local)] = heads[pl.ds(mp * share, share), :]
    for copy in held:
        copy.wait()
    copies.got(across)
    copies.swap(rows(1 - side + 2), rows(1 - side + 6), CORE)
    copies.finish()


def tokens_hop_kernel(heads, block, own, hopped, send_sems, recv_sems):
    place = Place()
    mp = place.mp
    share, local = own.shape[0], heads.shape[1]
    greet(place, (1, 2, 3, DEEP))
    copies = Copies(place, send_sems, recv_sems)
    for mask in (2, 3, 1):
        other = place.partner(mask)[1]
        copies.swap(heads.at[pl.ds(other * share, share), :], own.at[:, pl.ds(mp * local, local)], mask)
    copies.swap(block, hopped, DEEP)
    own[:, pl.ds(mp * local, local)] = heads[pl.ds(mp * share, share), :]
    copies.finish()


def heads_hop_kernel(own, block, heads, hopped, send_sems, recv_sems):
    place = Place()
    mp = place.mp
    share, local = own.shape[0], heads.shape[1]
    greet(place, (1, 2, 3, SIDE))
    copies = Copies(place, send_sems, recv_sems)
    for mask in (2, 3, 1):
        other = place.partner(mask)[1]
        copies.swap(own.at[:, pl.ds(other * local, local)], heads.at[pl.ds(mp * share, share), :], mask)
    copies.swap(block, hopped, SIDE)
    heads[pl.ds(mp * share, share), :] = own[:, pl.ds(mp * local, local)]
    copies.finish()


def to_tokens(heads, block, ident):
    shape = (heads.shape[0] // 4, heads.shape[1] * 4)
    return pl.pallas_call(
        tokens_hop_kernel,
        out_shape=(jax.ShapeDtypeStruct(shape, bf16), jax.ShapeDtypeStruct(block.shape, bf16)),
        in_specs=[VM, VM], out_specs=(VM, VM),
        scratch_shapes=[DMA((4,)), DMA((4,))], compiler_params=params(ident), name="to_tokens")(heads, block)


def to_tokens_last(heads, query_y, query_0, query_x, ident):
    shape = (heads.shape[0] // 4, heads.shape[1] * 4)
    width = query_0.shape[1]
    return pl.pallas_call(
        tokens_kernel,
        out_shape=(jax.ShapeDtypeStruct(shape, bf16), jax.ShapeDtypeStruct((width, width), bf16)),
        in_specs=[VM] * 4, out_specs=(VM, ANY),
        scratch_shapes=[DMA((8,)), DMA((8,)), DMA((3,))], compiler_params=params(ident),
        name="to_tokens_last")(heads, query_y, query_0, query_x)


def to_heads(own, block, ident):
    shape = (own.shape[0] * 4, own.shape[1] // 4)
    return pl.pallas_call(
        heads_hop_kernel,
        out_shape=(jax.ShapeDtypeStruct(shape, bf16), jax.ShapeDtypeStruct(block.shape, bf16)),
        in_specs=[VM, VM], out_specs=(VM, VM),
        scratch_shapes=[DMA((4,)), DMA((4,))], compiler_params=params(ident), name="to_heads")(own, block)


def quad_gather_kernel(own, rows, send_sems, recv_sems):
    place = Place()
    share = own.shape[0]
    half = share // 2
    greet(place, (Z_LOW, SIDE))
    copies = Copies(place, send_sems, recv_sems)
    a, b = pl.ds(0, half), pl.ds(half, half)

    def at(quarter, part):
        return rows.at[pl.ds(quarter * share + part * half, half), :]

    low_a = copies.swap(own.at[a, :], at(2, 0), Z_LOW)
    side_b = copies.swap(own.at[b, :], at(1, 1), SIDE)
    low_b = copies.swap(own.at[b, :], at(2, 1), Z_LOW)
    side_a = copies.swap(own.at[a, :], at(1, 0), SIDE)
    rows[0:share, :] = own[...]
    copies.got(low_a)
    copies.swap(at(2, 0), at(3, 0), SIDE)
    copies.got(side_b)
    copies.swap(at(1, 1), at(3, 1), Z_LOW)
    copies.finish()


def quad_gather(own, ident):
    return pl.pallas_call(
        quad_gather_kernel, out_shape=jax.ShapeDtypeStruct((own.shape[0] * 4, own.shape[1]), bf16),
        in_specs=[VM], out_specs=VM, scratch_shapes=[DMA((6,)), DMA((6,))],
        compiler_params=params(ident), name="quad_gather")(own)


def add_into(target, rows, *others, step=32):
    start, count = rows
    pieces = count // step

    def one(i, carry):
        total = target[pl.ds(start + i * step, step), :].astype(f32)
        for other in others:
            total = total + other[pl.ds(i * step, step), :].astype(f32)
        target[pl.ds(start + i * step, step), :] = total.astype(target.dtype)
        return carry

    lax.fori_loop(0, pieces, one, 0)


class QuadReduce:
    def __init__(self, copies, parts, relay, landed):
        self.copies, self.parts, self.relay, self.landed = copies, parts, relay, landed
        self.share = parts.shape[0] // 4
        self.half = self.share // 2

    def start(self):
        share, half = self.share, self.half
        self.first = self.copies.swap(self.parts.at[pl.ds(3 * share, half), :], self.relay.at[0], SIDE)
        self.second = self.copies.swap(self.parts.at[pl.ds(3 * share + half, half), :], self.relay.at[1], Z_LOW)
        self.side = [self.copies.swap(self.parts.at[pl.ds(share, half), :], self.landed.at[0, pl.ds(0, half), :], SIDE)]
        self.low = [self.copies.swap(self.parts.at[pl.ds(2 * share + half, half), :], self.landed.at[1, pl.ds(half, half), :], Z_LOW)]

    def relayed(self):
        share, half = self.share, self.half
        self.copies.got(self.first)
        add_into(self.parts, (2 * share, half), self.relay.at[0])
        self.low.append(self.copies.swap(self.parts.at[pl.ds(2 * share, half), :], self.landed.at[1, pl.ds(0, half), :], Z_LOW))
        self.copies.got(self.second)
        add_into(self.parts, (share + half, half), self.relay.at[1])
        self.side.append(self.copies.swap(self.parts.at[pl.ds(share + half, half), :], self.landed.at[0, pl.ds(half, half), :], SIDE))

    def arrived(self):
        for item in self.side + self.low:
            self.copies.got(item)


def quad_reduce_kernel(parts_in, total, parts, relay, landed, send_sems, recv_sems, local_sem):
    place = Place()
    load = pltpu.make_async_copy(parts_in, parts, local_sem)
    load.start()
    greet(place, (Z_LOW, SIDE))
    copies = Copies(place, send_sems, recv_sems)
    load.wait()
    reduce = QuadReduce(copies, parts, relay, landed)
    reduce.start()
    reduce.relayed()
    reduce.arrived()
    share = total.shape[0]

    def one(i, carry):
        here = pl.ds(i * 32, 32)
        total[here, :] = (parts[here, :].astype(f32) + landed[0, here, :].astype(f32)
                          + landed[1, here, :].astype(f32))
        return carry

    lax.fori_loop(0, share // 32, one, 0)
    copies.finish()


def quad_reduce(parts, ident):
    share, width = parts.shape[0] // 4, parts.shape[1]
    return pl.pallas_call(
        quad_reduce_kernel, out_shape=jax.ShapeDtypeStruct((share, width), f32),
        in_specs=[ANY], out_specs=VM,
        scratch_shapes=[pltpu.VMEM((share * 4, width), bf16), pltpu.VMEM((2, share // 2, width), bf16),
                        pltpu.VMEM((2, share, width), bf16), DMA((6,)), DMA((6,)), DMA],
        compiler_params=params(ident), name="quad_reduce")(parts)


def all_sum_kernel(value, total, got, send_sems, recv_sems):
    place = Place()
    masks = (1, 2, CORE, SIDE, DEEP)
    greet(place, masks)
    copies = Copies(place, send_sems, recv_sems)
    total[...] = value[...]
    for i, mask in enumerate(masks):
        item = copies.swap(total, got.at[i], mask)
        copies.got(item)
        item["copy"].wait_send()
        item["sent"] = True
        total[...] = total[...] + got[i]
    copies.finish()


def all_sum(value, ident):
    return pl.pallas_call(
        all_sum_kernel, out_shape=jax.ShapeDtypeStruct(value.shape, f32), in_specs=[VM], out_specs=VM,
        scratch_shapes=[pltpu.VMEM((5,) + value.shape, f32), DMA((5,)), DMA((5,))],
        compiler_params=params(ident), name="all_sum")(value)


ROWS=256
DOC_MOST=512


def key_range(block, seq_len):
    low = max(0, block * ROWS - DOC_MOST + 1) // ROWS * ROWS
    return low, min(seq_len, (block + 1) * ROWS)


def scores_turned(q, k, starts, low, first, scale):
    s = dot(k, q, 1, 1) * scale
    key_pos = low + lax.broadcasted_iota(jnp.int32, s.shape, 0)
    query_pos = first + lax.broadcasted_iota(jnp.int32, s.shape, 1)
    return jnp.where((key_pos >= starts) & (key_pos <= query_pos), s, -1e30)


def forward_kernel(starts_ref, q_ref, k_ref, v_ref, ctx_ref, lse_ref):
    seq_len = q_ref.shape[0]
    scale = HEAD_DIM ** -0.5
    for block in range(seq_len // ROWS):
        low, high = key_range(block, seq_len)
        here = pl.ds(block * ROWS, ROWS)
        k = k_ref[low:high, :]
        v = v_ref[low:high, :]
        s = scores_turned(q_ref[here, :], k, starts_ref[:, here], low, block * ROWS, scale)
        top = jnp.max(s, axis=0, keepdims=True)
        raised = jnp.exp(s - top)
        total = jnp.sum(raised, axis=0, keepdims=True)
        low_probs = (raised * (1.0 / total)).astype(bf16)
        ctx_ref[here, :] = dot(low_probs, v, 0, 0).astype(bf16)
        lse_ref[0, :, here] = top + jnp.log(total)


def backward_kernel(starts_ref, q_ref, k_ref, v_ref, grad_ref, lse_ref, dq_ref, dk_ref, dv_ref):
    seq_len = q_ref.shape[0]
    scale = HEAD_DIM ** -0.5
    for block in range(seq_len // ROWS):
        low, high = key_range(block, seq_len)
        here = pl.ds(block * ROWS, ROWS)
        k = k_ref[low:high, :]
        v = v_ref[low:high, :]
        q = q_ref[here, :]
        grad = grad_ref[here, :]
        s = scores_turned(q, k, starts_ref[:, here], low, block * ROWS, scale)
        probs = jnp.exp(s - lse_ref[0, :, here])
        grad_probs = dot(v, grad, 1, 1)
        spread = jnp.sum(probs * grad_probs, axis=0, keepdims=True)
        grad_s = (probs * (grad_probs - spread)).astype(bf16)
        dq_ref[here, :] = (dot(grad_s, k, 0, 0) * scale).astype(bf16)
        dk = dot(grad_s, q, 1, 0) * scale
        dv = dot(probs.astype(bf16), grad, 1, 0)
        old = max(low, min(high, block * ROWS))
        if low == 0 and block == 0:
            dk_ref[low:high, :] = dk
            dv_ref[low:high, :] = dv
        else:
            n = old - low
            dk_ref[low:old, :] += dk[:n]
            dv_ref[low:old, :] += dv[:n]
            dk_ref[old:high, :] = dk[n:]
            dv_ref[old:high, :] = dv[n:]


def specs(seq_len):
    row = pl.BlockSpec((1, seq_len), lambda h: (0, 0))
    head = pl.BlockSpec((seq_len, HEAD_DIM), lambda h: (0, h))
    lse = pl.BlockSpec((1, 1, seq_len), lambda h: (h, 0, 0))
    return row, head, lse


def attend(starts, q, k, v):
    seq_len, width = q.shape
    heads = width // HEAD_DIM
    row, head, lse = specs(seq_len)
    flops = heads * seq_len * seq_len * HEAD_DIM * 3
    return pl.pallas_call(
        forward_kernel, grid=(heads,),
        in_specs=[row, head, head, head], out_specs=(head, lse),
        out_shape=(jax.ShapeDtypeStruct(q.shape, bf16), jax.ShapeDtypeStruct((heads, 1, seq_len), f32)),
        cost_estimate=pl.CostEstimate(flops=flops, bytes_accessed=4 * q.size * 2, transcendentals=heads * seq_len * seq_len // 2),
        name="attend",
    )(starts, q, k, v)


def attend_back(starts, q, k, v, grad, lse_array):
    seq_len, width = q.shape
    heads = width // HEAD_DIM
    row, head, lse = specs(seq_len)
    flops = heads * seq_len * seq_len * HEAD_DIM * 7
    wide = jax.ShapeDtypeStruct(q.shape, f32)
    return pl.pallas_call(
        backward_kernel, grid=(heads,),
        in_specs=[row, head, head, head, head, lse], out_specs=(head, head, head),
        out_shape=(jax.ShapeDtypeStruct(q.shape, bf16), wide, wide),
        cost_estimate=pl.CostEstimate(flops=flops, bytes_accessed=9 * q.size * 2, transcendentals=heads * seq_len * seq_len // 2),
        name="attend_back",
    )(starts, q, k, v, grad, lse_array)


def starts_of(segments):
    return jnp.sum((segments[0][None, :] < segments[0][:, None]).astype(jnp.int32), axis=1)[None, :]


def hidden_cuts(hidden):
    cuts = []
    start = 0
    while start < hidden:
        size = min(512, hidden - start)
        cuts.append((start, size))
        start += size
    return cuts


def ffn_kernel(normed, cots_in, down_in, gate_in, up_in, total, fparts_out, sums_out,
               weights, tokens, acts, dparts, relay, landed, fparts,
               send_sems, recv_sems, local_sems, free_sem):
    place = Place()
    share, width = normed.shape
    hidden = down_in.shape[0]
    half = share // 2
    wide = width // 2
    cuts = hidden_cuts(hidden)
    copies = Copies(place, send_sems, recv_sems, local_sems)
    load_cots = copies.local(cots_in, tokens.at[0])
    load_w = [copies.local(w, weights.at[i]) for i, w in enumerate((down_in, gate_in, up_in))]
    greet(place, (Z_LOW, SIDE, CORE))

    def at(quarter, part):
        return tokens.at[1, pl.ds(quarter * share + part * half, half), :]

    a, b = pl.ds(0, half), pl.ds(half, half)
    low_a = copies.swap(normed.at[a, :], at(2, 0), Z_LOW)
    side_b = copies.swap(normed.at[b, :], at(1, 1), SIDE)
    low_b = copies.swap(normed.at[b, :], at(2, 1), Z_LOW)
    side_a = copies.swap(normed.at[a, :], at(1, 0), SIDE)
    tokens[1, 0:share, :] = normed[...]

    def block(r):
        here = pl.ds(r * share, share)
        for start, size in cuts:
            rows = tokens[1, here, :]
            gate = dot(rows, weights[1, start:start + size, :], 1, 1)
            up = dot(rows, weights[2, start:start + size, :], 1, 1)
            grad = dot(tokens[0, here, :], weights[0, start:start + size, :], 1, 1)
            sigmoid = jax.nn.sigmoid(gate)
            silu = gate * sigmoid
            acts[0, here, start:start + size] = (silu * up).astype(bf16)
            acts[1, here, start:start + size] = (
                grad * up * sigmoid * (1.0 + gate * (1.0 - sigmoid))).astype(bf16)
            acts[2, here, start:start + size] = (grad * silu).astype(bf16)

        def columns(n, carry):
            there = pl.ds(pl.multiple_of(n * 512, 512), 512)
            dparts[here, there] = (dot(acts[1, here, :], weights[1, :, there], 1, 0)
                                   + dot(acts[2, here, :], weights[2, :, there], 1, 0)).astype(bf16)
            fparts[here, there] = dot(acts[0, here, :], weights[0, :, there], 1, 0).astype(bf16)
            return carry

        lax.fori_loop(0, width // 512, columns, 0)

    for copy in load_w:
        copy.wait()
    load_cots.wait()
    got = {"across": None}

    def step(r, carry):
        @pl.when(r == 1)
        def _():
            low_a["copy"].wait_recv()
            side_b["copy"].wait_recv()
            forward[0].start()
            forward[1].start()
            side_a["copy"].wait_recv()
            low_b["copy"].wait_recv()

        @pl.when(r == 3)
        def _():
            forward[0].wait_recv()
            forward[1].wait_recv()
        block(r)
        return carry

    forward = [copies.describe(at(2, 0), at(3, 0), place.partner(SIDE), copies.count),
               copies.describe(at(1, 1), at(3, 1), place.partner(Z_LOW), copies.count + 1)]
    copies.count += 2
    lax.fori_loop(0, 4, step, 0)
    for item in (low_a, side_b, low_b, side_a):
        item["got"] = True
    pl.semaphore_signal(free_sem, inc=1, device_id=place.partner(CORE), device_id_type=MESH)
    reduce = QuadReduce(copies, dparts, relay, landed)
    reduce.start()
    save = copies.local(fparts, fparts_out)

    base = copies.count
    copies.count += 3

    def give_copy(i):
        return copies.describe(weights.at[i, :, pl.ds(0, wide)], weights.at[i, :, pl.ds(wide, wide)],
                               place.partner(CORE), base + i)

    def give(i, carry):
        right = tokens[jnp.minimum(i, 1), :, wide:]
        for start, size in cuts:
            weights[i, start:start + size, 0:wide] = dot(
                acts[i, :, start:start + size], right, 0, 0).astype(bf16)

        @pl.when(i == 0)
        def _():
            pl.semaphore_wait(free_sem, 1)
        give_copy(i).start()
        return carry

    lax.fori_loop(0, 3, give, 0)
    reduce.relayed()

    def keep(i, carry):
        give_copy(i).wait_recv()
        right = tokens[jnp.minimum(i, 1), :, 0:wide]
        for start, size in cuts:
            rows = slice(start, start + size)
            weights[i, rows, wide:] = (dot(acts[i, :, rows], right, 0, 0)
                                       + weights[i, rows, wide:].astype(f32)).astype(bf16)
        pltpu.make_async_copy(weights.at[i, :, pl.ds(wide, wide)], sums_out.at[i], local_sems.at[5 + i]).start()
        return carry

    lax.fori_loop(0, 3, keep, 0)
    reduce.arrived()

    def one(i, carry):
        here = pl.ds(i * 32, 32)
        total[here, :] = (dparts[here, :].astype(f32) + landed[0, here, :].astype(f32)
                          + landed[1, here, :].astype(f32))
        return carry

    lax.fori_loop(0, share // 32, one, 0)
    for i in range(3):
        give_copy(i).wait_send()
        pltpu.make_async_copy(weights.at[i, :, pl.ds(wide, wide)], sums_out.at[i], local_sems.at[5 + i]).wait()
    for copy in forward:
        copy.wait_send()
    save.wait()
    copies.finish()


def ffn_call(normed, cots, down, gate, up, ident):
    share, width = normed.shape
    hidden = down.shape[0]
    V = pltpu.VMEM
    flops = 2 * share * 4 * width * hidden * 9
    return pl.pallas_call(
        ffn_kernel,
        out_shape=(jax.ShapeDtypeStruct((share, width), f32), jax.ShapeDtypeStruct((share * 4, width), bf16),
                   jax.ShapeDtypeStruct((3, hidden, width // 2), bf16)),
        in_specs=[VM] + [ANY] * 4,
        out_specs=(VM, ANY, ANY),
        scratch_shapes=[
            V((3, hidden, width), bf16), V((2, share * 4, width), bf16), V((3, share * 4, hidden), bf16),
            V((share * 4, width), bf16), V((2, share // 2, width), bf16), V((2, share, width), bf16),
            V((share * 4, width), bf16),
            DMA((16,)), DMA((16,)), DMA((8,)), pltpu.SemaphoreType.REGULAR],
        compiler_params=params(ident, 63 << 20),
        cost_estimate=pl.CostEstimate(flops=flops, bytes_accessed=40 << 20, transcendentals=share * 4 * hidden),
        name="feed_forward",
    )(normed, cots, down, gate, up)


def absolute(place, spot):
    core, deep, side = spot // 4, (spot // 2) % 2, spot % 2
    return place.flip(place.dp, core + 4 * deep) - 2 * place.bit(SIDE) + 2 * side


def back_first_kernel(dn2, residual, cot, gain, context, out_whole, sums, query_0,
                      dres, heads, gain_part, query_x, down_sums, out_sums,
                      keep_d, deep_d, grad_low, wout, dctx, give_o, core_o,
                      send_sems, recv_sems, local_sems):
    place = Place()
    mp = place.mp
    share, width = dn2.shape
    hidden = keep_d.shape[0]
    local = heads.shape[1]
    wide = width // 2
    copies = Copies(place, send_sems, recv_sems, local_sems)
    loads = [copies.local(out_whole.at[pl.ds(z * local, local), :], wout.at[z]) for z in range(4)]
    load_d = copies.local(sums.at[0, :, pl.ds(0, wide // 2)], keep_d)
    greet(place, (1, 2, 3, CORE, SIDE, DEEP))
    in_d = copies.swap(sums.at[0, :, pl.ds(wide // 2, wide // 2)], deep_d, DEEP)
    copies.swap(query_0, query_x, SIDE)
    gain_part[...] = jnp.zeros_like(gain_part)

    def norm(i, carry):
        here = pl.ds(i * 32, 32)
        value = residual[here, :]
        inverse = lax.rsqrt(jnp.mean(value * value, axis=-1, keepdims=True) + epsilon)
        scaled = value * inverse
        grad = dn2[here, :]
        grad_scaled = grad * gain[...]
        back = inverse * (grad_scaled - scaled * jnp.mean(grad_scaled * scaled, axis=-1, keepdims=True))
        total = cot[here, :].astype(f32) + back
        dres[here, :] = total
        grad_low[here, :] = total.astype(bf16)
        gain_part[...] += jnp.sum(grad * scaled, axis=0, keepdims=True)
        return carry

    lax.fori_loop(0, share // 32, norm, 0)
    for copy in loads:
        copy.wait()
    for mask in (2, 3, 1, 0):
        other = place.partner(mask)[1]
        there = pl.ds(pl.multiple_of(other * local, local), local)
        piece = dot(grad_low[...], wout[other], 1, 1).astype(bf16)
        if mask:
            dctx[:, there] = piece
            copies.swap(dctx.at[:, there], heads.at[pl.ds(mp * share, share), :], mask)
        else:
            heads[pl.ds(mp * share, share), :] = piece
    chunks = width // 512
    base = copies.count
    copies.count += chunks

    def core_copy(n):
        rows = pl.ds(pl.multiple_of(n * 512, 512), 512)
        return copies.describe(give_o.at[rows, :], core_o.at[rows, :], place.partner(CORE), base + n)

    def give(n, carry):
        rows = pl.ds(pl.multiple_of(n * 512, 512), 512)
        give_o[rows, :] = dot(context[:, rows], grad_low[:, wide:], 0, 0).astype(bf16)
        core_copy(n).start()
        return carry

    lax.fori_loop(0, chunks, give, 0)

    def keep(n, carry):
        rows = pl.ds(pl.multiple_of(n * 512, 512), 512)
        core_copy(n).wait_recv()
        out_sums[rows, :] = (dot(context[:, rows], grad_low[:, :wide], 0, 0)
                             + core_o[rows, :].astype(f32)).astype(bf16)
        return carry

    lax.fori_loop(0, chunks, keep, 0)
    load_d.wait()
    copies.got(in_d)

    def add_d(n, carry):
        rows = pl.ds(n * 32, 32)
        down_sums[rows, :] = (keep_d[rows, :].astype(f32) + deep_d[rows, :].astype(f32)).astype(bf16)
        return carry

    lax.fori_loop(0, hidden // 32, add_d, 0)
    copies.finish()

    def sent(n, carry):
        core_copy(n).wait_send()
        return carry

    lax.fori_loop(0, chunks, sent, 0)


def back_first(dn2, residual, cot, gain, context, out_whole, sums, query_0, ident):
    share, width = dn2.shape
    hidden = sums.shape[1]
    V = pltpu.VMEM
    S = jax.ShapeDtypeStruct
    return pl.pallas_call(
        back_first_kernel,
        out_shape=(S((share, width), f32), S((share * 4, width // 4), bf16), S((1, width), f32),
                   S(query_0.shape, bf16), S((hidden, width // 4), bf16), S((width, width // 2), bf16)),
        in_specs=[VM] * 5 + [ANY, ANY, VM],
        out_specs=(VM,) * 6,
        scratch_shapes=[
            V((hidden, width // 4), bf16), V((hidden, width // 4), bf16), V((share, width), bf16),
            V((4, width // 4, width), bf16), V((share, width), bf16), V((width, width // 2), bf16),
            V((width, width // 2), bf16), DMA((12,)), DMA((12,)), DMA((5,))],
        compiler_params=params(ident, 60 << 20), name="back_first",
    )(dn2, residual, cot, gain, context, out_whole, sums, query_0)


def back_last_kernel(grad_q, rows_first, dres, inputs, gain, query_y, query_0, query_x,
                     sums, down_sums, out_sums, fparts, residual, gain_part,
                     down, gate, up, out, query, grad_input, output, gains, query_whole,
                     keep_f, deep_f, high_f, side_f, own_o, side_o, deep_o, z_o,
                     give_q, own_q, core_q, side_q, deep_q, parts, relay, landed,
                     grad_own, stream, dn1, gain_rows, gains_got,
                     send_sems, recv_sems, local_sems):
    place = Place()
    mp = place.mp
    side = place.bit(SIDE)
    share, width = dres.shape
    hidden, blk = down.shape
    half = hidden // 2
    local = grad_q.shape[1]
    zrow = out.shape[0]
    quarter = 2 * blk
    copies = Copies(place, send_sems, recv_sems, local_sems)
    load_rows = copies.local(rows_first, stream.at[pl.ds(0, share * 4), :])
    load_d = copies.local(down_sums, keep_f.at[0])
    load_p = copies.local(fparts, parts)
    load_f = [copies.local(sums.at[i, :, pl.ds(0, quarter)], keep_f.at[i]) for i in (1, 2)]
    load_o = copies.local(out_sums, own_o)

    def qrows(spot):
        return query_whole.at[pl.ds(spot * blk, blk), :]

    greet(place, (1, 2, 3, CORE, SIDE, DEEP))
    tokens_in = []
    for mask in (2, 3, 1):
        other = place.partner(mask)[1]
        tokens_in.append(copies.swap(grad_q.at[pl.ds(other * share, share), :],
                                     grad_own.at[:, pl.ds(mp * local, local)], mask))
    wq_across = copies.swap(query_y, qrows(side + 2), SIDE)
    deep_in = [None]
    for i in (1, 2):
        deep_in.append([copies.swap(sums.at[i, :, pl.ds(quarter + x * blk, blk)], deep_f.at[i - 1, :, pl.ds(x * blk, blk)], DEEP)
                        for x in (0, 1)])
    held = [copies.local(query_0, qrows(side)), copies.local(query_y, qrows(side + 2)),
            copies.local(query_x, qrows(1 - side))]
    wq_core = [copies.swap(query_0, qrows(side + 4), CORE), copies.swap(query_y, qrows(side + 6), CORE),
               copies.swap(query_x, qrows(1 - side + 4), CORE)]
    load_d.wait()
    give_rows = pl.ds(half, half)
    high_in = [[copies.swap(keep_f.at[0, give_rows, pl.ds(x * blk, blk)], high_f.at[0, :, pl.ds(x * blk, blk)], Z_HIGH)
                for x in (0, 1)]]
    grad_own[:, pl.ds(mp * local, local)] = grad_q[pl.ds(mp * share, share), :]
    load_rows.wait()
    wide = width // 2

    def product(first):
        return dot(stream[0:share * 4, first:first + wide], grad_q[...], 0, 0)

    give_q[...] = product(wide).astype(bf16)
    core_in_q = copies.swap(give_q, core_q, CORE)
    load_p.wait()
    reduce = QuadReduce(copies, parts, relay, landed)
    reduce.start()
    load_o.wait()

    def block_o(spot):
        return own_o.at[:, pl.ds(spot * blk, blk)]

    side_in_o = {y: copies.swap(block_o(2 * y + 1 - side), side_o.at[y], SIDE) for y in (1, 0)}
    keep_q = product(0)
    copies.got(core_in_q)
    own_q[...] = (keep_q + core_q[...].astype(f32)).astype(bf16)
    side_in_q = {y: copies.swap(own_q.at[pl.ds((2 * y + 1 - side) * blk, blk), :], side_q.at[y], SIDE) for y in (1, 0)}
    reduce.relayed()
    for copy in held:
        copy.wait()
    for item in tokens_in:
        copies.got(item)
    copies.got(wq_across)
    wq_core.append(copies.swap(qrows(1 - side + 2), qrows(1 - side + 6), CORE))
    for item in wq_core:
        copies.got(item)
    load_wq = copies.local(query_whole, stream)
    load_wq.wait()

    def first_back(n, carry):
        there = pl.ds(pl.multiple_of(n * 512, 512), 512)
        dn1[:, there] = dot(grad_own[...], stream[there, :], 1, 1)
        return carry

    lax.fori_loop(0, width // 512, first_back, 0)
    gain_rows[0:1, :] = jnp.zeros((1, width), f32)
    gain_rows[1:2, :] = gain_part[...]

    def norm(i, carry):
        here = pl.ds(i * 32, 32)
        value = inputs[here, :].astype(f32)
        inverse = lax.rsqrt(jnp.mean(value * value, axis=-1, keepdims=True) + epsilon)
        scaled = value * inverse
        grad = dn1[here, :]
        grad_scaled = grad * gain[...]
        back = inverse * (grad_scaled - scaled * jnp.mean(grad_scaled * scaled, axis=-1, keepdims=True))
        total = dres[here, :] + back
        for spot in range(8):
            there = pl.ds(pl.multiple_of(absolute(place, spot) * blk, blk), blk)
            grad_input[here, there] = total[:, spot * blk:(spot + 1) * blk]
        gain_rows[0:1, :] += jnp.sum(grad * scaled, axis=0, keepdims=True)
        return carry

    lax.fori_loop(0, share // 32, norm, 0)
    for spot in range(8):
        there = pl.ds(pl.multiple_of(absolute(place, spot) * blk, blk), blk)
        gains[:, there] = gain_rows[:, spot * blk:(spot + 1) * blk]
    gain_masks = (1, 2, CORE, SIDE, DEEP)
    gain_state = {"item": None, "at": 0}

    def gain_hop():
        if gain_state["item"] is not None:
            item = gain_state["item"]
            copies.got(item)
            item["copy"].wait_send()
            item["sent"] = True
            gains[...] = gains[...] + gains_got[gain_state["at"] - 1]
            gain_state["item"] = None
        if gain_state["at"] < len(gain_masks):
            gain_state["item"] = copies.swap(gains, gains_got.at[gain_state["at"]], gain_masks[gain_state["at"]])
            gain_state["at"] += 1

    def deep_sum(i):
        sent = []
        for x in (0, 1):
            copies.got(deep_in[i][x])
            there = pl.ds(x * blk, blk)
            add_into(keep_f.at[i, :, there], (half, half), deep_f.at[i - 1, give_rows, there], step=16)
            sent.append(copies.swap(keep_f.at[i, give_rows, there], high_f.at[i, :, there], Z_HIGH))
        for x in (0, 1):
            there = pl.ds(x * blk, blk)
            add_into(keep_f.at[i, :, there], (0, half), deep_f.at[i - 1, :, there], step=16)
        high_in.append(sent)

    def high_sum(i):
        for x in (0, 1):
            copies.got(high_in[i][x])
            add_into(keep_f.at[i, :, pl.ds(x * blk, blk)], (0, half), high_f.at[i, :, pl.ds(x * blk, blk)], step=16)
        there = pl.ds(pl.multiple_of((1 - side) * blk, blk), blk)
        return copies.swap(keep_f.at[i, pl.ds(0, half), there], side_f.at[i], SIDE)

    gain_hop()
    load_f[0].wait()
    deep_sum(1)
    gain_hop()
    side_in = [high_sum(0)]
    gain_hop()
    deep_in_q = None
    for y in (1, 0):
        copies.got(side_in_q[y])
        spot = 2 * y + side
        rows = pl.ds(pl.multiple_of(spot * blk, blk), blk)
        own_q[rows, :] = (own_q[rows, :].astype(f32) + side_q[y].astype(f32)).astype(bf16)
        if y:
            deep_in_q = copies.swap(own_q.at[rows, :], deep_q, DEEP)
    gain_hop()
    load_f[1].wait()
    deep_sum(2)
    gain_hop()
    deep_in_o = None
    for y in (1, 0):
        copies.got(side_in_o[y])
        there = pl.ds(pl.multiple_of((2 * y + side) * blk, blk), blk)
        add_into(own_o.at[:, there], (0, width), side_o.at[y])
        if y:
            deep_in_o = copies.swap(own_o.at[:, there], deep_o, DEEP)
    gain_hop()
    reduce.arrived()

    def finish_output(i, carry):
        here = pl.ds(i * 32, 32)
        total = (residual[here, :] + parts[here, :].astype(f32) + landed[0, here, :].astype(f32)
                 + landed[1, here, :].astype(f32)).astype(bf16)
        for spot in range(8):
            there = pl.ds(pl.multiple_of(absolute(place, spot) * blk, blk), blk)
            output[here, there] = total[:, spot * blk:(spot + 1) * blk]
        return carry

    lax.fori_loop(0, share // 32, finish_output, 0)
    mine = pl.ds(pl.multiple_of(side * blk, blk), blk)
    copies.got(deep_in_o)
    add_into(own_o.at[:, mine], (0, width), deep_o)
    z_in = []
    for n, mask in enumerate((2, 3, 1)):
        other = place.partner(mask)[1]
        z_in.append(copies.swap(own_o.at[pl.ds(other * zrow, zrow), mine], z_o.at[n], mask))
    copies.got(deep_in_q)
    query[...] = own_q[pl.ds(pl.multiple_of(side * blk, blk), blk), :].astype(f32) + deep_q[...].astype(f32)
    side_in.append(high_sum(1))
    side_in.append(high_sum(2))
    for item in z_in:
        copies.got(item)

    def add_z(i, carry):
        here = pl.ds(i * 32, 32)
        sum_ = own_o[pl.ds(mp * zrow + i * 32, 32), mine].astype(f32)
        for n in range(3):
            sum_ = sum_ + z_o[n, here, :].astype(f32)
        out[here, :] = sum_
        return carry

    lax.fori_loop(0, zrow // 32, add_z, 0)
    for i, target in enumerate((down, gate, up)):
        copies.got(side_in[i])

        def write(n, carry, i=i, target=target):
            target[pl.ds(side * half + n * 16, 16), :] = keep_f[i, pl.ds(n * 16, 16), mine].astype(f32)
            target[pl.ds((1 - side) * half + n * 16, 16), :] = side_f[i, pl.ds(n * 16, 16), :].astype(f32)
            return carry

        lax.fori_loop(0, half // 16, write, 0)
    copies.finish()


def back_last(grad_q, rows_first, dres, inputs, gain, query_y, query_0, query_x,
              sums, down_sums, out_sums, fparts, residual, gain_part, ident):
    share, width = dres.shape
    hidden = sums.shape[1]
    blk = width // 8
    half = hidden // 2
    local = grad_q.shape[1]
    V = pltpu.VMEM
    S = jax.ShapeDtypeStruct
    return pl.pallas_call(
        back_last_kernel,
        out_shape=(S((hidden, blk), f32),) * 3
        + (S((width // 4, blk), f32), S((blk, local), f32), S((share, width), f32), S((share, width), bf16),
           S((2, width), f32), S((width, width), bf16)),
        in_specs=[VM, ANY] + [VM] * 6 + [ANY] * 4 + [VM] * 2,
        out_specs=(VM,) * 8 + (ANY,),
        scratch_shapes=[
            V((3, hidden, 2 * blk), bf16), V((2, hidden, 2 * blk), bf16), V((3, half, 2 * blk), bf16),
            V((3, half, blk), bf16),
            V((width, width // 2), bf16), V((2, width, blk), bf16), V((width, blk), bf16),
            V((3, width // 4, blk), bf16),
            V((width // 2, local), bf16), V((width // 2, local), bf16), V((width // 2, local), bf16),
            V((2, blk, local), bf16), V((blk, local), bf16),
            V((share * 4, width), bf16), V((2, share // 2, width), bf16), V((2, share, width), bf16),
            V((share, width), bf16), V((width, width), bf16), V((share, width), f32),
            V((2, width), f32), V((5, 2, width), f32),
            DMA((48,)), DMA((48,)), DMA((12,))],
        compiler_params=params(ident, 63 << 20), name="back_last",
    )(grad_q, rows_first, dres, inputs, gain, query_y, query_0, query_x,
      sums, down_sums, out_sums, fparts, residual, gain_part)


class Grid:
    def __init__(self, dp):
        self.dp = dp
        self.size = dp * MP
        self.rest = []
        mask = 16
        while mask < self.size:
            self.rest.append(mask)
            mask *= 2
        self.relative = [CORE] + self.rest
        self.me = lax.axis_index("dp") * MP + lax.axis_index("mp")
        self.me_mp = lax.axis_index("mp")
        self.me_dp = lax.axis_index("dp")

    def swap(self, value, mask):
        return lax.ppermute(value, ("dp", "mp"), [(i, i ^ mask) for i in range(self.size)])

    def bit(self, mask):
        return (self.me // mask) % 2

    def spread(self, value):
        block = value.shape[-1] // self.dp
        pieces = []
        for spot in range(self.dp):
            flips = 0
            digits = spot >> 1
            for place, mask in enumerate(reversed(self.relative)):
                if (digits >> place) & 1:
                    flips |= mask // MP
            source = ((self.me_dp ^ flips) & ~(SIDE // MP)) | ((spot & 1) * (SIDE // MP))
            pieces.append(lax.dynamic_slice_in_dim(value, source * block, block, value.ndim - 1))
        return jnp.concatenate(pieces, axis=-1)

    def restore(self, value):
        block = value.shape[-1] // self.dp
        pieces = []
        for target in range(self.dp):
            flips = (self.me_dp ^ target) * MP
            spot = 0
            for mask in self.relative:
                spot = spot * 2 + (flips // mask) % 2
            spot = spot * 2 + (target * MP // SIDE) % 2
            pieces.append(lax.dynamic_slice_in_dim(value, spot * block, block, value.ndim - 1))
        return jnp.concatenate(pieces, axis=-1)

    def ordered(self, mine, theirs, mask, axis):
        high = self.bit(mask) == 1
        return jnp.concatenate(
            [jnp.where(high, theirs, mine), jnp.where(high, mine, theirs)], axis=axis
        )

    def line_gather(self, value):
        right, left = {0: value}, {0: value}
        for step in range(1, MP):
            right[step] = lax.ppermute(
                right[step - 1], "mp", [(j, j + 1) for j in range(step - 1, MP - 1)]
            )
            left[step] = lax.ppermute(
                left[step - 1], "mp", [(j, j - 1) for j in range(1, MP - step + 1)]
            )
        return [value] + [left[d] + right[MP - d] for d in range(1, MP)]

    def exchange_mp(self, value, split, join):
        return lax.all_to_all(value, "mp", split, join, tiled=True)

    def quad_gather(self, value):
        half = value.shape[0] // 2
        from_side = self.swap(value, SIDE)
        from_low = self.swap(value, Z_LOW)
        across = jnp.concatenate(
            [self.swap(from_low[:half], SIDE), self.swap(from_side[half:], Z_LOW)], axis=0
        )
        return [value, from_side, from_low, across]

    def quad_start(self, across):
        half = across.shape[0] // 2
        return self.swap(across[:half], SIDE), self.swap(across[half:], Z_LOW)

    def quad_finish(self, relayed, for_side, for_low, own):
        by_side, by_low = relayed
        half = own.shape[0] // 2
        low_sum = jnp.concatenate(
            [(for_low[:half] + by_side.astype(f32)), for_low[half:]], axis=0
        ).astype(bf16)
        side_sum = jnp.concatenate(
            [for_side[:half], for_side[half:] + by_low.astype(f32)], axis=0
        ).astype(bf16)
        return own + self.swap(side_sum, SIDE).astype(f32) + self.swap(low_sum, Z_LOW).astype(f32)

    def all_sum(self, value):
        mask = 1
        while mask < self.size:
            value = value + self.swap(value, mask)
            mask *= 2
        return value


def contract(left, right, left_dim, right_dim):
    return lax.dot_general(
        left, right, (((left_dim,), (right_dim,)), ((), ())), preferred_element_type=jnp.float32
    )


def root_inverse(values):
    return lax.rsqrt(jnp.mean(values * values, axis=-1, keepdims=True) + epsilon)


def norm_back(grad_normed, scaled, inverse, gain):
    grad_scaled = grad_normed * gain
    grad_values = inverse * (
        grad_scaled - scaled * jnp.mean(grad_scaled * scaled, axis=-1, keepdims=True)
    )
    return (grad_values, jnp.sum(grad_normed * scaled, axis=0))


def plain_body(
    inputs,
    keys_values,
    segment_ids,
    gain_first,
    gain_second,
    w_query,
    w_out,
    w_gate,
    w_up,
    w_down,
    cotangent,
):
    query_full, out_full = (
        lax.all_gather(w_query, "dp", axis=0, tiled=True),
        lax.all_gather(w_out, "dp", axis=1, tiled=True),
    )
    gate_full, up_full, down_full = (
        lax.all_gather(w_gate, "dp", axis=0, tiled=True),
        lax.all_gather(w_up, "dp", axis=0, tiled=True),
        lax.all_gather(w_down, "dp", axis=1, tiled=True),
    )
    tokens = inputs.astype(jnp.float32)
    inverse_first = root_inverse(tokens)
    scaled_first = tokens * inverse_first
    normed_first = (scaled_first * gain_first).astype(jnp.bfloat16)
    rows_first = lax.all_gather(normed_first, "mp", axis=0, tiled=True)
    queries = contract(rows_first, query_full, 1, 0).astype(jnp.bfloat16)
    seq_len = rows_first.shape[0]
    local_width = queries.shape[1]
    head_count = local_width // HEAD_DIM
    block_rows = min(512, seq_len)
    block_count = seq_len // block_rows
    score_scale = HEAD_DIM ** (-0.5)
    key_heads = keys_values[:, 0, :].reshape(seq_len, head_count, HEAD_DIM)
    value_heads = keys_values[:, 1, :].reshape(seq_len, head_count, HEAD_DIM)
    segments = segment_ids[0]
    key_pos = jnp.arange(seq_len, dtype=jnp.int32)

    def block_scores(first_row):
        query_block = lax.dynamic_slice_in_dim(queries, first_row, block_rows, 0).reshape(
            block_rows, head_count, HEAD_DIM
        )
        scores = (
            jnp.einsum("qhd,khd->hqk", query_block, key_heads, preferred_element_type=jnp.float32)
            * score_scale
        )
        query_pos = first_row + jnp.arange(block_rows, dtype=jnp.int32)
        query_seg = lax.dynamic_slice_in_dim(segments, first_row, block_rows, 0)
        allowed = (query_pos[:, None] >= key_pos[None, :]) & (
            query_seg[:, None] == segments[None, :]
        )
        return (query_block, jnp.where(allowed[None], scores, -1e30))

    def forward_block(block_index):
        query_block, scores = block_scores(block_index * block_rows)
        row_max = jnp.max(scores, axis=-1, keepdims=True)
        raised = jnp.exp(scores - row_max)
        row_total = jnp.sum(raised, axis=-1, keepdims=True)
        weights_low = (raised / row_total).astype(jnp.bfloat16)
        blended = jnp.einsum(
            "hqk,khd->qhd", weights_low, value_heads, preferred_element_type=jnp.float32
        )
        return (
            blended.reshape(block_rows, local_width).astype(jnp.bfloat16),
            (row_max + jnp.log(row_total))[..., 0],
        )

    context_blocks, log_totals = lax.map(forward_block, jnp.arange(block_count, dtype=jnp.int32))
    context = context_blocks.reshape(seq_len, local_width)
    attn_part = lax.psum_scatter(
        contract(context, out_full, 1, 0), "mp", scatter_dimension=0, tiled=True
    )
    residual = tokens + attn_part
    inverse_second = root_inverse(residual)
    scaled_second = residual * inverse_second
    normed_second = (scaled_second * gain_second).astype(jnp.bfloat16)
    rows_second = lax.all_gather(normed_second, "mp", axis=0, tiled=True)
    gate_proj = contract(rows_second, gate_full, 1, 0)
    up_proj = contract(rows_second, up_full, 1, 0)
    sigmoid_gate = jax.nn.sigmoid(gate_proj)
    silu_gate = gate_proj * sigmoid_gate
    hidden = (silu_gate * up_proj).astype(jnp.bfloat16)
    ffn_part = lax.psum_scatter(
        contract(hidden, down_full, 1, 0).astype(jnp.bfloat16),
        "mp",
        scatter_dimension=0,
        tiled=True,
    ).astype(jnp.float32)
    output = (residual + ffn_part).astype(jnp.bfloat16)
    cot_rows = lax.all_gather(cotangent, "mp", axis=0, tiled=True)
    grad_down_w = contract(hidden, cot_rows, 0, 0)
    grad_hidden = contract(cot_rows, down_full, 1, 1)
    grad_gate_act = (
        grad_hidden * up_proj * sigmoid_gate * (1.0 + gate_proj * (1.0 - sigmoid_gate))
    ).astype(jnp.bfloat16)
    grad_up_act = (grad_hidden * silu_gate).astype(jnp.bfloat16)
    grad_gate_w = contract(rows_second, grad_gate_act, 0, 0)
    grad_up_w = contract(rows_second, grad_up_act, 0, 0)
    grad_normed_second = lax.psum_scatter(
        contract(grad_gate_act, gate_full, 1, 1) + contract(grad_up_act, up_full, 1, 1),
        "mp",
        scatter_dimension=0,
        tiled=True,
    )
    grad_from_norm, gain_second_part = norm_back(
        grad_normed_second, scaled_second, inverse_second, gain_second
    )
    grad_residual = cotangent.astype(jnp.float32) + grad_from_norm
    attn_cot = lax.all_gather(grad_residual.astype(jnp.bfloat16), "mp", axis=0, tiled=True)
    grad_out_w = contract(context, attn_cot, 0, 0)
    grad_context = contract(attn_cot, out_full, 1, 1).astype(jnp.bfloat16)

    def backward_block(state_pair, block_index):
        grad_keys, grad_values = state_pair
        first_row = block_index * block_rows
        query_block, scores = block_scores(first_row)
        log_total = lax.dynamic_index_in_dim(log_totals, block_index, 0, keepdims=False)
        weights = jnp.exp(scores - log_total[..., None])
        grad_block = lax.dynamic_slice_in_dim(grad_context, first_row, block_rows, 0).reshape(
            block_rows, head_count, HEAD_DIM
        )
        grad_weights = jnp.einsum(
            "qhd,khd->hqk", grad_block, value_heads, preferred_element_type=jnp.float32
        )
        spread = jnp.sum(weights * grad_weights, axis=-1, keepdims=True)
        grad_scores = (weights * (grad_weights - spread)).astype(jnp.bfloat16)
        grad_query_block = (
            jnp.einsum("hqk,khd->qhd", grad_scores, key_heads, preferred_element_type=jnp.float32)
            * score_scale
        ).astype(jnp.bfloat16)
        grad_keys = (
            grad_keys
            + jnp.einsum(
                "hqk,qhd->khd", grad_scores, query_block, preferred_element_type=jnp.float32
            )
            * score_scale
        )
        grad_values = grad_values + jnp.einsum(
            "hqk,qhd->khd",
            weights.astype(jnp.bfloat16),
            grad_block,
            preferred_element_type=jnp.float32,
        )
        return ((grad_keys, grad_values), grad_query_block.reshape(block_rows, local_width))

    zero_state = jnp.zeros((seq_len, head_count, HEAD_DIM), jnp.float32)
    (grad_keys, grad_values), grad_query_blocks = lax.scan(
        backward_block, (zero_state, zero_state), jnp.arange(block_count, dtype=jnp.int32)
    )
    grad_queries = grad_query_blocks.reshape(seq_len, local_width)
    grad_kv = jnp.stack(
        [grad_keys.reshape(seq_len, local_width), grad_values.reshape(seq_len, local_width)], axis=1
    )
    grad_query_w = contract(rows_first, grad_queries, 0, 0)
    grad_normed_first = lax.psum_scatter(
        contract(grad_queries, query_full, 1, 1).astype(jnp.bfloat16),
        "mp",
        scatter_dimension=0,
        tiled=True,
    ).astype(jnp.float32)
    grad_from_first, gain_first_part = norm_back(
        grad_normed_first, scaled_first, inverse_first, gain_first
    )
    grad_input = grad_residual + grad_from_first
    gain_first_sum, gain_second_sum = lax.psum((gain_first_part, gain_second_part), ("dp", "mp"))
    query_shard, out_shard, gate_shard, up_shard, down_shard = (
        lax.psum_scatter(
            grad_query_w.astype(jnp.bfloat16), "dp", scatter_dimension=0, tiled=True
        ).astype(jnp.float32),
        lax.psum_scatter(
            grad_out_w.astype(jnp.bfloat16), "dp", scatter_dimension=1, tiled=True
        ).astype(jnp.float32),
        lax.psum_scatter(
            grad_gate_w.astype(jnp.bfloat16), "dp", scatter_dimension=0, tiled=True
        ).astype(jnp.float32),
        lax.psum_scatter(
            grad_up_w.astype(jnp.bfloat16), "dp", scatter_dimension=0, tiled=True
        ).astype(jnp.float32),
        lax.psum_scatter(
            grad_down_w.astype(jnp.bfloat16), "dp", scatter_dimension=1, tiled=True
        ).astype(jnp.float32),
    )
    return (
        output,
        grad_input,
        grad_kv,
        gain_first_sum,
        gain_second_sum,
        query_shard,
        out_shard,
        gate_shard,
        up_shard,
        down_shard,
    )


def fast_body(inputs, keys_values, segment_ids, gain_first, gain_second, w_query, w_out, w_gate,
              w_up, w_down, cotangent):
    grid = Grid(8)
    share = inputs.shape[0]
    hidden_half = w_down.shape[0] // 2
    inputs_here = grid.spread(inputs)
    tokens = inputs_here.astype(f32)
    gain_one = grid.spread(gain_first)
    gain_two = grid.spread(gain_second)
    cot_here = grid.spread(cotangent)
    inverse_first = root_inverse(tokens)
    scaled_first = tokens * inverse_first
    normed_first = (scaled_first * gain_one).astype(bf16)

    rows_first, cots, query_part, query_0, out_whole, gate_here, up_here, down_here = gather_call(
        normed_first, cot_here, w_query, w_out, w_gate.T, w_up.T, w_down)

    queries = contract(rows_first, query_part, 1, 0).astype(bf16)
    starts = starts_of(segment_ids)
    keys = keys_values[:, 0, :]
    values = keys_values[:, 1, :]
    context, log_totals = attend(starts, queries, keys, values)
    context_own, query_y = to_tokens(context, query_0, 2)
    residual = tokens + contract(context_own, out_whole, 1, 0)
    inverse_second = root_inverse(residual)
    scaled_second = residual * inverse_second
    normed_second = (scaled_second * gain_two).astype(bf16)
    grad_normed_second, ffn_parts, ffn_sums = ffn_call(normed_second, cots, down_here, gate_here, up_here, 3)

    grad_residual, grad_context, gain_second_part, query_x, down_sums, out_sums = back_first(
        grad_normed_second, residual, cot_here, gain_two[None], context_own, out_whole, ffn_sums, query_0, 5)
    grad_queries, grad_keys, grad_values = attend_back(
        starts, queries, keys, values, grad_context, log_totals)
    grad_kv = jnp.stack([grad_keys, grad_values], axis=1)
    down_shard, gate_shard, up_shard, out_shard, query_shard, grad_input, output, gains, _ = back_last(
        grad_queries, rows_first, grad_residual, inputs_here, gain_one[None], query_y, query_0, query_x,
        ffn_sums, down_sums, out_sums, ffn_parts, residual, gain_second_part, 6)
    return (output, grad_input, grad_kv, gains[0], gains[1], query_shard, out_shard,
            gate_shard.T, up_shard.T, down_shard)


def solution(mesh):
    in_specs = (
        P(("dp", "mp"), None),
        P("dp", None, "mp"),
        P("dp", None),
        P(),
        P(),
        P("dp", "mp"),
        P("mp", "dp"),
        P("dp", "mp"),
        P("dp", "mp"),
        P("mp", "dp"),
        P(("dp", "mp"), None),
    )
    out_specs = (
        P(("dp", "mp"), None),
        P(("dp", "mp"), None),
        P("dp", None, "mp"),
        P(),
        P(),
        P("dp", "mp"),
        P("mp", "dp"),
        P("dp", "mp"),
        P("dp", "mp"),
        P("mp", "dp"),
    )
    fast = mesh.shape["dp"] == 8 and mesh.shape["mp"] == 4
    body = fast_body if fast else plain_body
    return jax.shard_map(body, mesh=mesh, in_specs=in_specs, out_specs=out_specs, check_vma=False)
```

```python
import jax
import jax.numpy as jnp
from jax import lax
from jax.experimental import pallas as pl
from jax.experimental.pallas import tpu as pltpu
from jax.sharding import PartitionSpec as P

f32 = jnp.float32
bf16 = jnp.bfloat16
HEAD_DIM = 128
MP = 4
epsilon = 1e-06


MESH = pl.DeviceIdType.MESH
Z_LOW, Z_HIGH, CORE, SIDE, DEEP = 1, 2, 4, 8, 16
ANY = pl.BlockSpec(memory_space=pl.ANY)
VM = pl.BlockSpec(memory_space=pltpu.VMEM)


class Place:
    def __init__(self):
        self.dp = lax.axis_index("dp")
        self.mp = lax.axis_index("mp")

    def bit(self, mask):
        return ((self.dp * 4 + self.mp) // mask) % 2

    def partner(self, mask):
        flip_dp, flip_mp = mask // 4, mask % 4
        return (self.flip(self.dp, flip_dp), self.flip(self.mp, flip_mp))

    def flip(self, value, flips):
        for mask in (1, 2, 4):
            if flips & mask:
                value = value + mask - 2 * mask * ((value // mask) % 2)
        return value


class Copies:
    def __init__(self, place, send_sems, recv_sems, local_sems=None):
        self.place, self.send_sems, self.recv_sems = place, send_sems, recv_sems
        self.local_sems = local_sems
        self.count = 0
        self.local_count = 0
        self.pending = []

    def describe(self, source, target, device, slot):
        return pltpu.make_async_remote_copy(
            src_ref=source, dst_ref=target, send_sem=self.send_sems.at[slot],
            recv_sem=self.recv_sems.at[slot], device_id=device, device_id_type=MESH)

    def swap(self, source, target, mask):
        slot = self.count
        self.count += 1
        copy = self.describe(source, target, self.place.partner(mask), slot)
        copy.start()
        item = {"copy": copy, "got": False}
        self.pending.append(item)
        return item

    def got(self, item):
        if not item["got"]:
            item["got"] = True
            if "get_if" in item:
                @pl.when(item["get_if"])
                def _():
                    item["get"].wait_recv()
            else:
                item["copy"].wait_recv()

    def prepare(self, source, target, mask):
        slot = self.count
        self.count += 1
        item = {"copy": self.describe(source, target, self.place.partner(mask), slot), "got": False}
        self.pending.append(item)
        return item

    def prepare_step(self, block, mp_send, mp_get, direction, send_if, get_if):
        slot = self.count
        self.count += 1
        place = self.place
        device = (place.dp, jnp.clip(place.mp + direction, 0, 3))
        copy = self.describe(*block(jnp.clip(mp_send, 0, 3)), device, slot)
        get = self.describe(*block(jnp.clip(mp_get, 0, 3)), device, slot)
        item = {"copy": copy, "got": False, "send_if": send_if, "get_if": get_if, "get": get}
        self.pending.append(item)
        return item

    def start(self, item):
        if "send_if" in item:
            @pl.when(item["send_if"])
            def _():
                item["copy"].start()
        else:
            item["copy"].start()

    def step(self, *arguments):
        item = self.prepare_step(*arguments)
        self.start(item)
        return item

    def received(self, item):
        item["got"] = True
        if "get_if" in item:
            @pl.when(item["get_if"])
            def _():
                item["get"].wait_recv()
        else:
            item["copy"].wait_recv()

    def local(self, source, target):
        copy = pltpu.make_async_copy(source, target, self.local_sems.at[self.local_count])
        self.local_count += 1
        copy.start()
        return copy

    def finish(self):
        for item in self.pending:
            self.got(item)
        for item in self.pending:
            if "send_if" in item:
                @pl.when(item["send_if"])
                def _():
                    item["copy"].wait_send()
            elif "sent" not in item:
                item["copy"].wait_send()


def greet(place, masks):
    barrier = pltpu.get_barrier_semaphore()
    for mask in masks:
        pl.semaphore_signal(barrier, inc=1, device_id=place.partner(mask), device_id_type=MESH)
    pl.semaphore_wait(barrier, len(masks))


def absolute(place, spot):
    core, deep, side = spot // 4, (spot // 2) % 2, spot % 2
    return place.flip(place.dp, core + 4 * deep) - 2 * place.bit(SIDE) + 2 * side


DMA = pltpu.SemaphoreType.DMA


def dot(left, right, left_dim, right_dim):
    return lax.dot_general(
        left, right, (((left_dim,), (right_dim,)), ((), ())), preferred_element_type=f32)


def params(ident, vmem=32 << 20):
    return pltpu.CompilerParams(collective_id=ident, has_side_effects=True, vmem_limit_bytes=vmem)


def add_into(target, rows, *others, step=32):
    start, count = rows
    pieces = count // step

    def one(i, carry):
        total = target[pl.ds(start + i * step, step), :].astype(f32)
        for other in others:
            total = total + other[pl.ds(i * step, step), :].astype(f32)
        target[pl.ds(start + i * step, step), :] = total.astype(target.dtype)
        return carry

    lax.fori_loop(0, pieces, one, 0)


class QuadReduce:
    def __init__(self, copies, parts, relay, landed):
        self.copies, self.parts, self.relay, self.landed = copies, parts, relay, landed
        self.share = parts.shape[0] // 4
        self.half = self.share // 2

    def start(self):
        share, half = self.share, self.half
        self.first = self.copies.swap(self.parts.at[pl.ds(3 * share, half), :], self.relay.at[0], SIDE)
        self.second = self.copies.swap(self.parts.at[pl.ds(3 * share + half, half), :], self.relay.at[1], Z_LOW)
        self.side = [self.copies.swap(self.parts.at[pl.ds(share, half), :], self.landed.at[0, pl.ds(0, half), :], SIDE)]
        self.low = [self.copies.swap(self.parts.at[pl.ds(2 * share + half, half), :], self.landed.at[1, pl.ds(half, half), :], Z_LOW)]

    def relayed(self):
        share, half = self.share, self.half
        self.copies.got(self.first)
        add_into(self.parts, (2 * share, half), self.relay.at[0])
        self.low.append(self.copies.swap(self.parts.at[pl.ds(2 * share, half), :], self.landed.at[1, pl.ds(0, half), :], Z_LOW))
        self.copies.got(self.second)
        add_into(self.parts, (share + half, half), self.relay.at[1])
        self.side.append(self.copies.swap(self.parts.at[pl.ds(share + half, half), :], self.landed.at[0, pl.ds(half, half), :], SIDE))

    def arrived(self):
        for item in self.side + self.low:
            self.copies.got(item)


ROWS=256
DOC_MOST=512


def key_range(block, seq_len):
    low = max(0, block * ROWS - DOC_MOST + 1) // ROWS * ROWS
    return low, min(seq_len, (block + 1) * ROWS)


def scores_turned(q, k, starts, low, first, scale):
    s = dot(k, q, 1, 1) * scale
    key_pos = low + lax.broadcasted_iota(jnp.int32, s.shape, 0)
    query_pos = first + lax.broadcasted_iota(jnp.int32, s.shape, 1)
    return jnp.where((key_pos >= starts) & (key_pos <= query_pos), s, -1e30)


def attend_head(h, starts_ref, q_ref, k_ref, v_ref, ctx_ref, lse_ref):
    seq_len = q_ref.shape[0]
    scale = HEAD_DIM ** -0.5
    lanes = pl.ds(pl.multiple_of(h * HEAD_DIM, HEAD_DIM), HEAD_DIM)
    for block in range(seq_len // ROWS):
        low, high = key_range(block, seq_len)
        here = pl.ds(block * ROWS, ROWS)
        keys_here = pl.ds(low, high - low)
        s = scores_turned(q_ref[here, lanes], k_ref[keys_here, lanes], starts_ref[:, here], low, block * ROWS, scale)
        top = jnp.max(s, axis=0, keepdims=True)
        raised = jnp.exp(s - top)
        total = jnp.sum(raised, axis=0, keepdims=True)
        low_probs = (raised * (1.0 / total)).astype(bf16)
        ctx_ref[here, lanes] = dot(low_probs, v_ref[keys_here, lanes], 0, 0).astype(bf16)
        lse_ref[h, :, here] = top + jnp.log(total)


def backward_kernel(starts_ref, q_ref, k_ref, v_ref, grad_ref, lse_ref, dq_ref, dk_ref, dv_ref):
    seq_len = q_ref.shape[0]
    scale = HEAD_DIM ** -0.5
    for block in range(seq_len // ROWS):
        low, high = key_range(block, seq_len)
        here = pl.ds(block * ROWS, ROWS)
        k = k_ref[low:high, :]
        v = v_ref[low:high, :]
        q = q_ref[here, :]
        grad = grad_ref[here, :]
        s = scores_turned(q, k, starts_ref[:, here], low, block * ROWS, scale)
        probs = jnp.exp(s - lse_ref[0, :, here])
        grad_probs = dot(v, grad, 1, 1)
        spread = jnp.sum(probs * grad_probs, axis=0, keepdims=True)
        grad_s = (probs * (grad_probs - spread)).astype(bf16)
        dq_ref[here, :] = (dot(grad_s, k, 0, 0) * scale).astype(bf16)
        dk = dot(grad_s, q, 1, 0) * scale
        dv = dot(probs.astype(bf16), grad, 1, 0)
        old = max(low, min(high, block * ROWS))
        if low == 0 and block == 0:
            dk_ref[low:high, :] = dk
            dv_ref[low:high, :] = dv
        else:
            n = old - low
            dk_ref[low:old, :] += dk[:n]
            dv_ref[low:old, :] += dv[:n]
            dk_ref[old:high, :] = dk[n:]
            dv_ref[old:high, :] = dv[n:]


def specs(seq_len):
    row = pl.BlockSpec((1, seq_len), lambda h: (0, 0))
    head = pl.BlockSpec((seq_len, HEAD_DIM), lambda h: (0, h))
    lse = pl.BlockSpec((1, 1, seq_len), lambda h: (h, 0, 0))
    return row, head, lse


def attend_back(starts, q, k, v, grad, lse_array):
    seq_len, width = q.shape
    heads = width // HEAD_DIM
    row, head, lse = specs(seq_len)
    flops = heads * seq_len * seq_len * HEAD_DIM * 7
    wide = jax.ShapeDtypeStruct(q.shape, f32)
    return pl.pallas_call(
        backward_kernel, grid=(heads,),
        in_specs=[row, head, head, head, head, lse], out_specs=(head, head, head),
        out_shape=(jax.ShapeDtypeStruct(q.shape, bf16), wide, wide),
        cost_estimate=pl.CostEstimate(flops=flops, bytes_accessed=9 * q.size * 2, transcendentals=heads * seq_len * seq_len // 2),
        name="attend_back",
    )(starts, q, k, v, grad, lse_array)


def starts_of(segments):
    return jnp.sum((segments[0][None, :] < segments[0][:, None]).astype(jnp.int32), axis=1)[None, :]


def front_kernel(x, cot, gain_one_in, gain_two_in, wq, wo, wg, wu, wd, keys, values, starts,
                 rows_out, cots, gate, up, down, out_out, queries, context_own, lse, residual, normed,
                 x_here, cot_here, gain_one, gain_two,
                 first, rows, query, out, context,
                 send_sems, recv_sems, local_sems):
    place = Place()
    dp, mp = place.dp, place.mp
    side = place.bit(SIDE)
    copies = Copies(place, send_sems, recv_sems, local_sems)
    half = wd.shape[0] // 2
    blk = wd.shape[1]
    share, width = first.shape
    zrow = wo.shape[0]
    local = wq.shape[1]
    chunk = share // 2
    mats = ((wg, gate), (wu, up), (wd, down))
    own, across = side, 1 - side
    DEEPER, OTHER = 2, 4
    locals_ = []

    def tile(whole, z, spot):
        return whole.at[pl.ds(z * half, half), pl.ds(spot * blk, blk)]

    def qrows(spot):
        return query.at[pl.ds(spot * blk, blk), :]

    def columns(spot):
        return out.at[:, pl.ds(spot * blk, blk)]

    def row_block(c, source_is_input):
        def get(m):
            target = rows.at[pl.ds(m * share + c * chunk, chunk), :]
            source = first.at[pl.ds(c * chunk, chunk), :] if source_is_input else target
            return source, target
        return get

    def out_block(source_is_input):
        def get(m):
            target = out.at[pl.ds(m * zrow, zrow), pl.ds(own * blk, blk)]
            return (wo if source_is_input else target), target
        return get

    store = {}

    def line(step, block_of, key):
        store[("r", key, step)] = copies.step(block_of, mp - (step - 1), mp - step, 1,
                                              (mp >= step - 1) & (mp < 3), mp >= step)
        store[("l", key, step)] = copies.step(block_of, mp + (step - 1), mp + step, -1,
                                              (mp <= 3 - (step - 1)) & (mp > 0), mp <= 3 - step)

    def arrive(key, step):
        copies.got(store[("r", key, step)])
        copies.got(store[("l", key, step)])

    own_piece = [weight.at[pl.ds(side * half, half), :] for weight, _ in mats]
    zhop = [[], [], []]
    yhop = [[], [], []]

    def send_z(i, source, spot):
        zhop[i].append(copies.swap(source, tile(mats[i][1], 1, spot), Z_HIGH))

    def send_y(i, source, z, spot):
        yhop[i].append((copies.swap(source, tile(mats[i][1], z, spot + DEEPER), DEEP), z, spot + DEEPER))

    def core_tile(i, z, spot, source=None):
        piece = tile(mats[i][1], z, spot)
        copies.swap(piece if source is None else source, tile(mats[i][1], z, spot + OTHER), CORE)

    def core_query(spot, source=None):
        return copies.swap(qrows(spot) if source is None else source, qrows(spot + OTHER), CORE)

    def core_out(spot):
        return copies.swap(columns(spot), columns(spot + OTHER), CORE)

    greet(place, (1, 2, 3, CORE, SIDE, DEEP))
    line(1, out_block(True), "o")
    xhop = [copies.swap(weight.at[pl.ds((1 - side) * half, half), :], tile(whole, 0, own), SIDE)
            for weight, whole in mats]
    wq_y = copies.swap(wq, qrows(own + DEEPER), DEEP)
    for i in range(3):
        send_y(i, own_piece[i], 0, own)
    wq_x = [copies.swap(wq, qrows(own), SIDE)]
    wq_core = [core_query(own, wq)]
    send_z(0, own_piece[0], own)

    spots = [pl.ds(pl.multiple_of(absolute(place, s) * blk, blk), blk) for s in range(8)]
    for s in range(8):
        gain_one[:, s * blk:(s + 1) * blk] = gain_one_in[:, spots[s]]
        gain_two[:, s * blk:(s + 1) * blk] = gain_two_in[:, spots[s]]

    def norm_first(i, carry):
        here = pl.ds(i * 32, 32)
        for s in range(8):
            x_here[here, s * blk:(s + 1) * blk] = x[here, spots[s]]
            cot_here[here, s * blk:(s + 1) * blk] = cot[here, spots[s]]
        value = x_here[here, :].astype(f32)
        inverse = lax.rsqrt(jnp.mean(value * value, axis=-1, keepdims=True) + epsilon)
        first[here, :] = (value * inverse * gain_one[...]).astype(bf16)
        return carry

    lax.fori_loop(0, share // 32, norm_first, 0)
    for c in range(2):
        line(1, row_block(c, True), c)
    rows[pl.ds(mp * share, share), :] = first[...]
    query[pl.ds(own * blk, blk), :] = wq[...]
    out[pl.ds(mp * zrow, zrow), pl.ds(pl.multiple_of(own * blk, blk), blk)] = wo[...]
    locals_.append(copies.local(cot_here, cots.at[0:share, :]))
    for i in range(3):
        locals_.append(copies.local(own_piece[i], tile(mats[i][1], 0, own)))
        core_tile(i, 0, own, own_piece[i])
    copies.got(wq_y)
    wq_x.append(copies.swap(qrows(own + DEEPER), qrows(own + DEEPER), SIDE))
    wq_core.append(core_query(own + DEEPER))
    arrive("o", 1)
    line(2, out_block(False), "o")
    send_z(1, own_piece[1], own)
    send_z(2, own_piece[2], own)
    for i in range(3):
        copies.got(xhop[i])
        piece = tile(mats[i][1], 0, across)
        send_y(i, piece, 0, across)
        core_tile(i, 0, across)
    for item, spot in zip(wq_x, (across, across + DEEPER)):
        copies.got(item)
        wq_core.append(core_query(spot))
    for c in range(2):
        arrive(c, 1)
        line(2, row_block(c, False), c)
    arrive("o", 2)
    line(3, out_block(False), "o")
    for i in range(3):
        send_z(i, tile(mats[i][1], 0, across), across)
    cot_x = copies.swap(cot_here, cots.at[share:2 * share, :], SIDE)
    for i in range(2):
        copies.got(zhop[i][0])
        send_y(i, tile(mats[i][1], 1, own), 1, own)
        core_tile(i, 1, own)
    arrive("o", 3)
    out_y = copies.swap(columns(own), columns(own + DEEPER), DEEP)
    out_x = [copies.swap(columns(own), columns(own), SIDE)]
    out_core = [core_out(own)]
    for c in range(2):
        arrive(c, 2)
        line(3, row_block(c, False), c)
    copies.got(zhop[2][0])
    send_y(2, tile(mats[2][1], 1, own), 1, own)
    core_tile(2, 1, own)
    for copy in locals_:
        copy.wait()
    cot_z = copies.swap(cot_here, cots.at[2 * share:3 * share, :], Z_LOW)
    for item in wq_core:
        copies.got(item)
    copies.got(out_y)
    out_x.append(copies.swap(columns(own + DEEPER), columns(own + DEEPER), SIDE))
    out_core.append(core_out(own + DEEPER))
    for c in range(2):
        arrive(c, 3)
    save_rows = copies.local(rows, rows_out)

    def project(m, carry):
        here = pl.ds(pl.multiple_of(m * share, share), share)
        queries[here, :] = dot(rows[here, :], query[...], 1, 0).astype(bf16)
        return carry

    lax.fori_loop(0, 4, project, 0)

    def one_head(h, carry):
        attend_head(h, starts, queries, keys, values, context, lse)
        return carry

    lax.fori_loop(0, local // HEAD_DIM, one_head, 0)
    tokens_in = []
    for mask in (2, 3, 1):
        other = place.partner(mask)[1]
        tokens_in.append(copies.swap(context.at[pl.ds(other * share, share), :],
                                     context_own.at[:, pl.ds(mp * local, local)], mask))
    context_own[:, pl.ds(pl.multiple_of(mp * local, local), local)] = context[pl.ds(mp * share, share), :]
    for i in range(3):
        copies.got(zhop[i][1])
        send_y(i, tile(mats[i][1], 1, across), 1, across)
        core_tile(i, 1, across)
    for j in range(2):
        for i in range(3):
            item, z, spot = yhop[i][j]
            copies.got(item)
            core_tile(i, z, spot)
    copies.got(out_x[0])
    out_core.append(core_out(across))
    copies.got(cot_z)
    copies.swap(cots.at[2 * share:3 * share, :], cots.at[3 * share:4 * share, :], SIDE)
    copies.got(out_x[1])
    out_core.append(core_out(across + DEEPER))
    for i in range(3):
        item, z, spot = yhop[i][2]
        copies.got(item)
        core_tile(i, z, spot)
    for item in out_core + tokens_in:
        copies.got(item)
    save_out = copies.local(out, out_out)

    def project_out(n, carry):
        there = pl.ds(pl.multiple_of(n * 512, 512), 512)
        residual[:, there] = x_here[:, there].astype(f32) + dot(context_own[...], out[:, there], 1, 0)
        return carry

    lax.fori_loop(0, width // 512, project_out, 0)

    def norm_second(i, carry):
        here = pl.ds(i * 32, 32)
        value = residual[here, :]
        inverse = lax.rsqrt(jnp.mean(value * value, axis=-1, keepdims=True) + epsilon)
        normed[here, :] = (value * inverse * gain_two[...]).astype(bf16)
        return carry

    lax.fori_loop(0, share // 32, norm_second, 0)
    for i in range(3):
        item, z, spot = yhop[i][3]
        copies.got(item)
        core_tile(i, z, spot)
    save_rows.wait()
    save_out.wait()
    copies.finish()


def front_call(x, cot, gain_one, gain_two, wq, wo, wg, wu, wd, keys, values, starts, ident):
    share, width = x.shape
    hidden, blk = wd.shape
    seq_len, local = keys.shape
    V = pltpu.VMEM
    S = jax.ShapeDtypeStruct
    return pl.pallas_call(
        front_kernel,
        out_shape=(
            S((seq_len, width), bf16), S((seq_len, width), bf16), S((hidden, width), bf16), S((hidden, width), bf16),
            S((hidden, width), bf16), S((width, width), bf16), S((seq_len, local), bf16), S((share, width), bf16),
            S((local // HEAD_DIM, 1, seq_len), f32), S((share, width), f32), S((share, width), bf16),
            S((share, width), bf16), S((share, width), bf16), S((1, width), f32), S((1, width), f32)),
        in_specs=[VM] * 12,
        out_specs=(ANY,) * 6 + (VM,) * 9,
        scratch_shapes=[
            V((share, width), bf16), V((seq_len, width), bf16), V((width, local), bf16), V((width, width), bf16),
            V((seq_len, local), bf16), DMA((96,)), DMA((96,)), DMA((8,))],
        compiler_params=params(ident, 60 << 20), name="front",
    )(x, cot, gain_one, gain_two, wq, wo, wg, wu, wd, keys, values, starts)


def hidden_cuts(hidden):
    cuts = []
    start = 0
    while start < hidden:
        size = min(512, hidden - start)
        cuts.append((start, size))
        start += size
    return cuts


def ffn_kernel(normed, wq, cots_in, down_in, gate_in, up_in, total, query_0, query_y, fparts_out, sums_out,
               weights, tokens, acts, dparts, relay, landed, fparts,
               send_sems, recv_sems, local_sems, free_sem):
    place = Place()
    share, width = normed.shape
    hidden = down_in.shape[0]
    half = share // 2
    wide = width // 2
    cuts = hidden_cuts(hidden)
    copies = Copies(place, send_sems, recv_sems, local_sems)
    load_cots = copies.local(cots_in, tokens.at[0])
    load_w = [copies.local(w, weights.at[i]) for i, w in enumerate((down_in, gate_in, up_in))]
    mp = place.mp
    local = wq.shape[1]
    greet(place, (1, 2, 3, SIDE, CORE, DEEP))

    def at(quarter, part):
        return tokens.at[1, pl.ds(quarter * share + part * half, half), :]

    a, b = pl.ds(0, half), pl.ds(half, half)
    low_a = copies.swap(normed.at[a, :], at(2, 0), Z_LOW)
    side_b = copies.swap(normed.at[b, :], at(1, 1), SIDE)
    low_b = copies.swap(normed.at[b, :], at(2, 1), Z_LOW)
    side_a = copies.swap(normed.at[a, :], at(1, 0), SIDE)
    tokens[1, 0:share, :] = normed[...]

    def wide_block(source_is_input):
        def get(m):
            target = query_0.at[:, pl.ds(pl.multiple_of(m * local, local), local)]
            return (wq if source_is_input else target), target
        return get

    hops = []
    for hop in (1, 2, 3):
        block_of = wide_block(hop == 1)
        hops.append((
            copies.prepare_step(block_of, mp - (hop - 1), mp - hop, 1, (mp >= hop - 1) & (mp < 3), mp >= hop),
            copies.prepare_step(block_of, mp + (hop - 1), mp + hop, -1,
                                (mp <= 3 - (hop - 1)) & (mp > 0), mp <= 3 - hop)))
    over_deep = copies.prepare(query_0, query_y, DEEP)
    query_0[:, pl.ds(pl.multiple_of(mp * local, local), local)] = wq[...]
    for item in hops[0]:
        copies.start(item)

    def block(r):
        here = pl.ds(r * share, share)
        for start, size in cuts:
            rows = tokens[1, here, :]
            gate = dot(rows, weights[1, start:start + size, :], 1, 1)
            up = dot(rows, weights[2, start:start + size, :], 1, 1)
            grad = dot(tokens[0, here, :], weights[0, start:start + size, :], 1, 1)
            sigmoid = jax.nn.sigmoid(gate)
            silu = gate * sigmoid
            acts[0, here, start:start + size] = (silu * up).astype(bf16)
            acts[1, here, start:start + size] = (
                grad * up * sigmoid * (1.0 + gate * (1.0 - sigmoid))).astype(bf16)
            acts[2, here, start:start + size] = (grad * silu).astype(bf16)

        def columns(n, carry):
            there = pl.ds(pl.multiple_of(n * 512, 512), 512)
            dparts[here, there] = (dot(acts[1, here, :], weights[1, :, there], 1, 0)
                                   + dot(acts[2, here, :], weights[2, :, there], 1, 0)).astype(bf16)
            fparts[here, there] = dot(acts[0, here, :], weights[0, :, there], 1, 0).astype(bf16)
            return carry

        lax.fori_loop(0, width // 512, columns, 0)

    for copy in load_w:
        copy.wait()
    load_cots.wait()
    got = {"across": None}

    def step(r, carry):
        @pl.when(r == 1)
        def _():
            low_a["copy"].wait_recv()
            side_b["copy"].wait_recv()
            forward[0].start()
            forward[1].start()
            for item in hops[0]:
                copies.received(item)
            for item in hops[1]:
                copies.start(item)
            side_a["copy"].wait_recv()
            low_b["copy"].wait_recv()

        @pl.when(r == 2)
        def _():
            for item in hops[1]:
                copies.received(item)
            for item in hops[2]:
                copies.start(item)

        @pl.when(r == 3)
        def _():
            forward[0].wait_recv()
            forward[1].wait_recv()
            for item in hops[2]:
                copies.received(item)
            copies.start(over_deep)
        block(r)
        return carry

    forward = [copies.describe(at(2, 0), at(3, 0), place.partner(SIDE), copies.count),
               copies.describe(at(1, 1), at(3, 1), place.partner(Z_LOW), copies.count + 1)]
    copies.count += 2
    lax.fori_loop(0, 4, step, 0)
    for item in (low_a, side_b, low_b, side_a):
        item["got"] = True
    pl.semaphore_signal(free_sem, inc=1, device_id=place.partner(CORE), device_id_type=MESH)
    reduce = QuadReduce(copies, dparts, relay, landed)
    reduce.start()
    save = copies.local(fparts, fparts_out)

    base = copies.count
    copies.count += 3

    def give_copy(i):
        return copies.describe(weights.at[i, :, pl.ds(0, wide)], weights.at[i, :, pl.ds(wide, wide)],
                               place.partner(CORE), base + i)

    def give(i, carry):
        right = tokens[jnp.minimum(i, 1), :, wide:]
        for start, size in cuts:
            weights[i, start:start + size, 0:wide] = dot(
                acts[i, :, start:start + size], right, 0, 0).astype(bf16)

        @pl.when(i == 0)
        def _():
            pl.semaphore_wait(free_sem, 1)
        give_copy(i).start()
        return carry

    lax.fori_loop(0, 3, give, 0)
    reduce.relayed()

    def keep(i, carry):
        give_copy(i).wait_recv()
        right = tokens[jnp.minimum(i, 1), :, 0:wide]
        for start, size in cuts:
            rows = slice(start, start + size)
            weights[i, rows, wide:] = (dot(acts[i, :, rows], right, 0, 0)
                                       + weights[i, rows, wide:].astype(f32)).astype(bf16)
        pltpu.make_async_copy(weights.at[i, :, pl.ds(wide, wide)], sums_out.at[i], local_sems.at[5 + i]).start()
        return carry

    lax.fori_loop(0, 3, keep, 0)
    reduce.arrived()

    def one(i, carry):
        here = pl.ds(i * 32, 32)
        total[here, :] = (dparts[here, :].astype(f32) + landed[0, here, :].astype(f32)
                          + landed[1, here, :].astype(f32))
        return carry

    lax.fori_loop(0, share // 32, one, 0)
    for i in range(3):
        give_copy(i).wait_send()
        pltpu.make_async_copy(weights.at[i, :, pl.ds(wide, wide)], sums_out.at[i], local_sems.at[5 + i]).wait()
    for copy in forward:
        copy.wait_send()
    save.wait()
    copies.finish()


def ffn_call(normed, wq, cots, down, gate, up, ident):
    share, width = normed.shape
    hidden = down.shape[0]
    V = pltpu.VMEM
    flops = 2 * share * 4 * width * hidden * 9
    return pl.pallas_call(
        ffn_kernel,
        out_shape=(jax.ShapeDtypeStruct((share, width), f32), jax.ShapeDtypeStruct((share, width), bf16),
                   jax.ShapeDtypeStruct((share, width), bf16), jax.ShapeDtypeStruct((share * 4, width), bf16),
                   jax.ShapeDtypeStruct((3, hidden, width // 2), bf16)),
        in_specs=[VM] * 2 + [ANY] * 4,
        out_specs=(VM, VM, VM, ANY, ANY),
        scratch_shapes=[
            V((3, hidden, width), bf16), V((2, share * 4, width), bf16), V((3, share * 4, hidden), bf16),
            V((share * 4, width), bf16), V((2, share // 2, width), bf16), V((2, share, width), bf16),
            V((share * 4, width), bf16),
            DMA((24,)), DMA((24,)), DMA((8,)), pltpu.SemaphoreType.REGULAR],
        compiler_params=params(ident, 63 << 20),
        cost_estimate=pl.CostEstimate(flops=flops, bytes_accessed=40 << 20, transcendentals=share * 4 * hidden),
        name="feed_forward",
    )(normed, wq, cots, down, gate, up)


def back_first_kernel(dn2, residual, cot, gain, context, out_whole, sums, query_0,
                      dres, heads, gain_part, query_x, down_sums, out_sums,
                      keep_d, deep_d, grad_low, wout, dctx, give_o, core_o,
                      send_sems, recv_sems, local_sems):
    place = Place()
    mp = place.mp
    share, width = dn2.shape
    hidden = keep_d.shape[0]
    local = heads.shape[1]
    wide = width // 2
    copies = Copies(place, send_sems, recv_sems, local_sems)
    loads = [copies.local(out_whole.at[pl.ds(z * local, local), :], wout.at[z]) for z in range(4)]
    load_d = copies.local(sums.at[0, :, pl.ds(0, wide // 2)], keep_d)
    greet(place, (1, 2, 3, CORE, SIDE, DEEP))
    in_d = copies.swap(sums.at[0, :, pl.ds(wide // 2, wide // 2)], deep_d, DEEP)
    copies.swap(query_0, query_x, SIDE)
    gain_part[...] = jnp.zeros_like(gain_part)

    def norm(i, carry):
        here = pl.ds(i * 32, 32)
        value = residual[here, :]
        inverse = lax.rsqrt(jnp.mean(value * value, axis=-1, keepdims=True) + epsilon)
        scaled = value * inverse
        grad = dn2[here, :]
        grad_scaled = grad * gain[...]
        back = inverse * (grad_scaled - scaled * jnp.mean(grad_scaled * scaled, axis=-1, keepdims=True))
        total = cot[here, :].astype(f32) + back
        dres[here, :] = total
        grad_low[here, :] = total.astype(bf16)
        gain_part[...] += jnp.sum(grad * scaled, axis=0, keepdims=True)
        return carry

    lax.fori_loop(0, share // 32, norm, 0)
    for copy in loads:
        copy.wait()
    for mask in (2, 3, 1, 0):
        other = place.partner(mask)[1]
        there = pl.ds(pl.multiple_of(other * local, local), local)
        piece = dot(grad_low[...], wout[other], 1, 1).astype(bf16)
        if mask:
            dctx[:, there] = piece
            copies.swap(dctx.at[:, there], heads.at[pl.ds(mp * share, share), :], mask)
        else:
            heads[pl.ds(mp * share, share), :] = piece
    chunks = width // 512
    base = copies.count
    copies.count += chunks

    def core_copy(n):
        rows = pl.ds(pl.multiple_of(n * 512, 512), 512)
        return copies.describe(give_o.at[rows, :], core_o.at[rows, :], place.partner(CORE), base + n)

    def give(n, carry):
        rows = pl.ds(pl.multiple_of(n * 512, 512), 512)
        give_o[rows, :] = dot(context[:, rows], grad_low[:, wide:], 0, 0).astype(bf16)
        core_copy(n).start()
        return carry

    lax.fori_loop(0, chunks, give, 0)

    def keep(n, carry):
        rows = pl.ds(pl.multiple_of(n * 512, 512), 512)
        core_copy(n).wait_recv()
        out_sums[rows, :] = (dot(context[:, rows], grad_low[:, :wide], 0, 0)
                             + core_o[rows, :].astype(f32)).astype(bf16)
        return carry

    lax.fori_loop(0, chunks, keep, 0)
    load_d.wait()
    copies.got(in_d)

    def add_d(n, carry):
        rows = pl.ds(n * 32, 32)
        down_sums[rows, :] = (keep_d[rows, :].astype(f32) + deep_d[rows, :].astype(f32)).astype(bf16)
        return carry

    lax.fori_loop(0, hidden // 32, add_d, 0)
    copies.finish()

    def sent(n, carry):
        core_copy(n).wait_send()
        return carry

    lax.fori_loop(0, chunks, sent, 0)


def back_first(dn2, residual, cot, gain, context, out_whole, sums, query_0, ident):
    share, width = dn2.shape
    hidden = sums.shape[1]
    V = pltpu.VMEM
    S = jax.ShapeDtypeStruct
    return pl.pallas_call(
        back_first_kernel,
        out_shape=(S((share, width), f32), S((share * 4, width // 4), bf16), S((1, width), f32),
                   S(query_0.shape, bf16), S((hidden, width // 4), bf16), S((width, width // 2), bf16)),
        in_specs=[VM] * 5 + [ANY, ANY, VM],
        out_specs=(VM,) * 6,
        scratch_shapes=[
            V((hidden, width // 4), bf16), V((hidden, width // 4), bf16), V((share, width), bf16),
            V((4, width // 4, width), bf16), V((share, width), bf16), V((width, width // 2), bf16),
            V((width, width // 2), bf16), DMA((12,)), DMA((12,)), DMA((5,))],
        compiler_params=params(ident, 60 << 20), name="back_first",
    )(dn2, residual, cot, gain, context, out_whole, sums, query_0)


def back_last_kernel(grad_q, rows_first, dres, inputs, gain, query_y, query_0, query_x,
                     sums, down_sums, out_sums, fparts, residual, gain_part,
                     down, gate, up, out, query, grad_input, output, gains, query_whole,
                     keep_f, deep_f, high_f, side_f, own_o, side_o, deep_o, z_o,
                     give_q, own_q, core_q, side_q, deep_q, parts, relay, landed,
                     grad_own, stream, dn1, gain_rows, gains_got,
                     send_sems, recv_sems, local_sems):
    place = Place()
    mp = place.mp
    side = place.bit(SIDE)
    share, width = dres.shape
    hidden, blk = down.shape
    half = hidden // 2
    local = grad_q.shape[1]
    zrow = out.shape[0]
    quarter = 2 * blk
    copies = Copies(place, send_sems, recv_sems, local_sems)
    load_rows = copies.local(rows_first, stream.at[pl.ds(0, share * 4), :])
    load_d = copies.local(down_sums, keep_f.at[0])
    load_p = copies.local(fparts, parts)
    load_f = [copies.local(sums.at[i, :, pl.ds(0, quarter)], keep_f.at[i]) for i in (1, 2)]
    load_o = copies.local(out_sums, own_o)

    def qrows(spot):
        return query_whole.at[pl.ds(spot * blk, blk), :]

    greet(place, (1, 2, 3, CORE, SIDE, DEEP))
    tokens_in = []
    for mask in (2, 3, 1):
        other = place.partner(mask)[1]
        tokens_in.append(copies.swap(grad_q.at[pl.ds(other * share, share), :],
                                     grad_own.at[:, pl.ds(mp * local, local)], mask))
    wq_across = copies.swap(query_y, qrows(side + 2), SIDE)
    deep_in = [None]
    for i in (1, 2):
        deep_in.append([copies.swap(sums.at[i, :, pl.ds(quarter + x * blk, blk)], deep_f.at[i - 1, :, pl.ds(x * blk, blk)], DEEP)
                        for x in (0, 1)])
    held = [copies.local(query_0, qrows(side)), copies.local(query_y, qrows(side + 2)),
            copies.local(query_x, qrows(1 - side))]
    wq_core = [copies.swap(query_0, qrows(side + 4), CORE), copies.swap(query_y, qrows(side + 6), CORE),
               copies.swap(query_x, qrows(1 - side + 4), CORE)]
    load_d.wait()
    give_rows = pl.ds(half, half)
    high_in = [[copies.swap(keep_f.at[0, give_rows, pl.ds(x * blk, blk)], high_f.at[0, :, pl.ds(x * blk, blk)], Z_HIGH)
                for x in (0, 1)]]
    grad_own[:, pl.ds(mp * local, local)] = grad_q[pl.ds(mp * share, share), :]
    load_rows.wait()
    wide = width // 2

    def product(first):
        return dot(stream[0:share * 4, first:first + wide], grad_q[...], 0, 0)

    give_q[...] = product(wide).astype(bf16)
    core_in_q = copies.swap(give_q, core_q, CORE)
    load_p.wait()
    reduce = QuadReduce(copies, parts, relay, landed)
    reduce.start()
    load_o.wait()

    def block_o(spot):
        return own_o.at[:, pl.ds(spot * blk, blk)]

    side_in_o = {y: copies.swap(block_o(2 * y + 1 - side), side_o.at[y], SIDE) for y in (1, 0)}
    keep_q = product(0)
    copies.got(core_in_q)
    own_q[...] = (keep_q + core_q[...].astype(f32)).astype(bf16)
    side_in_q = {y: copies.swap(own_q.at[pl.ds((2 * y + 1 - side) * blk, blk), :], side_q.at[y], SIDE) for y in (1, 0)}
    reduce.relayed()
    for copy in held:
        copy.wait()
    for item in tokens_in:
        copies.got(item)
    copies.got(wq_across)
    wq_core.append(copies.swap(qrows(1 - side + 2), qrows(1 - side + 6), CORE))
    for item in wq_core:
        copies.got(item)
    load_wq = copies.local(query_whole, stream)
    load_wq.wait()

    def first_back(n, carry):
        there = pl.ds(pl.multiple_of(n * 512, 512), 512)
        dn1[:, there] = dot(grad_own[...], stream[there, :], 1, 1)
        return carry

    lax.fori_loop(0, width // 512, first_back, 0)
    gain_rows[0:1, :] = jnp.zeros((1, width), f32)
    gain_rows[1:2, :] = gain_part[...]

    def norm(i, carry):
        here = pl.ds(i * 32, 32)
        value = inputs[here, :].astype(f32)
        inverse = lax.rsqrt(jnp.mean(value * value, axis=-1, keepdims=True) + epsilon)
        scaled = value * inverse
        grad = dn1[here, :]
        grad_scaled = grad * gain[...]
        back = inverse * (grad_scaled - scaled * jnp.mean(grad_scaled * scaled, axis=-1, keepdims=True))
        total = dres[here, :] + back
        for spot in range(8):
            there = pl.ds(pl.multiple_of(absolute(place, spot) * blk, blk), blk)
            grad_input[here, there] = total[:, spot * blk:(spot + 1) * blk]
        gain_rows[0:1, :] += jnp.sum(grad * scaled, axis=0, keepdims=True)
        return carry

    lax.fori_loop(0, share // 32, norm, 0)
    for spot in range(8):
        there = pl.ds(pl.multiple_of(absolute(place, spot) * blk, blk), blk)
        gains[:, there] = gain_rows[:, spot * blk:(spot + 1) * blk]
    gain_masks = (1, 2, CORE, SIDE, DEEP)
    gain_state = {"item": None, "at": 0}

    def gain_hop():
        if gain_state["item"] is not None:
            item = gain_state["item"]
            copies.got(item)
            item["copy"].wait_send()
            item["sent"] = True
            gains[...] = gains[...] + gains_got[gain_state["at"] - 1]
            gain_state["item"] = None
        if gain_state["at"] < len(gain_masks):
            gain_state["item"] = copies.swap(gains, gains_got.at[gain_state["at"]], gain_masks[gain_state["at"]])
            gain_state["at"] += 1

    def deep_sum(i):
        sent = []
        for x in (0, 1):
            copies.got(deep_in[i][x])
            there = pl.ds(x * blk, blk)
            add_into(keep_f.at[i, :, there], (half, half), deep_f.at[i - 1, give_rows, there], step=16)
            sent.append(copies.swap(keep_f.at[i, give_rows, there], high_f.at[i, :, there], Z_HIGH))
        for x in (0, 1):
            there = pl.ds(x * blk, blk)
            add_into(keep_f.at[i, :, there], (0, half), deep_f.at[i - 1, :, there], step=16)
        high_in.append(sent)

    def high_sum(i):
        for x in (0, 1):
            copies.got(high_in[i][x])
            add_into(keep_f.at[i, :, pl.ds(x * blk, blk)], (0, half), high_f.at[i, :, pl.ds(x * blk, blk)], step=16)
        there = pl.ds(pl.multiple_of((1 - side) * blk, blk), blk)
        return copies.swap(keep_f.at[i, pl.ds(0, half), there], side_f.at[i], SIDE)

    gain_hop()
    load_f[0].wait()
    deep_sum(1)
    gain_hop()
    side_in = [high_sum(0)]
    gain_hop()
    deep_in_q = None
    for y in (1, 0):
        copies.got(side_in_q[y])
        spot = 2 * y + side
        rows = pl.ds(pl.multiple_of(spot * blk, blk), blk)
        own_q[rows, :] = (own_q[rows, :].astype(f32) + side_q[y].astype(f32)).astype(bf16)
        if y:
            deep_in_q = copies.swap(own_q.at[rows, :], deep_q, DEEP)
    gain_hop()
    load_f[1].wait()
    deep_sum(2)
    gain_hop()
    deep_in_o = None
    for y in (1, 0):
        copies.got(side_in_o[y])
        there = pl.ds(pl.multiple_of((2 * y + side) * blk, blk), blk)
        add_into(own_o.at[:, there], (0, width), side_o.at[y])
        if y:
            deep_in_o = copies.swap(own_o.at[:, there], deep_o, DEEP)
    gain_hop()
    reduce.arrived()

    def finish_output(i, carry):
        here = pl.ds(i * 32, 32)
        total = (residual[here, :] + parts[here, :].astype(f32) + landed[0, here, :].astype(f32)
                 + landed[1, here, :].astype(f32)).astype(bf16)
        for spot in range(8):
            there = pl.ds(pl.multiple_of(absolute(place, spot) * blk, blk), blk)
            output[here, there] = total[:, spot * blk:(spot + 1) * blk]
        return carry

    lax.fori_loop(0, share // 32, finish_output, 0)
    mine = pl.ds(pl.multiple_of(side * blk, blk), blk)
    copies.got(deep_in_o)
    add_into(own_o.at[:, mine], (0, width), deep_o)
    z_in = []
    for n, mask in enumerate((2, 3, 1)):
        other = place.partner(mask)[1]
        z_in.append(copies.swap(own_o.at[pl.ds(other * zrow, zrow), mine], z_o.at[n], mask))
    copies.got(deep_in_q)
    query[...] = own_q[pl.ds(pl.multiple_of(side * blk, blk), blk), :].astype(f32) + deep_q[...].astype(f32)
    side_in.append(high_sum(1))
    side_in.append(high_sum(2))
    for item in z_in:
        copies.got(item)

    def add_z(i, carry):
        here = pl.ds(i * 32, 32)
        sum_ = own_o[pl.ds(mp * zrow + i * 32, 32), mine].astype(f32)
        for n in range(3):
            sum_ = sum_ + z_o[n, here, :].astype(f32)
        out[here, :] = sum_
        return carry

    lax.fori_loop(0, zrow // 32, add_z, 0)
    for i, target in enumerate((down, gate, up)):
        copies.got(side_in[i])

        def write(n, carry, i=i, target=target):
            target[pl.ds(side * half + n * 16, 16), :] = keep_f[i, pl.ds(n * 16, 16), mine].astype(f32)
            target[pl.ds((1 - side) * half + n * 16, 16), :] = side_f[i, pl.ds(n * 16, 16), :].astype(f32)
            return carry

        lax.fori_loop(0, half // 16, write, 0)
    copies.finish()


def back_last(grad_q, rows_first, dres, inputs, gain, query_y, query_0, query_x,
              sums, down_sums, out_sums, fparts, residual, gain_part, ident):
    share, width = dres.shape
    hidden = sums.shape[1]
    blk = width // 8
    half = hidden // 2
    local = grad_q.shape[1]
    V = pltpu.VMEM
    S = jax.ShapeDtypeStruct
    return pl.pallas_call(
        back_last_kernel,
        out_shape=(S((hidden, blk), f32),) * 3
        + (S((width // 4, blk), f32), S((blk, local), f32), S((share, width), f32), S((share, width), bf16),
           S((2, width), f32), S((width, width), bf16)),
        in_specs=[VM, ANY] + [VM] * 6 + [ANY] * 4 + [VM] * 2,
        out_specs=(VM,) * 8 + (ANY,),
        scratch_shapes=[
            V((3, hidden, 2 * blk), bf16), V((2, hidden, 2 * blk), bf16), V((3, half, 2 * blk), bf16),
            V((3, half, blk), bf16),
            V((width, width // 2), bf16), V((2, width, blk), bf16), V((width, blk), bf16),
            V((3, width // 4, blk), bf16),
            V((width // 2, local), bf16), V((width // 2, local), bf16), V((width // 2, local), bf16),
            V((2, blk, local), bf16), V((blk, local), bf16),
            V((share * 4, width), bf16), V((2, share // 2, width), bf16), V((2, share, width), bf16),
            V((share, width), bf16), V((width, width), bf16), V((share, width), f32),
            V((2, width), f32), V((5, 2, width), f32),
            DMA((48,)), DMA((48,)), DMA((12,))],
        compiler_params=params(ident, 63 << 20), name="back_last",
    )(grad_q, rows_first, dres, inputs, gain, query_y, query_0, query_x,
      sums, down_sums, out_sums, fparts, residual, gain_part)


def contract(left, right, left_dim, right_dim):
    return lax.dot_general(
        left, right, (((left_dim,), (right_dim,)), ((), ())), preferred_element_type=jnp.float32
    )


def root_inverse(values):
    return lax.rsqrt(jnp.mean(values * values, axis=-1, keepdims=True) + epsilon)


def norm_back(grad_normed, scaled, inverse, gain):
    grad_scaled = grad_normed * gain
    grad_values = inverse * (
        grad_scaled - scaled * jnp.mean(grad_scaled * scaled, axis=-1, keepdims=True)
    )
    return (grad_values, jnp.sum(grad_normed * scaled, axis=0))


def plain_body(
    inputs,
    keys_values,
    segment_ids,
    gain_first,
    gain_second,
    w_query,
    w_out,
    w_gate,
    w_up,
    w_down,
    cotangent,
):
    query_full, out_full = (
        lax.all_gather(w_query, "dp", axis=0, tiled=True),
        lax.all_gather(w_out, "dp", axis=1, tiled=True),
    )
    gate_full, up_full, down_full = (
        lax.all_gather(w_gate, "dp", axis=0, tiled=True),
        lax.all_gather(w_up, "dp", axis=0, tiled=True),
        lax.all_gather(w_down, "dp", axis=1, tiled=True),
    )
    tokens = inputs.astype(jnp.float32)
    inverse_first = root_inverse(tokens)
    scaled_first = tokens * inverse_first
    normed_first = (scaled_first * gain_first).astype(jnp.bfloat16)
    rows_first = lax.all_gather(normed_first, "mp", axis=0, tiled=True)
    queries = contract(rows_first, query_full, 1, 0).astype(jnp.bfloat16)
    seq_len = rows_first.shape[0]
    local_width = queries.shape[1]
    head_count = local_width // HEAD_DIM
    block_rows = min(512, seq_len)
    block_count = seq_len // block_rows
    score_scale = HEAD_DIM ** (-0.5)
    key_heads = keys_values[:, 0, :].reshape(seq_len, head_count, HEAD_DIM)
    value_heads = keys_values[:, 1, :].reshape(seq_len, head_count, HEAD_DIM)
    segments = segment_ids[0]
    key_pos = jnp.arange(seq_len, dtype=jnp.int32)

    def block_scores(first_row):
        query_block = lax.dynamic_slice_in_dim(queries, first_row, block_rows, 0).reshape(
            block_rows, head_count, HEAD_DIM
        )
        scores = (
            jnp.einsum("qhd,khd->hqk", query_block, key_heads, preferred_element_type=jnp.float32)
            * score_scale
        )
        query_pos = first_row + jnp.arange(block_rows, dtype=jnp.int32)
        query_seg = lax.dynamic_slice_in_dim(segments, first_row, block_rows, 0)
        allowed = (query_pos[:, None] >= key_pos[None, :]) & (
            query_seg[:, None] == segments[None, :]
        )
        return (query_block, jnp.where(allowed[None], scores, -1e30))

    def forward_block(block_index):
        query_block, scores = block_scores(block_index * block_rows)
        row_max = jnp.max(scores, axis=-1, keepdims=True)
        raised = jnp.exp(scores - row_max)
        row_total = jnp.sum(raised, axis=-1, keepdims=True)
        weights_low = (raised / row_total).astype(jnp.bfloat16)
        blended = jnp.einsum(
            "hqk,khd->qhd", weights_low, value_heads, preferred_element_type=jnp.float32
        )
        return (
            blended.reshape(block_rows, local_width).astype(jnp.bfloat16),
            (row_max + jnp.log(row_total))[..., 0],
        )

    context_blocks, log_totals = lax.map(forward_block, jnp.arange(block_count, dtype=jnp.int32))
    context = context_blocks.reshape(seq_len, local_width)
    attn_part = lax.psum_scatter(
        contract(context, out_full, 1, 0), "mp", scatter_dimension=0, tiled=True
    )
    residual = tokens + attn_part
    inverse_second = root_inverse(residual)
    scaled_second = residual * inverse_second
    normed_second = (scaled_second * gain_second).astype(jnp.bfloat16)
    rows_second = lax.all_gather(normed_second, "mp", axis=0, tiled=True)
    gate_proj = contract(rows_second, gate_full, 1, 0)
    up_proj = contract(rows_second, up_full, 1, 0)
    sigmoid_gate = jax.nn.sigmoid(gate_proj)
    silu_gate = gate_proj * sigmoid_gate
    hidden = (silu_gate * up_proj).astype(jnp.bfloat16)
    ffn_part = lax.psum_scatter(
        contract(hidden, down_full, 1, 0).astype(jnp.bfloat16),
        "mp",
        scatter_dimension=0,
        tiled=True,
    ).astype(jnp.float32)
    output = (residual + ffn_part).astype(jnp.bfloat16)
    cot_rows = lax.all_gather(cotangent, "mp", axis=0, tiled=True)
    grad_down_w = contract(hidden, cot_rows, 0, 0)
    grad_hidden = contract(cot_rows, down_full, 1, 1)
    grad_gate_act = (
        grad_hidden * up_proj * sigmoid_gate * (1.0 + gate_proj * (1.0 - sigmoid_gate))
    ).astype(jnp.bfloat16)
    grad_up_act = (grad_hidden * silu_gate).astype(jnp.bfloat16)
    grad_gate_w = contract(rows_second, grad_gate_act, 0, 0)
    grad_up_w = contract(rows_second, grad_up_act, 0, 0)
    grad_normed_second = lax.psum_scatter(
        contract(grad_gate_act, gate_full, 1, 1) + contract(grad_up_act, up_full, 1, 1),
        "mp",
        scatter_dimension=0,
        tiled=True,
    )
    grad_from_norm, gain_second_part = norm_back(
        grad_normed_second, scaled_second, inverse_second, gain_second
    )
    grad_residual = cotangent.astype(jnp.float32) + grad_from_norm
    attn_cot = lax.all_gather(grad_residual.astype(jnp.bfloat16), "mp", axis=0, tiled=True)
    grad_out_w = contract(context, attn_cot, 0, 0)
    grad_context = contract(attn_cot, out_full, 1, 1).astype(jnp.bfloat16)

    def backward_block(state_pair, block_index):
        grad_keys, grad_values = state_pair
        first_row = block_index * block_rows
        query_block, scores = block_scores(first_row)
        log_total = lax.dynamic_index_in_dim(log_totals, block_index, 0, keepdims=False)
        weights = jnp.exp(scores - log_total[..., None])
        grad_block = lax.dynamic_slice_in_dim(grad_context, first_row, block_rows, 0).reshape(
            block_rows, head_count, HEAD_DIM
        )
        grad_weights = jnp.einsum(
            "qhd,khd->hqk", grad_block, value_heads, preferred_element_type=jnp.float32
        )
        spread = jnp.sum(weights * grad_weights, axis=-1, keepdims=True)
        grad_scores = (weights * (grad_weights - spread)).astype(jnp.bfloat16)
        grad_query_block = (
            jnp.einsum("hqk,khd->qhd", grad_scores, key_heads, preferred_element_type=jnp.float32)
            * score_scale
        ).astype(jnp.bfloat16)
        grad_keys = (
            grad_keys
            + jnp.einsum(
                "hqk,qhd->khd", grad_scores, query_block, preferred_element_type=jnp.float32
            )
            * score_scale
        )
        grad_values = grad_values + jnp.einsum(
            "hqk,qhd->khd",
            weights.astype(jnp.bfloat16),
            grad_block,
            preferred_element_type=jnp.float32,
        )
        return ((grad_keys, grad_values), grad_query_block.reshape(block_rows, local_width))

    zero_state = jnp.zeros((seq_len, head_count, HEAD_DIM), jnp.float32)
    (grad_keys, grad_values), grad_query_blocks = lax.scan(
        backward_block, (zero_state, zero_state), jnp.arange(block_count, dtype=jnp.int32)
    )
    grad_queries = grad_query_blocks.reshape(seq_len, local_width)
    grad_kv = jnp.stack(
        [grad_keys.reshape(seq_len, local_width), grad_values.reshape(seq_len, local_width)], axis=1
    )
    grad_query_w = contract(rows_first, grad_queries, 0, 0)
    grad_normed_first = lax.psum_scatter(
        contract(grad_queries, query_full, 1, 1).astype(jnp.bfloat16),
        "mp",
        scatter_dimension=0,
        tiled=True,
    ).astype(jnp.float32)
    grad_from_first, gain_first_part = norm_back(
        grad_normed_first, scaled_first, inverse_first, gain_first
    )
    grad_input = grad_residual + grad_from_first
    gain_first_sum, gain_second_sum = lax.psum((gain_first_part, gain_second_part), ("dp", "mp"))
    query_shard, out_shard, gate_shard, up_shard, down_shard = (
        lax.psum_scatter(
            grad_query_w.astype(jnp.bfloat16), "dp", scatter_dimension=0, tiled=True
        ).astype(jnp.float32),
        lax.psum_scatter(
            grad_out_w.astype(jnp.bfloat16), "dp", scatter_dimension=1, tiled=True
        ).astype(jnp.float32),
        lax.psum_scatter(
            grad_gate_w.astype(jnp.bfloat16), "dp", scatter_dimension=0, tiled=True
        ).astype(jnp.float32),
        lax.psum_scatter(
            grad_up_w.astype(jnp.bfloat16), "dp", scatter_dimension=0, tiled=True
        ).astype(jnp.float32),
        lax.psum_scatter(
            grad_down_w.astype(jnp.bfloat16), "dp", scatter_dimension=1, tiled=True
        ).astype(jnp.float32),
    )
    return (
        output,
        grad_input,
        grad_kv,
        gain_first_sum,
        gain_second_sum,
        query_shard,
        out_shard,
        gate_shard,
        up_shard,
        down_shard,
    )


def fast_body(inputs, keys_values, segment_ids, gain_first, gain_second, w_query, w_out, w_gate,
              w_up, w_down, cotangent):
    starts = starts_of(segment_ids)
    keys = keys_values[:, 0, :]
    values = keys_values[:, 1, :]
    (rows_first, cots, gate_here, up_here, down_here, out_whole, queries, context_own, log_totals, residual,
     normed_second, inputs_here, cot_here, gain_one, gain_two) = front_call(
        inputs, cotangent, gain_first[None], gain_second[None], w_query, w_out, w_gate.T, w_up.T, w_down,
        keys, values, starts, 1)
    grad_normed_second, query_0, query_y, ffn_parts, ffn_sums = ffn_call(
        normed_second, w_query, cots, down_here, gate_here, up_here, 3)
    grad_residual, grad_context, gain_second_part, query_x, down_sums, out_sums = back_first(
        grad_normed_second, residual, cot_here, gain_two, context_own, out_whole, ffn_sums, query_0, 5)
    grad_queries, grad_keys, grad_values = attend_back(
        starts, queries, keys, values, grad_context, log_totals)
    grad_kv = jnp.stack([grad_keys, grad_values], axis=1)
    down_shard, gate_shard, up_shard, out_shard, query_shard, grad_input, output, gains, _ = back_last(
        grad_queries, rows_first, grad_residual, inputs_here, gain_one, query_y, query_0, query_x,
        ffn_sums, down_sums, out_sums, ffn_parts, residual, gain_second_part, 6)
    return (output, grad_input, grad_kv, gains[0], gains[1], query_shard, out_shard,
            gate_shard.T, up_shard.T, down_shard)


def solution(mesh):
    in_specs = (
        P(("dp", "mp"), None),
        P("dp", None, "mp"),
        P("dp", None),
        P(),
        P(),
        P("dp", "mp"),
        P("mp", "dp"),
        P("dp", "mp"),
        P("dp", "mp"),
        P("mp", "dp"),
        P(("dp", "mp"), None),
    )
    out_specs = (
        P(("dp", "mp"), None),
        P(("dp", "mp"), None),
        P("dp", None, "mp"),
        P(),
        P(),
        P("dp", "mp"),
        P("mp", "dp"),
        P("dp", "mp"),
        P("dp", "mp"),
        P("mp", "dp"),
    )
    fast = mesh.shape["dp"] == 8 and mesh.shape["mp"] == 4
    body = fast_body if fast else plain_body
    return jax.shard_map(body, mesh=mesh, in_specs=in_specs, out_specs=out_specs, check_vma=False)
```

```python
import jax
import jax.numpy as jnp
from jax import lax
from jax.experimental import pallas as pl
from jax.experimental.pallas import tpu as pltpu
from jax.sharding import PartitionSpec as P

f32 = jnp.float32
bf16 = jnp.bfloat16
HEAD_DIM = 128
MP = 4
epsilon = 1e-06


MESH = pl.DeviceIdType.MESH
Z_LOW, Z_HIGH, CORE, SIDE, DEEP = 1, 2, 4, 8, 16
ANY = pl.BlockSpec(memory_space=pl.ANY)
VM = pl.BlockSpec(memory_space=pltpu.VMEM)


class Place:
    def __init__(self):
        self.dp = lax.axis_index("dp")
        self.mp = lax.axis_index("mp")

    def bit(self, mask):
        return ((self.dp * 4 + self.mp) // mask) % 2

    def partner(self, mask):
        flip_dp, flip_mp = mask // 4, mask % 4
        return (self.flip(self.dp, flip_dp), self.flip(self.mp, flip_mp))

    def flip(self, value, flips):
        for mask in (1, 2, 4):
            if flips & mask:
                value = value + mask - 2 * mask * ((value // mask) % 2)
        return value


class Copies:
    def __init__(self, place, send_sems, recv_sems, local_sems=None):
        self.place, self.send_sems, self.recv_sems = place, send_sems, recv_sems
        self.local_sems = local_sems
        self.count = 0
        self.local_count = 0
        self.pending = []

    def describe(self, source, target, device, slot):
        return pltpu.make_async_remote_copy(
            src_ref=source, dst_ref=target, send_sem=self.send_sems.at[slot],
            recv_sem=self.recv_sems.at[slot], device_id=device, device_id_type=MESH)

    def swap(self, source, target, mask):
        slot = self.count
        self.count += 1
        copy = self.describe(source, target, self.place.partner(mask), slot)
        copy.start()
        item = {"copy": copy, "got": False}
        self.pending.append(item)
        return item

    def got(self, item):
        if not item["got"]:
            item["got"] = True
            if "get_if" in item:
                @pl.when(item["get_if"])
                def _():
                    item["get"].wait_recv()
            else:
                item["copy"].wait_recv()

    def prepare(self, source, target, mask):
        slot = self.count
        self.count += 1
        item = {"copy": self.describe(source, target, self.place.partner(mask), slot), "got": False}
        self.pending.append(item)
        return item

    def prepare_step(self, block, mp_send, mp_get, direction, send_if, get_if):
        slot = self.count
        self.count += 1
        place = self.place
        device = (place.dp, jnp.clip(place.mp + direction, 0, 3))
        copy = self.describe(*block(jnp.clip(mp_send, 0, 3)), device, slot)
        get = self.describe(*block(jnp.clip(mp_get, 0, 3)), device, slot)
        item = {"copy": copy, "got": False, "send_if": send_if, "get_if": get_if, "get": get}
        self.pending.append(item)
        return item

    def start(self, item):
        if "send_if" in item:
            @pl.when(item["send_if"])
            def _():
                item["copy"].start()
        else:
            item["copy"].start()

    def step(self, *arguments):
        item = self.prepare_step(*arguments)
        self.start(item)
        return item

    def received(self, item):
        item["got"] = True
        if "get_if" in item:
            @pl.when(item["get_if"])
            def _():
                item["get"].wait_recv()
        else:
            item["copy"].wait_recv()

    def local(self, source, target):
        copy = pltpu.make_async_copy(source, target, self.local_sems.at[self.local_count])
        self.local_count += 1
        copy.start()
        return copy

    def finish(self):
        for item in self.pending:
            self.got(item)
        for item in self.pending:
            if "send_if" in item:
                @pl.when(item["send_if"])
                def _():
                    item["copy"].wait_send()
            elif "sent" not in item:
                item["copy"].wait_send()


def greet(place, masks):
    barrier = pltpu.get_barrier_semaphore()
    for mask in masks:
        pl.semaphore_signal(barrier, inc=1, device_id=place.partner(mask), device_id_type=MESH)
    pl.semaphore_wait(barrier, len(masks))


def absolute(place, spot):
    core, deep, side = spot // 4, (spot // 2) % 2, spot % 2
    return place.flip(place.dp, core + 4 * deep) - 2 * place.bit(SIDE) + 2 * side


DMA = pltpu.SemaphoreType.DMA


def dot(left, right, left_dim, right_dim):
    return lax.dot_general(
        left, right, (((left_dim,), (right_dim,)), ((), ())), preferred_element_type=f32)


def params(ident, vmem=32 << 20):
    return pltpu.CompilerParams(collective_id=ident, has_side_effects=True, vmem_limit_bytes=vmem)


def add_into(target, rows, *others, step=32):
    start, count = rows
    pieces = count // step

    def one(i, carry):
        total = target[pl.ds(start + i * step, step), :].astype(f32)
        for other in others:
            total = total + other[pl.ds(i * step, step), :].astype(f32)
        target[pl.ds(start + i * step, step), :] = total.astype(target.dtype)
        return carry

    lax.fori_loop(0, pieces, one, 0)


class QuadReduce:
    def __init__(self, copies, parts, relay, landed):
        self.copies, self.parts, self.relay, self.landed = copies, parts, relay, landed
        self.share = parts.shape[0] // 4
        self.half = self.share // 2

    def prepare(self):
        share, half = self.share, self.half
        self.first = self.copies.prepare(self.parts.at[pl.ds(3 * share, half), :], self.relay.at[0], SIDE)
        self.second = self.copies.prepare(self.parts.at[pl.ds(3 * share + half, half), :], self.relay.at[1], Z_LOW)
        self.side = [self.copies.prepare(self.parts.at[pl.ds(share, half), :], self.landed.at[0, pl.ds(0, half), :], SIDE)]
        self.low = [self.copies.prepare(self.parts.at[pl.ds(2 * share + half, half), :], self.landed.at[1, pl.ds(half, half), :], Z_LOW)]

    def start_across(self):
        self.copies.start(self.first)
        self.copies.start(self.second)
        self.copies.start(self.side[0])

    def start_rest(self):
        self.copies.start(self.low[0])

    def start(self):
        self.prepare()
        self.start_across()
        self.start_rest()

    def relayed(self):
        share, half = self.share, self.half
        self.copies.got(self.first)
        add_into(self.parts, (2 * share, half), self.relay.at[0])
        self.low.append(self.copies.swap(self.parts.at[pl.ds(2 * share, half), :], self.landed.at[1, pl.ds(0, half), :], Z_LOW))
        self.copies.got(self.second)
        add_into(self.parts, (share + half, half), self.relay.at[1])
        self.side.append(self.copies.swap(self.parts.at[pl.ds(share + half, half), :], self.landed.at[0, pl.ds(half, half), :], SIDE))

    def arrived(self):
        for item in self.side + self.low:
            self.copies.got(item)


ROWS=256
DOC_MOST=512
DOCS=16


def key_range(block, seq_len):
    low = max(0, block * ROWS - DOC_MOST + 1) // ROWS * ROWS
    return low, min(seq_len, (block + 1) * ROWS)


def scores_turned(q, k, starts, low, first, scale):
    s = dot(k, q, 1, 1) * scale
    key_pos = low + lax.broadcasted_iota(jnp.int32, s.shape, 0)
    query_pos = first + lax.broadcasted_iota(jnp.int32, s.shape, 1)
    return jnp.where((key_pos >= starts) & (key_pos <= query_pos), s, -1e30)


def attend_head(h, starts_ref, q_ref, k_ref, v_ref, ctx_ref, lse_ref):
    seq_len = q_ref.shape[0]
    scale = HEAD_DIM ** -0.5
    lanes = pl.ds(pl.multiple_of(h * HEAD_DIM, HEAD_DIM), HEAD_DIM)
    for block in range(seq_len // ROWS):
        low, high = key_range(block, seq_len)
        here = pl.ds(block * ROWS, ROWS)
        keys_here = pl.ds(low, high - low)
        s = scores_turned(q_ref[here, lanes], k_ref[keys_here, lanes], starts_ref[:, here], low, block * ROWS, scale)
        top = jnp.max(s, axis=0, keepdims=True)
        raised = jnp.exp(s - top)
        total = jnp.sum(raised, axis=0, keepdims=True)
        low_probs = (raised * (1.0 / total)).astype(bf16)
        ctx_ref[here, lanes] = dot(low_probs, v_ref[keys_here, lanes], 0, 0).astype(bf16)
        lse_ref[h, :, here] = top + jnp.log(total)


def attend_head_back(h, starts_ref, q_ref, k_ref, v_ref, grad_ref, lse_ref, dq_ref, pair_ref, dk_ref, dv_ref):
    seq_len = q_ref.shape[0]
    scale = HEAD_DIM ** -0.5
    lanes = pl.ds(pl.multiple_of(h * HEAD_DIM, HEAD_DIM), HEAD_DIM)
    for block in range(seq_len // ROWS):
        low, high = key_range(block, seq_len)
        here = pl.ds(block * ROWS, ROWS)
        k = k_ref[low:high, lanes]
        v = v_ref[low:high, lanes]
        q = q_ref[here, lanes]
        grad = grad_ref[here, lanes]
        s = scores_turned(q, k, starts_ref[:, here], low, block * ROWS, scale)
        probs = jnp.exp(s - lse_ref[h, :, here])
        grad_probs = dot(v, grad, 1, 1)
        spread = jnp.sum(probs * grad_probs, axis=0, keepdims=True)
        grad_s = (probs * (grad_probs - spread)).astype(bf16)
        dq_ref[here, lanes] = (dot(grad_s, k, 0, 0) * scale).astype(bf16)
        dk = dot(grad_s, q, 1, 0) * scale
        dv = dot(probs.astype(bf16), grad, 1, 0)
        old = block * ROWS
        if block:
            n = old - low
            dk_ref[low:old, :] += dk[:n]
            dv_ref[low:old, :] += dv[:n]
            dk_ref[old:high, :] = dk[n:]
            dv_ref[old:high, :] = dv[n:]
        else:
            dk_ref[low:high, :] = dk
            dv_ref[low:high, :] = dv
    pair_ref[:, 0, lanes] = dk_ref[...]
    pair_ref[:, 1, lanes] = dv_ref[...]


def front_kernel(x, cot, gain_one_in, gain_two_in, wq, wo, wg, wu, wd, pairs, segments,
                 rows_out, cots, gate, up, down, out_out, queries, context_own, lse, residual, normed,
                 x_here, cot_here, gain_one, gain_two, keys, values, starts,
                 first, rows, query, out, context,
                 send_sems, recv_sems, local_sems):
    place = Place()
    dp, mp = place.dp, place.mp
    side = place.bit(SIDE)
    copies = Copies(place, send_sems, recv_sems, local_sems)
    half = wd.shape[0] // 2
    blk = wd.shape[1]
    share, width = first.shape
    zrow = wo.shape[0]
    local = wq.shape[1]
    chunk = share // 2
    mats = ((wg, gate), (wu, up), (wd, down))
    own, across = side, 1 - side
    DEEPER, OTHER = 2, 4
    locals_ = []

    def tile(whole, z, spot):
        return whole.at[pl.ds(z * half, half), pl.ds(spot * blk, blk)]

    def qrows(spot):
        return query.at[pl.ds(spot * blk, blk), :]

    def columns(spot):
        return out.at[:, pl.ds(spot * blk, blk)]

    def row_block(c, source_is_input):
        def get(m):
            target = rows.at[pl.ds(m * share + c * chunk, chunk), :]
            source = first.at[pl.ds(c * chunk, chunk), :] if source_is_input else target
            return source, target
        return get

    def out_block(source_is_input):
        def get(m):
            target = out.at[pl.ds(m * zrow, zrow), pl.ds(own * blk, blk)]
            return (wo if source_is_input else target), target
        return get

    store = {}

    def line(step, block_of, key):
        store[("r", key, step)] = copies.step(block_of, mp - (step - 1), mp - step, 1,
                                              (mp >= step - 1) & (mp < 3), mp >= step)
        store[("l", key, step)] = copies.step(block_of, mp + (step - 1), mp + step, -1,
                                              (mp <= 3 - (step - 1)) & (mp > 0), mp <= 3 - step)

    def arrive(key, step):
        copies.got(store[("r", key, step)])
        copies.got(store[("l", key, step)])

    own_piece = [weight.at[pl.ds(side * half, half), :] for weight, _ in mats]
    zhop = [[], [], []]
    yhop = [[], [], []]

    def send_z(i, source, spot):
        zhop[i].append(copies.swap(source, tile(mats[i][1], 1, spot), Z_HIGH))

    def send_y(i, source, z, spot):
        yhop[i].append((copies.swap(source, tile(mats[i][1], z, spot + DEEPER), DEEP), z, spot + DEEPER))

    def core_tile(i, z, spot, source=None):
        piece = tile(mats[i][1], z, spot)
        copies.swap(piece if source is None else source, tile(mats[i][1], z, spot + OTHER), CORE)

    def core_query(spot, source=None):
        return copies.swap(qrows(spot) if source is None else source, qrows(spot + OTHER), CORE)

    def core_out(spot):
        return copies.swap(columns(spot), columns(spot + OTHER), CORE)

    greet(place, (1, 2, 3, CORE, SIDE, DEEP))
    line(1, out_block(True), "o")
    xhop = [copies.swap(weight.at[pl.ds((1 - side) * half, half), :], tile(whole, 0, own), SIDE)
            for weight, whole in mats]
    wq_y = copies.swap(wq, qrows(own + DEEPER), DEEP)
    for i in range(3):
        send_y(i, own_piece[i], 0, own)
    wq_x = [copies.swap(wq, qrows(own), SIDE)]
    wq_core = [core_query(own, wq)]

    spots = [pl.ds(pl.multiple_of(absolute(place, s) * blk, blk), blk) for s in range(8)]
    for s in range(8):
        gain_one[:, s * blk:(s + 1) * blk] = gain_one_in[:, spots[s]]
        gain_two[:, s * blk:(s + 1) * blk] = gain_two_in[:, spots[s]]

    def norm_first(i, carry):
        here = pl.ds(i * 32, 32)
        for s in range(8):
            x_here[here, s * blk:(s + 1) * blk] = x[here, spots[s]]
            cot_here[here, s * blk:(s + 1) * blk] = cot[here, spots[s]]
        value = x_here[here, :].astype(f32)
        inverse = lax.rsqrt(jnp.mean(value * value, axis=-1, keepdims=True) + epsilon)
        first[here, :] = (value * inverse * gain_one[...]).astype(bf16)
        return carry

    lax.fori_loop(0, share // 32, norm_first, 0)
    for c in range(2):
        line(1, row_block(c, True), c)

    def split(i, carry):
        here = pl.ds(i * 32, 32)
        both = pairs[here, :, :]
        keys[here, :] = both[:, 0, :]
        values[here, :] = both[:, 1, :]
        return carry

    lax.fori_loop(0, pairs.shape[0] // 32, split, 0)
    ids = segments[...]
    begun = jnp.zeros_like(ids)
    for document in range(DOCS - 1):
        size = jnp.sum((ids == document).astype(jnp.int32), axis=1, keepdims=True)
        begun = begun + jnp.where(ids > document, size, 0)
    starts[...] = begun
    rows[pl.ds(mp * share, share), :] = first[...]
    query[pl.ds(own * blk, blk), :] = wq[...]
    out[pl.ds(mp * zrow, zrow), pl.ds(pl.multiple_of(own * blk, blk), blk)] = wo[...]
    locals_.append(copies.local(cot_here, cots.at[0:share, :]))
    for i in range(3):
        locals_.append(copies.local(own_piece[i], tile(mats[i][1], 0, own)))
        core_tile(i, 0, own, own_piece[i])
    copies.got(wq_y)
    wq_x.append(copies.swap(qrows(own + DEEPER), qrows(own + DEEPER), SIDE))
    wq_core.append(core_query(own + DEEPER))
    arrive("o", 1)
    line(2, out_block(False), "o")
    for i in range(3):
        copies.got(xhop[i])
        piece = tile(mats[i][1], 0, across)
        send_y(i, piece, 0, across)
        core_tile(i, 0, across)
    for c in range(2):
        arrive(c, 1)
        line(2, row_block(c, False), c)
    for i in range(3):
        send_z(i, own_piece[i], own)
    for item, spot in zip(wq_x, (across, across + DEEPER)):
        copies.got(item)
        wq_core.append(core_query(spot))
    cot_x = copies.swap(cot_here, cots.at[share:2 * share, :], SIDE)
    arrive("o", 2)
    line(3, out_block(False), "o")
    for c in range(2):
        arrive(c, 2)
        line(3, row_block(c, False), c)
    cot_z = copies.swap(cot_here, cots.at[2 * share:3 * share, :], Z_LOW)
    arrive("o", 3)
    out_y = copies.swap(columns(own), columns(own + DEEPER), DEEP)
    out_x = [copies.swap(columns(own), columns(own), SIDE)]
    out_core = [core_out(own)]

    def across_z(i):
        copies.got(zhop[i][0])
        send_y(i, tile(mats[i][1], 1, own), 1, own)
        core_tile(i, 1, own)

    across_z(0)
    for copy in locals_:
        copy.wait()
    for item in wq_core:
        copies.got(item)
    for c in range(2):
        arrive(c, 3)
    save_rows = copies.local(rows, rows_out)

    def project(m, carry):
        here = pl.ds(pl.multiple_of(m * share, share), share)
        queries[here, :] = dot(rows[here, :], query[...], 1, 0).astype(bf16)
        return carry

    lax.fori_loop(0, 4, project, 0)

    def one_head(h, carry):
        attend_head(h, starts, queries, keys, values, context, lse)
        return carry

    lax.fori_loop(0, local // HEAD_DIM, one_head, 0)
    tokens_in = []
    for mask in (2, 3, 1):
        other = place.partner(mask)[1]
        tokens_in.append(copies.swap(context.at[pl.ds(other * share, share), :],
                                     context_own.at[:, pl.ds(mp * local, local)], mask))
    context_own[:, pl.ds(pl.multiple_of(mp * local, local), local)] = context[pl.ds(mp * share, share), :]
    for i in range(3):
        send_z(i, tile(mats[i][1], 0, across), across)
    across_z(1)
    across_z(2)
    copies.got(out_y)
    out_x.append(copies.swap(columns(own + DEEPER), columns(own + DEEPER), SIDE))
    out_core.append(core_out(own + DEEPER))
    copies.got(out_x[0])
    out_core.append(core_out(across))
    copies.got(cot_z)
    copies.swap(cots.at[2 * share:3 * share, :], cots.at[3 * share:4 * share, :], SIDE)
    for j in range(2):
        for i in range(3):
            item, z, spot = yhop[i][j]
            copies.got(item)
            core_tile(i, z, spot)
    copies.got(out_x[1])
    out_core.append(core_out(across + DEEPER))
    for item in out_core + tokens_in:
        copies.got(item)
    save_out = copies.local(out, out_out)

    def project_out(n, carry):
        there = pl.ds(pl.multiple_of(n * 512, 512), 512)
        residual[:, there] = x_here[:, there].astype(f32) + dot(context_own[...], out[:, there], 1, 0)
        return carry

    lax.fori_loop(0, width // 512, project_out, 0)

    def norm_second(i, carry):
        here = pl.ds(i * 32, 32)
        value = residual[here, :]
        inverse = lax.rsqrt(jnp.mean(value * value, axis=-1, keepdims=True) + epsilon)
        normed[here, :] = (value * inverse * gain_two[...]).astype(bf16)
        return carry

    lax.fori_loop(0, share // 32, norm_second, 0)
    for i in range(3):
        copies.got(zhop[i][1])
        send_y(i, tile(mats[i][1], 1, across), 1, across)
        core_tile(i, 1, across)
    for j in (2, 3):
        for i in range(3):
            item, z, spot = yhop[i][j]
            copies.got(item)
            core_tile(i, z, spot)
    save_rows.wait()
    save_out.wait()
    copies.finish()


def front_call(x, cot, gain_one, gain_two, wq, wo, wg, wu, wd, pairs, segments, ident):
    share, width = x.shape
    hidden, blk = wd.shape
    seq_len, _, local = pairs.shape
    V = pltpu.VMEM
    S = jax.ShapeDtypeStruct
    return pl.pallas_call(
        front_kernel,
        out_shape=(
            S((seq_len, width), bf16), S((seq_len, width), bf16), S((hidden, width), bf16), S((hidden, width), bf16),
            S((hidden, width), bf16), S((width, width), bf16), S((seq_len, local), bf16), S((share, width), bf16),
            S((local // HEAD_DIM, 1, seq_len), f32), S((share, width), f32), S((share, width), bf16),
            S((share, width), bf16), S((share, width), bf16), S((1, width), f32), S((1, width), f32),
            S((seq_len, local), bf16), S((seq_len, local), bf16), S((1, seq_len), jnp.int32)),
        in_specs=[VM] * 11,
        out_specs=(ANY,) * 6 + (VM,) * 12,
        scratch_shapes=[
            V((share, width), bf16), V((seq_len, width), bf16), V((width, local), bf16), V((width, width), bf16),
            V((seq_len, local), bf16), DMA((96,)), DMA((96,)), DMA((8,))],
        compiler_params=params(ident, 60 << 20), name="front",
    )(x, cot, gain_one, gain_two, wq, wo, wg, wu, wd, pairs, segments)


def hidden_cuts(hidden):
    cuts = []
    start = 0
    while start < hidden:
        size = min(512, hidden - start)
        cuts.append((start, size))
        start += size
    return cuts


def ffn_kernel(normed, wq, cots_in, down_in, gate_in, up_in, total, query_0, query_y, fparts_out, sums_out,
               weights, tokens, acts, dparts, relay, landed, fparts,
               send_sems, recv_sems, local_sems, free_sem):
    place = Place()
    share, width = normed.shape
    hidden = down_in.shape[0]
    half = share // 2
    wide = width // 2
    cuts = hidden_cuts(hidden)
    copies = Copies(place, send_sems, recv_sems, local_sems)
    load_cots = copies.local(cots_in, tokens.at[0])
    load_w = [copies.local(w, weights.at[i]) for i, w in enumerate((down_in, gate_in, up_in))]
    mp = place.mp
    local = wq.shape[1]
    greet(place, (1, 2, 3, SIDE, CORE, DEEP))

    def at(quarter, part):
        return tokens.at[1, pl.ds(quarter * share + part * half, half), :]

    a, b = pl.ds(0, half), pl.ds(half, half)
    low_a = copies.swap(normed.at[a, :], at(2, 0), Z_LOW)
    side_b = copies.swap(normed.at[b, :], at(1, 1), SIDE)
    low_b = copies.swap(normed.at[b, :], at(2, 1), Z_LOW)
    side_a = copies.swap(normed.at[a, :], at(1, 0), SIDE)
    tokens[1, 0:share, :] = normed[...]

    def wide_block(source_is_input):
        def get(m):
            target = query_0.at[:, pl.ds(pl.multiple_of(m * local, local), local)]
            return (wq if source_is_input else target), target
        return get

    hops = []
    for hop in (1, 2, 3):
        block_of = wide_block(hop == 1)
        hops.append((
            copies.prepare_step(block_of, mp - (hop - 1), mp - hop, 1, (mp >= hop - 1) & (mp < 3), mp >= hop),
            copies.prepare_step(block_of, mp + (hop - 1), mp + hop, -1,
                                (mp <= 3 - (hop - 1)) & (mp > 0), mp <= 3 - hop)))
    over_deep = copies.prepare(query_0, query_y, DEEP)
    query_0[:, pl.ds(pl.multiple_of(mp * local, local), local)] = wq[...]
    for item in hops[0]:
        copies.start(item)

    def block(r):
        here = pl.ds(r * share, share)
        for start, size in cuts:
            rows = tokens[1, here, :]
            gate = dot(rows, weights[1, start:start + size, :], 1, 1)
            up = dot(rows, weights[2, start:start + size, :], 1, 1)
            grad = dot(tokens[0, here, :], weights[0, start:start + size, :], 1, 1)
            sigmoid = jax.nn.sigmoid(gate)
            silu = gate * sigmoid
            acts[0, here, start:start + size] = (silu * up).astype(bf16)
            acts[1, here, start:start + size] = (
                grad * up * sigmoid * (1.0 + gate * (1.0 - sigmoid))).astype(bf16)
            acts[2, here, start:start + size] = (grad * silu).astype(bf16)

        def columns(n, carry):
            there = pl.ds(pl.multiple_of(n * 512, 512), 512)
            dparts[here, there] = (dot(acts[1, here, :], weights[1, :, there], 1, 0)
                                   + dot(acts[2, here, :], weights[2, :, there], 1, 0)).astype(bf16)
            fparts[here, there] = dot(acts[0, here, :], weights[0, :, there], 1, 0).astype(bf16)
            return carry

        lax.fori_loop(0, width // 512, columns, 0)

    for copy in load_w:
        copy.wait()
    load_cots.wait()
    got = {"across": None}

    def step(r, carry):
        @pl.when(r == 1)
        def _():
            low_a["copy"].wait_recv()
            side_b["copy"].wait_recv()
            forward[0].start()
            forward[1].start()
            for item in hops[0]:
                copies.received(item)
            for item in hops[1]:
                copies.start(item)
            side_a["copy"].wait_recv()
            low_b["copy"].wait_recv()

        @pl.when(r == 2)
        def _():
            for item in hops[1]:
                copies.received(item)
            for item in hops[2]:
                copies.start(item)

            forward[0].wait_recv()
            forward[1].wait_recv()

        @pl.when(r == 3)
        def _():
            for item in hops[2]:
                copies.received(item)
            copies.start(over_deep)
            reduce.start_across()
        block(jnp.where(r < 2, r, 5 - r))
        return carry

    reduce = QuadReduce(copies, dparts, relay, landed)
    reduce.prepare()

    forward = [copies.describe(at(2, 0), at(3, 0), place.partner(SIDE), copies.count),
               copies.describe(at(1, 1), at(3, 1), place.partner(Z_LOW), copies.count + 1)]
    copies.count += 2
    lax.fori_loop(0, 4, step, 0)
    for item in (low_a, side_b, low_b, side_a):
        item["got"] = True
    pl.semaphore_signal(free_sem, inc=1, device_id=place.partner(CORE), device_id_type=MESH)
    reduce.start_rest()
    save = copies.local(fparts, fparts_out)

    base = copies.count
    copies.count += 3

    def give_copy(i):
        return copies.describe(weights.at[i, :, pl.ds(0, wide)], weights.at[i, :, pl.ds(wide, wide)],
                               place.partner(CORE), base + i)

    def give(i, carry):
        right = tokens[jnp.minimum(i, 1), :, wide:]
        for start, size in cuts:
            weights[i, start:start + size, 0:wide] = dot(
                acts[i, :, start:start + size], right, 0, 0).astype(bf16)

        @pl.when(i == 0)
        def _():
            pl.semaphore_wait(free_sem, 1)
        give_copy(i).start()
        return carry

    reduce.relayed()
    lax.fori_loop(0, 3, give, 0)

    def keep(i, carry):
        give_copy(i).wait_recv()
        right = tokens[jnp.minimum(i, 1), :, 0:wide]
        for start, size in cuts:
            rows = slice(start, start + size)
            weights[i, rows, wide:] = (dot(acts[i, :, rows], right, 0, 0)
                                       + weights[i, rows, wide:].astype(f32)).astype(bf16)
        pltpu.make_async_copy(weights.at[i, :, pl.ds(wide, wide)], sums_out.at[i], local_sems.at[5 + i]).start()
        return carry

    lax.fori_loop(0, 3, keep, 0)
    reduce.arrived()

    def one(i, carry):
        here = pl.ds(i * 32, 32)
        total[here, :] = (dparts[here, :].astype(f32) + landed[0, here, :].astype(f32)
                          + landed[1, here, :].astype(f32))
        return carry

    lax.fori_loop(0, share // 32, one, 0)
    for i in range(3):
        give_copy(i).wait_send()
        pltpu.make_async_copy(weights.at[i, :, pl.ds(wide, wide)], sums_out.at[i], local_sems.at[5 + i]).wait()
    for copy in forward:
        copy.wait_send()
    save.wait()
    copies.finish()


def ffn_call(normed, wq, cots, down, gate, up, ident):
    share, width = normed.shape
    hidden = down.shape[0]
    V = pltpu.VMEM
    flops = 2 * share * 4 * width * hidden * 9
    return pl.pallas_call(
        ffn_kernel,
        out_shape=(jax.ShapeDtypeStruct((share, width), f32), jax.ShapeDtypeStruct((share, width), bf16),
                   jax.ShapeDtypeStruct((share, width), bf16), jax.ShapeDtypeStruct((share * 4, width), bf16),
                   jax.ShapeDtypeStruct((3, hidden, width // 2), bf16)),
        in_specs=[VM] * 2 + [ANY] * 4,
        out_specs=(VM, VM, VM, ANY, ANY),
        scratch_shapes=[
            V((3, hidden, width), bf16), V((2, share * 4, width), bf16), V((3, share * 4, hidden), bf16),
            V((share * 4, width), bf16), V((2, share // 2, width), bf16), V((2, share, width), bf16),
            V((share * 4, width), bf16),
            DMA((24,)), DMA((24,)), DMA((8,)), pltpu.SemaphoreType.REGULAR],
        compiler_params=params(ident, 63 << 20),
        cost_estimate=pl.CostEstimate(flops=flops, bytes_accessed=40 << 20, transcendentals=share * 4 * hidden),
        name="feed_forward",
    )(normed, wq, cots, down, gate, up)


def back_first_kernel(dn2, residual, cot, gain, context, queries, keys, values, lse, starts, query_0, query_y,
                      out_whole, sums,
                      dres, gain_part, query_x, query_xy, grad_q, pairs, down_sums, gate_sums, out_sums,
                      heads, keep_d, deep_d, high_d, deep_g, grad_low, wout, dctx, give_o, core_o, dk, dv,
                      send_sems, recv_sems, local_sems):
    place = Place()
    mp = place.mp
    share, width = dn2.shape
    hidden = keep_d.shape[0]
    half = hidden // 2
    local = heads.shape[1]
    wide = width // 2
    quarter = wide // 2
    blk = quarter // 2
    copies = Copies(place, send_sems, recv_sems, local_sems)
    loads = [copies.local(out_whole.at[pl.ds(z * local, local), :], wout.at[z]) for z in range(4)]
    load_d = copies.local(sums.at[0, :, pl.ds(0, quarter)], keep_d)
    load_g = copies.local(sums.at[1, :, pl.ds(0, quarter)], gate_sums)
    greet(place, (1, 2, 3, CORE, SIDE, DEEP))
    in_d, in_g = ([copies.swap(sums.at[i, :, pl.ds(quarter + x * blk, blk)], target.at[:, pl.ds(x * blk, blk)], DEEP)
                   for x in (0, 1)] for i, target in ((0, deep_d), (1, deep_g)))
    copies.swap(query_0, query_x, SIDE)
    copies.swap(query_y, query_xy, SIDE)
    gain_part[...] = jnp.zeros_like(gain_part)

    def norm(i, carry):
        here = pl.ds(i * 32, 32)
        value = residual[here, :]
        inverse = lax.rsqrt(jnp.mean(value * value, axis=-1, keepdims=True) + epsilon)
        scaled = value * inverse
        grad = dn2[here, :]
        grad_scaled = grad * gain[...]
        back = inverse * (grad_scaled - scaled * jnp.mean(grad_scaled * scaled, axis=-1, keepdims=True))
        total = cot[here, :].astype(f32) + back
        dres[here, :] = total
        grad_low[here, :] = total.astype(bf16)
        gain_part[...] += jnp.sum(grad * scaled, axis=0, keepdims=True)
        return carry

    lax.fori_loop(0, share // 32, norm, 0)
    for copy in loads:
        copy.wait()
    heads_in = []
    for mask in (2, 3, 1, 0):
        other = place.partner(mask)[1]
        there = pl.ds(pl.multiple_of(other * local, local), local)
        piece = dot(grad_low[...], wout[other], 1, 1).astype(bf16)
        if mask:
            dctx[:, there] = piece
            heads_in.append(copies.swap(dctx.at[:, there], heads.at[pl.ds(mp * share, share), :], mask))
        else:
            heads[pl.ds(mp * share, share), :] = piece
    chunks = width // 512
    base = copies.count
    copies.count += chunks

    def core_copy(n):
        rows = pl.ds(pl.multiple_of(n * 512, 512), 512)
        return copies.describe(give_o.at[rows, :], core_o.at[rows, :], place.partner(CORE), base + n)

    def give(n, carry):
        rows = pl.ds(pl.multiple_of(n * 512, 512), 512)
        give_o[rows, :] = dot(context[:, rows], grad_low[:, wide:], 0, 0).astype(bf16)
        core_copy(n).start()
        return carry

    lax.fori_loop(0, chunks, give, 0)

    def keep(n, carry):
        rows = pl.ds(pl.multiple_of(n * 512, 512), 512)
        core_copy(n).wait_recv()
        out_sums[rows, :] = (dot(context[:, rows], grad_low[:, :wide], 0, 0)
                             + core_o[rows, :].astype(f32)).astype(bf16)
        return carry

    lax.fori_loop(0, chunks, keep, 0)
    load_d.wait()
    give_rows = pl.ds(half, half)
    across = []
    for x in (0, 1):
        there = pl.ds(x * blk, blk)
        copies.got(in_d[x])
        add_into(keep_d.at[:, there], (half, half), deep_d.at[give_rows, there], step=16)
        across.append(copies.swap(keep_d.at[give_rows, there], high_d.at[:, there], Z_HIGH))
        add_into(keep_d.at[:, there], (0, half), deep_d.at[:, there], step=16)
    for item in heads_in:
        copies.got(item)

    def one_head(h, carry):
        attend_head_back(h, starts, queries, keys, values, heads, lse, grad_q, pairs, dk, dv)
        return carry

    lax.fori_loop(0, local // HEAD_DIM, one_head, 0)
    load_g.wait()
    for x in (0, 1):
        copies.got(in_g[x])
    add_into(gate_sums, (0, hidden), deep_g)
    for x in (0, 1):
        copies.got(across[x])

    def add_d(n, carry):
        rows = pl.ds(n * 16, 16)
        down_sums[rows, :] = (keep_d[rows, :].astype(f32) + high_d[rows, :].astype(f32)).astype(bf16)
        return carry

    lax.fori_loop(0, half // 16, add_d, 0)
    copies.finish()

    def sent(n, carry):
        core_copy(n).wait_send()
        return carry

    lax.fori_loop(0, chunks, sent, 0)


def back_first(dn2, residual, cot, gain, context, queries, keys, values, lse, starts, query_0, query_y,
               out_whole, sums, ident):
    share, width = dn2.shape
    hidden = sums.shape[1]
    half = hidden // 2
    seq_len, local = queries.shape
    quarter = width // 4
    V = pltpu.VMEM
    S = jax.ShapeDtypeStruct
    return pl.pallas_call(
        back_first_kernel,
        out_shape=(S((share, width), f32), S((1, width), f32), S(query_0.shape, bf16), S(query_0.shape, bf16),
                   S((seq_len, local), bf16), S((seq_len, 2, local), f32),
                   S((half, quarter), bf16), S((hidden, quarter), bf16), S((width, width // 2), bf16)),
        in_specs=[VM] * 12 + [ANY, ANY],
        out_specs=(VM,) * 9,
        scratch_shapes=[
            V((seq_len, local), bf16), V((hidden, quarter), bf16), V((hidden, quarter), bf16), V((half, quarter), bf16),
            V((hidden, quarter), bf16), V((share, width), bf16),
            V((4, width // 4, width), bf16), V((share, width), bf16), V((width, width // 2), bf16),
            V((width, width // 2), bf16), V((seq_len, HEAD_DIM), f32), V((seq_len, HEAD_DIM), f32),
            DMA((20,)), DMA((20,)), DMA((6,))],
        compiler_params=params(ident, 63 << 20), name="back_first",
    )(dn2, residual, cot, gain, context, queries, keys, values, lse, starts, query_0, query_y, out_whole, sums)


def back_last_kernel(grad_q, dres, inputs, gain, query_0, query_y, query_x, query_xy, residual, gain_part,
                     rows_first, sums, down_sums, gate_sums, out_sums, fparts,
                     down, gate, up, out, query, grad_input, output, gains,
                     keep_d, keep_g, keep_u, deep_u, high_g, high_u, side_f,
                     own_o, deep_o, side_o, z_o,
                     give_q, own_q, core_q, side_q, deep_q, parts, relay, landed,
                     grad_own, rows, query_far, dn1, gain_rows, gains_got,
                     send_sems, recv_sems, local_sems):
    place = Place()
    mp = place.mp
    side = place.bit(SIDE)
    share, width = dres.shape
    hidden, blk = down.shape
    half = hidden // 2
    local = grad_q.shape[1]
    zrow = out.shape[0]
    quarter = 2 * blk
    wide = width // 2
    copies = Copies(place, send_sems, recv_sems, local_sems)
    load_rows = copies.local(rows_first, rows)
    load_g = copies.local(gate_sums, keep_g)
    load_d = copies.local(down_sums, keep_d)
    load_o = copies.local(out_sums, own_o)
    load_u = copies.local(sums.at[2, :, pl.ds(0, quarter)], keep_u)
    load_p = copies.local(fparts, parts)
    greet(place, (1, 2, 3, CORE, SIDE, DEEP))
    tokens_in = []
    for mask in (2, 3, 1):
        other = place.partner(mask)[1]
        tokens_in.append(copies.swap(grad_q.at[pl.ds(other * share, share), :],
                                     grad_own.at[:, pl.ds(mp * local, local)], mask))
    in_u = [copies.swap(sums.at[2, :, pl.ds(quarter + x * blk, blk)], deep_u.at[:, pl.ds(x * blk, blk)], DEEP)
            for x in (0, 1)]
    near = (query_0, query_y, query_x, query_xy)
    far_in = [copies.swap(piece, query_far.at[n], CORE) for n, piece in enumerate(near)]
    give_rows = pl.ds(half, half)
    mine = pl.ds(pl.multiple_of(side * blk, blk), blk)
    theirs = pl.ds(pl.multiple_of((1 - side) * blk, blk), blk)
    load_g.wait()
    high_in_g = [copies.swap(keep_g.at[give_rows, pl.ds(x * blk, blk)], high_g.at[:, pl.ds(x * blk, blk)], Z_HIGH)
                 for x in (0, 1)]
    load_d.wait()
    side_in = [copies.swap(keep_d.at[:, theirs], side_f.at[0], SIDE)]
    load_o.wait()

    def block_o(deep, column):
        return own_o.at[:, pl.ds(pl.multiple_of((2 * deep + column) * blk, blk), blk)]

    deep_in_o = {column: copies.swap(block_o(1, x), deep_o.at[n], DEEP)
                 for n, (column, x) in enumerate((("theirs", 1 - side), ("mine", side)))}
    grad_own[:, pl.ds(pl.multiple_of(mp * local, local), local)] = grad_q[pl.ds(mp * share, share), :]
    load_rows.wait()

    def product(first):
        return dot(rows[:, first:first + wide], grad_q[...], 0, 0)

    give_q[...] = product(wide).astype(bf16)
    core_in_q = copies.swap(give_q, core_q, CORE)
    load_p.wait()
    reduce = QuadReduce(copies, parts, relay, landed)
    reduce.start()
    keep_q = product(0)
    copies.got(core_in_q)
    own_q[...] = (keep_q + core_q[...].astype(f32)).astype(bf16)
    side_in_q = {y: copies.swap(own_q.at[pl.ds((2 * y + 1 - side) * blk, blk), :], side_q.at[y], SIDE) for y in (1, 0)}
    for item in far_in:
        copies.got(item)
    for item in tokens_in:
        copies.got(item)
    spot_of = (side, side + 2, 1 - side, 3 - side)
    for n in range(4):
        dn1[:, pl.ds(pl.multiple_of(spot_of[n] * blk, blk), blk)] = dot(grad_own[...], near[n][...], 1, 1)
        dn1[:, pl.ds(pl.multiple_of((spot_of[n] + 4) * blk, blk), blk)] = dot(grad_own[...], query_far[n], 1, 1)
    gain_rows[0:1, :] = jnp.zeros((1, width), f32)
    gain_rows[1:2, :] = gain_part[...]
    spots = [pl.ds(pl.multiple_of(absolute(place, s) * blk, blk), blk) for s in range(8)]

    def norm(i, carry):
        here = pl.ds(i * 32, 32)
        value = inputs[here, :].astype(f32)
        inverse = lax.rsqrt(jnp.mean(value * value, axis=-1, keepdims=True) + epsilon)
        scaled = value * inverse
        grad = dn1[here, :]
        grad_scaled = grad * gain[...]
        back = inverse * (grad_scaled - scaled * jnp.mean(grad_scaled * scaled, axis=-1, keepdims=True))
        total = dres[here, :] + back
        for s in range(8):
            grad_input[here, spots[s]] = total[:, s * blk:(s + 1) * blk]
        gain_rows[0:1, :] += jnp.sum(grad * scaled, axis=0, keepdims=True)
        return carry

    lax.fori_loop(0, share // 32, norm, 0)
    for s in range(8):
        gains[:, spots[s]] = gain_rows[:, s * blk:(s + 1) * blk]
    gain_masks = (1, 2, CORE, SIDE, DEEP)
    gain_state = {"item": None, "at": 0}

    def gain_hop():
        if gain_state["item"] is not None:
            item = gain_state["item"]
            copies.got(item)
            item["copy"].wait_send()
            item["sent"] = True
            gains[...] = gains[...] + gains_got[gain_state["at"] - 1]
            gain_state["item"] = None
        if gain_state["at"] < len(gain_masks):
            gain_state["item"] = copies.swap(gains, gains_got.at[gain_state["at"]], gain_masks[gain_state["at"]])
            gain_state["at"] += 1

    gain_hop()
    load_u.wait()
    high_in_u = []
    for x in (0, 1):
        there = pl.ds(x * blk, blk)
        copies.got(in_u[x])
        add_into(keep_u.at[:, there], (half, half), deep_u.at[give_rows, there], step=16)
        high_in_u.append(copies.swap(keep_u.at[give_rows, there], high_u.at[:, there], Z_HIGH))
        add_into(keep_u.at[:, there], (0, half), deep_u.at[:, there], step=16)
    reduce.relayed()
    gain_hop()

    def high_sum(keep, high, items, i):
        for x in (0, 1):
            copies.got(items[x])
        add_into(keep.at[:, theirs], (0, half), high.at[:, theirs], step=16)
        side_in.append(copies.swap(keep.at[pl.ds(0, half), theirs], side_f.at[i], SIDE))
        add_into(keep.at[:, mine], (0, half), high.at[:, mine], step=16)

    deep_in_q = None
    for y in (1, 0):
        copies.got(side_in_q[y])
        here = pl.ds(pl.multiple_of((2 * y + side) * blk, blk), blk)
        own_q[here, :] = (own_q[here, :].astype(f32) + side_q[y].astype(f32)).astype(bf16)
        if y:
            deep_in_q = copies.swap(own_q.at[here, :], deep_q, DEEP)
    copies.got(deep_in_o["theirs"])
    add_into(block_o(0, 1 - side), (0, width), deep_o.at[0])
    side_in_o = copies.swap(block_o(0, 1 - side), side_o, SIDE)
    gain_hop()
    high_sum(keep_g, high_g, high_in_g, 1)
    gain_hop()
    copies.got(deep_in_o["mine"])
    add_into(block_o(0, side), (0, width), deep_o.at[1])
    gain_hop()
    reduce.arrived()

    def finish_output(i, carry):
        here = pl.ds(i * 32, 32)
        total = (residual[here, :] + parts[here, :].astype(f32) + landed[0, here, :].astype(f32)
                 + landed[1, here, :].astype(f32)).astype(bf16)
        for s in range(8):
            output[here, spots[s]] = total[:, s * blk:(s + 1) * blk]
        return carry

    lax.fori_loop(0, share // 32, finish_output, 0)
    gain_hop()
    copies.got(side_in_o)
    add_into(block_o(0, side), (0, width), side_o)
    z_in = []
    for n, mask in enumerate((2, 3, 1)):
        other = place.partner(mask)[1]
        z_in.append(copies.swap(own_o.at[pl.ds(other * zrow, zrow), mine], z_o.at[n], mask))
    copies.got(deep_in_q)
    query[...] = own_q[pl.ds(pl.multiple_of(side * blk, blk), blk), :].astype(f32) + deep_q[...].astype(f32)
    high_sum(keep_u, high_u, high_in_u, 2)
    for item in z_in:
        copies.got(item)

    def add_z(i, carry):
        here = pl.ds(i * 32, 32)
        sum_ = own_o[pl.ds(mp * zrow + i * 32, 32), mine].astype(f32)
        for n in range(3):
            sum_ = sum_ + z_o[n, here, :].astype(f32)
        out[here, :] = sum_
        return carry

    lax.fori_loop(0, zrow // 32, add_z, 0)
    for i, (target, keep) in enumerate(((down, keep_d), (gate, keep_g), (up, keep_u))):
        copies.got(side_in[i])

        def write(n, carry, i=i, target=target, keep=keep):
            target[pl.ds(side * half + n * 16, 16), :] = keep[pl.ds(n * 16, 16), mine].astype(f32)
            target[pl.ds((1 - side) * half + n * 16, 16), :] = side_f[i, pl.ds(n * 16, 16), :].astype(f32)
            return carry

        lax.fori_loop(0, half // 16, write, 0)
    copies.finish()


def back_last(grad_q, dres, inputs, gain, query_0, query_y, query_x, query_xy, residual, gain_part,
              rows_first, sums, down_sums, gate_sums, out_sums, fparts, ident):
    share, width = dres.shape
    hidden = sums.shape[1]
    blk = width // 8
    half = hidden // 2
    local = grad_q.shape[1]
    V = pltpu.VMEM
    S = jax.ShapeDtypeStruct
    return pl.pallas_call(
        back_last_kernel,
        out_shape=(S((hidden, blk), f32),) * 3
        + (S((width // 4, blk), f32), S((blk, local), f32), S((share, width), f32), S((share, width), bf16),
           S((2, width), f32)),
        in_specs=[VM] * 10 + [ANY] * 6,
        out_specs=(VM,) * 8,
        scratch_shapes=[
            V((half, 2 * blk), bf16), V((hidden, 2 * blk), bf16), V((hidden, 2 * blk), bf16), V((hidden, 2 * blk), bf16),
            V((half, 2 * blk), bf16), V((half, 2 * blk), bf16), V((3, half, blk), bf16),
            V((width, width // 2), bf16), V((2, width, blk), bf16), V((width, blk), bf16),
            V((3, width // 4, blk), bf16),
            V((width // 2, local), bf16), V((width // 2, local), bf16), V((width // 2, local), bf16),
            V((2, blk, local), bf16), V((blk, local), bf16),
            V((share * 4, width), bf16), V((2, share // 2, width), bf16), V((2, share, width), bf16),
            V((share, width), bf16), V((share * 4, width), bf16), V((4, blk, width), bf16), V((share, width), f32),
            V((2, width), f32), V((5, 2, width), f32),
            DMA((48,)), DMA((48,)), DMA((12,))],
        compiler_params=params(ident, 63 << 20), name="back_last",
    )(grad_q, dres, inputs, gain, query_0, query_y, query_x, query_xy, residual, gain_part,
      rows_first, sums, down_sums, gate_sums, out_sums, fparts)


def contract(left, right, left_dim, right_dim):
    return lax.dot_general(
        left, right, (((left_dim,), (right_dim,)), ((), ())), preferred_element_type=jnp.float32
    )


def root_inverse(values):
    return lax.rsqrt(jnp.mean(values * values, axis=-1, keepdims=True) + epsilon)


def norm_back(grad_normed, scaled, inverse, gain):
    grad_scaled = grad_normed * gain
    grad_values = inverse * (
        grad_scaled - scaled * jnp.mean(grad_scaled * scaled, axis=-1, keepdims=True)
    )
    return (grad_values, jnp.sum(grad_normed * scaled, axis=0))


def plain_body(
    inputs,
    keys_values,
    segment_ids,
    gain_first,
    gain_second,
    w_query,
    w_out,
    w_gate,
    w_up,
    w_down,
    cotangent,
):
    query_full, out_full = (
        lax.all_gather(w_query, "dp", axis=0, tiled=True),
        lax.all_gather(w_out, "dp", axis=1, tiled=True),
    )
    gate_full, up_full, down_full = (
        lax.all_gather(w_gate, "dp", axis=0, tiled=True),
        lax.all_gather(w_up, "dp", axis=0, tiled=True),
        lax.all_gather(w_down, "dp", axis=1, tiled=True),
    )
    tokens = inputs.astype(jnp.float32)
    inverse_first = root_inverse(tokens)
    scaled_first = tokens * inverse_first
    normed_first = (scaled_first * gain_first).astype(jnp.bfloat16)
    rows_first = lax.all_gather(normed_first, "mp", axis=0, tiled=True)
    queries = contract(rows_first, query_full, 1, 0).astype(jnp.bfloat16)
    seq_len = rows_first.shape[0]
    local_width = queries.shape[1]
    head_count = local_width // HEAD_DIM
    block_rows = min(512, seq_len)
    block_count = seq_len // block_rows
    score_scale = HEAD_DIM ** (-0.5)
    key_heads = keys_values[:, 0, :].reshape(seq_len, head_count, HEAD_DIM)
    value_heads = keys_values[:, 1, :].reshape(seq_len, head_count, HEAD_DIM)
    segments = segment_ids[0]
    key_pos = jnp.arange(seq_len, dtype=jnp.int32)

    def block_scores(first_row):
        query_block = lax.dynamic_slice_in_dim(queries, first_row, block_rows, 0).reshape(
            block_rows, head_count, HEAD_DIM
        )
        scores = (
            jnp.einsum("qhd,khd->hqk", query_block, key_heads, preferred_element_type=jnp.float32)
            * score_scale
        )
        query_pos = first_row + jnp.arange(block_rows, dtype=jnp.int32)
        query_seg = lax.dynamic_slice_in_dim(segments, first_row, block_rows, 0)
        allowed = (query_pos[:, None] >= key_pos[None, :]) & (
            query_seg[:, None] == segments[None, :]
        )
        return (query_block, jnp.where(allowed[None], scores, -1e30))

    def forward_block(block_index):
        query_block, scores = block_scores(block_index * block_rows)
        row_max = jnp.max(scores, axis=-1, keepdims=True)
        raised = jnp.exp(scores - row_max)
        row_total = jnp.sum(raised, axis=-1, keepdims=True)
        weights_low = (raised / row_total).astype(jnp.bfloat16)
        blended = jnp.einsum(
            "hqk,khd->qhd", weights_low, value_heads, preferred_element_type=jnp.float32
        )
        return (
            blended.reshape(block_rows, local_width).astype(jnp.bfloat16),
            (row_max + jnp.log(row_total))[..., 0],
        )

    context_blocks, log_totals = lax.map(forward_block, jnp.arange(block_count, dtype=jnp.int32))
    context = context_blocks.reshape(seq_len, local_width)
    attn_part = lax.psum_scatter(
        contract(context, out_full, 1, 0), "mp", scatter_dimension=0, tiled=True
    )
    residual = tokens + attn_part
    inverse_second = root_inverse(residual)
    scaled_second = residual * inverse_second
    normed_second = (scaled_second * gain_second).astype(jnp.bfloat16)
    rows_second = lax.all_gather(normed_second, "mp", axis=0, tiled=True)
    gate_proj = contract(rows_second, gate_full, 1, 0)
    up_proj = contract(rows_second, up_full, 1, 0)
    sigmoid_gate = jax.nn.sigmoid(gate_proj)
    silu_gate = gate_proj * sigmoid_gate
    hidden = (silu_gate * up_proj).astype(jnp.bfloat16)
    ffn_part = lax.psum_scatter(
        contract(hidden, down_full, 1, 0).astype(jnp.bfloat16),
        "mp",
        scatter_dimension=0,
        tiled=True,
    ).astype(jnp.float32)
    output = (residual + ffn_part).astype(jnp.bfloat16)
    cot_rows = lax.all_gather(cotangent, "mp", axis=0, tiled=True)
    grad_down_w = contract(hidden, cot_rows, 0, 0)
    grad_hidden = contract(cot_rows, down_full, 1, 1)
    grad_gate_act = (
        grad_hidden * up_proj * sigmoid_gate * (1.0 + gate_proj * (1.0 - sigmoid_gate))
    ).astype(jnp.bfloat16)
    grad_up_act = (grad_hidden * silu_gate).astype(jnp.bfloat16)
    grad_gate_w = contract(rows_second, grad_gate_act, 0, 0)
    grad_up_w = contract(rows_second, grad_up_act, 0, 0)
    grad_normed_second = lax.psum_scatter(
        contract(grad_gate_act, gate_full, 1, 1) + contract(grad_up_act, up_full, 1, 1),
        "mp",
        scatter_dimension=0,
        tiled=True,
    )
    grad_from_norm, gain_second_part = norm_back(
        grad_normed_second, scaled_second, inverse_second, gain_second
    )
    grad_residual = cotangent.astype(jnp.float32) + grad_from_norm
    attn_cot = lax.all_gather(grad_residual.astype(jnp.bfloat16), "mp", axis=0, tiled=True)
    grad_out_w = contract(context, attn_cot, 0, 0)
    grad_context = contract(attn_cot, out_full, 1, 1).astype(jnp.bfloat16)

    def backward_block(state_pair, block_index):
        grad_keys, grad_values = state_pair
        first_row = block_index * block_rows
        query_block, scores = block_scores(first_row)
        log_total = lax.dynamic_index_in_dim(log_totals, block_index, 0, keepdims=False)
        weights = jnp.exp(scores - log_total[..., None])
        grad_block = lax.dynamic_slice_in_dim(grad_context, first_row, block_rows, 0).reshape(
            block_rows, head_count, HEAD_DIM
        )
        grad_weights = jnp.einsum(
            "qhd,khd->hqk", grad_block, value_heads, preferred_element_type=jnp.float32
        )
        spread = jnp.sum(weights * grad_weights, axis=-1, keepdims=True)
        grad_scores = (weights * (grad_weights - spread)).astype(jnp.bfloat16)
        grad_query_block = (
            jnp.einsum("hqk,khd->qhd", grad_scores, key_heads, preferred_element_type=jnp.float32)
            * score_scale
        ).astype(jnp.bfloat16)
        grad_keys = (
            grad_keys
            + jnp.einsum(
                "hqk,qhd->khd", grad_scores, query_block, preferred_element_type=jnp.float32
            )
            * score_scale
        )
        grad_values = grad_values + jnp.einsum(
            "hqk,qhd->khd",
            weights.astype(jnp.bfloat16),
            grad_block,
            preferred_element_type=jnp.float32,
        )
        return ((grad_keys, grad_values), grad_query_block.reshape(block_rows, local_width))

    zero_state = jnp.zeros((seq_len, head_count, HEAD_DIM), jnp.float32)
    (grad_keys, grad_values), grad_query_blocks = lax.scan(
        backward_block, (zero_state, zero_state), jnp.arange(block_count, dtype=jnp.int32)
    )
    grad_queries = grad_query_blocks.reshape(seq_len, local_width)
    grad_kv = jnp.stack(
        [grad_keys.reshape(seq_len, local_width), grad_values.reshape(seq_len, local_width)], axis=1
    )
    grad_query_w = contract(rows_first, grad_queries, 0, 0)
    grad_normed_first = lax.psum_scatter(
        contract(grad_queries, query_full, 1, 1).astype(jnp.bfloat16),
        "mp",
        scatter_dimension=0,
        tiled=True,
    ).astype(jnp.float32)
    grad_from_first, gain_first_part = norm_back(
        grad_normed_first, scaled_first, inverse_first, gain_first
    )
    grad_input = grad_residual + grad_from_first
    gain_first_sum, gain_second_sum = lax.psum((gain_first_part, gain_second_part), ("dp", "mp"))
    query_shard, out_shard, gate_shard, up_shard, down_shard = (
        lax.psum_scatter(
            grad_query_w.astype(jnp.bfloat16), "dp", scatter_dimension=0, tiled=True
        ).astype(jnp.float32),
        lax.psum_scatter(
            grad_out_w.astype(jnp.bfloat16), "dp", scatter_dimension=1, tiled=True
        ).astype(jnp.float32),
        lax.psum_scatter(
            grad_gate_w.astype(jnp.bfloat16), "dp", scatter_dimension=0, tiled=True
        ).astype(jnp.float32),
        lax.psum_scatter(
            grad_up_w.astype(jnp.bfloat16), "dp", scatter_dimension=0, tiled=True
        ).astype(jnp.float32),
        lax.psum_scatter(
            grad_down_w.astype(jnp.bfloat16), "dp", scatter_dimension=1, tiled=True
        ).astype(jnp.float32),
    )
    return (
        output,
        grad_input,
        grad_kv,
        gain_first_sum,
        gain_second_sum,
        query_shard,
        out_shard,
        gate_shard,
        up_shard,
        down_shard,
    )


def fast_body(inputs, keys_values, segment_ids, gain_first, gain_second, w_query, w_out, w_gate,
              w_up, w_down, cotangent):
    (rows_first, cots, gate_here, up_here, down_here, out_whole, queries, context_own, log_totals, residual,
     normed_second, inputs_here, cot_here, gain_one, gain_two, keys, values, starts) = front_call(
        inputs, cotangent, gain_first[None], gain_second[None], w_query, w_out, w_gate.T, w_up.T, w_down,
        keys_values, segment_ids, 1)
    grad_normed_second, query_0, query_y, ffn_parts, ffn_sums = ffn_call(
        normed_second, w_query, cots, down_here, gate_here, up_here, 3)
    (grad_residual, gain_second_part, query_x, query_xy, grad_queries, grad_kv, down_sums, gate_sums,
     out_sums) = back_first(
        grad_normed_second, residual, cot_here, gain_two, context_own, queries, keys, values, log_totals, starts,
        query_0, query_y, out_whole, ffn_sums, 5)
    down_shard, gate_shard, up_shard, out_shard, query_shard, grad_input, output, gains = back_last(
        grad_queries, grad_residual, inputs_here, gain_one, query_0, query_y, query_x, query_xy, residual,
        gain_second_part, rows_first, ffn_sums, down_sums, gate_sums, out_sums, ffn_parts, 6)
    return (output, grad_input, grad_kv, gains[0], gains[1], query_shard, out_shard,
            gate_shard.T, up_shard.T, down_shard)


def solution(mesh):
    in_specs = (
        P(("dp", "mp"), None),
        P("dp", None, "mp"),
        P("dp", None),
        P(),
        P(),
        P("dp", "mp"),
        P("mp", "dp"),
        P("dp", "mp"),
        P("dp", "mp"),
        P("mp", "dp"),
        P(("dp", "mp"), None),
    )
    out_specs = (
        P(("dp", "mp"), None),
        P(("dp", "mp"), None),
        P("dp", None, "mp"),
        P(),
        P(),
        P("dp", "mp"),
        P("mp", "dp"),
        P("dp", "mp"),
        P("dp", "mp"),
        P("mp", "dp"),
    )
    fast = mesh.shape["dp"] == 8 and mesh.shape["mp"] == 4
    body = fast_body if fast else plain_body
    return jax.shard_map(body, mesh=mesh, in_specs=in_specs, out_specs=out_specs, check_vma=False)
```

```python
import jax
import jax.numpy as jnp
from jax import lax
from jax.experimental import pallas as pl
from jax.experimental.pallas import tpu as pltpu
from jax.sharding import PartitionSpec as P

f32 = jnp.float32
bf16 = jnp.bfloat16
HEAD_DIM = 128
MP = 4
epsilon = 1e-06


MESH = pl.DeviceIdType.MESH
Z_LOW, Z_HIGH, CORE, SIDE, DEEP = 1, 2, 4, 8, 16
ANY = pl.BlockSpec(memory_space=pl.ANY)
VM = pl.BlockSpec(memory_space=pltpu.VMEM)


class Place:
    def __init__(self):
        self.dp = lax.axis_index("dp")
        self.mp = lax.axis_index("mp")

    def bit(self, mask):
        return ((self.dp * 4 + self.mp) // mask) % 2

    def partner(self, mask):
        flip_dp, flip_mp = mask // 4, mask % 4
        return (self.flip(self.dp, flip_dp), self.flip(self.mp, flip_mp))

    def flip(self, value, flips):
        for mask in (1, 2, 4):
            if flips & mask:
                value = value + mask - 2 * mask * ((value // mask) % 2)
        return value


class Copies:
    def __init__(self, place, send_sems, recv_sems, local_sems=None):
        self.place, self.send_sems, self.recv_sems = place, send_sems, recv_sems
        self.local_sems = local_sems
        self.count = 0
        self.local_count = 0
        self.pending = []

    def describe(self, source, target, device, slot):
        return pltpu.make_async_remote_copy(
            src_ref=source, dst_ref=target, send_sem=self.send_sems.at[slot],
            recv_sem=self.recv_sems.at[slot], device_id=device, device_id_type=MESH)

    def swap(self, source, target, mask):
        slot = self.count
        self.count += 1
        copy = self.describe(source, target, self.place.partner(mask), slot)
        copy.start()
        item = {"copy": copy, "got": False}
        self.pending.append(item)
        return item

    def got(self, item):
        if not item["got"]:
            item["got"] = True
            if "get_if" in item:
                @pl.when(item["get_if"])
                def _():
                    item["get"].wait_recv()
            else:
                item["copy"].wait_recv()

    def prepare(self, source, target, mask):
        slot = self.count
        self.count += 1
        item = {"copy": self.describe(source, target, self.place.partner(mask), slot), "got": False}
        self.pending.append(item)
        return item

    def prepare_step(self, block, mp_send, mp_get, direction, send_if, get_if):
        slot = self.count
        self.count += 1
        place = self.place
        device = (place.dp, jnp.clip(place.mp + direction, 0, 3))
        copy = self.describe(*block(jnp.clip(mp_send, 0, 3)), device, slot)
        get = self.describe(*block(jnp.clip(mp_get, 0, 3)), device, slot)
        item = {"copy": copy, "got": False, "send_if": send_if, "get_if": get_if, "get": get}
        self.pending.append(item)
        return item

    def prepare_jump(self, source, target, landing, distance, send_if, get_if):
        slot = self.count
        self.count += 1
        place = self.place
        device = (place.dp, jnp.clip(place.mp + distance, 0, 3))
        item = {"copy": self.describe(source, target, device, slot), "got": False, "send_if": send_if,
                "get_if": get_if, "get": self.describe(source, landing, device, slot)}
        self.pending.append(item)
        return item

    def start(self, item):
        if "send_if" in item:
            @pl.when(item["send_if"])
            def _():
                item["copy"].start()
        else:
            item["copy"].start()

    def step(self, *arguments):
        item = self.prepare_step(*arguments)
        self.start(item)
        return item

    def received(self, item):
        if item["got"]:
            return
        item["got"] = True
        if "get_if" in item:
            @pl.when(item["get_if"])
            def _():
                item["get"].wait_recv()
        else:
            item["copy"].wait_recv()

    def local(self, source, target):
        copy = pltpu.make_async_copy(source, target, self.local_sems.at[self.local_count])
        self.local_count += 1
        copy.start()
        return copy

    def finish(self):
        for item in self.pending:
            self.got(item)
        for item in self.pending:
            if "send_if" in item:
                @pl.when(item["send_if"])
                def _():
                    item["copy"].wait_send()
            elif "sent" not in item:
                item["copy"].wait_send()


def greet(place, masks):
    barrier = pltpu.get_barrier_semaphore()
    for mask in masks:
        pl.semaphore_signal(barrier, inc=1, device_id=place.partner(mask), device_id_type=MESH)
    pl.semaphore_wait(barrier, len(masks))


def absolute(place, spot):
    core, deep, side = spot // 4, (spot // 2) % 2, spot % 2
    return place.flip(place.dp, core + 4 * deep) - 2 * place.bit(SIDE) + 2 * side


DMA = pltpu.SemaphoreType.DMA


def dot(left, right, left_dim, right_dim):
    return lax.dot_general(
        left, right, (((left_dim,), (right_dim,)), ((), ())), preferred_element_type=f32)


def params(ident, vmem=32 << 20):
    return pltpu.CompilerParams(collective_id=ident, has_side_effects=True, vmem_limit_bytes=vmem)


def add_into(target, rows, *others, step=32):
    start, count = rows
    pieces = count // step

    def one(i, carry):
        total = target[pl.ds(start + i * step, step), :].astype(f32)
        for other in others:
            total = total + other[pl.ds(i * step, step), :].astype(f32)
        target[pl.ds(start + i * step, step), :] = total.astype(target.dtype)
        return carry

    lax.fori_loop(0, pieces, one, 0)


class QuadReduce:
    def __init__(self, copies, parts, relay, landed):
        self.copies, self.parts, self.relay, self.landed = copies, parts, relay, landed
        self.share = parts.shape[0] // 4
        self.half = self.share // 2

    def prepare(self):
        share, half = self.share, self.half
        prepare, parts, landed = self.copies.prepare, self.parts, self.landed
        self.first = prepare(parts.at[pl.ds(3 * share, half), :], self.relay.at[0], SIDE)
        self.second = prepare(parts.at[pl.ds(3 * share + half, half), :], self.relay.at[1], Z_LOW)
        self.side = [prepare(parts.at[pl.ds(share, half), :], landed.at[0, pl.ds(0, half), :], SIDE),
                     prepare(parts.at[pl.ds(share + half, half), :], landed.at[0, pl.ds(half, half), :], SIDE)]
        self.low = [prepare(parts.at[pl.ds(2 * share + half, half), :], landed.at[1, pl.ds(half, half), :], Z_LOW),
                    prepare(parts.at[pl.ds(2 * share, half), :], landed.at[1, pl.ds(0, half), :], Z_LOW)]

    def start_across(self):
        self.copies.start(self.first)
        self.copies.start(self.second)
        self.copies.start(self.side[0])

    def start_rest(self):
        self.copies.start(self.low[0])

    def start(self):
        self.prepare()
        self.start_across()
        self.start_rest()

    def relayed_low(self):
        self.copies.received(self.first)
        add_into(self.parts, (2 * self.share, self.half), self.relay.at[0])
        self.copies.start(self.low[1])

    def relayed_side(self):
        self.copies.received(self.second)
        add_into(self.parts, (self.share + self.half, self.half), self.relay.at[1])
        self.copies.start(self.side[1])

    def relayed(self):
        self.relayed_low()
        self.relayed_side()

    def arrived(self):
        for item in self.side + self.low:
            self.copies.got(item)


ROWS=256
DOC_MOST=512
DOCS=16


def key_range(block, seq_len):
    low = max(0, block * ROWS - DOC_MOST + 1) // ROWS * ROWS
    return low, min(seq_len, (block + 1) * ROWS)


def scores_turned(q, k, starts, low, first, scale):
    s = dot(k, q, 1, 1) * scale
    key_pos = low + lax.broadcasted_iota(jnp.int32, s.shape, 0)
    query_pos = first + lax.broadcasted_iota(jnp.int32, s.shape, 1)
    return jnp.where((key_pos >= starts) & (key_pos <= query_pos), s, -1e30)


def attend_block(h, block, starts_ref, q_ref, k_ref, v_ref, ctx_ref, lse_ref):
    seq_len = q_ref.shape[0]
    scale = HEAD_DIM ** -0.5
    window = min(seq_len, DOC_MOST + ROWS)
    lanes = pl.ds(pl.multiple_of(h * HEAD_DIM, HEAD_DIM), HEAD_DIM)
    first = pl.multiple_of(block * ROWS, ROWS)
    low = pl.multiple_of(jnp.clip(first - DOC_MOST, 0, seq_len - window), ROWS)
    here = pl.ds(first, ROWS)
    keys_here = pl.ds(low, window)
    s = scores_turned(q_ref[here, lanes], k_ref[keys_here, lanes], starts_ref[:, here], low, first, scale)
    top = jnp.max(s, axis=0, keepdims=True)
    raised = jnp.exp(s - top)
    total = jnp.sum(raised, axis=0, keepdims=True)
    low_probs = (raised * (1.0 / total)).astype(bf16)
    ctx_ref[here, lanes] = dot(low_probs, v_ref[keys_here, lanes], 0, 0).astype(bf16)
    lse_ref[h, :, here] = top + jnp.log(total)


def attend_head_back(h, starts_ref, q_ref, k_ref, v_ref, grad_ref, lse_ref, dq_ref, pair_ref, dk_ref, dv_ref):
    seq_len = q_ref.shape[0]
    scale = HEAD_DIM ** -0.5
    lanes = pl.ds(pl.multiple_of(h * HEAD_DIM, HEAD_DIM), HEAD_DIM)
    for block in range(seq_len // ROWS):
        low, high = key_range(block, seq_len)
        here = pl.ds(block * ROWS, ROWS)
        k = k_ref[low:high, lanes]
        v = v_ref[low:high, lanes]
        q = q_ref[here, lanes]
        grad = grad_ref[here, lanes]
        s = scores_turned(q, k, starts_ref[:, here], low, block * ROWS, scale)
        probs = jnp.exp(s - lse_ref[h, :, here])
        grad_probs = dot(v, grad, 1, 1)
        spread = jnp.sum(probs * grad_probs, axis=0, keepdims=True)
        grad_s = (probs * (grad_probs - spread)).astype(bf16)
        dq_ref[here, lanes] = (dot(grad_s, k, 0, 0) * scale).astype(bf16)
        dk = dot(grad_s, q, 1, 0) * scale
        dv = dot(probs.astype(bf16), grad, 1, 0)
        old = block * ROWS
        if block:
            n = old - low
            dk_ref[low:old, :] += dk[:n]
            dv_ref[low:old, :] += dv[:n]
            dk_ref[old:high, :] = dk[n:]
            dv_ref[old:high, :] = dv[n:]
        else:
            dk_ref[low:high, :] = dk
            dv_ref[low:high, :] = dv
    pair_ref[:, 0, lanes] = dk_ref[...]
    pair_ref[:, 1, lanes] = dv_ref[...]


FRONT_ORDER = (
    2, 21, 48, 18, 0, 1, 8, 11, 57, 35, 5, 3, 13, 33, 4, 20, 19, 17, 28, 27, 42, 26, 66, 9, 36, 64, 12, 24,
    15, 6, 68, 67, 10, 34, 63, 29, 44, 23, 30, 14, 16, 73, 22, 50, 41, 37, 49, 54, 25, 46, 39, 65, 31, 56,
    53, 75, 59, 7, 43, 55, 52, 38, 40, 70, 72, 45, 69, 51, 74, 60, 61, 71, 58, 76, 32, 62, 47, 77,
)


def front_kernel(x, cot, gain_one_in, gain_two_in, wq, wo, wg, wu, wd, pairs, segments,
                 rows_out, cots, gate, up, down, out_out, queries, context_own, lse, residual, normed,
                 x_here, cot_here, gain_one, gain_two, keys, values, starts,
                 first, rows, query, out, context,
                 send_sems, recv_sems, local_sems):
    place = Place()
    dp, mp = place.dp, place.mp
    side = place.bit(SIDE)
    copies = Copies(place, send_sems, recv_sems, local_sems)
    half = wd.shape[0] // 2
    blk = wd.shape[1]
    share, width = first.shape
    zrow = wo.shape[0]
    local = wq.shape[1]
    chunk = share // 2
    mats = ((wg, gate), (wu, up), (wd, down))
    own, across = side, 1 - side
    DEEPER, OTHER = 2, 4
    locals_ = []

    def tile(whole, z, spot):
        return whole.at[pl.ds(z * half, half), pl.ds(spot * blk, blk)]

    def qrows(spot):
        return query.at[pl.ds(spot * blk, blk), :]

    def columns(spot):
        return out.at[:, pl.ds(spot * blk, blk)]

    def row_block(c, source_is_input):
        def get(m):
            target = rows.at[pl.ds(m * share + c * chunk, chunk), :]
            source = first.at[pl.ds(c * chunk, chunk), :] if source_is_input else target
            return source, target
        return get

    def out_block(source_is_input):
        def get(m):
            target = out.at[pl.ds(m * zrow, zrow), pl.ds(own * blk, blk)]
            return (wo if source_is_input else target), target
        return get

    items = {}

    def note(name, *copied):
        items[name] = list(copied)

    def line(step, block_of, name):
        note(name,
             copies.step(block_of, mp - (step - 1), mp - step, 1, (mp >= step - 1) & (mp < 3), mp >= step),
             copies.step(block_of, mp + (step - 1), mp + step, -1, (mp <= 3 - (step - 1)) & (mp > 0), mp <= 3 - step))

    own_piece = [weight.at[pl.ds(side * half, half), :] for weight, _ in mats]
    spots = [pl.ds(pl.multiple_of(absolute(place, s) * blk, blk), blk) for s in range(8)]
    inside = lambda m: (m >= 0) & (m <= 3)

    def context_jump(distance):
        source = context.at[pl.ds(jnp.clip(mp + distance, 0, 3) * share, share), :]

        def landing(m):
            return context_own.at[:, pl.ds(pl.multiple_of(jnp.clip(m, 0, 3) * local, local), local)]

        return copies.prepare_jump(source, landing(mp), landing(mp - distance), distance,
                                   inside(mp + distance), inside(mp - distance))

    jumps = {distance: context_jump(distance) for distance in (1, -1, 2, -2, 3, -3)}

    def attend_tokens(m):
        here = pl.ds(pl.multiple_of(m * share, share), share)
        queries[here, :] = dot(rows[here, :], query[...], 1, 0).astype(bf16)

        def one_head(h, carry):
            attend_block(h, m, starts, queries, keys, values, context, lse)
            return carry

        lax.fori_loop(0, local // HEAD_DIM, one_head, 0)

    def attend_from(distance):
        for away in (distance, -distance):
            @pl.when(inside(mp + away))
            def _(away=away):
                attend_tokens(mp + away)
                jumps[away]["copy"].start()
        note("A%d" % distance, jumps[distance], jumps[-distance])

    def norm_rows():
        for s in range(8):
            gain_one[:, s * blk:(s + 1) * blk] = gain_one_in[:, spots[s]]
            gain_two[:, s * blk:(s + 1) * blk] = gain_two_in[:, spots[s]]

        def norm_first(i, carry):
            here = pl.ds(i * 32, 32)
            for s in range(8):
                x_here[here, s * blk:(s + 1) * blk] = x[here, spots[s]]
                cot_here[here, s * blk:(s + 1) * blk] = cot[here, spots[s]]
            value = x_here[here, :].astype(f32)
            inverse = lax.rsqrt(jnp.mean(value * value, axis=-1, keepdims=True) + epsilon)
            first[here, :] = (value * inverse * gain_one[...]).astype(bf16)
            return carry

        lax.fori_loop(0, share // 32, norm_first, 0)
        rows[pl.ds(mp * share, share), :] = first[...]

    def split_pairs():
        def split(i, carry):
            here = pl.ds(i * 32, 32)
            both = pairs[here, :, :]
            keys[here, :] = both[:, 0, :]
            values[here, :] = both[:, 1, :]
            return carry

        lax.fori_loop(0, pairs.shape[0] // 32, split, 0)
        ids = segments[...]
        begun = jnp.zeros_like(ids)
        for document in range(DOCS - 1):
            size = jnp.sum((ids == document).astype(jnp.int32), axis=1, keepdims=True)
            begun = begun + jnp.where(ids > document, size, 0)
        starts[...] = begun
        query[pl.ds(own * blk, blk), :] = wq[...]
        out[pl.ds(mp * zrow, zrow), pl.ds(pl.multiple_of(own * blk, blk), blk)] = wo[...]
        locals_.append(copies.local(cot_here, cots.at[0:share, :]))
        for i in range(3):
            locals_.append(copies.local(own_piece[i], tile(mats[i][1], 0, own)))

    def send(name, source, target, mask):
        note(name, copies.swap(source, target, mask))

    tasks = {}

    def task(name, needs, action, *arguments):
        tasks[name] = (needs, lambda: action(*arguments))

    def copy(name, needs, source, target, mask):
        task(name, needs, send, name, source, target, mask)

    task("N", (), norm_rows)
    task("S", ("N",), split_pairs)
    task("o1", (), line, 1, out_block(True), "o1")
    task("o2", ("o1",), line, 2, out_block(False), "o2")
    task("o3", ("o2", "S"), line, 3, out_block(False), "o3")
    for c in range(2):
        task("n1%d" % c, ("N",), line, 1, row_block(c, True), "n1%d" % c)
        task("n2%d" % c, ("n1%d" % c,), line, 2, row_block(c, False), "n2%d" % c)
        task("n3%d" % c, ("n2%d" % c,), line, 3, row_block(c, False), "n3%d" % c)
    copy("qy", (), wq, qrows(own + DEEPER), DEEP)
    copy("qx", (), wq, qrows(own), SIDE)
    copy("qyx", ("qy",), qrows(own + DEEPER), qrows(own + DEEPER), SIDE)
    copy("q", (), wq, qrows(own + OTHER), CORE)
    for name, spot in (("qy", own + DEEPER), ("qx", across), ("qyx", across + DEEPER)):
        copy(name + "C", (name,), qrows(spot), qrows(spot + OTHER), CORE)
    for i, (weight, whole) in enumerate(mats):
        n = "%d" % i
        copy("x" + n, (), weight.at[pl.ds((1 - side) * half, half), :], tile(whole, 0, own), SIDE)
        for kind, needs, source, z, spot in (
                ("O", (), own_piece[i], 0, own), ("X", ("x" + n,), tile(whole, 0, across), 0, across)):
            copy("z" + kind + n, needs, source, tile(whole, 1, spot), Z_HIGH)
            for far, far_needs, far_source, row in (("", needs, source, 0), ("z", ("z" + kind + n,), tile(whole, 1, spot), 1)):
                name = far + kind + n
                copy("y" + name, far_needs, far_source, tile(whole, row, spot + DEEPER), DEEP)
                copy("c" + name, far_needs, far_source, tile(whole, row, spot + OTHER), CORE)
                copy("yc" + name, ("y" + name,), tile(whole, row, spot + DEEPER), tile(whole, row, spot + DEEPER + OTHER), CORE)
    copy("cx", ("N",), cot_here, cots.at[share:2 * share, :], SIDE)
    copy("cz", ("N",), cot_here, cots.at[2 * share:3 * share, :], Z_LOW)
    copy("czx", ("cz",), cots.at[2 * share:3 * share, :], cots.at[3 * share:4 * share, :], SIDE)
    copy("oy", ("o3",), columns(own), columns(own + DEEPER), DEEP)
    copy("ox", ("o3",), columns(own), columns(own), SIDE)
    copy("oyx", ("oy",), columns(own + DEEPER), columns(own + DEEPER), SIDE)
    for name, needs, spot in (("o", "o3", own), ("oy", "oy", own + DEEPER), ("ox", "ox", across), ("oyx", "oyx", across + DEEPER)):
        copy(name + "C", (needs,), columns(spot), columns(spot + OTHER), CORE)
    whole_query = ("q", "qyC", "qxC", "qyxC", "S")
    task("A0", whole_query, attend_tokens, mp)
    for distance in (1, 2, 3):
        task("A%d" % distance, ("A0", "n%d0" % distance, "n%d1" % distance), attend_from, distance)

    def finish_tokens():
        context_own[:, pl.ds(pl.multiple_of(mp * local, local), local)] = context[pl.ds(mp * share, share), :]
        locals_.append(copies.local(rows, rows_out))
        locals_.append(copies.local(out, out_out))

        def project_out(n, carry):
            there = pl.ds(pl.multiple_of(n * 512, 512), 512)
            residual[:, there] = x_here[:, there].astype(f32) + dot(context_own[...], out[:, there], 1, 0)
            return carry

        lax.fori_loop(0, width // 512, project_out, 0)

        def norm_second(i, carry):
            here = pl.ds(i * 32, 32)
            value = residual[here, :]
            inverse = lax.rsqrt(jnp.mean(value * value, axis=-1, keepdims=True) + epsilon)
            normed[here, :] = (value * inverse * gain_two[...]).astype(bf16)
            return carry

        lax.fori_loop(0, share // 32, norm_second, 0)

    task("F", ("A3", "oC", "oyC", "oxC", "oyxC", "A1", "A2"), finish_tokens)

    greet(place, (1, 2, 3, CORE, SIDE, DEEP))
    names = list(tasks)
    for index in FRONT_ORDER or range(len(names)):
        needs, action = tasks.pop(names[index])
        for need in needs:
            for item in items.get(need, ()):
                copies.got(item)
        action()
    assert not tasks
    for local_copy in locals_:
        local_copy.wait()
    copies.finish()


def front_call(x, cot, gain_one, gain_two, wq, wo, wg, wu, wd, pairs, segments, ident):
    share, width = x.shape
    hidden, blk = wd.shape
    seq_len, _, local = pairs.shape
    V = pltpu.VMEM
    S = jax.ShapeDtypeStruct
    return pl.pallas_call(
        front_kernel,
        out_shape=(
            S((seq_len, width), bf16), S((seq_len, width), bf16), S((hidden, width), bf16), S((hidden, width), bf16),
            S((hidden, width), bf16), S((width, width), bf16), S((seq_len, local), bf16), S((share, width), bf16),
            S((local // HEAD_DIM, 1, seq_len), f32), S((share, width), f32), S((share, width), bf16),
            S((share, width), bf16), S((share, width), bf16), S((1, width), f32), S((1, width), f32),
            S((seq_len, local), bf16), S((seq_len, local), bf16), S((1, seq_len), jnp.int32)),
        in_specs=[VM] * 11,
        out_specs=(ANY,) * 6 + (VM,) * 12,
        scratch_shapes=[
            V((share, width), bf16), V((seq_len, width), bf16), V((width, local), bf16), V((width, width), bf16),
            V((seq_len, local), bf16), DMA((96,)), DMA((96,)), DMA((8,))],
        compiler_params=params(ident, 60 << 20), name="front",
    )(x, cot, gain_one, gain_two, wq, wo, wg, wu, wd, pairs, segments)


def hidden_cuts(hidden):
    cuts = []
    start = 0
    while start < hidden:
        size = min(512, hidden - start)
        cuts.append((start, size))
        start += size
    return cuts


def ffn_kernel(normed, wq, cots_in, down_in, gate_in, up_in, total, query_0, query_y, fparts_out, sums_out,
               weights, tokens, acts, dparts, relay, landed, fparts,
               send_sems, recv_sems, local_sems, free_sem):
    place = Place()
    share, width = normed.shape
    hidden = down_in.shape[0]
    half = share // 2
    wide = width // 2
    cuts = hidden_cuts(hidden)
    copies = Copies(place, send_sems, recv_sems, local_sems)
    load_cots = copies.local(cots_in, tokens.at[0])
    load_w = [copies.local(w, weights.at[i]) for i, w in enumerate((down_in, gate_in, up_in))]
    mp = place.mp
    local = wq.shape[1]
    greet(place, (1, 2, 3, SIDE, CORE, DEEP))

    def at(quarter, part):
        return tokens.at[1, pl.ds(quarter * share + part * half, half), :]

    a, b = pl.ds(0, half), pl.ds(half, half)
    low_a = copies.swap(normed.at[a, :], at(2, 0), Z_LOW)
    side_b = copies.swap(normed.at[b, :], at(1, 1), SIDE)
    low_b = copies.swap(normed.at[b, :], at(2, 1), Z_LOW)
    side_a = copies.swap(normed.at[a, :], at(1, 0), SIDE)
    tokens[1, 0:share, :] = normed[...]

    def wide_block(source_is_input):
        def get(m):
            target = query_0.at[:, pl.ds(pl.multiple_of(m * local, local), local)]
            return (wq if source_is_input else target), target
        return get

    hops = []
    for hop in (1, 2, 3):
        block_of = wide_block(hop == 1)
        hops.append((
            copies.prepare_step(block_of, mp - (hop - 1), mp - hop, 1, (mp >= hop - 1) & (mp < 3), mp >= hop),
            copies.prepare_step(block_of, mp + (hop - 1), mp + hop, -1,
                                (mp <= 3 - (hop - 1)) & (mp > 0), mp <= 3 - hop)))
    over_deep = copies.prepare(query_0, query_y, DEEP)
    for item in hops[0]:
        copies.start(item)
    query_0[:, pl.ds(pl.multiple_of(mp * local, local), local)] = wq[...]

    def block(r, between):
        here = pl.ds(r * share, share)
        for start, size in cuts:
            rows = tokens[1, here, :]
            gate = dot(rows, weights[1, start:start + size, :], 1, 1)
            up = dot(rows, weights[2, start:start + size, :], 1, 1)
            grad = dot(tokens[0, here, :], weights[0, start:start + size, :], 1, 1)
            sigmoid = jax.nn.sigmoid(gate)
            silu = gate * sigmoid
            acts[0, here, start:start + size] = (silu * up).astype(bf16)
            acts[1, here, start:start + size] = (
                grad * up * sigmoid * (1.0 + gate * (1.0 - sigmoid))).astype(bf16)
            acts[2, here, start:start + size] = (grad * silu).astype(bf16)

        between()

        def columns(n, carry):
            there = pl.ds(pl.multiple_of(n * 512, 512), 512)
            dparts[here, there] = (dot(acts[1, here, :], weights[1, :, there], 1, 0)
                                   + dot(acts[2, here, :], weights[2, :, there], 1, 0)).astype(bf16)
            fparts[here, there] = dot(acts[0, here, :], weights[0, :, there], 1, 0).astype(bf16)
            return carry

        lax.fori_loop(0, width // 512, columns, 0)

    for copy in load_w:
        copy.wait()
    load_cots.wait()
    got = {"across": None}

    def pass_on(r, turn, landed_hop, next_hop):
        @pl.when(r == turn)
        def _():
            for item in landed_hop:
                copies.received(item)
            for item in next_hop:
                copies.start(item)

    def step(r, carry):
        @pl.when(r == 1)
        def _():
            low_a["copy"].wait_recv()
            side_b["copy"].wait_recv()
            forward[0].start()
            forward[1].start()
            side_a["copy"].wait_recv()
            low_b["copy"].wait_recv()

        @pl.when(r == 2)
        def _():
            forward[0].wait_recv()
            forward[1].wait_recv()

        pass_on(r, 2, hops[0], hops[1])
        pass_on(r, 3, hops[2], (over_deep,))

        @pl.when(r == 3)
        def _():
            reduce.start_across()
        block(jnp.where(r < 2, r, 5 - r), lambda: pass_on(r, 2, hops[1], hops[2]))
        return carry

    reduce = QuadReduce(copies, dparts, relay, landed)
    reduce.prepare()

    forward = [copies.describe(at(2, 0), at(3, 0), place.partner(SIDE), copies.count),
               copies.describe(at(1, 1), at(3, 1), place.partner(Z_LOW), copies.count + 1)]
    copies.count += 2
    lax.fori_loop(0, 4, step, 0)
    for item in (low_a, side_b, low_b, side_a):
        item["got"] = True
    pl.semaphore_signal(free_sem, inc=1, device_id=place.partner(CORE), device_id_type=MESH)
    reduce.start_rest()
    save = copies.local(fparts, fparts_out)

    base = copies.count
    copies.count += 3

    def give_copy(i):
        return copies.describe(weights.at[i, :, pl.ds(0, wide)], weights.at[i, :, pl.ds(wide, wide)],
                               place.partner(CORE), base + i)

    def give(i, carry):
        right = tokens[jnp.minimum(i, 1), :, wide:]
        for start, size in cuts:
            weights[i, start:start + size, 0:wide] = dot(
                acts[i, :, start:start + size], right, 0, 0).astype(bf16)

        @pl.when(i == 0)
        def _():
            pl.semaphore_wait(free_sem, 1)
        give_copy(i).start()

        @pl.when(i == 0)
        def _():
            reduce.relayed_low()

        @pl.when(i == 1)
        def _():
            reduce.relayed_side()
        return carry

    lax.fori_loop(0, 3, give, 0)

    def keep(i, carry):
        give_copy(i).wait_recv()
        right = tokens[jnp.minimum(i, 1), :, 0:wide]
        for start, size in cuts:
            rows = slice(start, start + size)
            weights[i, rows, wide:] = (dot(acts[i, :, rows], right, 0, 0)
                                       + weights[i, rows, wide:].astype(f32)).astype(bf16)
        pltpu.make_async_copy(weights.at[i, :, pl.ds(wide, wide)], sums_out.at[i], local_sems.at[5 + i]).start()
        return carry

    lax.fori_loop(0, 3, keep, 0)
    reduce.arrived()

    def one(i, carry):
        here = pl.ds(i * 32, 32)
        total[here, :] = (dparts[here, :].astype(f32) + landed[0, here, :].astype(f32)
                          + landed[1, here, :].astype(f32))
        return carry

    lax.fori_loop(0, share // 32, one, 0)
    for i in range(3):
        give_copy(i).wait_send()
        pltpu.make_async_copy(weights.at[i, :, pl.ds(wide, wide)], sums_out.at[i], local_sems.at[5 + i]).wait()
    for copy in forward:
        copy.wait_send()
    save.wait()
    copies.finish()


def ffn_call(normed, wq, cots, down, gate, up, ident):
    share, width = normed.shape
    hidden = down.shape[0]
    V = pltpu.VMEM
    flops = 2 * share * 4 * width * hidden * 9
    return pl.pallas_call(
        ffn_kernel,
        out_shape=(jax.ShapeDtypeStruct((share, width), f32), jax.ShapeDtypeStruct((share, width), bf16),
                   jax.ShapeDtypeStruct((share, width), bf16), jax.ShapeDtypeStruct((share * 4, width), bf16),
                   jax.ShapeDtypeStruct((3, hidden, width // 2), bf16)),
        in_specs=[VM] * 2 + [ANY] * 4,
        out_specs=(VM, VM, VM, ANY, ANY),
        scratch_shapes=[
            V((3, hidden, width), bf16), V((2, share * 4, width), bf16), V((3, share * 4, hidden), bf16),
            V((share * 4, width), bf16), V((2, share // 2, width), bf16), V((2, share, width), bf16),
            V((share * 4, width), bf16),
            DMA((24,)), DMA((24,)), DMA((8,)), pltpu.SemaphoreType.REGULAR],
        compiler_params=params(ident, 63 << 20),
        cost_estimate=pl.CostEstimate(flops=flops, bytes_accessed=40 << 20, transcendentals=share * 4 * hidden),
        name="feed_forward",
    )(normed, wq, cots, down, gate, up)


def back_first_kernel(dn2, residual, cot, gain, context, queries, keys, values, lse, starts, query_0, query_y,
                      out_whole, sums,
                      dres, gain_part, query_x, query_xy, grad_q, pairs, down_sums, gate_sums, out_sums,
                      heads, keep_d, deep_d, high_d, deep_g, grad_low, wout, dctx, give_o, core_o, dk, dv,
                      send_sems, recv_sems, local_sems):
    place = Place()
    mp = place.mp
    share, width = dn2.shape
    hidden = keep_d.shape[0]
    half = hidden // 2
    local = heads.shape[1]
    wide = width // 2
    quarter = wide // 2
    blk = quarter // 2
    copies = Copies(place, send_sems, recv_sems, local_sems)
    loads = [copies.local(out_whole.at[pl.ds(z * local, local), :], wout.at[z]) for z in range(4)]
    load_d = copies.local(sums.at[0, :, pl.ds(0, quarter)], keep_d)
    load_g = copies.local(sums.at[1, :, pl.ds(0, blk)], gate_sums)
    greet(place, (1, 2, 3, CORE, SIDE, DEEP))
    in_d = [copies.swap(sums.at[0, :, pl.ds(quarter + x * blk, blk)], deep_d.at[:, pl.ds(x * blk, blk)], DEEP)
            for x in (0, 1)]
    copies.swap(query_0, query_x, SIDE)
    copies.swap(query_y, query_xy, SIDE)
    gain_part[...] = jnp.zeros_like(gain_part)

    def norm(i, carry):
        here = pl.ds(i * 32, 32)
        value = residual[here, :]
        inverse = lax.rsqrt(jnp.mean(value * value, axis=-1, keepdims=True) + epsilon)
        scaled = value * inverse
        grad = dn2[here, :]
        grad_scaled = grad * gain[...]
        back = inverse * (grad_scaled - scaled * jnp.mean(grad_scaled * scaled, axis=-1, keepdims=True))
        total = cot[here, :].astype(f32) + back
        dres[here, :] = total
        grad_low[here, :] = total.astype(bf16)
        gain_part[...] += jnp.sum(grad * scaled, axis=0, keepdims=True)
        return carry

    lax.fori_loop(0, share // 32, norm, 0)
    for copy in loads:
        copy.wait()
    heads_in = []
    for mask in (2, 3, 1, 0):
        other = place.partner(mask)[1]
        there = pl.ds(pl.multiple_of(other * local, local), local)
        piece = dot(grad_low[...], wout[other], 1, 1).astype(bf16)
        if mask:
            dctx[:, there] = piece
            heads_in.append(copies.swap(dctx.at[:, there], heads.at[pl.ds(mp * share, share), :], mask))
        else:
            heads[pl.ds(mp * share, share), :] = piece
    chunks = width // 512
    base = copies.count
    copies.count += chunks

    def core_copy(n):
        rows = pl.ds(pl.multiple_of(n * 512, 512), 512)
        return copies.describe(give_o.at[rows, :], core_o.at[rows, :], place.partner(CORE), base + n)

    def give(n, carry):
        rows = pl.ds(pl.multiple_of(n * 512, 512), 512)
        give_o[rows, :] = dot(context[:, rows], grad_low[:, wide:], 0, 0).astype(bf16)
        core_copy(n).start()
        return carry

    lax.fori_loop(0, chunks, give, 0)

    def keep(n, carry):
        rows = pl.ds(pl.multiple_of(n * 512, 512), 512)
        core_copy(n).wait_recv()
        out_sums[rows, :] = (dot(context[:, rows], grad_low[:, :wide], 0, 0)
                             + core_o[rows, :].astype(f32)).astype(bf16)
        return carry

    lax.fori_loop(0, chunks, keep, 0)
    in_g = copies.swap(sums.at[1, :, pl.ds(quarter, blk)], deep_g, DEEP)
    load_d.wait()
    give_rows = pl.ds(half, half)
    across = []
    for x in (0, 1):
        there = pl.ds(x * blk, blk)
        copies.got(in_d[x])
        add_into(keep_d.at[:, there], (half, half), deep_d.at[give_rows, there], step=16)
        across.append(copies.swap(keep_d.at[give_rows, there], high_d.at[:, there], Z_HIGH))
        add_into(keep_d.at[:, there], (0, half), deep_d.at[:, there], step=16)
    for item in heads_in:
        copies.got(item)

    def one_head(h, carry):
        attend_head_back(h, starts, queries, keys, values, heads, lse, grad_q, pairs, dk, dv)
        return carry

    lax.fori_loop(0, local // HEAD_DIM, one_head, 0)
    load_g.wait()
    copies.got(in_g)
    add_into(gate_sums, (0, hidden), deep_g)
    for x in (0, 1):
        copies.got(across[x])

    def add_d(n, carry):
        rows = pl.ds(n * 16, 16)
        down_sums[rows, :] = (keep_d[rows, :].astype(f32) + high_d[rows, :].astype(f32)).astype(bf16)
        return carry

    lax.fori_loop(0, half // 16, add_d, 0)
    copies.finish()

    def sent(n, carry):
        core_copy(n).wait_send()
        return carry

    lax.fori_loop(0, chunks, sent, 0)


def back_first(dn2, residual, cot, gain, context, queries, keys, values, lse, starts, query_0, query_y,
               out_whole, sums, ident):
    share, width = dn2.shape
    hidden = sums.shape[1]
    half = hidden // 2
    seq_len, local = queries.shape
    quarter = width // 4
    V = pltpu.VMEM
    S = jax.ShapeDtypeStruct
    return pl.pallas_call(
        back_first_kernel,
        out_shape=(S((share, width), f32), S((1, width), f32), S(query_0.shape, bf16), S(query_0.shape, bf16),
                   S((seq_len, local), bf16), S((seq_len, 2, local), f32),
                   S((half, quarter), bf16), S((hidden, quarter // 2), bf16), S((width, width // 2), bf16)),
        in_specs=[VM] * 12 + [ANY, ANY],
        out_specs=(VM,) * 9,
        scratch_shapes=[
            V((seq_len, local), bf16), V((hidden, quarter), bf16), V((hidden, quarter), bf16), V((half, quarter), bf16),
            V((hidden, quarter // 2), bf16), V((share, width), bf16),
            V((4, width // 4, width), bf16), V((share, width), bf16), V((width, width // 2), bf16),
            V((width, width // 2), bf16), V((seq_len, HEAD_DIM), f32), V((seq_len, HEAD_DIM), f32),
            DMA((20,)), DMA((20,)), DMA((6,))],
        compiler_params=params(ident, 63 << 20), name="back_first",
    )(dn2, residual, cot, gain, context, queries, keys, values, lse, starts, query_0, query_y, out_whole, sums)


BACK_ORDER = (
    3, 0, 10, 5, 9, 7, 12, 17, 4, 6, 1, 13, 22, 2, 14, 15, 18, 19, 21, 11, 8, 16, 24, 23, 28, 34, 25, 26,
    27, 20, 30, 31, 32, 36, 29, 35, 33,
)


def back_last_kernel(grad_q, dres, inputs, gain, query_0, query_y, query_x, query_xy, residual, gain_part,
                     rows_first, sums, down_sums, gate_sums, out_sums, fparts,
                     down, gate, up, out, query, grad_input, output, gains,
                     keep_d, keep_g, keep_u, deep_g, deep_u, high_g, high_u, side_f,
                     own_o, deep_o, side_o, z_o,
                     give_q, own_q, core_q, side_q, deep_q, parts, relay, landed,
                     grad_own, rows, query_far, dn1, gain_rows, gains_got,
                     send_sems, recv_sems, local_sems):
    place = Place()
    mp = place.mp
    side = place.bit(SIDE)
    share, width = dres.shape
    hidden, blk = down.shape
    half = hidden // 2
    local = grad_q.shape[1]
    zrow = out.shape[0]
    quarter = 2 * blk
    wide = width // 2
    copies = Copies(place, send_sems, recv_sems, local_sems)
    load_rows = copies.local(rows_first, rows)
    load_g = copies.local(gate_sums, keep_g.at[:, pl.ds(0, blk)])
    load_h = copies.local(sums.at[1, :, pl.ds(blk, blk)], keep_g.at[:, pl.ds(blk, blk)])
    load_d = copies.local(down_sums, keep_d)
    load_o = copies.local(out_sums, own_o)
    load_u = copies.local(sums.at[2, :, pl.ds(0, quarter)], keep_u)
    load_p = copies.local(fparts, parts)
    near = (query_0, query_y, query_x, query_xy)
    spot_of = (side, side + 2, 1 - side, 3 - side)
    give_rows = pl.ds(half, half)
    mine = pl.ds(pl.multiple_of(side * blk, blk), blk)
    theirs = pl.ds(pl.multiple_of((1 - side) * blk, blk), blk)
    spots = [pl.ds(pl.multiple_of(absolute(place, s) * blk, blk), blk) for s in range(8)]
    reduce = QuadReduce(copies, parts, relay, landed)
    items = {}
    tasks = {}
    loaded = set()

    def note(name, *copied):
        items[name] = list(copied)

    def task(name, needs, action, *arguments):
        tasks[name] = (needs, lambda: action(*arguments))

    def ready(name, *loads):
        if name not in loaded:
            loaded.add(name)
            for load in loads:
                load.wait()

    def block_o(deep, column):
        return own_o.at[:, pl.ds(pl.multiple_of((2 * deep + column) * blk, blk), blk)]

    def rows_q(deep, column):
        return pl.ds(pl.multiple_of((2 * deep + column) * blk, blk), blk)

    def send_tokens():
        sent = []
        for mask in (2, 3, 1):
            other = place.partner(mask)[1]
            sent.append(copies.swap(grad_q.at[pl.ds(other * share, share), :],
                                    grad_own.at[:, pl.ds(mp * local, local)], mask))
        note("dq", *sent)
        grad_own[:, pl.ds(pl.multiple_of(mp * local, local), local)] = grad_q[pl.ds(mp * share, share), :]

    def send_up(x):
        note("u%d" % x, copies.swap(sums.at[2, :, pl.ds(quarter + x * blk, blk)], deep_u.at[:, pl.ds(x * blk, blk)], DEEP))

    def send_near():
        note("f", *[copies.swap(piece, query_far.at[n], CORE) for n, piece in enumerate(near)])

    def send_gate():
        ready("g", load_g)
        there = pl.ds(0, blk)
        note("zg0", copies.swap(keep_g.at[give_rows, there], high_g.at[:, there], Z_HIGH))

    def send_gate_deep():
        note("g1", copies.swap(sums.at[1, :, pl.ds(quarter + blk, blk)], deep_g, DEEP))

    def gate_sum():
        ready("h", load_h)
        there = pl.ds(blk, blk)
        add_into(keep_g.at[:, there], (half, half), deep_g.at[give_rows, :], step=16)
        note("zg1", copies.swap(keep_g.at[give_rows, there], high_g.at[:, there], Z_HIGH))
        add_into(keep_g.at[:, there], (0, half), deep_g, step=16)

    def send_down():
        ready("d", load_d)
        note("xd", copies.swap(keep_d.at[:, theirs], side_f.at[0], SIDE))

    def send_out(name, n, x):
        ready("o", load_o)
        note(name, copies.swap(block_o(1, x), deep_o.at[n], DEEP))

    def product(first):
        ready("w", load_rows)
        return dot(rows[:, first:first + wide], grad_q[...], 0, 0)

    def query_give():
        give_q[...] = product(wide).astype(bf16)
        note("qc", copies.swap(give_q, core_q, CORE))

    def query_keep():
        own_q[...] = (product(0) + core_q[...].astype(f32)).astype(bf16)
        for y in (1, 0):
            note("qs%d" % y, copies.swap(own_q.at[rows_q(y, 1 - side), :], side_q.at[y], SIDE))

    def query_side(y):
        here = rows_q(y, side)
        own_q[here, :] = (own_q[here, :].astype(f32) + side_q[y].astype(f32)).astype(bf16)
        if y:
            note("qd", copies.swap(own_q.at[here, :], deep_q, DEEP))

    def query_done():
        query[...] = own_q[rows_q(0, side), :].astype(f32) + deep_q[...].astype(f32)

    def reduce_start():
        ready("p", load_p)
        reduce.start()
        note("r1", reduce.first, reduce.second)

    def first_product():
        for n in range(4):
            dn1[:, pl.ds(pl.multiple_of(spot_of[n] * blk, blk), blk)] = dot(grad_own[...], near[n][...], 1, 1)
            dn1[:, pl.ds(pl.multiple_of((spot_of[n] + 4) * blk, blk), blk)] = dot(grad_own[...], query_far[n], 1, 1)

    def first_norm():
        gain_rows[0:1, :] = jnp.zeros((1, width), f32)
        gain_rows[1:2, :] = gain_part[...]

        def norm(i, carry):
            here = pl.ds(i * 32, 32)
            value = inputs[here, :].astype(f32)
            inverse = lax.rsqrt(jnp.mean(value * value, axis=-1, keepdims=True) + epsilon)
            scaled = value * inverse
            grad = dn1[here, :]
            grad_scaled = grad * gain[...]
            back = inverse * (grad_scaled - scaled * jnp.mean(grad_scaled * scaled, axis=-1, keepdims=True))
            total = dres[here, :] + back
            for s in range(8):
                grad_input[here, spots[s]] = total[:, s * blk:(s + 1) * blk]
            gain_rows[0:1, :] += jnp.sum(grad * scaled, axis=0, keepdims=True)
            return carry

        lax.fori_loop(0, share // 32, norm, 0)
        for s in range(8):
            gains[:, spots[s]] = gain_rows[:, s * blk:(s + 1) * blk]

    gain_masks = (1, 2, CORE, SIDE, DEEP)

    def gain_hop(n):
        if n:
            item = items["h%d" % (n - 1)][0]
            item["copy"].wait_send()
            item["sent"] = True
            gains[...] = gains[...] + gains_got[n - 1]
        if n < len(gain_masks):
            note("h%d" % n, copies.swap(gains, gains_got.at[n], gain_masks[n]))

    def up_sum(x):
        ready("u", load_u)
        there = pl.ds(x * blk, blk)
        add_into(keep_u.at[:, there], (half, half), deep_u.at[give_rows, there], step=16)
        note("zu%d" % x, copies.swap(keep_u.at[give_rows, there], high_u.at[:, there], Z_HIGH))
        add_into(keep_u.at[:, there], (0, half), deep_u.at[:, there], step=16)

    def high_sum(name, keep, high, i):
        add_into(keep.at[:, theirs], (0, half), high.at[:, theirs], step=16)
        note(name, copies.swap(keep.at[pl.ds(0, half), theirs], side_f.at[i], SIDE))
        add_into(keep.at[:, mine], (0, half), high.at[:, mine], step=16)

    def out_side():
        add_into(block_o(0, 1 - side), (0, width), deep_o.at[0])
        note("os", copies.swap(block_o(0, 1 - side), side_o, SIDE))

    def out_mine():
        add_into(block_o(0, side), (0, width), deep_o.at[1])

    def out_rows():
        add_into(block_o(0, side), (0, width), side_o)
        note("oz", *[copies.swap(own_o.at[pl.ds(place.partner(mask)[1] * zrow, zrow), mine], z_o.at[n], mask)
                     for n, mask in enumerate((2, 3, 1))])

    def out_done():
        def add_z(i, carry):
            here = pl.ds(i * 32, 32)
            sum_ = own_o[pl.ds(mp * zrow + i * 32, 32), mine].astype(f32)
            for n in range(3):
                sum_ = sum_ + z_o[n, here, :].astype(f32)
            out[here, :] = sum_
            return carry

        lax.fori_loop(0, zrow // 32, add_z, 0)

    def output_done():
        reduce.arrived()

        def finish_output(i, carry):
            here = pl.ds(i * 32, 32)
            total = (residual[here, :] + parts[here, :].astype(f32) + landed[0, here, :].astype(f32)
                     + landed[1, here, :].astype(f32)).astype(bf16)
            for s in range(8):
                output[here, spots[s]] = total[:, s * blk:(s + 1) * blk]
            return carry

        lax.fori_loop(0, share // 32, finish_output, 0)

    def weight_done(i, target, keep):
        def write(n, carry):
            target[pl.ds(side * half + n * 16, 16), :] = keep[pl.ds(n * 16, 16), mine].astype(f32)
            target[pl.ds((1 - side) * half + n * 16, 16), :] = side_f[i, pl.ds(n * 16, 16), :].astype(f32)
            return carry

        lax.fori_loop(0, half // 16, write, 0)

    task("dq", (), send_tokens)
    task("g1", (), send_gate_deep)
    task("u0", (), send_up, 0)
    task("u1", (), send_up, 1)
    task("f", (), send_near)
    task("zg0", (), send_gate)
    task("xd", (), send_down)
    task("ot", (), send_out, "ot", 0, 1 - side)
    task("om", (), send_out, "om", 1, side)
    task("qc", (), query_give)
    task("r1", (), reduce_start)
    task("zg1", ("g1",), gate_sum)
    task("qk", ("qc",), query_keep)
    task("dn1", ("f", "dq"), first_product)
    task("N", ("dn1",), first_norm)
    task("h0", ("N",), gain_hop, 0)
    task("zu0", ("u0",), up_sum, 0)
    task("zu1", ("u1",), up_sum, 1)
    task("r2", ("r1",), reduce.relayed)
    task("h1", ("h0",), gain_hop, 1)
    task("qy1", ("qk", "qs1"), query_side, 1)
    task("qy0", ("qk", "qs0"), query_side, 0)
    task("os", ("ot",), out_side)
    task("h2", ("h1",), gain_hop, 2)
    task("xg", ("zg0", "zg1"), high_sum, "xg", keep_g, high_g, 1)
    task("h3", ("h2",), gain_hop, 3)
    task("O", ("om",), out_mine)
    task("h4", ("h3",), gain_hop, 4)
    task("R", ("r2",), output_done)
    task("h5", ("h4",), gain_hop, 5)
    task("oz", ("os", "O"), out_rows)
    task("Q", ("qy1", "qy0", "qd"), query_done)
    task("xu", ("zu0", "zu1"), high_sum, "xu", keep_u, high_u, 2)
    task("OD", ("oz",), out_done)
    task("DD", ("xd",), weight_done, 0, down, keep_d)
    task("GD", ("xg",), weight_done, 1, gate, keep_g)
    task("UD", ("xu",), weight_done, 2, up, keep_u)
    greet(place, (1, 2, 3, CORE, SIDE, DEEP))
    names = list(tasks)
    for index in BACK_ORDER or range(len(names)):
        needs, action = tasks.pop(names[index])
        for need in needs:
            for item in items.get(need, ()):
                copies.got(item)
        action()
    assert not tasks
    copies.finish()


def back_last(grad_q, dres, inputs, gain, query_0, query_y, query_x, query_xy, residual, gain_part,
              rows_first, sums, down_sums, gate_sums, out_sums, fparts, ident):
    share, width = dres.shape
    hidden = sums.shape[1]
    blk = width // 8
    half = hidden // 2
    local = grad_q.shape[1]
    V = pltpu.VMEM
    S = jax.ShapeDtypeStruct
    return pl.pallas_call(
        back_last_kernel,
        out_shape=(S((hidden, blk), f32),) * 3
        + (S((width // 4, blk), f32), S((blk, local), f32), S((share, width), f32), S((share, width), bf16),
           S((2, width), f32)),
        in_specs=[VM] * 10 + [ANY] * 6,
        out_specs=(VM,) * 8,
        scratch_shapes=[
            V((half, 2 * blk), bf16), V((hidden, 2 * blk), bf16), V((hidden, 2 * blk), bf16), V((hidden, blk), bf16),
            V((hidden, 2 * blk), bf16),
            V((half, 2 * blk), bf16), V((half, 2 * blk), bf16), V((3, half, blk), bf16),
            V((width, width // 2), bf16), V((2, width, blk), bf16), V((width, blk), bf16),
            V((3, width // 4, blk), bf16),
            V((width // 2, local), bf16), V((width // 2, local), bf16), V((width // 2, local), bf16),
            V((2, blk, local), bf16), V((blk, local), bf16),
            V((share * 4, width), bf16), V((2, share // 2, width), bf16), V((2, share, width), bf16),
            V((share, width), bf16), V((share * 4, width), bf16), V((4, blk, width), bf16), V((share, width), f32),
            V((2, width), f32), V((5, 2, width), f32),
            DMA((48,)), DMA((48,)), DMA((12,))],
        compiler_params=params(ident, 63 << 20), name="back_last",
    )(grad_q, dres, inputs, gain, query_0, query_y, query_x, query_xy, residual, gain_part,
      rows_first, sums, down_sums, gate_sums, out_sums, fparts)


def hand_over_kernel(*refs):
    count = (len(refs) - 2) // 3
    sources, targets, held = refs[:count], refs[count:2 * count], refs[2 * count:3 * count]
    in_sems, out_sems = refs[-2:]
    loads = [pltpu.make_async_copy(sources[n], held[n], in_sems.at[n]) for n in range(count)]
    stores = [pltpu.make_async_copy(held[n], targets[n], out_sems.at[n]) for n in range(count)]
    for load in loads:
        load.start()
    for load, store in zip(loads, stores):
        load.wait()
        store.start()
    for store in stores:
        store.wait()


def hand_over(*arrays):
    n = len(arrays)
    return pl.pallas_call(
        hand_over_kernel, out_shape=tuple(jax.ShapeDtypeStruct(a.shape, a.dtype) for a in arrays),
        in_specs=[ANY] * n, out_specs=(ANY,) * n,
        scratch_shapes=[pltpu.VMEM(a.shape, a.dtype) for a in arrays] + [DMA((n,)), DMA((n,))],
        compiler_params=pltpu.CompilerParams(vmem_limit_bytes=63 << 20), name="hand_over")(*arrays)


def contract(left, right, left_dim, right_dim):
    return lax.dot_general(
        left, right, (((left_dim,), (right_dim,)), ((), ())), preferred_element_type=jnp.float32
    )


def root_inverse(values):
    return lax.rsqrt(jnp.mean(values * values, axis=-1, keepdims=True) + epsilon)


def norm_back(grad_normed, scaled, inverse, gain):
    grad_scaled = grad_normed * gain
    grad_values = inverse * (
        grad_scaled - scaled * jnp.mean(grad_scaled * scaled, axis=-1, keepdims=True)
    )
    return (grad_values, jnp.sum(grad_normed * scaled, axis=0))


def plain_body(
    inputs,
    keys_values,
    segment_ids,
    gain_first,
    gain_second,
    w_query,
    w_out,
    w_gate,
    w_up,
    w_down,
    cotangent,
):
    query_full, out_full = (
        lax.all_gather(w_query, "dp", axis=0, tiled=True),
        lax.all_gather(w_out, "dp", axis=1, tiled=True),
    )
    gate_full, up_full, down_full = (
        lax.all_gather(w_gate, "dp", axis=0, tiled=True),
        lax.all_gather(w_up, "dp", axis=0, tiled=True),
        lax.all_gather(w_down, "dp", axis=1, tiled=True),
    )
    tokens = inputs.astype(jnp.float32)
    inverse_first = root_inverse(tokens)
    scaled_first = tokens * inverse_first
    normed_first = (scaled_first * gain_first).astype(jnp.bfloat16)
    rows_first = lax.all_gather(normed_first, "mp", axis=0, tiled=True)
    queries = contract(rows_first, query_full, 1, 0).astype(jnp.bfloat16)
    seq_len = rows_first.shape[0]
    local_width = queries.shape[1]
    head_count = local_width // HEAD_DIM
    block_rows = min(512, seq_len)
    block_count = seq_len // block_rows
    score_scale = HEAD_DIM ** (-0.5)
    key_heads = keys_values[:, 0, :].reshape(seq_len, head_count, HEAD_DIM)
    value_heads = keys_values[:, 1, :].reshape(seq_len, head_count, HEAD_DIM)
    segments = segment_ids[0]
    key_pos = jnp.arange(seq_len, dtype=jnp.int32)

    def block_scores(first_row):
        query_block = lax.dynamic_slice_in_dim(queries, first_row, block_rows, 0).reshape(
            block_rows, head_count, HEAD_DIM
        )
        scores = (
            jnp.einsum("qhd,khd->hqk", query_block, key_heads, preferred_element_type=jnp.float32)
            * score_scale
        )
        query_pos = first_row + jnp.arange(block_rows, dtype=jnp.int32)
        query_seg = lax.dynamic_slice_in_dim(segments, first_row, block_rows, 0)
        allowed = (query_pos[:, None] >= key_pos[None, :]) & (
            query_seg[:, None] == segments[None, :]
        )
        return (query_block, jnp.where(allowed[None], scores, -1e30))

    def forward_block(block_index):
        query_block, scores = block_scores(block_index * block_rows)
        row_max = jnp.max(scores, axis=-1, keepdims=True)
        raised = jnp.exp(scores - row_max)
        row_total = jnp.sum(raised, axis=-1, keepdims=True)
        weights_low = (raised / row_total).astype(jnp.bfloat16)
        blended = jnp.einsum(
            "hqk,khd->qhd", weights_low, value_heads, preferred_element_type=jnp.float32
        )
        return (
            blended.reshape(block_rows, local_width).astype(jnp.bfloat16),
            (row_max + jnp.log(row_total))[..., 0],
        )

    context_blocks, log_totals = lax.map(forward_block, jnp.arange(block_count, dtype=jnp.int32))
    context = context_blocks.reshape(seq_len, local_width)
    attn_part = lax.psum_scatter(
        contract(context, out_full, 1, 0), "mp", scatter_dimension=0, tiled=True
    )
    residual = tokens + attn_part
    inverse_second = root_inverse(residual)
    scaled_second = residual * inverse_second
    normed_second = (scaled_second * gain_second).astype(jnp.bfloat16)
    rows_second = lax.all_gather(normed_second, "mp", axis=0, tiled=True)
    gate_proj = contract(rows_second, gate_full, 1, 0)
    up_proj = contract(rows_second, up_full, 1, 0)
    sigmoid_gate = jax.nn.sigmoid(gate_proj)
    silu_gate = gate_proj * sigmoid_gate
    hidden = (silu_gate * up_proj).astype(jnp.bfloat16)
    ffn_part = lax.psum_scatter(
        contract(hidden, down_full, 1, 0).astype(jnp.bfloat16),
        "mp",
        scatter_dimension=0,
        tiled=True,
    ).astype(jnp.float32)
    output = (residual + ffn_part).astype(jnp.bfloat16)
    cot_rows = lax.all_gather(cotangent, "mp", axis=0, tiled=True)
    grad_down_w = contract(hidden, cot_rows, 0, 0)
    grad_hidden = contract(cot_rows, down_full, 1, 1)
    grad_gate_act = (
        grad_hidden * up_proj * sigmoid_gate * (1.0 + gate_proj * (1.0 - sigmoid_gate))
    ).astype(jnp.bfloat16)
    grad_up_act = (grad_hidden * silu_gate).astype(jnp.bfloat16)
    grad_gate_w = contract(rows_second, grad_gate_act, 0, 0)
    grad_up_w = contract(rows_second, grad_up_act, 0, 0)
    grad_normed_second = lax.psum_scatter(
        contract(grad_gate_act, gate_full, 1, 1) + contract(grad_up_act, up_full, 1, 1),
        "mp",
        scatter_dimension=0,
        tiled=True,
    )
    grad_from_norm, gain_second_part = norm_back(
        grad_normed_second, scaled_second, inverse_second, gain_second
    )
    grad_residual = cotangent.astype(jnp.float32) + grad_from_norm
    attn_cot = lax.all_gather(grad_residual.astype(jnp.bfloat16), "mp", axis=0, tiled=True)
    grad_out_w = contract(context, attn_cot, 0, 0)
    grad_context = contract(attn_cot, out_full, 1, 1).astype(jnp.bfloat16)

    def backward_block(state_pair, block_index):
        grad_keys, grad_values = state_pair
        first_row = block_index * block_rows
        query_block, scores = block_scores(first_row)
        log_total = lax.dynamic_index_in_dim(log_totals, block_index, 0, keepdims=False)
        weights = jnp.exp(scores - log_total[..., None])
        grad_block = lax.dynamic_slice_in_dim(grad_context, first_row, block_rows, 0).reshape(
            block_rows, head_count, HEAD_DIM
        )
        grad_weights = jnp.einsum(
            "qhd,khd->hqk", grad_block, value_heads, preferred_element_type=jnp.float32
        )
        spread = jnp.sum(weights * grad_weights, axis=-1, keepdims=True)
        grad_scores = (weights * (grad_weights - spread)).astype(jnp.bfloat16)
        grad_query_block = (
            jnp.einsum("hqk,khd->qhd", grad_scores, key_heads, preferred_element_type=jnp.float32)
            * score_scale
        ).astype(jnp.bfloat16)
        grad_keys = (
            grad_keys
            + jnp.einsum(
                "hqk,qhd->khd", grad_scores, query_block, preferred_element_type=jnp.float32
            )
            * score_scale
        )
        grad_values = grad_values + jnp.einsum(
            "hqk,qhd->khd",
            weights.astype(jnp.bfloat16),
            grad_block,
            preferred_element_type=jnp.float32,
        )
        return ((grad_keys, grad_values), grad_query_block.reshape(block_rows, local_width))

    zero_state = jnp.zeros((seq_len, head_count, HEAD_DIM), jnp.float32)
    (grad_keys, grad_values), grad_query_blocks = lax.scan(
        backward_block, (zero_state, zero_state), jnp.arange(block_count, dtype=jnp.int32)
    )
    grad_queries = grad_query_blocks.reshape(seq_len, local_width)
    grad_kv = jnp.stack(
        [grad_keys.reshape(seq_len, local_width), grad_values.reshape(seq_len, local_width)], axis=1
    )
    grad_query_w = contract(rows_first, grad_queries, 0, 0)
    grad_normed_first = lax.psum_scatter(
        contract(grad_queries, query_full, 1, 1).astype(jnp.bfloat16),
        "mp",
        scatter_dimension=0,
        tiled=True,
    ).astype(jnp.float32)
    grad_from_first, gain_first_part = norm_back(
        grad_normed_first, scaled_first, inverse_first, gain_first
    )
    grad_input = grad_residual + grad_from_first
    gain_first_sum, gain_second_sum = lax.psum((gain_first_part, gain_second_part), ("dp", "mp"))
    query_shard, out_shard, gate_shard, up_shard, down_shard = (
        lax.psum_scatter(
            grad_query_w.astype(jnp.bfloat16), "dp", scatter_dimension=0, tiled=True
        ).astype(jnp.float32),
        lax.psum_scatter(
            grad_out_w.astype(jnp.bfloat16), "dp", scatter_dimension=1, tiled=True
        ).astype(jnp.float32),
        lax.psum_scatter(
            grad_gate_w.astype(jnp.bfloat16), "dp", scatter_dimension=0, tiled=True
        ).astype(jnp.float32),
        lax.psum_scatter(
            grad_up_w.astype(jnp.bfloat16), "dp", scatter_dimension=0, tiled=True
        ).astype(jnp.float32),
        lax.psum_scatter(
            grad_down_w.astype(jnp.bfloat16), "dp", scatter_dimension=1, tiled=True
        ).astype(jnp.float32),
    )
    return (
        output,
        grad_input,
        grad_kv,
        gain_first_sum,
        gain_second_sum,
        query_shard,
        out_shard,
        gate_shard,
        up_shard,
        down_shard,
    )


def fast_body(inputs, keys_values, segment_ids, gain_first, gain_second, w_query, w_out, w_gate,
              w_up, w_down, cotangent):
    (rows_first, cots, gate_here, up_here, down_here, out_whole, queries, context_own, log_totals, residual,
     normed_second, inputs_here, cot_here, gain_one, gain_two, keys, values, starts) = front_call(
        inputs, cotangent, gain_first[None], gain_second[None], w_query, w_out, w_gate.T, w_up.T, w_down,
        keys_values, segment_ids, 1)
    grad_normed_second, query_0, query_y, ffn_parts, ffn_sums = ffn_call(
        normed_second, w_query, cots, down_here, gate_here, up_here, 3)
    (grad_residual, gain_second_part, query_x, query_xy, grad_queries, grad_kv, down_sums, gate_sums,
     out_sums) = back_first(
        grad_normed_second, residual, cot_here, gain_two, context_own, queries, keys, values, log_totals, starts,
        query_0, query_y, out_whole, ffn_sums, 5)
    down_shard, gate_shard, up_shard, out_shard, query_shard, grad_input, output, gains = back_last(
        grad_queries, grad_residual, inputs_here, gain_one, query_0, query_y, query_x, query_xy, residual,
        gain_second_part, rows_first, ffn_sums, down_sums, gate_sums, out_sums, ffn_parts, 6)
    (grad_kv, grad_input, output, down_shard, out_shard, query_shard, gate_shard, up_shard) = hand_over(
        grad_kv, grad_input, output, down_shard, out_shard, query_shard, gate_shard, up_shard)
    return (output, grad_input, grad_kv, gains[0], gains[1], query_shard, out_shard,
            gate_shard.T, up_shard.T, down_shard)


def solution(mesh):
    in_specs = (
        P(("dp", "mp"), None),
        P("dp", None, "mp"),
        P("dp", None),
        P(),
        P(),
        P("dp", "mp"),
        P("mp", "dp"),
        P("dp", "mp"),
        P("dp", "mp"),
        P("mp", "dp"),
        P(("dp", "mp"), None),
    )
    out_specs = (
        P(("dp", "mp"), None),
        P(("dp", "mp"), None),
        P("dp", None, "mp"),
        P(),
        P(),
        P("dp", "mp"),
        P("mp", "dp"),
        P("dp", "mp"),
        P("dp", "mp"),
        P("mp", "dp"),
    )
    fast = mesh.shape["dp"] == 8 and mesh.shape["mp"] == 4
    body = fast_body if fast else plain_body
    return jax.shard_map(body, mesh=mesh, in_specs=in_specs, out_specs=out_specs, check_vma=False)
```

```python
import jax
import jax.numpy as jnp
from jax import lax
from jax.experimental import pallas as pl
from jax.experimental.pallas import tpu as pltpu
from jax.sharding import PartitionSpec as P

f32 = jnp.float32
bf16 = jnp.bfloat16
HEAD_DIM = 128
MP = 4
epsilon = 1e-06


MESH = pl.DeviceIdType.MESH
Z_LOW, Z_HIGH, CORE, SIDE, DEEP = 1, 2, 4, 8, 16
ANY = pl.BlockSpec(memory_space=pl.ANY)
VM = pl.BlockSpec(memory_space=pltpu.VMEM)


class Place:
    def __init__(self):
        self.dp = lax.axis_index("dp")
        self.mp = lax.axis_index("mp")

    def bit(self, mask):
        return ((self.dp * 4 + self.mp) // mask) % 2

    def partner(self, mask):
        flip_dp, flip_mp = mask // 4, mask % 4
        return (self.flip(self.dp, flip_dp), self.flip(self.mp, flip_mp))

    def flip(self, value, flips):
        for mask in (1, 2, 4):
            if flips & mask:
                value = value + mask - 2 * mask * ((value // mask) % 2)
        return value


class Copies:
    def __init__(self, place, send_sems, recv_sems, local_sems=None):
        self.place, self.send_sems, self.recv_sems = place, send_sems, recv_sems
        self.local_sems = local_sems
        self.count = 0
        self.local_count = 0
        self.pending = []

    def describe(self, source, target, device, slot):
        return pltpu.make_async_remote_copy(
            src_ref=source, dst_ref=target, send_sem=self.send_sems.at[slot],
            recv_sem=self.recv_sems.at[slot], device_id=device, device_id_type=MESH)

    def swap(self, source, target, mask):
        slot = self.count
        self.count += 1
        copy = self.describe(source, target, self.place.partner(mask), slot)
        copy.start()
        item = {"copy": copy, "got": False}
        self.pending.append(item)
        return item

    def got(self, item):
        if not item["got"]:
            item["got"] = True
            if "get_if" in item:
                @pl.when(item["get_if"])
                def _():
                    item["get"].wait_recv()
            else:
                item["copy"].wait_recv()

    def prepare(self, source, target, mask):
        slot = self.count
        self.count += 1
        item = {"copy": self.describe(source, target, self.place.partner(mask), slot), "got": False}
        self.pending.append(item)
        return item

    def prepare_step(self, block, mp_send, mp_get, direction, send_if, get_if):
        slot = self.count
        self.count += 1
        place = self.place
        device = (place.dp, jnp.clip(place.mp + direction, 0, 3))
        copy = self.describe(*block(jnp.clip(mp_send, 0, 3)), device, slot)
        get = self.describe(*block(jnp.clip(mp_get, 0, 3)), device, slot)
        item = {"copy": copy, "got": False, "send_if": send_if, "get_if": get_if, "get": get}
        self.pending.append(item)
        return item

    def prepare_jump(self, source, target, landing, distance, send_if, get_if):
        slot = self.count
        self.count += 1
        place = self.place
        device = (place.dp, jnp.clip(place.mp + distance, 0, 3))
        item = {"copy": self.describe(source, target, device, slot), "got": False, "send_if": send_if,
                "get_if": get_if, "get": self.describe(source, landing, device, slot)}
        self.pending.append(item)
        return item

    def start(self, item):
        if "send_if" in item:
            @pl.when(item["send_if"])
            def _():
                item["copy"].start()
        else:
            item["copy"].start()

    def step(self, *arguments):
        item = self.prepare_step(*arguments)
        self.start(item)
        return item

    def received(self, item):
        if item["got"]:
            return
        item["got"] = True
        if "get_if" in item:
            @pl.when(item["get_if"])
            def _():
                item["get"].wait_recv()
        else:
            item["copy"].wait_recv()

    def local(self, source, target):
        copy = pltpu.make_async_copy(source, target, self.local_sems.at[self.local_count])
        self.local_count += 1
        copy.start()
        return copy

    def finish(self):
        for item in self.pending:
            self.got(item)
        for item in self.pending:
            if "send_if" in item:
                @pl.when(item["send_if"])
                def _():
                    item["copy"].wait_send()
            elif "sent" not in item:
                item["copy"].wait_send()


def greet(place, masks):
    barrier = pltpu.get_barrier_semaphore()
    for mask in masks:
        pl.semaphore_signal(barrier, inc=1, device_id=place.partner(mask), device_id_type=MESH)
    pl.semaphore_wait(barrier, len(masks))


def absolute(place, spot):
    core, deep, side = spot // 4, (spot // 2) % 2, spot % 2
    return place.flip(place.dp, core + 4 * deep) - 2 * place.bit(SIDE) + 2 * side


DMA = pltpu.SemaphoreType.DMA


def dot(left, right, left_dim, right_dim):
    return lax.dot_general(
        left, right, (((left_dim,), (right_dim,)), ((), ())), preferred_element_type=f32)


def params(ident, vmem=32 << 20):
    return pltpu.CompilerParams(collective_id=ident, has_side_effects=True, vmem_limit_bytes=vmem)


def add_into(target, rows, *others, step=32):
    start, count = rows
    pieces = count // step

    def one(i, carry):
        total = target[pl.ds(start + i * step, step), :].astype(f32)
        for other in others:
            total = total + other[pl.ds(i * step, step), :].astype(f32)
        target[pl.ds(start + i * step, step), :] = total.astype(target.dtype)
        return carry

    lax.fori_loop(0, pieces, one, 0)


class QuadReduce:
    def __init__(self, copies, parts, relay, landed):
        self.copies, self.parts, self.relay, self.landed = copies, parts, relay, landed
        self.share = parts.shape[0] // 4
        self.half = self.share // 2

    def prepare(self):
        share, half = self.share, self.half
        prepare, parts, landed = self.copies.prepare, self.parts, self.landed
        self.first = prepare(parts.at[pl.ds(3 * share, half), :], self.relay.at[0], SIDE)
        self.second = prepare(parts.at[pl.ds(3 * share + half, half), :], self.relay.at[1], Z_LOW)
        self.side = [prepare(parts.at[pl.ds(share, half), :], landed.at[0, pl.ds(0, half), :], SIDE),
                     prepare(parts.at[pl.ds(share + half, half), :], landed.at[0, pl.ds(half, half), :], SIDE)]
        self.low = [prepare(parts.at[pl.ds(2 * share + half, half), :], landed.at[1, pl.ds(half, half), :], Z_LOW),
                    prepare(parts.at[pl.ds(2 * share, half), :], landed.at[1, pl.ds(0, half), :], Z_LOW)]

    def start_across(self):
        self.copies.start(self.first)
        self.copies.start(self.second)
        self.copies.start(self.side[0])

    def start_rest(self):
        self.copies.start(self.low[0])

    def start(self):
        self.prepare()
        self.start_across()
        self.start_rest()

    def relayed_low(self):
        self.copies.received(self.first)
        add_into(self.parts, (2 * self.share, self.half), self.relay.at[0])
        self.copies.start(self.low[1])

    def relayed_side(self):
        self.copies.received(self.second)
        add_into(self.parts, (self.share + self.half, self.half), self.relay.at[1])
        self.copies.start(self.side[1])

    def relayed(self):
        self.relayed_low()
        self.relayed_side()

    def arrived(self):
        for item in self.side + self.low:
            self.copies.got(item)


ROWS=256
DOC_MOST=512
DOCS=16


def key_range(block, seq_len):
    low = max(0, block * ROWS - DOC_MOST + 1) // ROWS * ROWS
    return low, min(seq_len, (block + 1) * ROWS)


def scores_turned(q, k, starts, low, first, scale):
    s = dot(k, q, 1, 1) * scale
    key_pos = low + lax.broadcasted_iota(jnp.int32, s.shape, 0)
    query_pos = first + lax.broadcasted_iota(jnp.int32, s.shape, 1)
    return jnp.where((key_pos >= starts) & (key_pos <= query_pos), s, -1e30)


def attend_block(h, block, starts_ref, q_ref, k_ref, v_ref, ctx_ref, lse_ref):
    seq_len = q_ref.shape[0]
    scale = HEAD_DIM ** -0.5
    window = min(seq_len, DOC_MOST + ROWS)
    lanes = pl.ds(pl.multiple_of(h * HEAD_DIM, HEAD_DIM), HEAD_DIM)
    first = pl.multiple_of(block * ROWS, ROWS)
    low = pl.multiple_of(jnp.clip(first - DOC_MOST, 0, seq_len - window), ROWS)
    here = pl.ds(first, ROWS)
    keys_here = pl.ds(low, window)
    s = scores_turned(q_ref[here, lanes], k_ref[keys_here, lanes], starts_ref[:, here], low, first, scale)
    top = jnp.max(s, axis=0, keepdims=True)
    raised = jnp.exp(s - top)
    total = jnp.sum(raised, axis=0, keepdims=True)
    low_probs = (raised * (1.0 / total)).astype(bf16)
    ctx_ref[here, lanes] = dot(low_probs, v_ref[keys_here, lanes], 0, 0).astype(bf16)
    lse_ref[h, :, here] = top + jnp.log(total)


def attend_head_back(h, starts_ref, q_ref, k_ref, v_ref, grad_ref, lse_ref, dq_ref, pair_ref, dk_ref, dv_ref):
    seq_len = q_ref.shape[0]
    scale = HEAD_DIM ** -0.5
    lanes = pl.ds(pl.multiple_of(h * HEAD_DIM, HEAD_DIM), HEAD_DIM)
    for block in range(seq_len // ROWS):
        low, high = key_range(block, seq_len)
        here = pl.ds(block * ROWS, ROWS)
        k = k_ref[low:high, lanes]
        v = v_ref[low:high, lanes]
        q = q_ref[here, lanes]
        grad = grad_ref[here, lanes]
        s = scores_turned(q, k, starts_ref[:, here], low, block * ROWS, scale)
        probs = jnp.exp(s - lse_ref[h, :, here])
        grad_probs = dot(v, grad, 1, 1)
        spread = jnp.sum(probs * grad_probs, axis=0, keepdims=True)
        grad_s = (probs * (grad_probs - spread)).astype(bf16)
        dq_ref[here, lanes] = (dot(grad_s, k, 0, 0) * scale).astype(bf16)
        dk = dot(grad_s, q, 1, 0) * scale
        dv = dot(probs.astype(bf16), grad, 1, 0)
        old = block * ROWS
        if block:
            n = old - low
            dk_ref[low:old, :] += dk[:n]
            dv_ref[low:old, :] += dv[:n]
            dk_ref[old:high, :] = dk[n:]
            dv_ref[old:high, :] = dv[n:]
        else:
            dk_ref[low:high, :] = dk
            dv_ref[low:high, :] = dv
    pair_ref[:, 0, lanes] = dk_ref[...]
    pair_ref[:, 1, lanes] = dv_ref[...]


FRONT_ORDER = (
    2, 21, 48, 18, 0, 1, 8, 11, 57, 35, 5, 3, 13, 33, 4, 20, 19, 17, 28, 27, 42, 26, 66, 9, 36, 64, 12, 24,
    15, 6, 68, 67, 10, 34, 63, 29, 44, 23, 30, 14, 16, 73, 22, 50, 41, 37, 49, 54, 25, 46, 39, 65, 31, 56,
    53, 75, 59, 7, 43, 55, 52, 38, 40, 70, 72, 45, 69, 51, 74, 60, 61, 71, 58, 76, 32, 62, 47, 77,
)


def front_kernel(x, cot, gain_one_in, gain_two_in, wq, wo, wg, wu, wd, pairs, segments,
                 rows_out, cots, gate, up, down, out_out, queries_to, context_own, lse, residual, normed,
                 x_to, cot_to, gain_one, gain_two, keys_to, values_to, starts,
                 queries, x_here, cot_here, keys, values, first, rows, query, out, context,
                 send_sems, recv_sems, local_sems):
    place = Place()
    dp, mp = place.dp, place.mp
    side = place.bit(SIDE)
    copies = Copies(place, send_sems, recv_sems, local_sems)
    half = wd.shape[0] // 2
    blk = wd.shape[1]
    share, width = first.shape
    zrow = wo.shape[0]
    local = wq.shape[1]
    chunk = share // 2
    mats = ((wg, gate), (wu, up), (wd, down))
    own, across = side, 1 - side
    DEEPER, OTHER = 2, 4
    locals_ = []

    def tile(whole, z, spot):
        return whole.at[pl.ds(z * half, half), pl.ds(spot * blk, blk)]

    def qrows(spot):
        return query.at[pl.ds(spot * blk, blk), :]

    def columns(spot):
        return out.at[:, pl.ds(spot * blk, blk)]

    def row_block(c, source_is_input):
        def get(m):
            target = rows.at[pl.ds(m * share + c * chunk, chunk), :]
            source = first.at[pl.ds(c * chunk, chunk), :] if source_is_input else target
            return source, target
        return get

    def out_block(source_is_input):
        def get(m):
            target = out.at[pl.ds(m * zrow, zrow), pl.ds(own * blk, blk)]
            return (wo if source_is_input else target), target
        return get

    items = {}

    def note(name, *copied):
        items[name] = list(copied)

    def line(step, block_of, name):
        note(name,
             copies.step(block_of, mp - (step - 1), mp - step, 1, (mp >= step - 1) & (mp < 3), mp >= step),
             copies.step(block_of, mp + (step - 1), mp + step, -1, (mp <= 3 - (step - 1)) & (mp > 0), mp <= 3 - step))

    own_piece = [weight.at[pl.ds(side * half, half), :] for weight, _ in mats]
    spots = [pl.ds(pl.multiple_of(absolute(place, s) * blk, blk), blk) for s in range(8)]
    inside = lambda m: (m >= 0) & (m <= 3)

    def context_jump(distance):
        source = context.at[pl.ds(jnp.clip(mp + distance, 0, 3) * share, share), :]

        def landing(m):
            return context_own.at[:, pl.ds(pl.multiple_of(jnp.clip(m, 0, 3) * local, local), local)]

        return copies.prepare_jump(source, landing(mp), landing(mp - distance), distance,
                                   inside(mp + distance), inside(mp - distance))

    jumps = {distance: context_jump(distance) for distance in (1, -1, 2, -2, 3, -3)}

    def attend_tokens(m):
        here = pl.ds(pl.multiple_of(m * share, share), share)
        queries[here, :] = dot(rows[here, :], query[...], 1, 0).astype(bf16)

        def one_head(h, carry):
            attend_block(h, m, starts, queries, keys, values, context, lse)
            return carry

        lax.fori_loop(0, local // HEAD_DIM, one_head, 0)

    def attend_from(distance):
        for away in (distance, -distance):
            @pl.when(inside(mp + away))
            def _(away=away):
                attend_tokens(mp + away)
                jumps[away]["copy"].start()
        note("A%d" % distance, jumps[distance], jumps[-distance])

    def norm_rows():
        for s in range(8):
            gain_one[:, s * blk:(s + 1) * blk] = gain_one_in[:, spots[s]]
            gain_two[:, s * blk:(s + 1) * blk] = gain_two_in[:, spots[s]]

        def norm_first(i, carry):
            here = pl.ds(i * 32, 32)
            for s in range(8):
                x_here[here, s * blk:(s + 1) * blk] = x[here, spots[s]]
                cot_here[here, s * blk:(s + 1) * blk] = cot[here, spots[s]]
            value = x_here[here, :].astype(f32)
            inverse = lax.rsqrt(jnp.mean(value * value, axis=-1, keepdims=True) + epsilon)
            first[here, :] = (value * inverse * gain_one[...]).astype(bf16)
            return carry

        lax.fori_loop(0, share // 32, norm_first, 0)
        rows[pl.ds(mp * share, share), :] = first[...]
        locals_.append(copies.local(x_here, x_to))
        locals_.append(copies.local(cot_here, cot_to))

    def split_pairs():
        def split(i, carry):
            here = pl.ds(i * 32, 32)
            both = pairs[here, :, :]
            keys[here, :] = both[:, 0, :]
            values[here, :] = both[:, 1, :]
            return carry

        lax.fori_loop(0, pairs.shape[0] // 32, split, 0)
        ids = segments[...]
        begun = jnp.zeros_like(ids)
        for document in range(DOCS - 1):
            size = jnp.sum((ids == document).astype(jnp.int32), axis=1, keepdims=True)
            begun = begun + jnp.where(ids > document, size, 0)
        starts[...] = begun
        locals_.append(copies.local(keys, keys_to))
        locals_.append(copies.local(values, values_to))
        query[pl.ds(own * blk, blk), :] = wq[...]
        out[pl.ds(mp * zrow, zrow), pl.ds(pl.multiple_of(own * blk, blk), blk)] = wo[...]
        locals_.append(copies.local(cot_here, cots.at[0:share, :]))
        for i in range(3):
            locals_.append(copies.local(own_piece[i], tile(mats[i][1], 0, own)))

    def send(name, source, target, mask):
        note(name, copies.swap(source, target, mask))

    tasks = {}

    def task(name, needs, action, *arguments):
        tasks[name] = (needs, lambda: action(*arguments))

    def copy(name, needs, source, target, mask):
        task(name, needs, send, name, source, target, mask)

    task("N", (), norm_rows)
    task("S", ("N",), split_pairs)
    task("o1", (), line, 1, out_block(True), "o1")
    task("o2", ("o1",), line, 2, out_block(False), "o2")
    task("o3", ("o2", "S"), line, 3, out_block(False), "o3")
    for c in range(2):
        task("n1%d" % c, ("N",), line, 1, row_block(c, True), "n1%d" % c)
        task("n2%d" % c, ("n1%d" % c,), line, 2, row_block(c, False), "n2%d" % c)
        task("n3%d" % c, ("n2%d" % c,), line, 3, row_block(c, False), "n3%d" % c)
    copy("qy", (), wq, qrows(own + DEEPER), DEEP)
    copy("qx", (), wq, qrows(own), SIDE)
    copy("qyx", ("qy",), qrows(own + DEEPER), qrows(own + DEEPER), SIDE)
    copy("q", (), wq, qrows(own + OTHER), CORE)
    for name, spot in (("qy", own + DEEPER), ("qx", across), ("qyx", across + DEEPER)):
        copy(name + "C", (name,), qrows(spot), qrows(spot + OTHER), CORE)
    for i, (weight, whole) in enumerate(mats):
        n = "%d" % i
        copy("x" + n, (), weight.at[pl.ds((1 - side) * half, half), :], tile(whole, 0, own), SIDE)
        for kind, needs, source, z, spot in (
                ("O", (), own_piece[i], 0, own), ("X", ("x" + n,), tile(whole, 0, across), 0, across)):
            copy("z" + kind + n, needs, source, tile(whole, 1, spot), Z_HIGH)
            for far, far_needs, far_source, row in (("", needs, source, 0), ("z", ("z" + kind + n,), tile(whole, 1, spot), 1)):
                name = far + kind + n
                copy("y" + name, far_needs, far_source, tile(whole, row, spot + DEEPER), DEEP)
                copy("c" + name, far_needs, far_source, tile(whole, row, spot + OTHER), CORE)
                copy("yc" + name, ("y" + name,), tile(whole, row, spot + DEEPER), tile(whole, row, spot + DEEPER + OTHER), CORE)
    copy("cx", ("N",), cot_here, cots.at[share:2 * share, :], SIDE)
    copy("cz", ("N",), cot_here, cots.at[2 * share:3 * share, :], Z_LOW)
    copy("czx", ("cz",), cots.at[2 * share:3 * share, :], cots.at[3 * share:4 * share, :], SIDE)
    copy("oy", ("o3",), columns(own), columns(own + DEEPER), DEEP)
    copy("ox", ("o3",), columns(own), columns(own), SIDE)
    copy("oyx", ("oy",), columns(own + DEEPER), columns(own + DEEPER), SIDE)
    for name, needs, spot in (("o", "o3", own), ("oy", "oy", own + DEEPER), ("ox", "ox", across), ("oyx", "oyx", across + DEEPER)):
        copy(name + "C", (needs,), columns(spot), columns(spot + OTHER), CORE)
    whole_query = ("q", "qyC", "qxC", "qyxC", "S")
    task("A0", whole_query, attend_tokens, mp)
    for distance in (1, 2, 3):
        task("A%d" % distance, ("A0", "n%d0" % distance, "n%d1" % distance), attend_from, distance)

    def finish_tokens():
        context_own[:, pl.ds(pl.multiple_of(mp * local, local), local)] = context[pl.ds(mp * share, share), :]
        locals_.append(copies.local(rows, rows_out))
        locals_.append(copies.local(queries, queries_to))
        locals_.append(copies.local(out, out_out))

        def project_out(n, carry):
            there = pl.ds(pl.multiple_of(n * 512, 512), 512)
            residual[:, there] = x_here[:, there].astype(f32) + dot(context_own[...], out[:, there], 1, 0)
            return carry

        lax.fori_loop(0, width // 512, project_out, 0)

        def norm_second(i, carry):
            here = pl.ds(i * 32, 32)
            value = residual[here, :]
            inverse = lax.rsqrt(jnp.mean(value * value, axis=-1, keepdims=True) + epsilon)
            normed[here, :] = (value * inverse * gain_two[...]).astype(bf16)
            return carry

        lax.fori_loop(0, share // 32, norm_second, 0)

    task("F", ("A3", "oC", "oyC", "oxC", "oyxC", "A1", "A2"), finish_tokens)

    greet(place, (1, 2, 3, CORE, SIDE, DEEP))
    names = list(tasks)
    for index in FRONT_ORDER or range(len(names)):
        needs, action = tasks.pop(names[index])
        for need in needs:
            for item in items.get(need, ()):
                copies.got(item)
        action()
    assert not tasks
    for local_copy in locals_:
        local_copy.wait()
    copies.finish()


def front_call(x, cot, gain_one, gain_two, wq, wo, wg, wu, wd, pairs, segments, ident):
    share, width = x.shape
    hidden, blk = wd.shape
    seq_len, _, local = pairs.shape
    V = pltpu.VMEM
    S = jax.ShapeDtypeStruct
    return pl.pallas_call(
        front_kernel,
        out_shape=(
            S((seq_len, width), bf16), S((seq_len, width), bf16), S((hidden, width), bf16), S((hidden, width), bf16),
            S((hidden, width), bf16), S((width, width), bf16), S((seq_len, local), bf16), S((share, width), bf16),
            S((local // HEAD_DIM, 1, seq_len), f32), S((share, width), f32), S((share, width), bf16),
            S((share, width), bf16), S((share, width), bf16), S((1, width), f32), S((1, width), f32),
            S((seq_len, local), bf16), S((seq_len, local), bf16), S((1, seq_len), jnp.int32)),
        in_specs=[VM] * 11,
        out_specs=(ANY,) * 7 + (VM,) * 4 + (ANY,) * 2 + (VM,) * 2 + (ANY,) * 2 + (VM,),
        scratch_shapes=[
            V((seq_len, local), bf16), V((share, width), bf16), V((share, width), bf16), V((seq_len, local), bf16),
            V((seq_len, local), bf16),
            V((share, width), bf16), V((seq_len, width), bf16), V((width, local), bf16), V((width, width), bf16),
            V((seq_len, local), bf16), DMA((96,)), DMA((96,)), DMA((12,))],
        compiler_params=params(ident, 60 << 20), name="front",
    )(x, cot, gain_one, gain_two, wq, wo, wg, wu, wd, pairs, segments)


def hidden_cuts(hidden):
    cuts = []
    start = 0
    while start < hidden:
        size = min(512, hidden - start)
        cuts.append((start, size))
        start += size
    return cuts


def ffn_kernel(normed, wq, cots_in, down_in, gate_in, up_in, total, query_0, query_y, fparts_out, sums_out,
               weights, tokens, acts, dparts, relay, landed, fparts,
               send_sems, recv_sems, local_sems, free_sem):
    place = Place()
    share, width = normed.shape
    hidden = down_in.shape[0]
    half = share // 2
    wide = width // 2
    cuts = hidden_cuts(hidden)
    copies = Copies(place, send_sems, recv_sems, local_sems)
    load_cots = copies.local(cots_in, tokens.at[0])
    load_w = [copies.local(w, weights.at[i]) for i, w in enumerate((down_in, gate_in, up_in))]
    mp = place.mp
    local = wq.shape[1]
    greet(place, (1, 2, 3, SIDE, CORE, DEEP))

    def at(quarter, part):
        return tokens.at[1, pl.ds(quarter * share + part * half, half), :]

    a, b = pl.ds(0, half), pl.ds(half, half)
    low_a = copies.swap(normed.at[a, :], at(2, 0), Z_LOW)
    side_b = copies.swap(normed.at[b, :], at(1, 1), SIDE)
    low_b = copies.swap(normed.at[b, :], at(2, 1), Z_LOW)
    side_a = copies.swap(normed.at[a, :], at(1, 0), SIDE)
    tokens[1, 0:share, :] = normed[...]

    def wide_block(source_is_input):
        def get(m):
            target = query_0.at[:, pl.ds(pl.multiple_of(m * local, local), local)]
            return (wq if source_is_input else target), target
        return get

    hops = []
    for hop in (1, 2, 3):
        block_of = wide_block(hop == 1)
        hops.append((
            copies.prepare_step(block_of, mp - (hop - 1), mp - hop, 1, (mp >= hop - 1) & (mp < 3), mp >= hop),
            copies.prepare_step(block_of, mp + (hop - 1), mp + hop, -1,
                                (mp <= 3 - (hop - 1)) & (mp > 0), mp <= 3 - hop)))
    over_deep = copies.prepare(query_0, query_y, DEEP)
    for item in hops[0]:
        copies.start(item)
    query_0[:, pl.ds(pl.multiple_of(mp * local, local), local)] = wq[...]

    def block(r, between):
        here = pl.ds(r * share, share)
        for start, size in cuts:
            rows = tokens[1, here, :]
            gate = dot(rows, weights[1, start:start + size, :], 1, 1)
            up = dot(rows, weights[2, start:start + size, :], 1, 1)
            grad = dot(tokens[0, here, :], weights[0, start:start + size, :], 1, 1)
            sigmoid = jax.nn.sigmoid(gate)
            silu = gate * sigmoid
            acts[0, here, start:start + size] = (silu * up).astype(bf16)
            acts[1, here, start:start + size] = (
                grad * up * sigmoid * (1.0 + gate * (1.0 - sigmoid))).astype(bf16)
            acts[2, here, start:start + size] = (grad * silu).astype(bf16)

        between()

        def columns(n, carry):
            there = pl.ds(pl.multiple_of(n * 512, 512), 512)
            dparts[here, there] = (dot(acts[1, here, :], weights[1, :, there], 1, 0)
                                   + dot(acts[2, here, :], weights[2, :, there], 1, 0)).astype(bf16)
            fparts[here, there] = dot(acts[0, here, :], weights[0, :, there], 1, 0).astype(bf16)
            return carry

        lax.fori_loop(0, width // 512, columns, 0)

    for copy in load_w:
        copy.wait()
    load_cots.wait()
    got = {"across": None}

    def pass_on(r, turn, landed_hop, next_hop):
        @pl.when(r == turn)
        def _():
            for item in landed_hop:
                copies.received(item)
            for item in next_hop:
                copies.start(item)

    def step(r, carry):
        @pl.when(r == 1)
        def _():
            low_a["copy"].wait_recv()
            side_b["copy"].wait_recv()
            forward[0].start()
            forward[1].start()
            side_a["copy"].wait_recv()
            low_b["copy"].wait_recv()

        @pl.when(r == 2)
        def _():
            forward[0].wait_recv()
            forward[1].wait_recv()

        pass_on(r, 2, hops[0], hops[1])
        pass_on(r, 3, hops[2], (over_deep,))

        @pl.when(r == 3)
        def _():
            reduce.start_across()
        block(jnp.where(r < 2, r, 5 - r), lambda: pass_on(r, 2, hops[1], hops[2]))
        return carry

    reduce = QuadReduce(copies, dparts, relay, landed)
    reduce.prepare()

    forward = [copies.describe(at(2, 0), at(3, 0), place.partner(SIDE), copies.count),
               copies.describe(at(1, 1), at(3, 1), place.partner(Z_LOW), copies.count + 1)]
    copies.count += 2
    lax.fori_loop(0, 4, step, 0)
    for item in (low_a, side_b, low_b, side_a):
        item["got"] = True
    pl.semaphore_signal(free_sem, inc=1, device_id=place.partner(CORE), device_id_type=MESH)
    reduce.start_rest()
    save = copies.local(fparts, fparts_out)

    base = copies.count
    copies.count += 3

    def give_copy(i):
        return copies.describe(weights.at[i, :, pl.ds(0, wide)], weights.at[i, :, pl.ds(wide, wide)],
                               place.partner(CORE), base + i)

    def give(i, carry):
        right = tokens[jnp.minimum(i, 1), :, wide:]
        for start, size in cuts:
            weights[i, start:start + size, 0:wide] = dot(
                acts[i, :, start:start + size], right, 0, 0).astype(bf16)

        @pl.when(i == 0)
        def _():
            pl.semaphore_wait(free_sem, 1)
        give_copy(i).start()

        @pl.when(i == 0)
        def _():
            reduce.relayed_low()

        @pl.when(i == 1)
        def _():
            reduce.relayed_side()
        return carry

    lax.fori_loop(0, 3, give, 0)

    def keep(i, carry):
        give_copy(i).wait_recv()
        right = tokens[jnp.minimum(i, 1), :, 0:wide]
        for start, size in cuts:
            rows = slice(start, start + size)
            weights[i, rows, wide:] = (dot(acts[i, :, rows], right, 0, 0)
                                       + weights[i, rows, wide:].astype(f32)).astype(bf16)
        pltpu.make_async_copy(weights.at[i, :, pl.ds(wide, wide)], sums_out.at[i], local_sems.at[5 + i]).start()
        return carry

    lax.fori_loop(0, 3, keep, 0)
    reduce.arrived()

    def one(i, carry):
        here = pl.ds(i * 32, 32)
        total[here, :] = (dparts[here, :].astype(f32) + landed[0, here, :].astype(f32)
                          + landed[1, here, :].astype(f32))
        return carry

    lax.fori_loop(0, share // 32, one, 0)
    for i in range(3):
        give_copy(i).wait_send()
        pltpu.make_async_copy(weights.at[i, :, pl.ds(wide, wide)], sums_out.at[i], local_sems.at[5 + i]).wait()
    for copy in forward:
        copy.wait_send()
    save.wait()
    copies.finish()


def ffn_call(normed, wq, cots, down, gate, up, ident):
    share, width = normed.shape
    hidden = down.shape[0]
    V = pltpu.VMEM
    flops = 2 * share * 4 * width * hidden * 9
    return pl.pallas_call(
        ffn_kernel,
        out_shape=(jax.ShapeDtypeStruct((share, width), f32), jax.ShapeDtypeStruct((share, width), bf16),
                   jax.ShapeDtypeStruct((share, width), bf16), jax.ShapeDtypeStruct((share * 4, width), bf16),
                   jax.ShapeDtypeStruct((3, hidden, width // 2), bf16)),
        in_specs=[VM] * 2 + [ANY] * 4,
        out_specs=(VM, VM, VM, ANY, ANY),
        scratch_shapes=[
            V((3, hidden, width), bf16), V((2, share * 4, width), bf16), V((3, share * 4, hidden), bf16),
            V((share * 4, width), bf16), V((2, share // 2, width), bf16), V((2, share, width), bf16),
            V((share * 4, width), bf16),
            DMA((24,)), DMA((24,)), DMA((8,)), pltpu.SemaphoreType.REGULAR],
        compiler_params=params(ident, 63 << 20),
        cost_estimate=pl.CostEstimate(flops=flops, bytes_accessed=40 << 20, transcendentals=share * 4 * hidden),
        name="feed_forward",
    )(normed, wq, cots, down, gate, up)


def back_first_kernel(dn2, residual, cot, gain, lse, starts, context_in, queries_in, keys_in, values_in,
                      query_0, query_y, out_whole, sums,
                      dres_out, gain_part, query_x, query_xy, grad_q, pairs_out, down_sums, gate_sums, sums_out,
                      context, queries, keys, values, dres, pairs, out_sums, heads, keep_d, deep_d, high_d, deep_g, grad_low, wout, dctx, give_o, core_o, dk, dv,
                      send_sems, recv_sems, local_sems):
    place = Place()
    mp = place.mp
    share, width = dn2.shape
    hidden = keep_d.shape[0]
    half = hidden // 2
    local = heads.shape[1]
    wide = width // 2
    quarter = wide // 2
    blk = quarter // 2
    copies = Copies(place, send_sems, recv_sems, local_sems)
    loads = [copies.local(out_whole.at[pl.ds(z * local, local), :], wout.at[z]) for z in range(4)]
    load_d = copies.local(sums.at[0, :, pl.ds(0, quarter)], keep_d)
    late = [copies.local(*pair) for pair in ((context_in, context), (queries_in, queries), (keys_in, keys),
                                             (values_in, values))]
    load_g = copies.local(sums.at[1, :, pl.ds(0, blk)], gate_sums)
    greet(place, (1, 2, 3, CORE, SIDE, DEEP))
    in_d = [copies.swap(sums.at[0, :, pl.ds(quarter + x * blk, blk)], deep_d.at[:, pl.ds(x * blk, blk)], DEEP)
            for x in (0, 1)]
    copies.swap(query_0, query_x, SIDE)
    copies.swap(query_y, query_xy, SIDE)
    gain_part[...] = jnp.zeros_like(gain_part)

    def norm(i, carry):
        here = pl.ds(i * 32, 32)
        value = residual[here, :]
        inverse = lax.rsqrt(jnp.mean(value * value, axis=-1, keepdims=True) + epsilon)
        scaled = value * inverse
        grad = dn2[here, :]
        grad_scaled = grad * gain[...]
        back = inverse * (grad_scaled - scaled * jnp.mean(grad_scaled * scaled, axis=-1, keepdims=True))
        total = cot[here, :].astype(f32) + back
        dres[here, :] = total
        grad_low[here, :] = total.astype(bf16)
        gain_part[...] += jnp.sum(grad * scaled, axis=0, keepdims=True)
        return carry

    lax.fori_loop(0, share // 32, norm, 0)
    saves = [copies.local(dres, dres_out)]
    for copy in loads + late:
        copy.wait()
    heads_in = []
    for mask in (2, 3, 1, 0):
        other = place.partner(mask)[1]
        there = pl.ds(pl.multiple_of(other * local, local), local)
        piece = dot(grad_low[...], wout[other], 1, 1).astype(bf16)
        if mask:
            dctx[:, there] = piece
            heads_in.append(copies.swap(dctx.at[:, there], heads.at[pl.ds(mp * share, share), :], mask))
        else:
            heads[pl.ds(mp * share, share), :] = piece
    chunks = width // 512
    base = copies.count
    copies.count += chunks

    def core_copy(n):
        rows = pl.ds(pl.multiple_of(n * 512, 512), 512)
        return copies.describe(give_o.at[rows, :], core_o.at[rows, :], place.partner(CORE), base + n)

    def give(n, carry):
        rows = pl.ds(pl.multiple_of(n * 512, 512), 512)
        give_o[rows, :] = dot(context[:, rows], grad_low[:, wide:], 0, 0).astype(bf16)
        core_copy(n).start()
        return carry

    lax.fori_loop(0, chunks, give, 0)

    def keep(n, carry):
        rows = pl.ds(pl.multiple_of(n * 512, 512), 512)
        core_copy(n).wait_recv()
        out_sums[rows, :] = (dot(context[:, rows], grad_low[:, :wide], 0, 0)
                             + core_o[rows, :].astype(f32)).astype(bf16)
        return carry

    lax.fori_loop(0, chunks, keep, 0)
    saves.append(copies.local(out_sums, sums_out))
    in_g = copies.swap(sums.at[1, :, pl.ds(quarter, blk)], deep_g, DEEP)
    load_d.wait()
    give_rows = pl.ds(half, half)
    across = []
    for x in (0, 1):
        there = pl.ds(x * blk, blk)
        copies.got(in_d[x])
        add_into(keep_d.at[:, there], (half, half), deep_d.at[give_rows, there], step=16)
        across.append(copies.swap(keep_d.at[give_rows, there], high_d.at[:, there], Z_HIGH))
        add_into(keep_d.at[:, there], (0, half), deep_d.at[:, there], step=16)
    for item in heads_in:
        copies.got(item)

    def one_head(h, carry):
        attend_head_back(h, starts, queries, keys, values, heads, lse, grad_q, pairs, dk, dv)
        return carry

    lax.fori_loop(0, local // HEAD_DIM, one_head, 0)
    saves.append(copies.local(pairs, pairs_out))
    load_g.wait()
    copies.got(in_g)
    add_into(gate_sums, (0, hidden), deep_g)
    for x in (0, 1):
        copies.got(across[x])

    def add_d(n, carry):
        rows = pl.ds(n * 16, 16)
        down_sums[rows, :] = (keep_d[rows, :].astype(f32) + high_d[rows, :].astype(f32)).astype(bf16)
        return carry

    lax.fori_loop(0, half // 16, add_d, 0)
    for copy in saves:
        copy.wait()
    copies.finish()

    def sent(n, carry):
        core_copy(n).wait_send()
        return carry

    lax.fori_loop(0, chunks, sent, 0)


def back_first(dn2, residual, cot, gain, context, queries, keys, values, lse, starts, query_0, query_y,
               out_whole, sums, ident):
    share, width = dn2.shape
    hidden = sums.shape[1]
    half = hidden // 2
    seq_len, local = queries.shape
    quarter = width // 4
    V = pltpu.VMEM
    S = jax.ShapeDtypeStruct
    return pl.pallas_call(
        back_first_kernel,
        out_shape=(S((share, width), f32), S((1, width), f32), S(query_0.shape, bf16), S(query_0.shape, bf16),
                   S((seq_len, local), bf16), S((seq_len, 2, local), f32),
                   S((half, quarter), bf16), S((hidden, quarter // 2), bf16), S((width, width // 2), bf16)),
        in_specs=[VM] * 6 + [ANY] * 8,
        out_specs=(ANY, VM, ANY, ANY, VM, ANY, VM, VM, ANY),
        scratch_shapes=[
            V((share, width), bf16), V((seq_len, local), bf16), V((seq_len, local), bf16), V((seq_len, local), bf16),
            V((share, width), f32), V((seq_len, 2, local), f32), V((width, width // 2), bf16),
            V((seq_len, local), bf16), V((hidden, quarter), bf16), V((hidden, quarter), bf16), V((half, quarter), bf16),
            V((hidden, quarter // 2), bf16), V((share, width), bf16),
            V((4, width // 4, width), bf16), V((share, width), bf16), V((width, width // 2), bf16),
            V((width, width // 2), bf16), V((seq_len, HEAD_DIM), f32), V((seq_len, HEAD_DIM), f32),
            DMA((20,)), DMA((20,)), DMA((13,))],
        compiler_params=params(ident, 63 << 20), name="back_first",
    )(dn2, residual, cot, gain, lse, starts, context, queries, keys, values, query_0, query_y, out_whole, sums)


BACK_ORDER = (
    3, 0, 10, 5, 9, 7, 12, 17, 4, 6, 1, 13, 22, 2, 14, 15, 18, 19, 21, 11, 8, 16, 24, 23, 28, 34, 25, 26,
    27, 20, 30, 31, 32, 36, 29, 35, 33,
)


def back_last_kernel(grad_q, gain, gain_part, dres_in, inputs_in, residual_in, query_0, query_y, query_x, query_xy,
                     rows_first, sums, down_sums, gate_sums, out_sums, fparts,
                     down_to, gate_to, up, out, query, input_to, output_to, gains,
                     dres, inputs, residual, near, down, gate, grad_input, output, keep_d, keep_g, keep_u, deep_g, deep_u, high_g, high_u, side_f,
                     own_o, deep_o, side_o, z_o,
                     give_q, own_q, core_q, side_q, deep_q, parts, relay, landed,
                     grad_own, rows, query_far, dn1, gain_rows, gains_got,
                     send_sems, recv_sems, local_sems):
    place = Place()
    mp = place.mp
    side = place.bit(SIDE)
    share, width = dres.shape
    hidden, blk = up.shape
    half = hidden // 2
    local = grad_q.shape[1]
    zrow = out.shape[0]
    saves = []
    quarter = 2 * blk
    wide = width // 2
    copies = Copies(place, send_sems, recv_sems, local_sems)
    load_rows = copies.local(rows_first, rows)
    load_g = copies.local(gate_sums, keep_g.at[:, pl.ds(0, blk)])
    load_h = copies.local(sums.at[1, :, pl.ds(blk, blk)], keep_g.at[:, pl.ds(blk, blk)])
    load_d = copies.local(down_sums, keep_d)
    load_o = copies.local(out_sums, own_o)
    load_u = copies.local(sums.at[2, :, pl.ds(0, quarter)], keep_u)
    load_p = copies.local(fparts, parts)
    near_in = (query_0, query_y, query_x, query_xy)
    load_near = [copies.local(piece, near.at[n]) for n, piece in enumerate(near_in)]
    load_late = [copies.local(*pair) for pair in ((dres_in, dres), (inputs_in, inputs), (residual_in, residual))]
    spot_of = (side, side + 2, 1 - side, 3 - side)
    give_rows = pl.ds(half, half)
    mine = pl.ds(pl.multiple_of(side * blk, blk), blk)
    theirs = pl.ds(pl.multiple_of((1 - side) * blk, blk), blk)
    spots = [pl.ds(pl.multiple_of(absolute(place, s) * blk, blk), blk) for s in range(8)]
    reduce = QuadReduce(copies, parts, relay, landed)
    items = {}
    tasks = {}
    loaded = set()

    def note(name, *copied):
        items[name] = list(copied)

    def task(name, needs, action, *arguments):
        tasks[name] = (needs, lambda: action(*arguments))

    def ready(name, *loads):
        if name not in loaded:
            loaded.add(name)
            for load in loads:
                load.wait()

    def block_o(deep, column):
        return own_o.at[:, pl.ds(pl.multiple_of((2 * deep + column) * blk, blk), blk)]

    def rows_q(deep, column):
        return pl.ds(pl.multiple_of((2 * deep + column) * blk, blk), blk)

    def send_tokens():
        sent = []
        for mask in (2, 3, 1):
            other = place.partner(mask)[1]
            sent.append(copies.swap(grad_q.at[pl.ds(other * share, share), :],
                                    grad_own.at[:, pl.ds(mp * local, local)], mask))
        note("dq", *sent)
        grad_own[:, pl.ds(pl.multiple_of(mp * local, local), local)] = grad_q[pl.ds(mp * share, share), :]

    def send_up(x):
        note("u%d" % x, copies.swap(sums.at[2, :, pl.ds(quarter + x * blk, blk)], deep_u.at[:, pl.ds(x * blk, blk)], DEEP))

    def send_near():
        note("f", *[copies.swap(piece, query_far.at[n], CORE) for n, piece in enumerate(near_in)])

    def send_gate():
        ready("g", load_g)
        there = pl.ds(0, blk)
        note("zg0", copies.swap(keep_g.at[give_rows, there], high_g.at[:, there], Z_HIGH))

    def send_gate_deep():
        note("g1", copies.swap(sums.at[1, :, pl.ds(quarter + blk, blk)], deep_g, DEEP))

    def gate_sum():
        ready("h", load_h)
        there = pl.ds(blk, blk)
        add_into(keep_g.at[:, there], (half, half), deep_g.at[give_rows, :], step=16)
        note("zg1", copies.swap(keep_g.at[give_rows, there], high_g.at[:, there], Z_HIGH))
        add_into(keep_g.at[:, there], (0, half), deep_g, step=16)

    def send_down():
        ready("d", load_d)
        note("xd", copies.swap(keep_d.at[:, theirs], side_f.at[0], SIDE))

    def send_out(name, n, x):
        ready("o", load_o)
        note(name, copies.swap(block_o(1, x), deep_o.at[n], DEEP))

    def product(first):
        ready("w", load_rows)
        return dot(rows[:, first:first + wide], grad_q[...], 0, 0)

    def query_give():
        give_q[...] = product(wide).astype(bf16)
        note("qc", copies.swap(give_q, core_q, CORE))

    def query_keep():
        own_q[...] = (product(0) + core_q[...].astype(f32)).astype(bf16)
        for y in (1, 0):
            note("qs%d" % y, copies.swap(own_q.at[rows_q(y, 1 - side), :], side_q.at[y], SIDE))

    def query_side(y):
        here = rows_q(y, side)
        own_q[here, :] = (own_q[here, :].astype(f32) + side_q[y].astype(f32)).astype(bf16)
        if y:
            note("qd", copies.swap(own_q.at[here, :], deep_q, DEEP))

    def query_done():
        query[...] = own_q[rows_q(0, side), :].astype(f32) + deep_q[...].astype(f32)

    def reduce_start():
        ready("p", load_p)
        reduce.start()
        note("r1", reduce.first, reduce.second)

    def first_product():
        for load in load_near:
            load.wait()
        for n in range(4):
            dn1[:, pl.ds(pl.multiple_of(spot_of[n] * blk, blk), blk)] = dot(grad_own[...], near[n], 1, 1)
            dn1[:, pl.ds(pl.multiple_of((spot_of[n] + 4) * blk, blk), blk)] = dot(grad_own[...], query_far[n], 1, 1)

    def first_norm():
        ready("v", *load_late)
        gain_rows[0:1, :] = jnp.zeros((1, width), f32)
        gain_rows[1:2, :] = gain_part[...]

        def norm(i, carry):
            here = pl.ds(i * 32, 32)
            value = inputs[here, :].astype(f32)
            inverse = lax.rsqrt(jnp.mean(value * value, axis=-1, keepdims=True) + epsilon)
            scaled = value * inverse
            grad = dn1[here, :]
            grad_scaled = grad * gain[...]
            back = inverse * (grad_scaled - scaled * jnp.mean(grad_scaled * scaled, axis=-1, keepdims=True))
            total = dres[here, :] + back
            for s in range(8):
                grad_input[here, spots[s]] = total[:, s * blk:(s + 1) * blk]
            gain_rows[0:1, :] += jnp.sum(grad * scaled, axis=0, keepdims=True)
            return carry

        lax.fori_loop(0, share // 32, norm, 0)
        saves.append(copies.local(grad_input, input_to))
        for s in range(8):
            gains[:, spots[s]] = gain_rows[:, s * blk:(s + 1) * blk]

    gain_masks = (1, 2, CORE, SIDE, DEEP)

    def gain_hop(n):
        if n:
            item = items["h%d" % (n - 1)][0]
            item["copy"].wait_send()
            item["sent"] = True
            gains[...] = gains[...] + gains_got[n - 1]
        if n < len(gain_masks):
            note("h%d" % n, copies.swap(gains, gains_got.at[n], gain_masks[n]))

    def up_sum(x):
        ready("u", load_u)
        there = pl.ds(x * blk, blk)
        add_into(keep_u.at[:, there], (half, half), deep_u.at[give_rows, there], step=16)
        note("zu%d" % x, copies.swap(keep_u.at[give_rows, there], high_u.at[:, there], Z_HIGH))
        add_into(keep_u.at[:, there], (0, half), deep_u.at[:, there], step=16)

    def high_sum(name, keep, high, i):
        add_into(keep.at[:, theirs], (0, half), high.at[:, theirs], step=16)
        note(name, copies.swap(keep.at[pl.ds(0, half), theirs], side_f.at[i], SIDE))
        add_into(keep.at[:, mine], (0, half), high.at[:, mine], step=16)

    def out_side():
        add_into(block_o(0, 1 - side), (0, width), deep_o.at[0])
        note("os", copies.swap(block_o(0, 1 - side), side_o, SIDE))

    def out_mine():
        add_into(block_o(0, side), (0, width), deep_o.at[1])

    def out_rows():
        add_into(block_o(0, side), (0, width), side_o)
        note("oz", *[copies.swap(own_o.at[pl.ds(place.partner(mask)[1] * zrow, zrow), mine], z_o.at[n], mask)
                     for n, mask in enumerate((2, 3, 1))])

    def out_done():
        def add_z(i, carry):
            here = pl.ds(i * 32, 32)
            sum_ = own_o[pl.ds(mp * zrow + i * 32, 32), mine].astype(f32)
            for n in range(3):
                sum_ = sum_ + z_o[n, here, :].astype(f32)
            out[here, :] = sum_
            return carry

        lax.fori_loop(0, zrow // 32, add_z, 0)

    def output_done():
        ready("v", *load_late)
        reduce.arrived()

        def finish_output(i, carry):
            here = pl.ds(i * 32, 32)
            total = (residual[here, :] + parts[here, :].astype(f32) + landed[0, here, :].astype(f32)
                     + landed[1, here, :].astype(f32)).astype(bf16)
            for s in range(8):
                output[here, spots[s]] = total[:, s * blk:(s + 1) * blk]
            return carry

        lax.fori_loop(0, share // 32, finish_output, 0)
        saves.append(copies.local(output, output_to))

    def weight_done(i, target, keep, final):
        def write(n, carry):
            target[pl.ds(side * half + n * 16, 16), :] = keep[pl.ds(n * 16, 16), mine].astype(f32)
            target[pl.ds((1 - side) * half + n * 16, 16), :] = side_f[i, pl.ds(n * 16, 16), :].astype(f32)
            return carry

        lax.fori_loop(0, half // 16, write, 0)
        if final is not None:
            saves.append(copies.local(target, final))

    task("dq", (), send_tokens)
    task("g1", (), send_gate_deep)
    task("u0", (), send_up, 0)
    task("u1", (), send_up, 1)
    task("f", (), send_near)
    task("zg0", (), send_gate)
    task("xd", (), send_down)
    task("ot", (), send_out, "ot", 0, 1 - side)
    task("om", (), send_out, "om", 1, side)
    task("qc", (), query_give)
    task("r1", (), reduce_start)
    task("zg1", ("g1",), gate_sum)
    task("qk", ("qc",), query_keep)
    task("dn1", ("f", "dq"), first_product)
    task("N", ("dn1",), first_norm)
    task("h0", ("N",), gain_hop, 0)
    task("zu0", ("u0",), up_sum, 0)
    task("zu1", ("u1",), up_sum, 1)
    task("r2", ("r1",), reduce.relayed)
    task("h1", ("h0",), gain_hop, 1)
    task("qy1", ("qk", "qs1"), query_side, 1)
    task("qy0", ("qk", "qs0"), query_side, 0)
    task("os", ("ot",), out_side)
    task("h2", ("h1",), gain_hop, 2)
    task("xg", ("zg0", "zg1"), high_sum, "xg", keep_g, high_g, 1)
    task("h3", ("h2",), gain_hop, 3)
    task("O", ("om",), out_mine)
    task("h4", ("h3",), gain_hop, 4)
    task("R", ("r2",), output_done)
    task("h5", ("h4",), gain_hop, 5)
    task("oz", ("os", "O"), out_rows)
    task("Q", ("qy1", "qy0", "qd"), query_done)
    task("xu", ("zu0", "zu1"), high_sum, "xu", keep_u, high_u, 2)
    task("OD", ("oz",), out_done)
    task("DD", ("xd",), weight_done, 0, down, keep_d, down_to)
    task("GD", ("xg",), weight_done, 1, gate, keep_g, gate_to)
    task("UD", ("xu",), weight_done, 2, up, keep_u, None)
    greet(place, (1, 2, 3, CORE, SIDE, DEEP))
    names = list(tasks)
    for index in BACK_ORDER or range(len(names)):
        needs, action = tasks.pop(names[index])
        for need in needs:
            for item in items.get(need, ()):
                copies.got(item)
        action()
    assert not tasks
    for copy in saves:
        copy.wait()
    copies.finish()


def back_last(grad_q, dres, inputs, gain, query_0, query_y, query_x, query_xy, residual, gain_part,
              rows_first, sums, down_sums, gate_sums, out_sums, fparts, ident):
    share, width = dres.shape
    hidden = sums.shape[1]
    blk = width // 8
    half = hidden // 2
    local = grad_q.shape[1]
    V = pltpu.VMEM
    S = jax.ShapeDtypeStruct
    return pl.pallas_call(
        back_last_kernel,
        out_shape=(S((hidden, blk), f32),) * 3
        + (S((width // 4, blk), f32), S((blk, local), f32), S((share, width), f32), S((share, width), bf16),
           S((2, width), f32)),
        in_specs=[VM] * 3 + [ANY] * 13,
        out_specs=(ANY, ANY, VM, VM, VM, ANY, ANY, VM),
        scratch_shapes=[
            V((share, width), f32), V((share, width), bf16), V((share, width), f32), V((4, blk, width), bf16),
            V((hidden, blk), f32), V((hidden, blk), f32), V((share, width), f32), V((share, width), bf16),
            V((half, 2 * blk), bf16), V((hidden, 2 * blk), bf16), V((hidden, 2 * blk), bf16), V((hidden, blk), bf16),
            V((hidden, 2 * blk), bf16),
            V((half, 2 * blk), bf16), V((half, 2 * blk), bf16), V((3, half, blk), bf16),
            V((width, width // 2), bf16), V((2, width, blk), bf16), V((width, blk), bf16),
            V((3, width // 4, blk), bf16),
            V((width // 2, local), bf16), V((width // 2, local), bf16), V((width // 2, local), bf16),
            V((2, blk, local), bf16), V((blk, local), bf16),
            V((share * 4, width), bf16), V((2, share // 2, width), bf16), V((2, share, width), bf16),
            V((share, width), bf16), V((share * 4, width), bf16), V((4, blk, width), bf16), V((share, width), f32),
            V((2, width), f32), V((5, 2, width), f32),
            DMA((48,)), DMA((48,)), DMA((20,))],
        compiler_params=params(ident, 63 << 20), name="back_last",
    )(grad_q, gain, gain_part, dres, inputs, residual, query_0, query_y, query_x, query_xy,
      rows_first, sums, down_sums, gate_sums, out_sums, fparts)


def hand_over_kernel(*refs):
    count = (len(refs) - 2) // 3
    sources, targets, held = refs[:count], refs[count:2 * count], refs[2 * count:3 * count]
    in_sems, out_sems = refs[-2:]
    loads = [pltpu.make_async_copy(sources[n], held[n], in_sems.at[n]) for n in range(count)]
    stores = [pltpu.make_async_copy(held[n], targets[n], out_sems.at[n]) for n in range(count)]
    for load in loads:
        load.start()
    for load, store in zip(loads, stores):
        load.wait()
        store.start()
    for store in stores:
        store.wait()


def hand_over(*arrays):
    n = len(arrays)
    return pl.pallas_call(
        hand_over_kernel, out_shape=tuple(jax.ShapeDtypeStruct(a.shape, a.dtype) for a in arrays),
        in_specs=[ANY] * n, out_specs=(ANY,) * n,
        scratch_shapes=[pltpu.VMEM(a.shape, a.dtype) for a in arrays] + [DMA((n,)), DMA((n,))],
        compiler_params=pltpu.CompilerParams(vmem_limit_bytes=63 << 20), name="hand_over")(*arrays)


def contract(left, right, left_dim, right_dim):
    return lax.dot_general(
        left, right, (((left_dim,), (right_dim,)), ((), ())), preferred_element_type=jnp.float32
    )


def root_inverse(values):
    return lax.rsqrt(jnp.mean(values * values, axis=-1, keepdims=True) + epsilon)


def norm_back(grad_normed, scaled, inverse, gain):
    grad_scaled = grad_normed * gain
    grad_values = inverse * (
        grad_scaled - scaled * jnp.mean(grad_scaled * scaled, axis=-1, keepdims=True)
    )
    return (grad_values, jnp.sum(grad_normed * scaled, axis=0))


def plain_body(
    inputs,
    keys_values,
    segment_ids,
    gain_first,
    gain_second,
    w_query,
    w_out,
    w_gate,
    w_up,
    w_down,
    cotangent,
):
    query_full, out_full = (
        lax.all_gather(w_query, "dp", axis=0, tiled=True),
        lax.all_gather(w_out, "dp", axis=1, tiled=True),
    )
    gate_full, up_full, down_full = (
        lax.all_gather(w_gate, "dp", axis=0, tiled=True),
        lax.all_gather(w_up, "dp", axis=0, tiled=True),
        lax.all_gather(w_down, "dp", axis=1, tiled=True),
    )
    tokens = inputs.astype(jnp.float32)
    inverse_first = root_inverse(tokens)
    scaled_first = tokens * inverse_first
    normed_first = (scaled_first * gain_first).astype(jnp.bfloat16)
    rows_first = lax.all_gather(normed_first, "mp", axis=0, tiled=True)
    queries = contract(rows_first, query_full, 1, 0).astype(jnp.bfloat16)
    seq_len = rows_first.shape[0]
    local_width = queries.shape[1]
    head_count = local_width // HEAD_DIM
    block_rows = min(512, seq_len)
    block_count = seq_len // block_rows
    score_scale = HEAD_DIM ** (-0.5)
    key_heads = keys_values[:, 0, :].reshape(seq_len, head_count, HEAD_DIM)
    value_heads = keys_values[:, 1, :].reshape(seq_len, head_count, HEAD_DIM)
    segments = segment_ids[0]
    key_pos = jnp.arange(seq_len, dtype=jnp.int32)

    def block_scores(first_row):
        query_block = lax.dynamic_slice_in_dim(queries, first_row, block_rows, 0).reshape(
            block_rows, head_count, HEAD_DIM
        )
        scores = (
            jnp.einsum("qhd,khd->hqk", query_block, key_heads, preferred_element_type=jnp.float32)
            * score_scale
        )
        query_pos = first_row + jnp.arange(block_rows, dtype=jnp.int32)
        query_seg = lax.dynamic_slice_in_dim(segments, first_row, block_rows, 0)
        allowed = (query_pos[:, None] >= key_pos[None, :]) & (
            query_seg[:, None] == segments[None, :]
        )
        return (query_block, jnp.where(allowed[None], scores, -1e30))

    def forward_block(block_index):
        query_block, scores = block_scores(block_index * block_rows)
        row_max = jnp.max(scores, axis=-1, keepdims=True)
        raised = jnp.exp(scores - row_max)
        row_total = jnp.sum(raised, axis=-1, keepdims=True)
        weights_low = (raised / row_total).astype(jnp.bfloat16)
        blended = jnp.einsum(
            "hqk,khd->qhd", weights_low, value_heads, preferred_element_type=jnp.float32
        )
        return (
            blended.reshape(block_rows, local_width).astype(jnp.bfloat16),
            (row_max + jnp.log(row_total))[..., 0],
        )

    context_blocks, log_totals = lax.map(forward_block, jnp.arange(block_count, dtype=jnp.int32))
    context = context_blocks.reshape(seq_len, local_width)
    attn_part = lax.psum_scatter(
        contract(context, out_full, 1, 0), "mp", scatter_dimension=0, tiled=True
    )
    residual = tokens + attn_part
    inverse_second = root_inverse(residual)
    scaled_second = residual * inverse_second
    normed_second = (scaled_second * gain_second).astype(jnp.bfloat16)
    rows_second = lax.all_gather(normed_second, "mp", axis=0, tiled=True)
    gate_proj = contract(rows_second, gate_full, 1, 0)
    up_proj = contract(rows_second, up_full, 1, 0)
    sigmoid_gate = jax.nn.sigmoid(gate_proj)
    silu_gate = gate_proj * sigmoid_gate
    hidden = (silu_gate * up_proj).astype(jnp.bfloat16)
    ffn_part = lax.psum_scatter(
        contract(hidden, down_full, 1, 0).astype(jnp.bfloat16),
        "mp",
        scatter_dimension=0,
        tiled=True,
    ).astype(jnp.float32)
    output = (residual + ffn_part).astype(jnp.bfloat16)
    cot_rows = lax.all_gather(cotangent, "mp", axis=0, tiled=True)
    grad_down_w = contract(hidden, cot_rows, 0, 0)
    grad_hidden = contract(cot_rows, down_full, 1, 1)
    grad_gate_act = (
        grad_hidden * up_proj * sigmoid_gate * (1.0 + gate_proj * (1.0 - sigmoid_gate))
    ).astype(jnp.bfloat16)
    grad_up_act = (grad_hidden * silu_gate).astype(jnp.bfloat16)
    grad_gate_w = contract(rows_second, grad_gate_act, 0, 0)
    grad_up_w = contract(rows_second, grad_up_act, 0, 0)
    grad_normed_second = lax.psum_scatter(
        contract(grad_gate_act, gate_full, 1, 1) + contract(grad_up_act, up_full, 1, 1),
        "mp",
        scatter_dimension=0,
        tiled=True,
    )
    grad_from_norm, gain_second_part = norm_back(
        grad_normed_second, scaled_second, inverse_second, gain_second
    )
    grad_residual = cotangent.astype(jnp.float32) + grad_from_norm
    attn_cot = lax.all_gather(grad_residual.astype(jnp.bfloat16), "mp", axis=0, tiled=True)
    grad_out_w = contract(context, attn_cot, 0, 0)
    grad_context = contract(attn_cot, out_full, 1, 1).astype(jnp.bfloat16)

    def backward_block(state_pair, block_index):
        grad_keys, grad_values = state_pair
        first_row = block_index * block_rows
        query_block, scores = block_scores(first_row)
        log_total = lax.dynamic_index_in_dim(log_totals, block_index, 0, keepdims=False)
        weights = jnp.exp(scores - log_total[..., None])
        grad_block = lax.dynamic_slice_in_dim(grad_context, first_row, block_rows, 0).reshape(
            block_rows, head_count, HEAD_DIM
        )
        grad_weights = jnp.einsum(
            "qhd,khd->hqk", grad_block, value_heads, preferred_element_type=jnp.float32
        )
        spread = jnp.sum(weights * grad_weights, axis=-1, keepdims=True)
        grad_scores = (weights * (grad_weights - spread)).astype(jnp.bfloat16)
        grad_query_block = (
            jnp.einsum("hqk,khd->qhd", grad_scores, key_heads, preferred_element_type=jnp.float32)
            * score_scale
        ).astype(jnp.bfloat16)
        grad_keys = (
            grad_keys
            + jnp.einsum(
                "hqk,qhd->khd", grad_scores, query_block, preferred_element_type=jnp.float32
            )
            * score_scale
        )
        grad_values = grad_values + jnp.einsum(
            "hqk,qhd->khd",
            weights.astype(jnp.bfloat16),
            grad_block,
            preferred_element_type=jnp.float32,
        )
        return ((grad_keys, grad_values), grad_query_block.reshape(block_rows, local_width))

    zero_state = jnp.zeros((seq_len, head_count, HEAD_DIM), jnp.float32)
    (grad_keys, grad_values), grad_query_blocks = lax.scan(
        backward_block, (zero_state, zero_state), jnp.arange(block_count, dtype=jnp.int32)
    )
    grad_queries = grad_query_blocks.reshape(seq_len, local_width)
    grad_kv = jnp.stack(
        [grad_keys.reshape(seq_len, local_width), grad_values.reshape(seq_len, local_width)], axis=1
    )
    grad_query_w = contract(rows_first, grad_queries, 0, 0)
    grad_normed_first = lax.psum_scatter(
        contract(grad_queries, query_full, 1, 1).astype(jnp.bfloat16),
        "mp",
        scatter_dimension=0,
        tiled=True,
    ).astype(jnp.float32)
    grad_from_first, gain_first_part = norm_back(
        grad_normed_first, scaled_first, inverse_first, gain_first
    )
    grad_input = grad_residual + grad_from_first
    gain_first_sum, gain_second_sum = lax.psum((gain_first_part, gain_second_part), ("dp", "mp"))
    query_shard, out_shard, gate_shard, up_shard, down_shard = (
        lax.psum_scatter(
            grad_query_w.astype(jnp.bfloat16), "dp", scatter_dimension=0, tiled=True
        ).astype(jnp.float32),
        lax.psum_scatter(
            grad_out_w.astype(jnp.bfloat16), "dp", scatter_dimension=1, tiled=True
        ).astype(jnp.float32),
        lax.psum_scatter(
            grad_gate_w.astype(jnp.bfloat16), "dp", scatter_dimension=0, tiled=True
        ).astype(jnp.float32),
        lax.psum_scatter(
            grad_up_w.astype(jnp.bfloat16), "dp", scatter_dimension=0, tiled=True
        ).astype(jnp.float32),
        lax.psum_scatter(
            grad_down_w.astype(jnp.bfloat16), "dp", scatter_dimension=1, tiled=True
        ).astype(jnp.float32),
    )
    return (
        output,
        grad_input,
        grad_kv,
        gain_first_sum,
        gain_second_sum,
        query_shard,
        out_shard,
        gate_shard,
        up_shard,
        down_shard,
    )


def fast_body(inputs, keys_values, segment_ids, gain_first, gain_second, w_query, w_out, w_gate,
              w_up, w_down, cotangent):
    (rows_first, cots, gate_here, up_here, down_here, out_whole, queries, context_own, log_totals, residual,
     normed_second, inputs_here, cot_here, gain_one, gain_two, keys, values, starts) = front_call(
        inputs, cotangent, gain_first[None], gain_second[None], w_query, w_out, w_gate.T, w_up.T, w_down,
        keys_values, segment_ids, 1)
    grad_normed_second, query_0, query_y, ffn_parts, ffn_sums = ffn_call(
        normed_second, w_query, cots, down_here, gate_here, up_here, 3)
    (grad_residual, gain_second_part, query_x, query_xy, grad_queries, grad_kv, down_sums, gate_sums,
     out_sums) = back_first(
        grad_normed_second, residual, cot_here, gain_two, context_own, queries, keys, values, log_totals, starts,
        query_0, query_y, out_whole, ffn_sums, 5)
    down_shard, gate_shard, up_shard, out_shard, query_shard, grad_input, output, gains = back_last(
        grad_queries, grad_residual, inputs_here, gain_one, query_0, query_y, query_x, query_xy, residual,
        gain_second_part, rows_first, ffn_sums, down_sums, gate_sums, out_sums, ffn_parts, 6)
    (grad_kv, grad_input, output, down_shard, out_shard, query_shard, gate_shard, up_shard) = hand_over(
        grad_kv, grad_input, output, down_shard, out_shard, query_shard, gate_shard, up_shard)
    return (output, grad_input, grad_kv, gains[0], gains[1], query_shard, out_shard,
            gate_shard.T, up_shard.T, down_shard)


def solution(mesh):
    in_specs = (
        P(("dp", "mp"), None),
        P("dp", None, "mp"),
        P("dp", None),
        P(),
        P(),
        P("dp", "mp"),
        P("mp", "dp"),
        P("dp", "mp"),
        P("dp", "mp"),
        P("mp", "dp"),
        P(("dp", "mp"), None),
    )
    out_specs = (
        P(("dp", "mp"), None),
        P(("dp", "mp"), None),
        P("dp", None, "mp"),
        P(),
        P(),
        P("dp", "mp"),
        P("mp", "dp"),
        P("dp", "mp"),
        P("dp", "mp"),
        P("mp", "dp"),
    )
    fast = mesh.shape["dp"] == 8 and mesh.shape["mp"] == 4
    body = fast_body if fast else plain_body
    return jax.shard_map(body, mesh=mesh, in_specs=in_specs, out_specs=out_specs, check_vma=False)
```

```python
import jax
import jax.numpy as jnp
from jax import lax
from jax.experimental import pallas as pl
from jax.experimental.pallas import tpu as pltpu
from jax.sharding import PartitionSpec as P

f32 = jnp.float32
bf16 = jnp.bfloat16
HEAD_DIM = 128
MP = 4
epsilon = 1e-06


MESH = pl.DeviceIdType.MESH
Z_LOW, Z_HIGH, CORE, SIDE, DEEP = 1, 2, 4, 8, 16
ANY = pl.BlockSpec(memory_space=pl.ANY)
VM = pl.BlockSpec(memory_space=pltpu.VMEM)


class Place:
    def __init__(self):
        self.dp = lax.axis_index("dp")
        self.mp = lax.axis_index("mp")

    def bit(self, mask):
        return ((self.dp * 4 + self.mp) // mask) % 2

    def partner(self, mask):
        flip_dp, flip_mp = mask // 4, mask % 4
        return (self.flip(self.dp, flip_dp), self.flip(self.mp, flip_mp))

    def flip(self, value, flips):
        for mask in (1, 2, 4):
            if flips & mask:
                value = value + mask - 2 * mask * ((value // mask) % 2)
        return value


class Copies:
    def __init__(self, place, send_sems, recv_sems, local_sems=None):
        self.place, self.send_sems, self.recv_sems = place, send_sems, recv_sems
        self.local_sems = local_sems
        self.count = 0
        self.local_count = 0
        self.pending = []

    def describe(self, source, target, device, slot):
        return pltpu.make_async_remote_copy(
            src_ref=source, dst_ref=target, send_sem=self.send_sems.at[slot],
            recv_sem=self.recv_sems.at[slot], device_id=device, device_id_type=MESH)

    def swap(self, source, target, mask):
        slot = self.count
        self.count += 1
        copy = self.describe(source, target, self.place.partner(mask), slot)
        copy.start()
        item = {"copy": copy, "got": False}
        self.pending.append(item)
        return item

    def got(self, item):
        if not item["got"]:
            item["got"] = True
            if "get_if" in item:
                @pl.when(item["get_if"])
                def _():
                    item["get"].wait_recv()
            else:
                item["copy"].wait_recv()

    def prepare(self, source, target, mask):
        slot = self.count
        self.count += 1
        item = {"copy": self.describe(source, target, self.place.partner(mask), slot), "got": False}
        self.pending.append(item)
        return item

    def prepare_step(self, block, mp_send, mp_get, direction, send_if, get_if):
        slot = self.count
        self.count += 1
        place = self.place
        device = (place.dp, jnp.clip(place.mp + direction, 0, 3))
        copy = self.describe(*block(jnp.clip(mp_send, 0, 3)), device, slot)
        get = self.describe(*block(jnp.clip(mp_get, 0, 3)), device, slot)
        item = {"copy": copy, "got": False, "send_if": send_if, "get_if": get_if, "get": get}
        self.pending.append(item)
        return item

    def prepare_jump(self, source, target, landing, distance, send_if, get_if):
        slot = self.count
        self.count += 1
        place = self.place
        device = (place.dp, jnp.clip(place.mp + distance, 0, 3))
        item = {"copy": self.describe(source, target, device, slot), "got": False, "send_if": send_if,
                "get_if": get_if, "get": self.describe(source, landing, device, slot)}
        self.pending.append(item)
        return item

    def start(self, item):
        if "send_if" in item:
            @pl.when(item["send_if"])
            def _():
                item["copy"].start()
        else:
            item["copy"].start()

    def step(self, *arguments):
        item = self.prepare_step(*arguments)
        self.start(item)
        return item

    def received(self, item):
        if item["got"]:
            return
        item["got"] = True
        if "get_if" in item:
            @pl.when(item["get_if"])
            def _():
                item["get"].wait_recv()
        else:
            item["copy"].wait_recv()

    def local(self, source, target):
        copy = pltpu.make_async_copy(source, target, self.local_sems.at[self.local_count])
        self.local_count += 1
        copy.start()
        return copy

    def finish(self):
        for item in self.pending:
            self.got(item)
        for item in self.pending:
            if "send_if" in item:
                @pl.when(item["send_if"])
                def _():
                    item["copy"].wait_send()
            elif "sent" not in item:
                item["copy"].wait_send()


def greet(place, masks):
    barrier = pltpu.get_barrier_semaphore()
    for mask in masks:
        pl.semaphore_signal(barrier, inc=1, device_id=place.partner(mask), device_id_type=MESH)
    pl.semaphore_wait(barrier, len(masks))


def absolute(place, spot):
    core, deep, side = spot // 4, (spot // 2) % 2, spot % 2
    return place.flip(place.dp, core + 4 * deep) - 2 * place.bit(SIDE) + 2 * side


DMA = pltpu.SemaphoreType.DMA


def dot(left, right, left_dim, right_dim):
    return lax.dot_general(
        left, right, (((left_dim,), (right_dim,)), ((), ())), preferred_element_type=f32)


def params(ident, vmem=32 << 20):
    return pltpu.CompilerParams(collective_id=ident, has_side_effects=True, vmem_limit_bytes=vmem)


def add_into(target, rows, *others, step=32):
    start, count = rows
    pieces = count // step

    def one(i, carry):
        total = target[pl.ds(start + i * step, step), :].astype(f32)
        for other in others:
            total = total + other[pl.ds(i * step, step), :].astype(f32)
        target[pl.ds(start + i * step, step), :] = total.astype(target.dtype)
        return carry

    lax.fori_loop(0, pieces, one, 0)


class QuadReduce:
    def __init__(self, copies, parts, relay, landed):
        self.copies, self.parts, self.relay, self.landed = copies, parts, relay, landed
        self.share = parts.shape[0] // 4
        self.half = self.share // 2

    def prepare(self):
        share, half = self.share, self.half
        prepare, parts, landed = self.copies.prepare, self.parts, self.landed
        self.first = prepare(parts.at[pl.ds(3 * share, half), :], self.relay.at[0], SIDE)
        self.second = prepare(parts.at[pl.ds(3 * share + half, half), :], self.relay.at[1], Z_LOW)
        self.side = [prepare(parts.at[pl.ds(share, half), :], landed.at[0, pl.ds(0, half), :], SIDE),
                     prepare(parts.at[pl.ds(share + half, half), :], landed.at[0, pl.ds(half, half), :], SIDE)]
        self.low = [prepare(parts.at[pl.ds(2 * share + half, half), :], landed.at[1, pl.ds(half, half), :], Z_LOW),
                    prepare(parts.at[pl.ds(2 * share, half), :], landed.at[1, pl.ds(0, half), :], Z_LOW)]

    def start_across(self):
        self.copies.start(self.first)
        self.copies.start(self.second)
        self.copies.start(self.side[0])

    def start_rest(self):
        self.copies.start(self.low[0])

    def start(self):
        self.prepare()
        self.start_across()
        self.start_rest()

    def relayed_low(self):
        self.copies.received(self.first)
        add_into(self.parts, (2 * self.share, self.half), self.relay.at[0])
        self.copies.start(self.low[1])

    def relayed_side(self):
        self.copies.received(self.second)
        add_into(self.parts, (self.share + self.half, self.half), self.relay.at[1])
        self.copies.start(self.side[1])

    def relayed(self):
        self.relayed_low()
        self.relayed_side()

    def arrived(self):
        for item in self.side + self.low:
            self.copies.got(item)


ROWS=256
DOC_MOST=512
DOCS=16


def key_range(block, seq_len):
    low = max(0, block * ROWS - DOC_MOST + 1) // ROWS * ROWS
    return low, min(seq_len, (block + 1) * ROWS)


def scores_turned(q, k, starts, low, first, scale):
    s = dot(k, q, 1, 1) * scale
    key_pos = low + lax.broadcasted_iota(jnp.int32, s.shape, 0)
    query_pos = first + lax.broadcasted_iota(jnp.int32, s.shape, 1)
    return jnp.where((key_pos >= starts) & (key_pos <= query_pos), s, -1e30)


def attend_block(h, block, starts_ref, q_ref, k_ref, v_ref, ctx_ref, lse_ref):
    seq_len = q_ref.shape[0]
    scale = HEAD_DIM ** -0.5
    window = min(seq_len, DOC_MOST + ROWS)
    lanes = pl.ds(pl.multiple_of(h * HEAD_DIM, HEAD_DIM), HEAD_DIM)
    first = pl.multiple_of(block * ROWS, ROWS)
    low = pl.multiple_of(jnp.clip(first - DOC_MOST, 0, seq_len - window), ROWS)
    here = pl.ds(first, ROWS)
    keys_here = pl.ds(low, window)
    s = scores_turned(q_ref[here, lanes], k_ref[keys_here, lanes], starts_ref[:, here], low, first, scale)
    top = jnp.max(s, axis=0, keepdims=True)
    raised = jnp.exp(s - top)
    total = jnp.sum(raised, axis=0, keepdims=True)
    low_probs = (raised * (1.0 / total)).astype(bf16)
    ctx_ref[here, lanes] = dot(low_probs, v_ref[keys_here, lanes], 0, 0).astype(bf16)
    lse_ref[h, :, here] = top + jnp.log(total)


def attend_head_back(h, starts_ref, q_ref, k_ref, v_ref, grad_ref, lse_ref, dq_ref, pair_ref, dk_ref, dv_ref):
    seq_len = q_ref.shape[0]
    scale = HEAD_DIM ** -0.5
    lanes = pl.ds(pl.multiple_of(h * HEAD_DIM, HEAD_DIM), HEAD_DIM)
    for block in range(seq_len // ROWS):
        low, high = key_range(block, seq_len)
        here = pl.ds(block * ROWS, ROWS)
        k = k_ref[low:high, lanes]
        v = v_ref[low:high, lanes]
        q = q_ref[here, lanes]
        grad = grad_ref[here, lanes]
        s = scores_turned(q, k, starts_ref[:, here], low, block * ROWS, scale)
        probs = jnp.exp(s - lse_ref[h, :, here])
        grad_probs = dot(v, grad, 1, 1)
        spread = jnp.sum(probs * grad_probs, axis=0, keepdims=True)
        grad_s = (probs * (grad_probs - spread)).astype(bf16)
        dq_ref[here, lanes] = (dot(grad_s, k, 0, 0) * scale).astype(bf16)
        dk = dot(grad_s, q, 1, 0) * scale
        dv = dot(probs.astype(bf16), grad, 1, 0)
        old = block * ROWS
        if block:
            n = old - low
            dk_ref[low:old, :] += dk[:n]
            dv_ref[low:old, :] += dv[:n]
            dk_ref[old:high, :] = dk[n:]
            dv_ref[old:high, :] = dv[n:]
        else:
            dk_ref[low:high, :] = dk
            dv_ref[low:high, :] = dv
    pair_ref[:, 0, lanes] = dk_ref[...]
    pair_ref[:, 1, lanes] = dv_ref[...]


FRONT_ORDER = (
    2, 21, 48, 18, 0, 1, 8, 11, 57, 35, 5, 3, 13, 33, 4, 20, 19, 17, 28, 27, 42, 26, 66, 9, 36, 64, 12, 24,
    15, 6, 68, 67, 10, 34, 63, 29, 44, 23, 30, 14, 16, 73, 22, 50, 41, 37, 49, 54, 25, 46, 39, 65, 31, 56,
    53, 75, 59, 7, 43, 55, 52, 38, 40, 70, 72, 45, 69, 51, 74, 60, 61, 71, 58, 76, 32, 62, 47, 77,
)


def front_kernel(x, cot, gain_one_in, gain_two_in, wq, wo, wg, wu, wd, pairs, segments,
                 rows_out, cots, gate, up, down, out_out, queries_to, context_own, lse, residual, normed,
                 x_to, cot_to, gain_one, gain_two, keys_to, values_to, starts,
                 queries, x_here, cot_here, keys, values, first, rows, query, out, context,
                 send_sems, recv_sems, local_sems):
    place = Place()
    dp, mp = place.dp, place.mp
    side = place.bit(SIDE)
    copies = Copies(place, send_sems, recv_sems, local_sems)
    half = wd.shape[0] // 2
    blk = wd.shape[1]
    share, width = first.shape
    zrow = wo.shape[0]
    local = wq.shape[1]
    chunk = share // 2
    mats = ((wg, gate), (wu, up), (wd, down))
    own, across = side, 1 - side
    DEEPER, OTHER = 2, 4
    locals_ = []

    def tile(whole, z, spot):
        return whole.at[pl.ds(z * half, half), pl.ds(spot * blk, blk)]

    def qrows(spot):
        return query.at[pl.ds(spot * blk, blk), :]

    def columns(spot):
        return out.at[:, pl.ds(spot * blk, blk)]

    def row_block(c, source_is_input):
        def get(m):
            target = rows.at[pl.ds(m * share + c * chunk, chunk), :]
            source = first.at[pl.ds(c * chunk, chunk), :] if source_is_input else target
            return source, target
        return get

    def out_block(source_is_input):
        def get(m):
            target = out.at[pl.ds(m * zrow, zrow), pl.ds(own * blk, blk)]
            return (wo if source_is_input else target), target
        return get

    items = {}

    def note(name, *copied):
        items[name] = list(copied)

    def line(step, block_of, name):
        note(name,
             copies.step(block_of, mp - (step - 1), mp - step, 1, (mp >= step - 1) & (mp < 3), mp >= step),
             copies.step(block_of, mp + (step - 1), mp + step, -1, (mp <= 3 - (step - 1)) & (mp > 0), mp <= 3 - step))

    own_piece = [weight.at[pl.ds(side * half, half), :] for weight, _ in mats]
    spots = [pl.ds(pl.multiple_of(absolute(place, s) * blk, blk), blk) for s in range(8)]
    inside = lambda m: (m >= 0) & (m <= 3)

    def context_jump(distance):
        source = context.at[pl.ds(jnp.clip(mp + distance, 0, 3) * share, share), :]

        def landing(m):
            return context_own.at[:, pl.ds(pl.multiple_of(jnp.clip(m, 0, 3) * local, local), local)]

        return copies.prepare_jump(source, landing(mp), landing(mp - distance), distance,
                                   inside(mp + distance), inside(mp - distance))

    jumps = {distance: context_jump(distance) for distance in (1, -1, 2, -2, 3, -3)}

    def attend_tokens(m):
        here = pl.ds(pl.multiple_of(m * share, share), share)
        queries[here, :] = dot(rows[here, :], query[...], 1, 0).astype(bf16)

        def one_head(h, carry):
            attend_block(h, m, starts, queries, keys, values, context, lse)
            return carry

        lax.fori_loop(0, local // HEAD_DIM, one_head, 0)

    def attend_from(distance):
        for away in (distance, -distance):
            @pl.when(inside(mp + away))
            def _(away=away):
                attend_tokens(mp + away)
                jumps[away]["copy"].start()
        note("A%d" % distance, jumps[distance], jumps[-distance])

    def norm_rows():
        for s in range(8):
            gain_one[:, s * blk:(s + 1) * blk] = gain_one_in[:, spots[s]]
            gain_two[:, s * blk:(s + 1) * blk] = gain_two_in[:, spots[s]]

        def norm_first(i, carry):
            here = pl.ds(i * 32, 32)
            for s in range(8):
                x_here[here, s * blk:(s + 1) * blk] = x[here, spots[s]]
                cot_here[here, s * blk:(s + 1) * blk] = cot[here, spots[s]]
            value = x_here[here, :].astype(f32)
            inverse = lax.rsqrt(jnp.mean(value * value, axis=-1, keepdims=True) + epsilon)
            first[here, :] = (value * inverse * gain_one[...]).astype(bf16)
            return carry

        lax.fori_loop(0, share // 32, norm_first, 0)
        rows[pl.ds(mp * share, share), :] = first[...]
        locals_.append(copies.local(x_here, x_to))
        locals_.append(copies.local(cot_here, cot_to))

    def split_pairs():
        def split(i, carry):
            here = pl.ds(i * 32, 32)
            both = pairs[here, :, :]
            keys[here, :] = both[:, 0, :]
            values[here, :] = both[:, 1, :]
            return carry

        lax.fori_loop(0, pairs.shape[0] // 32, split, 0)
        ids = segments[...]
        begun = jnp.zeros_like(ids)
        for document in range(DOCS - 1):
            size = jnp.sum((ids == document).astype(jnp.int32), axis=1, keepdims=True)
            begun = begun + jnp.where(ids > document, size, 0)
        starts[...] = begun
        locals_.append(copies.local(keys, keys_to))
        locals_.append(copies.local(values, values_to))
        query[pl.ds(own * blk, blk), :] = wq[...]
        out[pl.ds(mp * zrow, zrow), pl.ds(pl.multiple_of(own * blk, blk), blk)] = wo[...]
        locals_.append(copies.local(cot_here, cots.at[0:share, :]))
        for i in range(3):
            locals_.append(copies.local(own_piece[i], tile(mats[i][1], 0, own)))

    def send(name, source, target, mask):
        note(name, copies.swap(source, target, mask))

    tasks = {}

    def task(name, needs, action, *arguments):
        tasks[name] = (needs, lambda: action(*arguments))

    def copy(name, needs, source, target, mask):
        task(name, needs, send, name, source, target, mask)

    task("N", (), norm_rows)
    task("S", ("N",), split_pairs)
    task("o1", (), line, 1, out_block(True), "o1")
    task("o2", ("o1",), line, 2, out_block(False), "o2")
    task("o3", ("o2", "S"), line, 3, out_block(False), "o3")
    for c in range(2):
        task("n1%d" % c, ("N",), line, 1, row_block(c, True), "n1%d" % c)
        task("n2%d" % c, ("n1%d" % c,), line, 2, row_block(c, False), "n2%d" % c)
        task("n3%d" % c, ("n2%d" % c,), line, 3, row_block(c, False), "n3%d" % c)
    copy("qy", (), wq, qrows(own + DEEPER), DEEP)
    copy("qx", (), wq, qrows(own), SIDE)
    copy("qyx", ("qy",), qrows(own + DEEPER), qrows(own + DEEPER), SIDE)
    copy("q", (), wq, qrows(own + OTHER), CORE)
    for name, spot in (("qy", own + DEEPER), ("qx", across), ("qyx", across + DEEPER)):
        copy(name + "C", (name,), qrows(spot), qrows(spot + OTHER), CORE)
    for i, (weight, whole) in enumerate(mats):
        n = "%d" % i
        copy("x" + n, (), weight.at[pl.ds((1 - side) * half, half), :], tile(whole, 0, own), SIDE)
        for kind, needs, source, z, spot in (
                ("O", (), own_piece[i], 0, own), ("X", ("x" + n,), tile(whole, 0, across), 0, across)):
            copy("z" + kind + n, needs, source, tile(whole, 1, spot), Z_HIGH)
            for far, far_needs, far_source, row in (("", needs, source, 0), ("z", ("z" + kind + n,), tile(whole, 1, spot), 1)):
                name = far + kind + n
                copy("y" + name, far_needs, far_source, tile(whole, row, spot + DEEPER), DEEP)
                copy("c" + name, far_needs, far_source, tile(whole, row, spot + OTHER), CORE)
                copy("yc" + name, ("y" + name,), tile(whole, row, spot + DEEPER), tile(whole, row, spot + DEEPER + OTHER), CORE)
    copy("cx", ("N",), cot_here, cots.at[share:2 * share, :], SIDE)
    copy("cz", ("N",), cot_here, cots.at[2 * share:3 * share, :], Z_LOW)
    copy("czx", ("cz",), cots.at[2 * share:3 * share, :], cots.at[3 * share:4 * share, :], SIDE)
    copy("oy", ("o3",), columns(own), columns(own + DEEPER), DEEP)
    copy("ox", ("o3",), columns(own), columns(own), SIDE)
    copy("oyx", ("oy",), columns(own + DEEPER), columns(own + DEEPER), SIDE)
    for name, needs, spot in (("o", "o3", own), ("oy", "oy", own + DEEPER), ("ox", "ox", across), ("oyx", "oyx", across + DEEPER)):
        copy(name + "C", (needs,), columns(spot), columns(spot + OTHER), CORE)
    whole_query = ("q", "qyC", "qxC", "qyxC", "S")
    task("A0", whole_query, attend_tokens, mp)
    for distance in (1, 2, 3):
        task("A%d" % distance, ("A0", "n%d0" % distance, "n%d1" % distance), attend_from, distance)

    def finish_tokens():
        context_own[:, pl.ds(pl.multiple_of(mp * local, local), local)] = context[pl.ds(mp * share, share), :]
        locals_.append(copies.local(rows, rows_out))
        locals_.append(copies.local(queries, queries_to))
        locals_.append(copies.local(out, out_out))

        def project_out(n, carry):
            there = pl.ds(pl.multiple_of(n * 512, 512), 512)
            residual[:, there] = x_here[:, there].astype(f32) + dot(context_own[...], out[:, there], 1, 0)
            return carry

        lax.fori_loop(0, width // 512, project_out, 0)

        def norm_second(i, carry):
            here = pl.ds(i * 32, 32)
            value = residual[here, :]
            inverse = lax.rsqrt(jnp.mean(value * value, axis=-1, keepdims=True) + epsilon)
            normed[here, :] = (value * inverse * gain_two[...]).astype(bf16)
            return carry

        lax.fori_loop(0, share // 32, norm_second, 0)

    task("F", ("A3", "oC", "oyC", "oxC", "oyxC", "A1", "A2"), finish_tokens)

    greet(place, (1, 2, 3, CORE, SIDE, DEEP))
    names = list(tasks)
    for index in FRONT_ORDER or range(len(names)):
        needs, action = tasks.pop(names[index])
        for need in needs:
            for item in items.get(need, ()):
                copies.got(item)
        action()
    assert not tasks
    for local_copy in locals_:
        local_copy.wait()
    copies.finish()


def front_call(x, cot, gain_one, gain_two, wq, wo, wg, wu, wd, pairs, segments, ident):
    share, width = x.shape
    hidden, blk = wd.shape
    seq_len, _, local = pairs.shape
    V = pltpu.VMEM
    S = jax.ShapeDtypeStruct
    return pl.pallas_call(
        front_kernel,
        out_shape=(
            S((seq_len, width), bf16), S((seq_len, width), bf16), S((hidden, width), bf16), S((hidden, width), bf16),
            S((hidden, width), bf16), S((width, width), bf16), S((seq_len, local), bf16), S((share, width), bf16),
            S((local // HEAD_DIM, 1, seq_len), f32), S((share, width), f32), S((share, width), bf16),
            S((share, width), bf16), S((share, width), bf16), S((1, width), f32), S((1, width), f32),
            S((seq_len, local), bf16), S((seq_len, local), bf16), S((1, seq_len), jnp.int32)),
        in_specs=[VM] * 11,
        out_specs=(ANY,) * 7 + (VM,) * 4 + (ANY,) * 2 + (VM,) * 2 + (ANY,) * 2 + (VM,),
        scratch_shapes=[
            V((seq_len, local), bf16), V((share, width), bf16), V((share, width), bf16), V((seq_len, local), bf16),
            V((seq_len, local), bf16),
            V((share, width), bf16), V((seq_len, width), bf16), V((width, local), bf16), V((width, width), bf16),
            V((seq_len, local), bf16), DMA((96,)), DMA((96,)), DMA((12,))],
        compiler_params=params(ident, 60 << 20), name="front",
    )(x, cot, gain_one, gain_two, wq, wo, wg, wu, wd, pairs, segments)


def hidden_cuts(hidden):
    cuts = []
    start = 0
    while start < hidden:
        size = min(512, hidden - start)
        cuts.append((start, size))
        start += size
    return cuts


def ffn_kernel(normed, wq, cots_in, down_in, gate_in, up_in, total, query_0, query_y, fparts_out, sums_out,
               weights, tokens, acts, dparts, relay, landed, fparts,
               send_sems, recv_sems, local_sems, free_sem):
    place = Place()
    share, width = normed.shape
    hidden = down_in.shape[0]
    half = share // 2
    wide = width // 2
    cuts = hidden_cuts(hidden)
    copies = Copies(place, send_sems, recv_sems, local_sems)
    load_cots = copies.local(cots_in, tokens.at[0])
    load_w = [copies.local(w, weights.at[i]) for i, w in enumerate((down_in, gate_in, up_in))]
    mp = place.mp
    local = wq.shape[1]
    greet(place, (1, 2, 3, SIDE, CORE, DEEP))

    def at(quarter, part):
        return tokens.at[1, pl.ds(quarter * share + part * half, half), :]

    a, b = pl.ds(0, half), pl.ds(half, half)
    low_a = copies.swap(normed.at[a, :], at(2, 0), Z_LOW)
    side_b = copies.swap(normed.at[b, :], at(1, 1), SIDE)
    low_b = copies.swap(normed.at[b, :], at(2, 1), Z_LOW)
    side_a = copies.swap(normed.at[a, :], at(1, 0), SIDE)
    tokens[1, 0:share, :] = normed[...]

    def wide_block(source_is_input):
        def get(m):
            target = query_0.at[:, pl.ds(pl.multiple_of(m * local, local), local)]
            return (wq if source_is_input else target), target
        return get

    hops = []
    for hop in (1, 2, 3):
        block_of = wide_block(hop == 1)
        hops.append((
            copies.prepare_step(block_of, mp - (hop - 1), mp - hop, 1, (mp >= hop - 1) & (mp < 3), mp >= hop),
            copies.prepare_step(block_of, mp + (hop - 1), mp + hop, -1,
                                (mp <= 3 - (hop - 1)) & (mp > 0), mp <= 3 - hop)))
    over_deep = copies.prepare(query_0, query_y, DEEP)
    for item in hops[0]:
        copies.start(item)
    query_0[:, pl.ds(pl.multiple_of(mp * local, local), local)] = wq[...]

    def block(r, between):
        here = pl.ds(r * share, share)
        for start, size in cuts:
            rows = tokens[1, here, :]
            gate = dot(rows, weights[1, start:start + size, :], 1, 1)
            up = dot(rows, weights[2, start:start + size, :], 1, 1)
            grad = dot(tokens[0, here, :], weights[0, start:start + size, :], 1, 1)
            sigmoid = jax.nn.sigmoid(gate)
            silu = gate * sigmoid
            acts[0, here, start:start + size] = (silu * up).astype(bf16)
            acts[1, here, start:start + size] = (
                grad * up * sigmoid * (1.0 + gate * (1.0 - sigmoid))).astype(bf16)
            acts[2, here, start:start + size] = (grad * silu).astype(bf16)

        between()

        def columns(n, carry):
            there = pl.ds(pl.multiple_of(n * 512, 512), 512)
            dparts[here, there] = (dot(acts[1, here, :], weights[1, :, there], 1, 0)
                                   + dot(acts[2, here, :], weights[2, :, there], 1, 0)).astype(bf16)
            fparts[here, there] = dot(acts[0, here, :], weights[0, :, there], 1, 0).astype(bf16)
            return carry

        lax.fori_loop(0, width // 512, columns, 0)

    for copy in load_w:
        copy.wait()
    load_cots.wait()
    got = {"across": None}

    def pass_on(r, turn, landed_hop, next_hop):
        @pl.when(r == turn)
        def _():
            for item in landed_hop:
                copies.received(item)
            for item in next_hop:
                copies.start(item)

    def step(r, carry):
        @pl.when(r == 1)
        def _():
            low_a["copy"].wait_recv()
            side_b["copy"].wait_recv()
            forward[0].start()
            forward[1].start()
            side_a["copy"].wait_recv()
            low_b["copy"].wait_recv()

        @pl.when(r == 2)
        def _():
            forward[0].wait_recv()
            forward[1].wait_recv()

        pass_on(r, 2, hops[0], hops[1])
        pass_on(r, 3, hops[2], (over_deep,))

        @pl.when(r == 3)
        def _():
            reduce.start_across()
        block(jnp.where(r < 2, r, 5 - r), lambda: pass_on(r, 2, hops[1], hops[2]))
        return carry

    reduce = QuadReduce(copies, dparts, relay, landed)
    reduce.prepare()

    forward = [copies.describe(at(2, 0), at(3, 0), place.partner(SIDE), copies.count),
               copies.describe(at(1, 1), at(3, 1), place.partner(Z_LOW), copies.count + 1)]
    copies.count += 2
    lax.fori_loop(0, 4, step, 0)
    for item in (low_a, side_b, low_b, side_a):
        item["got"] = True
    pl.semaphore_signal(free_sem, inc=1, device_id=place.partner(CORE), device_id_type=MESH)
    reduce.start_rest()
    save = copies.local(fparts, fparts_out)

    base = copies.count
    copies.count += 3

    def give_copy(i):
        return copies.describe(weights.at[i, :, pl.ds(0, wide)], weights.at[i, :, pl.ds(wide, wide)],
                               place.partner(CORE), base + i)

    def give(i, carry):
        right = tokens[jnp.minimum(i, 1), :, wide:]
        for start, size in cuts:
            weights[i, start:start + size, 0:wide] = dot(
                acts[i, :, start:start + size], right, 0, 0).astype(bf16)

        @pl.when(i == 0)
        def _():
            pl.semaphore_wait(free_sem, 1)
        give_copy(i).start()

        @pl.when(i == 0)
        def _():
            reduce.relayed_low()

        @pl.when(i == 1)
        def _():
            reduce.relayed_side()
        return carry

    lax.fori_loop(0, 3, give, 0)

    def keep(i, carry):
        give_copy(i).wait_recv()
        right = tokens[jnp.minimum(i, 1), :, 0:wide]
        for start, size in cuts:
            rows = slice(start, start + size)
            weights[i, rows, wide:] = (dot(acts[i, :, rows], right, 0, 0)
                                       + weights[i, rows, wide:].astype(f32)).astype(bf16)
        pltpu.make_async_copy(weights.at[i, :, pl.ds(wide, wide)], sums_out.at[i], local_sems.at[5 + i]).start()
        return carry

    lax.fori_loop(0, 3, keep, 0)
    reduce.arrived()

    def one(i, carry):
        here = pl.ds(i * 32, 32)
        total[here, :] = (dparts[here, :].astype(f32) + landed[0, here, :].astype(f32)
                          + landed[1, here, :].astype(f32))
        return carry

    lax.fori_loop(0, share // 32, one, 0)
    for i in range(3):
        give_copy(i).wait_send()
        pltpu.make_async_copy(weights.at[i, :, pl.ds(wide, wide)], sums_out.at[i], local_sems.at[5 + i]).wait()
    for copy in forward:
        copy.wait_send()
    save.wait()
    copies.finish()


def ffn_call(normed, wq, cots, down, gate, up, ident):
    share, width = normed.shape
    hidden = down.shape[0]
    V = pltpu.VMEM
    flops = 2 * share * 4 * width * hidden * 9
    return pl.pallas_call(
        ffn_kernel,
        out_shape=(jax.ShapeDtypeStruct((share, width), f32), jax.ShapeDtypeStruct((share, width), bf16),
                   jax.ShapeDtypeStruct((share, width), bf16), jax.ShapeDtypeStruct((share * 4, width), bf16),
                   jax.ShapeDtypeStruct((3, hidden, width // 2), bf16)),
        in_specs=[VM] * 2 + [ANY] * 4,
        out_specs=(VM, VM, VM, ANY, ANY),
        scratch_shapes=[
            V((3, hidden, width), bf16), V((2, share * 4, width), bf16), V((3, share * 4, hidden), bf16),
            V((share * 4, width), bf16), V((2, share // 2, width), bf16), V((2, share, width), bf16),
            V((share * 4, width), bf16),
            DMA((24,)), DMA((24,)), DMA((8,)), pltpu.SemaphoreType.REGULAR],
        compiler_params=params(ident, 63 << 20),
        cost_estimate=pl.CostEstimate(flops=flops, bytes_accessed=40 << 20, transcendentals=share * 4 * hidden),
        name="feed_forward",
    )(normed, wq, cots, down, gate, up)


def back_first_kernel(dn2, residual, cot, gain, lse, starts, context_in, queries_in, keys_in, values_in,
                      query_0, query_y, out_whole, sums,
                      dres_out, gain_part, query_x, query_xy, grad_q, pairs_out, down_sums, gate_sums, sums_out,
                      context, queries, keys, values, dres, pairs, out_sums, heads, keep_d, deep_d, high_d, deep_g, grad_low, wout, dctx, give_o, core_o, dk, dv,
                      send_sems, recv_sems, local_sems):
    place = Place()
    mp = place.mp
    share, width = dn2.shape
    hidden = keep_d.shape[0]
    half = hidden // 2
    local = heads.shape[1]
    wide = width // 2
    quarter = wide // 2
    blk = quarter // 2
    copies = Copies(place, send_sems, recv_sems, local_sems)
    loads = [copies.local(out_whole.at[pl.ds(z * local, local), :], wout.at[z]) for z in range(4)]
    load_d = copies.local(sums.at[0, :, pl.ds(0, quarter)], keep_d)
    late = [copies.local(*pair) for pair in ((context_in, context), (queries_in, queries), (keys_in, keys),
                                             (values_in, values))]
    load_g = copies.local(sums.at[1, :, pl.ds(0, blk)], gate_sums)
    greet(place, (1, 2, 3, CORE, SIDE, DEEP))
    in_d = [copies.swap(sums.at[0, :, pl.ds(quarter + x * blk, blk)], deep_d.at[:, pl.ds(x * blk, blk)], DEEP)
            for x in (0, 1)]
    copies.swap(query_0, query_x, SIDE)
    copies.swap(query_y, query_xy, SIDE)
    gain_part[...] = jnp.zeros_like(gain_part)

    def norm(i, carry):
        here = pl.ds(i * 32, 32)
        value = residual[here, :]
        inverse = lax.rsqrt(jnp.mean(value * value, axis=-1, keepdims=True) + epsilon)
        scaled = value * inverse
        grad = dn2[here, :]
        grad_scaled = grad * gain[...]
        back = inverse * (grad_scaled - scaled * jnp.mean(grad_scaled * scaled, axis=-1, keepdims=True))
        total = cot[here, :].astype(f32) + back
        dres[here, :] = total
        grad_low[here, :] = total.astype(bf16)
        gain_part[...] += jnp.sum(grad * scaled, axis=0, keepdims=True)
        return carry

    lax.fori_loop(0, share // 32, norm, 0)
    saves = [copies.local(dres, dres_out)]
    for copy in loads + late:
        copy.wait()
    heads_in = []
    for mask in (2, 3, 1, 0):
        other = place.partner(mask)[1]
        there = pl.ds(pl.multiple_of(other * local, local), local)
        piece = dot(grad_low[...], wout[other], 1, 1).astype(bf16)
        if mask:
            dctx[:, there] = piece
            heads_in.append(copies.swap(dctx.at[:, there], heads.at[pl.ds(mp * share, share), :], mask))
        else:
            heads[pl.ds(mp * share, share), :] = piece
    chunks = width // 512
    base = copies.count
    copies.count += chunks

    def core_copy(n):
        rows = pl.ds(pl.multiple_of(n * 512, 512), 512)
        return copies.describe(give_o.at[rows, :], core_o.at[rows, :], place.partner(CORE), base + n)

    def give(n, carry):
        rows = pl.ds(pl.multiple_of(n * 512, 512), 512)
        give_o[rows, :] = dot(context[:, rows], grad_low[:, wide:], 0, 0).astype(bf16)
        core_copy(n).start()
        return carry

    lax.fori_loop(0, chunks, give, 0)

    def keep(n, carry):
        rows = pl.ds(pl.multiple_of(n * 512, 512), 512)
        core_copy(n).wait_recv()
        out_sums[rows, :] = (dot(context[:, rows], grad_low[:, :wide], 0, 0)
                             + core_o[rows, :].astype(f32)).astype(bf16)
        return carry

    lax.fori_loop(0, chunks, keep, 0)
    saves.append(copies.local(out_sums, sums_out))
    in_g = copies.swap(sums.at[1, :, pl.ds(quarter, blk)], deep_g, DEEP)
    load_d.wait()
    give_rows = pl.ds(half, half)
    across = []
    for x in (0, 1):
        there = pl.ds(x * blk, blk)
        copies.got(in_d[x])
        add_into(keep_d.at[:, there], (half, half), deep_d.at[give_rows, there], step=16)
        across.append(copies.swap(keep_d.at[give_rows, there], high_d.at[:, there], Z_HIGH))
        add_into(keep_d.at[:, there], (0, half), deep_d.at[:, there], step=16)
    for item in heads_in:
        copies.got(item)

    def one_head(h, carry):
        attend_head_back(h, starts, queries, keys, values, heads, lse, grad_q, pairs, dk, dv)
        return carry

    lax.fori_loop(0, local // HEAD_DIM, one_head, 0)
    saves.append(copies.local(pairs, pairs_out))
    load_g.wait()
    copies.got(in_g)
    add_into(gate_sums, (0, hidden), deep_g)
    for x in (0, 1):
        copies.got(across[x])

    def add_d(n, carry):
        rows = pl.ds(n * 16, 16)
        down_sums[rows, :] = (keep_d[rows, :].astype(f32) + high_d[rows, :].astype(f32)).astype(bf16)
        return carry

    lax.fori_loop(0, half // 16, add_d, 0)
    for copy in saves:
        copy.wait()
    copies.finish()

    def sent(n, carry):
        core_copy(n).wait_send()
        return carry

    lax.fori_loop(0, chunks, sent, 0)


def back_first(dn2, residual, cot, gain, context, queries, keys, values, lse, starts, query_0, query_y,
               out_whole, sums, ident):
    share, width = dn2.shape
    hidden = sums.shape[1]
    half = hidden // 2
    seq_len, local = queries.shape
    quarter = width // 4
    V = pltpu.VMEM
    S = jax.ShapeDtypeStruct
    return pl.pallas_call(
        back_first_kernel,
        out_shape=(S((share, width), f32), S((1, width), f32), S(query_0.shape, bf16), S(query_0.shape, bf16),
                   S((seq_len, local), bf16), S((seq_len, 2, local), f32),
                   S((half, quarter), bf16), S((hidden, quarter // 2), bf16), S((width, width // 2), bf16)),
        in_specs=[VM] * 6 + [ANY] * 8,
        out_specs=(ANY, VM, ANY, ANY, VM, ANY, VM, VM, ANY),
        scratch_shapes=[
            V((share, width), bf16), V((seq_len, local), bf16), V((seq_len, local), bf16), V((seq_len, local), bf16),
            V((share, width), f32), V((seq_len, 2, local), f32), V((width, width // 2), bf16),
            V((seq_len, local), bf16), V((hidden, quarter), bf16), V((hidden, quarter), bf16), V((half, quarter), bf16),
            V((hidden, quarter // 2), bf16), V((share, width), bf16),
            V((4, width // 4, width), bf16), V((share, width), bf16), V((width, width // 2), bf16),
            V((width, width // 2), bf16), V((seq_len, HEAD_DIM), f32), V((seq_len, HEAD_DIM), f32),
            DMA((20,)), DMA((20,)), DMA((13,))],
        compiler_params=params(ident, 63 << 20), name="back_first",
    )(dn2, residual, cot, gain, lse, starts, context, queries, keys, values, query_0, query_y, out_whole, sums)


BACK_ORDER = (
    3, 0, 10, 5, 9, 7, 12, 17, 4, 6, 1, 13, 22, 2, 14, 15, 18, 19, 21, 11, 8, 16, 24, 23, 28, 34, 25, 26,
    27, 20, 30, 31, 32, 36, 29, 35, 33,
)


def back_last_kernel(grad_q, gain, gain_part, dres_in, inputs_in, residual_in, query_0, query_y, query_x, query_xy,
                     rows_first, sums, down_sums, gate_sums, out_sums, fparts,
                     down_to, gate_to, up, out, query, input_to, output_to, gains,
                     dres, inputs, residual, near, down, gate, grad_input, output, keep_d, keep_g, keep_u, deep_g, deep_u, high_g, high_u, side_f,
                     own_o, deep_o, side_o, z_o,
                     give_q, own_q, core_q, side_q, deep_q, parts, relay, landed,
                     grad_own, rows, query_far, dn1, gain_rows, gains_got,
                     send_sems, recv_sems, local_sems):
    place = Place()
    mp = place.mp
    side = place.bit(SIDE)
    share, width = dres.shape
    hidden, blk = up.shape
    half = hidden // 2
    local = grad_q.shape[1]
    zrow = out.shape[0]
    saves = []
    quarter = 2 * blk
    wide = width // 2
    copies = Copies(place, send_sems, recv_sems, local_sems)
    load_rows = copies.local(rows_first, rows)
    load_g = copies.local(gate_sums, keep_g.at[:, pl.ds(0, blk)])
    load_h = copies.local(sums.at[1, :, pl.ds(blk, blk)], keep_g.at[:, pl.ds(blk, blk)])
    load_d = copies.local(down_sums, keep_d)
    load_o = copies.local(out_sums, own_o)
    load_u = copies.local(sums.at[2, :, pl.ds(0, quarter)], keep_u)
    load_p = copies.local(fparts, parts)
    near_in = (query_0, query_y, query_x, query_xy)
    load_near = [copies.local(piece, near.at[n]) for n, piece in enumerate(near_in)]
    load_late = [copies.local(*pair) for pair in ((dres_in, dres), (inputs_in, inputs), (residual_in, residual))]
    spot_of = (side, side + 2, 1 - side, 3 - side)
    give_rows = pl.ds(half, half)
    mine = pl.ds(pl.multiple_of(side * blk, blk), blk)
    theirs = pl.ds(pl.multiple_of((1 - side) * blk, blk), blk)
    spots = [pl.ds(pl.multiple_of(absolute(place, s) * blk, blk), blk) for s in range(8)]
    reduce = QuadReduce(copies, parts, relay, landed)
    items = {}
    tasks = {}
    loaded = set()

    def note(name, *copied):
        items[name] = list(copied)

    def task(name, needs, action, *arguments):
        tasks[name] = (needs, lambda: action(*arguments))

    def ready(name, *loads):
        if name not in loaded:
            loaded.add(name)
            for load in loads:
                load.wait()

    def block_o(deep, column):
        return own_o.at[:, pl.ds(pl.multiple_of((2 * deep + column) * blk, blk), blk)]

    def rows_q(deep, column):
        return pl.ds(pl.multiple_of((2 * deep + column) * blk, blk), blk)

    def send_tokens():
        sent = []
        for mask in (2, 3, 1):
            other = place.partner(mask)[1]
            sent.append(copies.swap(grad_q.at[pl.ds(other * share, share), :],
                                    grad_own.at[:, pl.ds(mp * local, local)], mask))
        note("dq", *sent)
        grad_own[:, pl.ds(pl.multiple_of(mp * local, local), local)] = grad_q[pl.ds(mp * share, share), :]

    def send_up(x):
        note("u%d" % x, copies.swap(sums.at[2, :, pl.ds(quarter + x * blk, blk)], deep_u.at[:, pl.ds(x * blk, blk)], DEEP))

    def send_near():
        note("f", *[copies.swap(piece, query_far.at[n], CORE) for n, piece in enumerate(near_in)])

    def send_gate():
        ready("g", load_g)
        there = pl.ds(0, blk)
        note("zg0", copies.swap(keep_g.at[give_rows, there], high_g.at[:, there], Z_HIGH))

    def send_gate_deep():
        note("g1", copies.swap(sums.at[1, :, pl.ds(quarter + blk, blk)], deep_g, DEEP))

    def gate_sum():
        ready("h", load_h)
        there = pl.ds(blk, blk)
        add_into(keep_g.at[:, there], (half, half), deep_g.at[give_rows, :], step=16)
        note("zg1", copies.swap(keep_g.at[give_rows, there], high_g.at[:, there], Z_HIGH))
        add_into(keep_g.at[:, there], (0, half), deep_g, step=16)

    def send_down():
        ready("d", load_d)
        note("xd", copies.swap(keep_d.at[:, theirs], side_f.at[0], SIDE))

    def send_out(name, n, x):
        ready("o", load_o)
        note(name, copies.swap(block_o(1, x), deep_o.at[n], DEEP))

    def product(first):
        ready("w", load_rows)
        return dot(rows[:, first:first + wide], grad_q[...], 0, 0)

    def query_give():
        give_q[...] = product(wide).astype(bf16)
        note("qc", copies.swap(give_q, core_q, CORE))

    def query_keep():
        own_q[...] = (product(0) + core_q[...].astype(f32)).astype(bf16)
        for y in (1, 0):
            note("qs%d" % y, copies.swap(own_q.at[rows_q(y, 1 - side), :], side_q.at[y], SIDE))

    def query_side(y):
        here = rows_q(y, side)
        own_q[here, :] = (own_q[here, :].astype(f32) + side_q[y].astype(f32)).astype(bf16)
        if y:
            note("qd", copies.swap(own_q.at[here, :], deep_q, DEEP))

    def query_done():
        query[...] = own_q[rows_q(0, side), :].astype(f32) + deep_q[...].astype(f32)

    def reduce_start():
        ready("p", load_p)
        reduce.start()
        note("r1", reduce.first, reduce.second)

    def first_product():
        for load in load_near:
            load.wait()
        for n in range(4):
            dn1[:, pl.ds(pl.multiple_of(spot_of[n] * blk, blk), blk)] = dot(grad_own[...], near[n], 1, 1)
            dn1[:, pl.ds(pl.multiple_of((spot_of[n] + 4) * blk, blk), blk)] = dot(grad_own[...], query_far[n], 1, 1)

    def first_norm():
        ready("v", *load_late)
        gain_rows[0:1, :] = jnp.zeros((1, width), f32)
        gain_rows[1:2, :] = gain_part[...]

        def norm(i, carry):
            here = pl.ds(i * 32, 32)
            value = inputs[here, :].astype(f32)
            inverse = lax.rsqrt(jnp.mean(value * value, axis=-1, keepdims=True) + epsilon)
            scaled = value * inverse
            grad = dn1[here, :]
            grad_scaled = grad * gain[...]
            back = inverse * (grad_scaled - scaled * jnp.mean(grad_scaled * scaled, axis=-1, keepdims=True))
            total = dres[here, :] + back
            for s in range(8):
                grad_input[here, spots[s]] = total[:, s * blk:(s + 1) * blk]
            gain_rows[0:1, :] += jnp.sum(grad * scaled, axis=0, keepdims=True)
            return carry

        lax.fori_loop(0, share // 32, norm, 0)
        saves.append(copies.local(grad_input, input_to))
        for s in range(8):
            gains[:, spots[s]] = gain_rows[:, s * blk:(s + 1) * blk]

    gain_masks = (1, 2, CORE, SIDE, DEEP)

    def gain_hop(n):
        if n:
            item = items["h%d" % (n - 1)][0]
            item["copy"].wait_send()
            item["sent"] = True
            gains[...] = gains[...] + gains_got[n - 1]
        if n < len(gain_masks):
            note("h%d" % n, copies.swap(gains, gains_got.at[n], gain_masks[n]))

    def up_sum(x):
        ready("u", load_u)
        there = pl.ds(x * blk, blk)
        add_into(keep_u.at[:, there], (half, half), deep_u.at[give_rows, there], step=16)
        note("zu%d" % x, copies.swap(keep_u.at[give_rows, there], high_u.at[:, there], Z_HIGH))
        add_into(keep_u.at[:, there], (0, half), deep_u.at[:, there], step=16)

    def high_sum(name, keep, high, i):
        add_into(keep.at[:, theirs], (0, half), high.at[:, theirs], step=16)
        note(name, copies.swap(keep.at[pl.ds(0, half), theirs], side_f.at[i], SIDE))
        add_into(keep.at[:, mine], (0, half), high.at[:, mine], step=16)

    def out_side():
        add_into(block_o(0, 1 - side), (0, width), deep_o.at[0])
        note("os", copies.swap(block_o(0, 1 - side), side_o, SIDE))

    def out_mine():
        add_into(block_o(0, side), (0, width), deep_o.at[1])

    def out_rows():
        add_into(block_o(0, side), (0, width), side_o)
        note("oz", *[copies.swap(own_o.at[pl.ds(place.partner(mask)[1] * zrow, zrow), mine], z_o.at[n], mask)
                     for n, mask in enumerate((2, 3, 1))])

    def out_done():
        def add_z(i, carry):
            here = pl.ds(i * 32, 32)
            sum_ = own_o[pl.ds(mp * zrow + i * 32, 32), mine].astype(f32)
            for n in range(3):
                sum_ = sum_ + z_o[n, here, :].astype(f32)
            out[here, :] = sum_
            return carry

        lax.fori_loop(0, zrow // 32, add_z, 0)

    def output_done():
        ready("v", *load_late)
        reduce.arrived()

        def finish_output(i, carry):
            here = pl.ds(i * 32, 32)
            total = (residual[here, :] + parts[here, :].astype(f32) + landed[0, here, :].astype(f32)
                     + landed[1, here, :].astype(f32)).astype(bf16)
            for s in range(8):
                output[here, spots[s]] = total[:, s * blk:(s + 1) * blk]
            return carry

        lax.fori_loop(0, share // 32, finish_output, 0)
        saves.append(copies.local(output, output_to))

    def weight_done(i, target, keep, final):
        def write(n, carry):
            target[pl.ds(side * half + n * 16, 16), :] = keep[pl.ds(n * 16, 16), mine]
            target[pl.ds((1 - side) * half + n * 16, 16), :] = side_f[i, pl.ds(n * 16, 16), :]
            return carry

        lax.fori_loop(0, half // 16, write, 0)
        if final is not None:
            saves.append(copies.local(target, final))

    task("dq", (), send_tokens)
    task("g1", (), send_gate_deep)
    task("u0", (), send_up, 0)
    task("u1", (), send_up, 1)
    task("f", (), send_near)
    task("zg0", (), send_gate)
    task("xd", (), send_down)
    task("ot", (), send_out, "ot", 0, 1 - side)
    task("om", (), send_out, "om", 1, side)
    task("qc", (), query_give)
    task("r1", (), reduce_start)
    task("zg1", ("g1",), gate_sum)
    task("qk", ("qc",), query_keep)
    task("dn1", ("f", "dq"), first_product)
    task("N", ("dn1",), first_norm)
    task("h0", ("N",), gain_hop, 0)
    task("zu0", ("u0",), up_sum, 0)
    task("zu1", ("u1",), up_sum, 1)
    task("r2", ("r1",), reduce.relayed)
    task("h1", ("h0",), gain_hop, 1)
    task("qy1", ("qk", "qs1"), query_side, 1)
    task("qy0", ("qk", "qs0"), query_side, 0)
    task("os", ("ot",), out_side)
    task("h2", ("h1",), gain_hop, 2)
    task("xg", ("zg0", "zg1"), high_sum, "xg", keep_g, high_g, 1)
    task("h3", ("h2",), gain_hop, 3)
    task("O", ("om",), out_mine)
    task("h4", ("h3",), gain_hop, 4)
    task("R", ("r2",), output_done)
    task("h5", ("h4",), gain_hop, 5)
    task("oz", ("os", "O"), out_rows)
    task("Q", ("qy1", "qy0", "qd"), query_done)
    task("xu", ("zu0", "zu1"), high_sum, "xu", keep_u, high_u, 2)
    task("OD", ("oz",), out_done)
    task("DD", ("xd",), weight_done, 0, down, keep_d, down_to)
    task("GD", ("xg",), weight_done, 1, gate, keep_g, gate_to)
    task("UD", ("xu",), weight_done, 2, up, keep_u, None)
    greet(place, (1, 2, 3, CORE, SIDE, DEEP))
    names = list(tasks)
    for index in BACK_ORDER or range(len(names)):
        needs, action = tasks.pop(names[index])
        for need in needs:
            for item in items.get(need, ()):
                copies.got(item)
        action()
    assert not tasks
    for copy in saves:
        copy.wait()
    copies.finish()


def back_last(grad_q, dres, inputs, gain, query_0, query_y, query_x, query_xy, residual, gain_part,
              rows_first, sums, down_sums, gate_sums, out_sums, fparts, ident):
    share, width = dres.shape
    hidden = sums.shape[1]
    blk = width // 8
    half = hidden // 2
    local = grad_q.shape[1]
    V = pltpu.VMEM
    S = jax.ShapeDtypeStruct
    return pl.pallas_call(
        back_last_kernel,
        out_shape=(S((hidden, blk), bf16),) * 3
        + (S((width // 4, blk), f32), S((blk, local), f32), S((share, width), f32), S((share, width), bf16),
           S((2, width), f32)),
        in_specs=[VM] * 3 + [ANY] * 13,
        out_specs=(ANY, ANY, VM, VM, VM, ANY, ANY, VM),
        scratch_shapes=[
            V((share, width), f32), V((share, width), bf16), V((share, width), f32), V((4, blk, width), bf16),
            V((hidden, blk), bf16), V((hidden, blk), bf16), V((share, width), f32), V((share, width), bf16),
            V((half, 2 * blk), bf16), V((hidden, 2 * blk), bf16), V((hidden, 2 * blk), bf16), V((hidden, blk), bf16),
            V((hidden, 2 * blk), bf16),
            V((half, 2 * blk), bf16), V((half, 2 * blk), bf16), V((3, half, blk), bf16),
            V((width, width // 2), bf16), V((2, width, blk), bf16), V((width, blk), bf16),
            V((3, width // 4, blk), bf16),
            V((width // 2, local), bf16), V((width // 2, local), bf16), V((width // 2, local), bf16),
            V((2, blk, local), bf16), V((blk, local), bf16),
            V((share * 4, width), bf16), V((2, share // 2, width), bf16), V((2, share, width), bf16),
            V((share, width), bf16), V((share * 4, width), bf16), V((4, blk, width), bf16), V((share, width), f32),
            V((2, width), f32), V((5, 2, width), f32),
            DMA((48,)), DMA((48,)), DMA((20,))],
        compiler_params=params(ident, 63 << 20), name="back_last",
    )(grad_q, gain, gain_part, dres, inputs, residual, query_0, query_y, query_x, query_xy,
      rows_first, sums, down_sums, gate_sums, out_sums, fparts)


def hand_over_kernel(*refs):
    count = (len(refs) - 5) // 3
    sources, targets, held = refs[:count], refs[count:2 * count], refs[2 * count:3 * count]
    widened = refs[3 * count:3 * count + 3]
    in_sems, out_sems = refs[-2:]
    loads = [pltpu.make_async_copy(sources[n], held[n], in_sems.at[n]) for n in range(count)]
    for load in loads:
        load.start()
    stores = []
    for n in range(count):
        loads[n].wait()
        holder = held[n]
        if n >= count - 3:
            holder = widened[n - count + 3]
            holder[...] = held[n][...].astype(f32)
        store = pltpu.make_async_copy(holder, targets[n], out_sems.at[n])
        store.start()
        stores.append(store)
    for store in stores:
        store.wait()


def hand_over(*arrays):
    n = len(arrays)
    wide = [jax.ShapeDtypeStruct(a.shape, f32) for a in arrays[-3:]]
    return pl.pallas_call(
        hand_over_kernel,
        out_shape=tuple([jax.ShapeDtypeStruct(a.shape, a.dtype) for a in arrays[:-3]] + wide),
        in_specs=[ANY] * n, out_specs=(ANY,) * n,
        scratch_shapes=[pltpu.VMEM(a.shape, a.dtype) for a in arrays]
        + [pltpu.VMEM(w.shape, f32) for w in wide] + [DMA((n,)), DMA((n,))],
        compiler_params=pltpu.CompilerParams(vmem_limit_bytes=63 << 20), name="hand_over")(*arrays)


def contract(left, right, left_dim, right_dim):
    return lax.dot_general(
        left, right, (((left_dim,), (right_dim,)), ((), ())), preferred_element_type=jnp.float32
    )


def root_inverse(values):
    return lax.rsqrt(jnp.mean(values * values, axis=-1, keepdims=True) + epsilon)


def norm_back(grad_normed, scaled, inverse, gain):
    grad_scaled = grad_normed * gain
    grad_values = inverse * (
        grad_scaled - scaled * jnp.mean(grad_scaled * scaled, axis=-1, keepdims=True)
    )
    return (grad_values, jnp.sum(grad_normed * scaled, axis=0))


def plain_body(
    inputs,
    keys_values,
    segment_ids,
    gain_first,
    gain_second,
    w_query,
    w_out,
    w_gate,
    w_up,
    w_down,
    cotangent,
):
    query_full, out_full = (
        lax.all_gather(w_query, "dp", axis=0, tiled=True),
        lax.all_gather(w_out, "dp", axis=1, tiled=True),
    )
    gate_full, up_full, down_full = (
        lax.all_gather(w_gate, "dp", axis=0, tiled=True),
        lax.all_gather(w_up, "dp", axis=0, tiled=True),
        lax.all_gather(w_down, "dp", axis=1, tiled=True),
    )
    tokens = inputs.astype(jnp.float32)
    inverse_first = root_inverse(tokens)
    scaled_first = tokens * inverse_first
    normed_first = (scaled_first * gain_first).astype(jnp.bfloat16)
    rows_first = lax.all_gather(normed_first, "mp", axis=0, tiled=True)
    queries = contract(rows_first, query_full, 1, 0).astype(jnp.bfloat16)
    seq_len = rows_first.shape[0]
    local_width = queries.shape[1]
    head_count = local_width // HEAD_DIM
    block_rows = min(512, seq_len)
    block_count = seq_len // block_rows
    score_scale = HEAD_DIM ** (-0.5)
    key_heads = keys_values[:, 0, :].reshape(seq_len, head_count, HEAD_DIM)
    value_heads = keys_values[:, 1, :].reshape(seq_len, head_count, HEAD_DIM)
    segments = segment_ids[0]
    key_pos = jnp.arange(seq_len, dtype=jnp.int32)

    def block_scores(first_row):
        query_block = lax.dynamic_slice_in_dim(queries, first_row, block_rows, 0).reshape(
            block_rows, head_count, HEAD_DIM
        )
        scores = (
            jnp.einsum("qhd,khd->hqk", query_block, key_heads, preferred_element_type=jnp.float32)
            * score_scale
        )
        query_pos = first_row + jnp.arange(block_rows, dtype=jnp.int32)
        query_seg = lax.dynamic_slice_in_dim(segments, first_row, block_rows, 0)
        allowed = (query_pos[:, None] >= key_pos[None, :]) & (
            query_seg[:, None] == segments[None, :]
        )
        return (query_block, jnp.where(allowed[None], scores, -1e30))

    def forward_block(block_index):
        query_block, scores = block_scores(block_index * block_rows)
        row_max = jnp.max(scores, axis=-1, keepdims=True)
        raised = jnp.exp(scores - row_max)
        row_total = jnp.sum(raised, axis=-1, keepdims=True)
        weights_low = (raised / row_total).astype(jnp.bfloat16)
        blended = jnp.einsum(
            "hqk,khd->qhd", weights_low, value_heads, preferred_element_type=jnp.float32
        )
        return (
            blended.reshape(block_rows, local_width).astype(jnp.bfloat16),
            (row_max + jnp.log(row_total))[..., 0],
        )

    context_blocks, log_totals = lax.map(forward_block, jnp.arange(block_count, dtype=jnp.int32))
    context = context_blocks.reshape(seq_len, local_width)
    attn_part = lax.psum_scatter(
        contract(context, out_full, 1, 0), "mp", scatter_dimension=0, tiled=True
    )
    residual = tokens + attn_part
    inverse_second = root_inverse(residual)
    scaled_second = residual * inverse_second
    normed_second = (scaled_second * gain_second).astype(jnp.bfloat16)
    rows_second = lax.all_gather(normed_second, "mp", axis=0, tiled=True)
    gate_proj = contract(rows_second, gate_full, 1, 0)
    up_proj = contract(rows_second, up_full, 1, 0)
    sigmoid_gate = jax.nn.sigmoid(gate_proj)
    silu_gate = gate_proj * sigmoid_gate
    hidden = (silu_gate * up_proj).astype(jnp.bfloat16)
    ffn_part = lax.psum_scatter(
        contract(hidden, down_full, 1, 0).astype(jnp.bfloat16),
        "mp",
        scatter_dimension=0,
        tiled=True,
    ).astype(jnp.float32)
    output = (residual + ffn_part).astype(jnp.bfloat16)
    cot_rows = lax.all_gather(cotangent, "mp", axis=0, tiled=True)
    grad_down_w = contract(hidden, cot_rows, 0, 0)
    grad_hidden = contract(cot_rows, down_full, 1, 1)
    grad_gate_act = (
        grad_hidden * up_proj * sigmoid_gate * (1.0 + gate_proj * (1.0 - sigmoid_gate))
    ).astype(jnp.bfloat16)
    grad_up_act = (grad_hidden * silu_gate).astype(jnp.bfloat16)
    grad_gate_w = contract(rows_second, grad_gate_act, 0, 0)
    grad_up_w = contract(rows_second, grad_up_act, 0, 0)
    grad_normed_second = lax.psum_scatter(
        contract(grad_gate_act, gate_full, 1, 1) + contract(grad_up_act, up_full, 1, 1),
        "mp",
        scatter_dimension=0,
        tiled=True,
    )
    grad_from_norm, gain_second_part = norm_back(
        grad_normed_second, scaled_second, inverse_second, gain_second
    )
    grad_residual = cotangent.astype(jnp.float32) + grad_from_norm
    attn_cot = lax.all_gather(grad_residual.astype(jnp.bfloat16), "mp", axis=0, tiled=True)
    grad_out_w = contract(context, attn_cot, 0, 0)
    grad_context = contract(attn_cot, out_full, 1, 1).astype(jnp.bfloat16)

    def backward_block(state_pair, block_index):
        grad_keys, grad_values = state_pair
        first_row = block_index * block_rows
        query_block, scores = block_scores(first_row)
        log_total = lax.dynamic_index_in_dim(log_totals, block_index, 0, keepdims=False)
        weights = jnp.exp(scores - log_total[..., None])
        grad_block = lax.dynamic_slice_in_dim(grad_context, first_row, block_rows, 0).reshape(
            block_rows, head_count, HEAD_DIM
        )
        grad_weights = jnp.einsum(
            "qhd,khd->hqk", grad_block, value_heads, preferred_element_type=jnp.float32
        )
        spread = jnp.sum(weights * grad_weights, axis=-1, keepdims=True)
        grad_scores = (weights * (grad_weights - spread)).astype(jnp.bfloat16)
        grad_query_block = (
            jnp.einsum("hqk,khd->qhd", grad_scores, key_heads, preferred_element_type=jnp.float32)
            * score_scale
        ).astype(jnp.bfloat16)
        grad_keys = (
            grad_keys
            + jnp.einsum(
                "hqk,qhd->khd", grad_scores, query_block, preferred_element_type=jnp.float32
            )
            * score_scale
        )
        grad_values = grad_values + jnp.einsum(
            "hqk,qhd->khd",
            weights.astype(jnp.bfloat16),
            grad_block,
            preferred_element_type=jnp.float32,
        )
        return ((grad_keys, grad_values), grad_query_block.reshape(block_rows, local_width))

    zero_state = jnp.zeros((seq_len, head_count, HEAD_DIM), jnp.float32)
    (grad_keys, grad_values), grad_query_blocks = lax.scan(
        backward_block, (zero_state, zero_state), jnp.arange(block_count, dtype=jnp.int32)
    )
    grad_queries = grad_query_blocks.reshape(seq_len, local_width)
    grad_kv = jnp.stack(
        [grad_keys.reshape(seq_len, local_width), grad_values.reshape(seq_len, local_width)], axis=1
    )
    grad_query_w = contract(rows_first, grad_queries, 0, 0)
    grad_normed_first = lax.psum_scatter(
        contract(grad_queries, query_full, 1, 1).astype(jnp.bfloat16),
        "mp",
        scatter_dimension=0,
        tiled=True,
    ).astype(jnp.float32)
    grad_from_first, gain_first_part = norm_back(
        grad_normed_first, scaled_first, inverse_first, gain_first
    )
    grad_input = grad_residual + grad_from_first
    gain_first_sum, gain_second_sum = lax.psum((gain_first_part, gain_second_part), ("dp", "mp"))
    query_shard, out_shard, gate_shard, up_shard, down_shard = (
        lax.psum_scatter(
            grad_query_w.astype(jnp.bfloat16), "dp", scatter_dimension=0, tiled=True
        ).astype(jnp.float32),
        lax.psum_scatter(
            grad_out_w.astype(jnp.bfloat16), "dp", scatter_dimension=1, tiled=True
        ).astype(jnp.float32),
        lax.psum_scatter(
            grad_gate_w.astype(jnp.bfloat16), "dp", scatter_dimension=0, tiled=True
        ).astype(jnp.float32),
        lax.psum_scatter(
            grad_up_w.astype(jnp.bfloat16), "dp", scatter_dimension=0, tiled=True
        ).astype(jnp.float32),
        lax.psum_scatter(
            grad_down_w.astype(jnp.bfloat16), "dp", scatter_dimension=1, tiled=True
        ).astype(jnp.float32),
    )
    return (
        output,
        grad_input,
        grad_kv,
        gain_first_sum,
        gain_second_sum,
        query_shard,
        out_shard,
        gate_shard,
        up_shard,
        down_shard,
    )


def fast_body(inputs, keys_values, segment_ids, gain_first, gain_second, w_query, w_out, w_gate,
              w_up, w_down, cotangent):
    (rows_first, cots, gate_here, up_here, down_here, out_whole, queries, context_own, log_totals, residual,
     normed_second, inputs_here, cot_here, gain_one, gain_two, keys, values, starts) = front_call(
        inputs, cotangent, gain_first[None], gain_second[None], w_query, w_out, w_gate.T, w_up.T, w_down,
        keys_values, segment_ids, 1)
    grad_normed_second, query_0, query_y, ffn_parts, ffn_sums = ffn_call(
        normed_second, w_query, cots, down_here, gate_here, up_here, 3)
    (grad_residual, gain_second_part, query_x, query_xy, grad_queries, grad_kv, down_sums, gate_sums,
     out_sums) = back_first(
        grad_normed_second, residual, cot_here, gain_two, context_own, queries, keys, values, log_totals, starts,
        query_0, query_y, out_whole, ffn_sums, 5)
    down_shard, gate_shard, up_shard, out_shard, query_shard, grad_input, output, gains = back_last(
        grad_queries, grad_residual, inputs_here, gain_one, query_0, query_y, query_x, query_xy, residual,
        gain_second_part, rows_first, ffn_sums, down_sums, gate_sums, out_sums, ffn_parts, 6)
    (grad_kv, grad_input, output, out_shard, query_shard, down_shard, gate_shard, up_shard) = hand_over(
        grad_kv, grad_input, output, out_shard, query_shard, down_shard, gate_shard, up_shard)
    return (output, grad_input, grad_kv, gains[0], gains[1], query_shard, out_shard,
            gate_shard.T, up_shard.T, down_shard)


def solution(mesh):
    in_specs = (
        P(("dp", "mp"), None),
        P("dp", None, "mp"),
        P("dp", None),
        P(),
        P(),
        P("dp", "mp"),
        P("mp", "dp"),
        P("dp", "mp"),
        P("dp", "mp"),
        P("mp", "dp"),
        P(("dp", "mp"), None),
    )
    out_specs = (
        P(("dp", "mp"), None),
        P(("dp", "mp"), None),
        P("dp", None, "mp"),
        P(),
        P(),
        P("dp", "mp"),
        P("mp", "dp"),
        P("dp", "mp"),
        P("dp", "mp"),
        P("mp", "dp"),
    )
    fast = mesh.shape["dp"] == 8 and mesh.shape["mp"] == 4
    body = fast_body if fast else plain_body
    return jax.shard_map(body, mesh=mesh, in_specs=in_specs, out_specs=out_specs, check_vma=False)
```
